32 devices in a mesh: dp: 4 (over y, x), row: 4 (over z), col: 2 (over core).
Axes of the slice: x: 2, y: 2, z: 4, core: 2. Of those that a mesh axis runs over, the one named last changes fastest.
Arguments:
- layer_input: bfloat16 [8192, 768], P(('dp', 'row'), 'col'), may hold values from -6 to 6
- cotangent: bfloat16 [8192, 768], P(('dp', 'row'), 'col'), may hold values from -6 to 6
- labels: int32 [4], P('dp'), may hold values from 0 to 2
- block_ids: int32 [8192], P('dp'), may hold values from 0 to 63, never falling along the last dimension, each value on 1 to 256 neighbouring positions
- w_query: bfloat16 [768, 768], P('row', 'col'), may hold values from -0.21875 to 0.21875
- b_query: bfloat16 [768], P('col'), may hold values from -1.75 to 1.75
- w_key: bfloat16 [768, 768], P('row', 'col'), may hold values from -0.21875 to 0.21875
- w_value: bfloat16 [768, 768], P('row', 'col'), may hold values from -0.21875 to 0.21875
- b_value: bfloat16 [768], P('col'), may hold values from -0.125 to 0.125
- w_output: bfloat16 [768, 768], P('col', 'row'), may hold values from -6 to 6
- b_output: bfloat16 [768], P('col'), may hold values from -1.75 to 1.75
- ln1_gain: bfloat16 [768], P('col'), may hold values from 0.5 to 1.5
- ln1_bias: bfloat16 [768], P('col'), may hold values from -1.75 to 1.75
- w_inner: bfloat16 [768, 3072], P('row', 'col'), may hold values from -0.21875 to 0.21875
- b_inner: bfloat16 [3072], P('col'), may hold values from -1.75 to 1.75
- w_outer: bfloat16 [3072, 768], P('col', 'row'), may hold values from -0.109375 to 0.109375
- b_outer: bfloat16 [768], P('col'), may hold values from -1.75 to 1.75
- ln2_gain: bfloat16 [768], P('col'), may hold values from 0.5 to 1.5
- ln2_bias: bfloat16 [768], P('col'), may hold values from -1.75 to 1.75
- w_pooler: bfloat16 [768, 768], replicated, may hold values from -0.21875 to 0.21875
- b_pooler: bfloat16 [768], replicated, may hold values from -1.75 to 1.75
- w_classes: bfloat16 [768, 3], replicated, may hold values from -0.4375 to 0.4375
- b_classes: bfloat16 [3], replicated, may hold values from -3 to 3
Outputs:
- output: bfloat16 [8192, 768], P(('dp', 'row'), 'col')
- logits: float32 [4, 3], P('dp')
- grad_input: bfloat16 [8192, 768], P(('dp', 'row'), 'col')
- grad_w_query: float32 [768, 768], P('row', 'col')
- grad_b_query: float32 [768], P('col')
- grad_w_key: float32 [768, 768], P('row', 'col')
- grad_w_value: float32 [768, 768], P('row', 'col')
- grad_b_value: float32 [768], P('col')
- grad_w_output: float32 [768, 768], P('col', 'row')
- grad_b_output: float32 [768], P('col')
- grad_ln1_gain: float32 [768], P('col')
- grad_ln1_bias: float32 [768], P('col')
- grad_w_inner: float32 [768, 3072], P('row', 'col')
- grad_b_inner: float32 [3072], P('col')
- grad_w_outer: float32 [3072, 768], P('col', 'row')
- grad_b_outer: float32 [768], P('col')
- grad_ln2_gain: float32 [768], P('col')
- grad_ln2_bias: float32 [768], P('col')
- grad_w_pooler: float32 [768, 768], replicated
- grad_b_pooler: float32 [768], replicated
- grad_w_classes: float32 [768, 3], replicated
- grad_b_classes: float32 [3], replicated
The draws below stay inside these ranges and needn't reach their ends.
Inputs may be any that keep to these rules, and one draw needn't show every extreme that they name: `block_ids`: block numbers never fall along the tokens; a block holds 1 to 256 tokens and some block holds exactly 256.
All inputs are finite; a program needn't handle non-finite values.
Results may differ from the reference program's by a relative error of at most 0.02.
Values may be sent and summed in bfloat16 or wider, within the bound.
A program may use at most 192 MiB of HBM per device.

```python
import math
import jax
import jax.numpy as jnp
import numpy as np
from jax import lax

D = 768
HEADS = 12
HEAD = 64
FF = 3072
CLASSES = 3
BLOCK = 256
TOK_DEV = 512
SEQS = 4
TOKENS = 8192
N_DP = 4
N_ROW = 4


def touch_ends(values, rng, low, top_value):
    extent = values.shape
    spot = [jax.random.randint(jax.random.fold_in(rng, axis), (), 0, extent[axis]) for axis in range(len(extent))]
    values = values.at[tuple(spot)].set(low)
    longest = extent.index(max(extent))
    spot[longest] = (spot[longest] + 1) % extent[longest]
    return values.at[tuple(spot)].set(top_value)


def steps_of(own_key, extent, cuts, low, high):
    factor_of = 1.0
    for dim, parts in cuts:
        heights = jax.random.uniform(jax.random.fold_in(jax.random.fold_in(own_key, 6), dim), (parts,), jnp.float32, low / len(cuts), high / len(cuts))
        factor_of = factor_of * jnp.repeat(jnp.exp(heights), extent[dim] // parts).reshape((-1,) + (1,) * (len(extent) - 1 - dim))
    return factor_of


def profile(count, total, reach, skew):
    portions = [(1 << 20) // math.isqrt(rank ** skew) + 1 for rank in range(2, count + 1)]
    rest, holding = total - reach - (count - 1), [1] * (count - 1)
    while rest > 0:
        candidates = [i for i in range(count - 1) if holding[i] < reach]
        pool, left = sum([portions[i] for i in candidates]), rest
        for i in candidates:
            addition = min(reach - holding[i], max(1, left * portions[i] // pool), rest)
            holding[i] = holding[i] + addition
            rest = rest - addition
    return np.array([reach] + holding)


def uneven(stream_key, count, total, most, skew):
    if count == 2:
        one = jax.random.randint(stream_key, (), max(1, total - most), min(most, total - 1) + 1)
        return jnp.stack([one, total - one])
    tallies = jnp.asarray(profile(count, total, most, skew), jnp.int32)
    twos = (count - 1) // 2
    source_of, sink = tallies[1:1 + 2 * twos:2], tallies[2:2 + 2 * twos:2]
    margin = jnp.minimum(source_of - 1, most - sink)
    passed = jax.random.randint(jax.random.fold_in(stream_key, 1), (twos,), 0, 1 << 20) % (margin + 1)
    tallies = tallies.at[1:1 + 2 * twos:2].set(source_of - passed).at[2:2 + 2 * twos:2].set(sink + passed)
    return tallies[jax.random.permutation(jax.random.fold_in(stream_key, 2), count)]


def bell_draw(own_key, shape, spread, reach, shards=(), held_as=jnp.bfloat16):
    factor_of = steps_of(own_key, shape, shards, -0.22, 0.18) if shards else 1.0
    entries = jax.random.normal(own_key, shape, jnp.float32) * spread * factor_of
    return jnp.minimum(jnp.maximum(entries, -reach), reach).astype(held_as)


def setup_inputs(seed: int = 0) -> dict:
    arg_keys = jax.random.split(jax.random.key(seed), 24)
    return {
        "layer_input": bell_draw(arg_keys[0], (TOKENS, D), 1.0, 6.0, ((0, 16), (1, 2))),
        "cotangent": bell_draw(arg_keys[1], (TOKENS, D), 1.0, 6.0, ((0, 16), (1, 2))),
        "labels": touch_ends(jax.random.randint(arg_keys[2], (SEQS,), 0, CLASSES), jax.random.fold_in(arg_keys[2], 1), 0, CLASSES - 1).astype(jnp.int32),
        "block_ids": jnp.searchsorted(jnp.cumsum(uneven(arg_keys[3], 2 * TOKENS // BLOCK, TOKENS, BLOCK, 1)), jnp.arange(TOKENS), side="right").astype(jnp.int32),
        "w_query": bell_draw(arg_keys[4], (D, D), D ** -0.5, 0.21875, ((0, 4), (1, 2))),
        "b_query": bell_draw(arg_keys[5], (D,), 0.3, 1.75, ((0, 2),)),
        "w_key": bell_draw(arg_keys[6], (D, D), D ** -0.5, 0.21875, ((0, 4), (1, 2))),
        "w_value": bell_draw(arg_keys[7], (D, D), D ** -0.5, 0.21875, ((0, 4), (1, 2))),
        "b_value": bell_draw(arg_keys[8], (D,), 0.02, 0.125, ((0, 2),)),
        "w_output": bell_draw(arg_keys[9], (D, D), 1.0 ** -0.5, 6.0, ((0, 2), (1, 4))),
        "b_output": bell_draw(arg_keys[10], (D,), 0.3, 1.75, ((0, 2),)),
        "ln1_gain": jnp.clip(1.0 + 0.1 * jax.random.normal(arg_keys[11], (D,), jnp.float32), 0.5, 1.5).astype(jnp.bfloat16),
        "ln1_bias": bell_draw(arg_keys[12], (D,), 0.3, 1.75, ((0, 2),)),
        "w_inner": bell_draw(arg_keys[13], (D, FF), D ** -0.5, 0.21875, ((0, 4), (1, 2))),
        "b_inner": bell_draw(arg_keys[14], (FF,), 0.3, 1.75, ((0, 2),)),
        "w_outer": bell_draw(arg_keys[15], (FF, D), FF ** -0.5, 0.109375, ((0, 2), (1, 4))),
        "b_outer": bell_draw(arg_keys[16], (D,), 0.3, 1.75, ((0, 2),)),
        "ln2_gain": jnp.clip(1.0 + 0.1 * jax.random.normal(arg_keys[17], (D,), jnp.float32), 0.5, 1.5).astype(jnp.bfloat16),
        "ln2_bias": bell_draw(arg_keys[18], (D,), 0.3, 1.75, ((0, 2),)),
        "w_pooler": bell_draw(arg_keys[19], (D, D), D ** -0.5, 0.21875),
        "b_pooler": bell_draw(arg_keys[20], (D,), 0.3, 1.75),
        "w_classes": bell_draw(arg_keys[21], (D, CLASSES), (D // 4) ** -0.5, 0.4375),
        "b_classes": bell_draw(arg_keys[22], (CLASSES,), 0.5, 3.0),
    }


highest = lax.Precision.HIGHEST
epsilon = 1e-05
root_half = 0.7071067811865476

@jax.custom_vjp
def low(v):
    return lax.optimization_barrier(v.astype(jnp.bfloat16)).astype(jnp.float32)

@jax.custom_vjp
def low_back(v):
    return v

def low_keep(v):
    return (low(v), None)

def low_pass(kept, grad):
    return (grad,)

def back_keep(v):
    return (v, None)

def back_low(kept, grad):
    return (low(grad),)
low.defvjp(low_keep, low_pass)
low_back.defvjp(back_keep, back_low)

def matmul(left, right):
    return jnp.dot(left, right, precision=highest, preferred_element_type=jnp.float32)

def layer_norm(hidden, gain, shift):
    row_mean = lax.optimization_barrier(jnp.mean(hidden, axis=-1, keepdims=True))
    row_var = lax.optimization_barrier(jnp.mean(hidden * hidden, axis=-1, keepdims=True)) - row_mean * row_mean
    inv_scale = lax.rsqrt(row_var + epsilon)
    return (hidden - row_mean) * inv_scale * gain + shift

def gelu_exact(values):
    return values * 0.5 * (1.0 + lax.erf(values * root_half))

def attention(queries, keys_proj, values_proj, seq_ids):
    length = queries.shape[0]
    query_rows = min(512, length)
    score_scale = HEAD ** (-0.5)
    keys3 = keys_proj.reshape(length, HEADS, HEAD)
    values3 = values_proj.reshape(length, HEADS, HEAD)

    def one_block(block_item):
        query_block, query_ids = block_item
        scores = jnp.einsum('qhd,khd->hqk', query_block, keys3, precision=highest) * score_scale
        scores = low_back(scores)
        allowed = seq_ids[None, :] <= query_ids[:, None]
        scores = jnp.where(allowed[None], scores, -1e+30)
        probs = jax.nn.softmax(scores, axis=-1)
        return jnp.einsum('hqk,khd->qhd', low(probs), values3, precision=highest)
    blocks = lax.map(jax.checkpoint(one_block), (queries.reshape(length // query_rows, query_rows, HEADS, HEAD), seq_ids.reshape(length // query_rows, query_rows)))
    return blocks.reshape(length, HEADS * HEAD)

def forward(params, tokens, seq_ids, label):
    w_query, b_query, w_key, w_value, b_value, w_output, b_output, ln1_gain, ln1_bias, w_inner, b_inner, w_outer, b_outer, ln2_gain, ln2_bias, w_pooler, b_pooler, w_classes, b_classes = params
    queries = low(low_back(matmul(tokens, w_query) + b_query))
    keys_proj = low(low_back(matmul(tokens, w_key)))
    values_proj = low(low_back(matmul(tokens, w_value) + b_value))
    context = low(low_back(attention(queries, keys_proj, values_proj, seq_ids)))
    hidden_one = tokens + low_back(matmul(context, w_output)) + b_output
    stream = layer_norm(hidden_one, ln1_gain, ln1_bias)
    pre_act = low_back(matmul(low(stream), w_inner) + b_inner)
    activ = low(gelu_exact(pre_act))
    hidden_two = stream + low_back(matmul(activ, w_outer)) + b_outer
    result = layer_norm(hidden_two, ln2_gain, ln2_bias)
    first_row = low(result[0:1])
    pooled = jnp.tanh(matmul(first_row, w_pooler) + b_pooler)
    logits = matmul(pooled, w_classes) + b_classes
    onehot = (jnp.arange(logits.shape[1]).astype(jnp.int32) == label).astype(jnp.float32)
    loss = jax.nn.logsumexp(logits[0]) - jnp.sum(logits[0] * onehot)
    return ((result, loss), logits)

def reference(layer_input, cotangent, labels, block_ids, w_query, b_query, w_key, w_value, b_value, w_output, b_output, ln1_gain, ln1_bias, w_inner, b_inner, w_outer, b_outer, ln2_gain, ln2_bias, w_pooler, b_pooler, w_classes, b_classes):
    params = tuple((arr.astype(jnp.float32) for arr in (w_query, b_query, w_key, w_value, b_value, w_output, b_output, ln1_gain, ln1_bias, w_inner, b_inner, w_outer, b_outer, ln2_gain, ln2_bias, w_pooler, b_pooler, w_classes, b_classes)))
    length = TOK_DEV * N_ROW
    inputs_seq = layer_input.astype(jnp.float32).reshape(N_DP, length, D)
    cots_seq = cotangent.astype(jnp.float32).reshape(N_DP, length, D)
    ids_seq = block_ids.reshape(N_DP, length)

    def one_sequence(summed, seq_item):
        seq_input, seq_cot, seq_ids, label = seq_item

        def seq_forward(param_tuple, tokens):
            return forward(param_tuple, tokens, seq_ids, label)
        primal, pullback, seq_logits = jax.vjp(seq_forward, params, seq_input, has_aux=True)
        grad_params, grad_tokens = pullback((seq_cot, jnp.float32(1.0)))
        summed = jax.tree.map(lambda left, right: left + right, summed, grad_params)
        return (summed, (primal[0].astype(jnp.bfloat16), seq_logits, grad_tokens.astype(jnp.bfloat16)))
    zeros = jax.tree.map(jnp.zeros_like, params)
    summed, (outputs, all_logits, grad_inputs) = lax.scan(one_sequence, zeros, (inputs_seq, cots_seq, ids_seq, labels))
    return (outputs.reshape(N_DP * length, D), all_logits.reshape(N_DP, CLASSES), grad_inputs.reshape(N_DP * length, D), summed[0], summed[1], summed[2], summed[3], summed[4], summed[5], summed[6], summed[7], summed[8], summed[9], summed[10], summed[11], summed[12], summed[13], summed[14], summed[15], summed[16], summed[17], summed[18])
```

```python
import functools

import jax
import jax.numpy as jnp
from jax import lax
from jax.experimental import pallas as pl
from jax.experimental.pallas import tpu as pltpu
from jax.sharding import PartitionSpec as P

HEAD = 64


highest = lax.Precision.HIGHEST
epsilon = 1e-05
root_half = 0.7071067811865476
inv_root_tau = 0.3989422804014327
masked_score = -1e30


def gelu_exact(values):
    return values * 0.5 * (1.0 + lax.erf(values * root_half))


def gelu_slope(values):
    return 0.5 * (1.0 + lax.erf(values * root_half)) + values * inv_root_tau * jnp.exp(
        -0.5 * values * values
    )


def project(left, right):
    return jnp.dot(left, right, preferred_element_type=jnp.float32)


def contract_first(left, right):
    return lax.dot_general(
        left, right, (((0,), (0,)), ((), ())), preferred_element_type=jnp.float32
    )


def contract_last(left, right):
    return lax.dot_general(
        left, right, (((1,), (1,)), ((), ())), preferred_element_type=jnp.float32
    )


def gather_features(values):
    return lax.all_gather(values, "col", axis=1, tiled=True)


def sum_features(values):
    return lax.psum_scatter(
        values.astype(jnp.bfloat16), "col", scatter_dimension=1, tiled=True
    ).astype(jnp.float32)


def feature_totals(first_part, second_part):
    return lax.psum((jnp.sum(first_part, axis=1), jnp.sum(second_part, axis=1)), "col")


def norm_forward(hidden, gain, shift, features):
    row_total, square_total = feature_totals(hidden, hidden * hidden)
    row_mean = row_total / features
    row_var = square_total / features - row_mean * row_mean
    inv_scale = lax.rsqrt(row_var + epsilon)
    normed = (hidden - row_mean[:, None]) * inv_scale[:, None]
    return (normed * gain + shift, normed, inv_scale)


def norm_backward(grad, normed, inv_scale, gain, features):
    scaled = grad * gain
    first_total, second_total = feature_totals(scaled, scaled * normed)
    return inv_scale[:, None] * (
        scaled - (first_total / features)[:, None] - normed * (second_total / features)[:, None]
    )


def key_split(piece_rows, rows_dev):
    return (piece_rows // rows_dev, rows_dev)


def body(
    layer_input,
    cotangent,
    labels,
    block_ids,
    w_query,
    b_query,
    w_key,
    w_value,
    b_value,
    w_output,
    b_output,
    ln1_gain,
    ln1_bias,
    w_inner,
    b_inner,
    w_outer,
    b_outer,
    ln2_gain,
    ln2_bias,
    w_pooler,
    b_pooler,
    w_classes,
    b_classes,
):
    f32 = jnp.float32
    bf16 = jnp.bfloat16
    rows_dev, feat_col = layer_input.shape
    heads_col = feat_col // HEAD
    features = feat_col * lax.axis_size("col")
    row_index = lax.axis_index("row")
    col_index = lax.axis_index("col")
    seq_index = lax.axis_index("dp")
    seq_count = lax.axis_size("dp")
    score_scale = HEAD ** (-0.5)
    query_ids = lax.dynamic_slice_in_dim(block_ids, row_index * rows_dev, rows_dev)
    last_query = query_ids[rows_dev - 1]
    wq_full, wk_full, wv_full, w1_full = (
        lax.all_gather(w_query, "row", axis=0, tiled=True),
        lax.all_gather(w_key, "row", axis=0, tiled=True),
        lax.all_gather(w_value, "row", axis=0, tiled=True),
        lax.all_gather(w_inner, "row", axis=0, tiled=True),
    )
    wo_full, w2_full = (
        lax.all_gather(w_output, "row", axis=1, tiled=True),
        lax.all_gather(w_outer, "row", axis=1, tiled=True),
    )
    input_whole = gather_features(layer_input)
    queries = (project(input_whole, wq_full) + b_query.astype(f32)).astype(bf16)
    keys_local = project(input_whole, wk_full).astype(bf16)
    values_local = (project(input_whole, wv_full) + b_value.astype(f32)).astype(bf16)
    queries3 = queries.reshape(rows_dev, heads_col, HEAD)
    start_state = (
        jnp.full((heads_col, rows_dev), masked_score, f32),
        jnp.zeros((heads_col, rows_dev), f32),
        jnp.zeros((heads_col, rows_dev, HEAD), f32),
    )
    running = start_state
    keys_piece = lax.all_gather(keys_local, "row", axis=0, tiled=True)
    values_piece = lax.all_gather(values_local, "row", axis=0, tiled=True)
    piece_rows = keys_piece.shape[0]
    number, block_rows = key_split(piece_rows, rows_dev)
    keys4 = keys_piece.reshape(number, block_rows, heads_col, HEAD)
    values4 = values_piece.reshape(number, block_rows, heads_col, HEAD)
    piece_ids = block_ids.reshape(number, block_rows)

    def attend_block_work(state, block_item):
        peak_score, row_mass, accum = state
        keys3, values3, key_ids = block_item
        scores = (
            jnp.einsum("qhd,khd->hqk", queries3, keys3, preferred_element_type=f32) * score_scale
        )
        allowed = (key_ids[None, :] <= query_ids[:, None])[None]
        block_top = jnp.max(jnp.where(allowed, scores, masked_score), axis=2)
        new_peak = jnp.maximum(peak_score, block_top)
        weights = jnp.where(allowed, jnp.exp(scores - new_peak[:, :, None]), 0.0)
        factor = jnp.exp(peak_score - new_peak)
        row_mass = row_mass * factor + jnp.sum(weights, axis=2)
        accum = accum * factor[:, :, None] + jnp.einsum(
            "hqk,khd->hqd", weights.astype(bf16), values3, preferred_element_type=f32
        )
        return (new_peak, row_mass, accum)

    def attend_block_step(state, block_item):
        state = lax.cond(
            block_item[2][0] > last_query, lambda st, item: st, attend_block_work, state, block_item
        )
        return (state, None)

    running, unused = lax.scan(attend_block_step, running, (keys4, values4, piece_ids))
    peak_score, row_mass, accum = running
    mixed = accum / row_mass[:, :, None]
    log_mass = peak_score + jnp.log(row_mass)
    context_low = mixed.transpose(1, 0, 2).reshape(rows_dev, feat_col).astype(bf16)
    attn_branch = sum_features(project(context_low, wo_full))
    hidden_one = layer_input.astype(f32) + attn_branch + b_output.astype(f32)
    gain_one = ln1_gain.astype(f32)
    stream, normed_one, inv_one = norm_forward(hidden_one, gain_one, ln1_bias.astype(f32), features)
    stream_whole = gather_features(stream.astype(bf16))
    pre_act = project(stream_whole, w1_full) + b_inner.astype(f32)
    activ = gelu_exact(pre_act).astype(bf16)
    ffn_branch = sum_features(project(activ, w2_full))
    hidden_two = stream + ffn_branch + b_outer.astype(f32)
    gain_two = ln2_gain.astype(f32)
    result, normed_two, inv_two = norm_forward(hidden_two, gain_two, ln2_bias.astype(f32), features)
    output = result.astype(bf16)
    row_zero = (row_index == 0).astype(f32)
    pool_input = gather_features(output[0:1])
    pooled = jnp.tanh(project(pool_input, w_pooler) + b_pooler.astype(f32))
    classes_f32 = w_classes.astype(f32)
    logits_own = jnp.dot(pooled, classes_f32, precision=highest) + b_classes.astype(f32)
    onehot = (jnp.arange(w_classes.shape[1]) == labels[0]).astype(f32)
    grad_logits = jax.nn.softmax(logits_own, axis=-1) - onehot[None, :]
    g_w_classes = jnp.dot(pooled.T, grad_logits, precision=highest)
    g_b_classes = grad_logits[0]
    grad_pre_pool = jnp.dot(grad_logits, classes_f32.T, precision=highest) * (1.0 - pooled * pooled)
    g_b_pooler = grad_pre_pool[0]
    g_w_pooler = jnp.dot(pool_input.astype(f32).T, grad_pre_pool, precision=highest)
    grad_first = jnp.dot(grad_pre_pool, w_pooler.astype(f32).T, precision=highest)
    first_col = lax.dynamic_slice_in_dim(grad_first[0], col_index * feat_col, feat_col)
    grad_result = cotangent.astype(f32).at[0].add(first_col * row_zero)
    logits_table = lax.dynamic_update_slice_in_dim(
        jnp.zeros((seq_count, w_classes.shape[1]), f32), logits_own * row_zero, seq_index, 0
    )
    g_ln2_gain = jnp.sum(grad_result * normed_two, axis=0)
    g_ln2_bias = jnp.sum(grad_result, axis=0)
    grad_hidden_two = norm_backward(grad_result, normed_two, inv_two, gain_two, features)
    g_b_outer = jnp.sum(grad_hidden_two, axis=0)
    branch_two_whole = gather_features(grad_hidden_two.astype(bf16))
    g_w_outer_full = contract_first(activ, branch_two_whole)
    grad_act = contract_last(branch_two_whole, w2_full)
    grad_pre = (grad_act * gelu_slope(pre_act)).astype(bf16)
    g_b_inner = jnp.sum(grad_pre.astype(f32), axis=0)
    g_w_inner_full = contract_first(stream_whole, grad_pre)
    grad_stream = grad_hidden_two + sum_features(contract_last(grad_pre, w1_full))
    g_ln1_gain = jnp.sum(grad_stream * normed_one, axis=0)
    g_ln1_bias = jnp.sum(grad_stream, axis=0)
    grad_hidden_one = norm_backward(grad_stream, normed_one, inv_one, gain_one, features)
    g_b_output = jnp.sum(grad_hidden_one, axis=0)
    branch_one_whole = gather_features(grad_hidden_one.astype(bf16))
    g_w_output_full = contract_first(context_low, branch_one_whole)
    grad_context = contract_last(branch_one_whole, wo_full).astype(bf16)
    grad_ctx3 = grad_context.reshape(rows_dev, heads_col, HEAD)
    delta = jnp.sum(grad_ctx3.astype(f32).transpose(1, 0, 2) * mixed, axis=2)

    def score_grads(queries_blk, grad_ctx_blk, keys3, values3, allowed, lse_blk, delta_blk):
        scores = (
            jnp.einsum("qhd,khd->hqk", queries_blk, keys3, preferred_element_type=f32) * score_scale
        )
        probs = jnp.where(allowed, jnp.exp(scores - lse_blk[:, :, None]), 0.0)
        grad_probs = jnp.einsum("qhd,khd->hqk", grad_ctx_blk, values3, preferred_element_type=f32)
        grad_scores = (probs * (grad_probs - delta_blk[:, :, None])).astype(bf16)
        return (probs, grad_scores)

    zero_q = jnp.zeros((rows_dev, heads_col, HEAD), f32)
    keys_piece = lax.all_gather(keys_local, "row", axis=0, tiled=True)
    values_piece = lax.all_gather(values_local, "row", axis=0, tiled=True)
    piece_rows = keys_piece.shape[0]
    number, block_rows = key_split(piece_rows, rows_dev)
    keys4 = keys_piece.reshape(number, block_rows, heads_col, HEAD)
    values4 = values_piece.reshape(number, block_rows, heads_col, HEAD)
    piece_ids = block_ids.reshape(number, block_rows)

    def make_block_work(accum_q, block_item):
        keys3, values3, key_ids = block_item
        allowed = (key_ids[None, :] <= query_ids[:, None])[None]
        probs, grad_scores = score_grads(
            queries3, grad_ctx3, keys3, values3, allowed, log_mass, delta
        )
        accum_q = (
            accum_q
            + jnp.einsum("hqk,khd->qhd", grad_scores, keys3, preferred_element_type=f32)
            * score_scale
        )
        part_k = (
            jnp.einsum("hqk,qhd->khd", grad_scores, queries3, preferred_element_type=f32)
            * score_scale
        )
        part_v = jnp.einsum(
            "hqk,qhd->khd", probs.astype(bf16), grad_ctx3, preferred_element_type=f32
        )
        return (accum_q, (part_k, part_v))

    def block_skip(accum_q, block_item):
        empty = jnp.zeros((block_rows, heads_col, HEAD), f32)
        return (accum_q, (empty, empty))

    def make_block_step(accum_q, block_item):
        return lax.cond(
            block_item[2][0] > last_query, block_skip, make_block_work, accum_q, block_item
        )

    grad_q = zero_q
    grad_q, (parts_k, parts_v) = lax.scan(make_block_step, grad_q, (keys4, values4, piece_ids))
    parts_k = parts_k.reshape(piece_rows, feat_col)
    parts_v = parts_v.reshape(piece_rows, feat_col)
    grad_k_all = parts_k
    grad_v_all = parts_v
    back_result = (grad_q, grad_k_all, grad_v_all)
    grad_q3, grad_k_all, grad_v_all = back_result
    grad_keys, grad_values = (
        lax.psum_scatter(
            grad_k_all.astype(jnp.bfloat16), "row", scatter_dimension=0, tiled=True
        ).astype(jnp.float32),
        lax.psum_scatter(
            grad_v_all.astype(jnp.bfloat16), "row", scatter_dimension=0, tiled=True
        ).astype(jnp.float32),
    )
    queries_grad = grad_q3.reshape(rows_dev, feat_col).astype(bf16)
    keys_grad = grad_keys.astype(bf16)
    values_grad = grad_values.astype(bf16)
    g_b_query = jnp.sum(queries_grad.astype(f32), axis=0)
    g_b_value = jnp.sum(values_grad.astype(f32), axis=0)
    g_w_query_full = contract_first(input_whole, queries_grad)
    g_w_key_full = contract_first(input_whole, keys_grad)
    g_w_value_full = contract_first(input_whole, values_grad)
    grad_input_whole = (
        contract_last(queries_grad, wq_full)
        + contract_last(keys_grad, wk_full)
        + contract_last(values_grad, wv_full)
    )
    grad_input = (grad_hidden_one + sum_features(grad_input_whole)).astype(bf16)
    in_rows = w_query.shape[0]
    out_cols = w_output.shape[1]
    (
        sum_wq,
        sum_wk,
        sum_wv,
        sum_w1,
        sum_wo,
        sum_w2,
        g_w_pooler,
        g_b_pooler,
        g_w_classes,
        g_b_classes,
        g_b_query,
        g_b_value,
        g_b_output,
        g_ln1_gain,
        g_ln1_bias,
        g_b_inner,
        g_b_outer,
        g_ln2_gain,
        g_ln2_bias,
        logits_all,
    ) = lax.psum(
        (
            g_w_query_full,
            g_w_key_full,
            g_w_value_full,
            g_w_inner_full,
            g_w_output_full,
            g_w_outer_full,
            g_w_pooler * row_zero,
            g_b_pooler * row_zero,
            g_w_classes * row_zero,
            g_b_classes * row_zero,
            g_b_query,
            g_b_value,
            g_b_output,
            g_ln1_gain,
            g_ln1_bias,
            g_b_inner,
            g_b_outer,
            g_ln2_gain,
            g_ln2_bias,
            logits_table,
        ),
        ("dp", "row"),
    )
    row_start = row_index * in_rows
    col_start = row_index * out_cols
    g_w_query = lax.dynamic_slice_in_dim(sum_wq, row_start, in_rows, 0)
    g_w_key = lax.dynamic_slice_in_dim(sum_wk, row_start, in_rows, 0)
    g_w_value = lax.dynamic_slice_in_dim(sum_wv, row_start, in_rows, 0)
    g_w_inner = lax.dynamic_slice_in_dim(sum_w1, row_start, in_rows, 0)
    g_w_output = lax.dynamic_slice_in_dim(sum_wo, col_start, out_cols, 1)
    g_w_outer = lax.dynamic_slice_in_dim(sum_w2, col_start, out_cols, 1)
    logits = lax.dynamic_slice_in_dim(logits_all, seq_index, 1, 0)
    return (
        output,
        logits,
        grad_input,
        g_w_query,
        g_b_query,
        g_w_key,
        g_w_value,
        g_b_value,
        g_w_output,
        g_b_output,
        g_ln1_gain,
        g_ln1_bias,
        g_w_inner,
        g_b_inner,
        g_w_outer,
        g_b_outer,
        g_ln2_gain,
        g_ln2_bias,
        g_w_pooler,
        g_b_pooler,
        g_w_classes,
        g_b_classes,
    )


MESH_IDS = pl.DeviceIdType.MESH
ROWS = 4
VMEM_BYTES = 64000 * 1024


def place():
    return lax.axis_index("dp"), lax.axis_index("row"), lax.axis_index("col")


class Links:
    def __init__(self, send, recv):
        self.send, self.recv = send, recv
        self.sends, self.recvs, self.open = 0, 0, []

    def slots(self, count):
        base = self.recvs
        self.recvs += count
        return base

    def push(self, source, target, slot, device, when=None):
        copy = pltpu.make_async_remote_copy(
            src_ref=source,
            dst_ref=target,
            send_sem=self.send.at[self.sends],
            recv_sem=self.recv.at[slot],
            device_id=device,
            device_id_type=MESH_IDS,
        )
        self.sends += 1
        if when is None:
            copy.start()
        else:
            pl.when(when)(lambda: copy.start())
        self.open.append((copy, when))

    def arrive(self, target, slot, device, when=None):
        copy = pltpu.make_async_remote_copy(
            src_ref=target,
            dst_ref=target,
            send_sem=self.send.at[0],
            recv_sem=self.recv.at[slot],
            device_id=device,
            device_id_type=MESH_IDS,
        )
        if when is None:
            copy.wait_recv()
        else:
            pl.when(when)(lambda: copy.wait_recv())

    def drain(self):
        for copy, when in self.open:
            if when is None:
                copy.wait_send()
            else:
                pl.when(when)(lambda copy=copy: copy.wait_send())
        self.open = []


def meet(devices):
    barrier = pltpu.get_barrier_semaphore()
    for device in devices:
        pl.semaphore_signal(barrier, inc=1, device_id=device, device_id_type=MESH_IDS)
    pl.semaphore_wait(barrier, len(devices))


def within(value):
    return (value >= 0) & (value < ROWS)


def steps_of_line(row):
    for step in (1, 2, 3):
        for way in (1, -1):
            source = row - way * step
            yield step, way, (3 - step if way == 1 else step - 1), source, within(source)


def columns(col, width):
    return pl.ds(pl.multiple_of(col * width, 128), width)


def gather_kernel(widths, x, cot, vec, *refs):
    count = len(widths)
    shards, refs = refs[:count], refs[count:]
    x_all, cot_own, vec_all = refs[:3]
    fulls = refs[3 : 3 + count]
    send, recv, local = refs[3 + count :]
    dp, row, col = place()
    links = Links(send, recv)
    feat = x.shape[1]
    mate = (dp, row, 1 - col)
    at_row = lambda other: (dp, other, col)
    at_dp = lambda flip: (dp ^ flip, row, col)
    meet([at_row(lax.rem(row + k, ROWS)) for k in (1, 2, 3)] + [at_dp(1), at_dp(2), mate])

    half = x.shape[0] // 2
    mine = lax.rem(row + col, 2)
    x_at = lambda k: x_all.at[k, :, columns(col, feat)]
    w_at = lambda i, k, q: fulls[i].at[k, q, :, columns(col, widths[i])]
    row_at = lambda i, k: fulls[i].at[k, :, :, columns(col, widths[i])]
    x_mate_at = lambda k: x_all.at[k, :, columns(1 - col, feat)]
    row_mate_at = lambda i, k: fulls[i].at[k, :, :, columns(1 - col, widths[i])]

    line_x = links.slots(3)
    line_w = [links.slots(3) for _ in widths]
    first_w = [links.slots(3) for _ in widths]
    second_w = [links.slots(6) for _ in widths]
    mate_x = links.slots(4)
    mate_w = [links.slots(4) for _ in widths]
    mate_cot, mate_vec = links.slots(1), links.slots(1)

    copies = [pltpu.make_async_copy(x, x_at(row), local.at[0])]
    copies += [
        pltpu.make_async_copy(shards[i], row_at(i, row), local.at[1 + i]) for i in range(count)
    ]
    copies += [
        pltpu.make_async_copy(
            cot.at[pl.ds(pl.multiple_of(mine * half, 128), half)],
            cot_own.at[:, columns(col, feat)],
            local.at[1 + count],
        ),
        pltpu.make_async_copy(vec, vec_all.at[col], local.at[2 + count]),
    ]

    def relay(step):
        for way in (1, -1):
            held, onward = row - way * (step - 1), row + way
            ok = within(held) & within(onward)
            slot = 3 - step if way == 1 else step - 1
            links.push(x if step == 1 else x_at(held), x_at(held), line_x + slot, at_row(onward), ok)
            for i in range(count):
                source = shards[i].at[dp] if step == 1 else w_at(i, held, dp)
                links.push(source, w_at(i, held, dp), line_w[i] + slot, at_row(onward), ok)

    relay(1)
    links.push(x, x_at(row), mate_x, mate)
    links.push(
        cot.at[pl.ds(pl.multiple_of((1 - mine) * half, 128), half)],
        cot_own.at[:, columns(col, feat)],
        mate_cot,
        mate,
    )
    links.push(vec, vec_all.at[col], mate_vec, mate)
    for i in range(count):
        links.push(shards[i], row_at(i, row), mate_w[i], mate)
    for copy in copies:
        copy.start()
    steps = list(steps_of_line(row))
    turn = lambda i, slot: (1, 2) if (i + slot) % 2 == 0 else (2, 1)
    for step in (1, 2, 3):
        for at_step, way, slot, k, ok in steps:
            if at_step != step:
                continue
            links.arrive(x_at(k), line_x + slot, mate, ok)
            for i in range(count):
                links.arrive(w_at(i, k, dp), line_w[i] + slot, mate, ok)
        if step < 3:
            relay(step + 1)
        for at_step, way, slot, k, ok in steps:
            if at_step != step:
                continue
            links.push(x_at(k), x_at(k), mate_x + 1 + slot, mate, ok)
            for i in range(count):
                one, two = turn(i, slot)
                links.push(w_at(i, k, dp), w_at(i, k, dp), first_w[i] + slot, at_dp(one), ok)
    for slot in range(3):
        k = lax.rem(row + slot + 1, ROWS)
        for i in range(count):
            one, two = turn(i, slot)
            links.arrive(w_at(i, k, dp ^ one), first_w[i] + slot, mate)
            links.push(w_at(i, k, dp), w_at(i, k, dp), second_w[i] + 2 * slot, at_dp(two))
            links.push(
                w_at(i, k, dp ^ one), w_at(i, k, dp ^ one), second_w[i] + 2 * slot + 1, at_dp(two)
            )
    for slot in range(3):
        k = lax.rem(row + slot + 1, ROWS)
        for i in range(count):
            one, two = turn(i, slot)
            links.arrive(w_at(i, k, dp ^ two), second_w[i] + 2 * slot, mate)
            links.arrive(w_at(i, k, dp ^ 3), second_w[i] + 2 * slot + 1, mate)
            links.push(row_at(i, k), row_at(i, k), mate_w[i] + 1 + slot, mate)
    links.arrive(x_mate_at(row), mate_x, mate)
    links.arrive(cot_own.at[:, columns(1 - col, feat)], mate_cot, mate)
    links.arrive(vec_all.at[1 - col], mate_vec, mate)
    for i in range(count):
        links.arrive(row_mate_at(i, row), mate_w[i], mate)
    for slot in range(3):
        k = lax.rem(row + slot + 1, ROWS)
        links.arrive(x_mate_at(k), mate_x + 1 + slot, mate)
        for i in range(count):
            links.arrive(row_mate_at(i, k), mate_w[i] + 1 + slot, mate)
    for copy in copies:
        copy.wait()
    links.drain()


IN_VMEM = pl.BlockSpec(memory_space=pltpu.VMEM)
IN_PLACE = pl.BlockSpec(memory_space=pl.ANY)


def comm_params(number):
    return pltpu.CompilerParams(
        collective_id=number, has_side_effects=True, vmem_limit_bytes=VMEM_BYTES
    )


def gather_all(x, cot, vec, shards):
    widths = [shard.shape[1] for shard in shards]
    rows, feat = x.shape
    low = x.dtype
    part = shards[0].shape[0] // 4
    shapes = [
        jax.ShapeDtypeStruct((ROWS, rows, 2 * feat), low),
        jax.ShapeDtypeStruct((rows // 2, 2 * feat), low),
        jax.ShapeDtypeStruct((2,) + vec.shape, vec.dtype),
    ] + [jax.ShapeDtypeStruct((ROWS, 4, part, 2 * width), low) for width in widths]
    return pl.pallas_call(
        functools.partial(gather_kernel, widths),
        out_shape=shapes,
        in_specs=[IN_VMEM] * (3 + len(shards)),
        out_specs=[IN_PLACE] * len(shapes),
        scratch_shapes=[
            pltpu.SemaphoreType.DMA((160,)),
            pltpu.SemaphoreType.DMA((96,)),
            pltpu.SemaphoreType.DMA((16,)),
        ],
        compiler_params=comm_params(1),
        name="gather_all",
    )(x, cot, vec, *[shard.reshape(4, part, -1) for shard in shards])


def swap_kernel(split, *refs):
    blocks, out_blocks = refs[0], refs[1 + split]
    send, recv, local = refs[-3:]
    dp, row, col = place()
    links = Links(send, recv)
    mate = (dp, row, 1 - col)
    peers = [lax.rem(row + k, ROWS) for k in (1, 2, 3)]
    meet([(dp, peer, col) for peer in peers] + ([mate] if split else []))
    base = links.slots(4)
    for number, peer in enumerate(peers):
        links.push(blocks.at[peer], out_blocks.at[row], base + 2 - number, (dp, peer, col))
    keep = [pltpu.make_async_copy(blocks.at[row], out_blocks.at[row], local.at[0])]
    if split:
        whole, halves = refs[1], refs[3]
        half, feat = whole.shape[0], whole.shape[1] // 2
        mine = lax.rem(row + col, 2)
        own_rows = pl.ds(pl.multiple_of(mine * half, 128), half)
        keep.append(
            pltpu.make_async_copy(
                whole.at[:, columns(col, feat)], halves.at[own_rows], local.at[1]
            )
        )
        links.push(whole.at[:, columns(1 - col, feat)], halves.at[own_rows], base + 3, mate)
        other_rows = pl.ds(pl.multiple_of((1 - mine) * half, 128), half)
    for copy in keep:
        copy.start()
    for number, peer in enumerate(peers):
        links.arrive(out_blocks.at[peer], base + number, mate)
    if split:
        links.arrive(halves.at[other_rows], base + 3, mate)
    for copy in keep:
        copy.wait()
    links.drain()


def swap_blocks(blocks, number, whole=None):
    split = 0 if whole is None else 1
    shapes = [jax.ShapeDtypeStruct(blocks.shape, blocks.dtype)]
    if split:
        shapes.append(
            jax.ShapeDtypeStruct((2 * whole.shape[0], whole.shape[1] // 2), whole.dtype)
        )
    return pl.pallas_call(
        functools.partial(swap_kernel, split),
        out_shape=shapes,
        in_specs=[IN_VMEM] * (1 + split),
        out_specs=[IN_VMEM] * (1 + split),
        scratch_shapes=[
            pltpu.SemaphoreType.DMA((4,)),
            pltpu.SemaphoreType.DMA((4,)),
            pltpu.SemaphoreType.DMA((2,)),
        ],
        compiler_params=comm_params(number),
        name="swap_blocks",
    )(blocks, *([whole] if split else []))


def add_into(total, *others):
    def one(step, carry):
        value = total[step].astype(jnp.float32)
        for other in others:
            value = value + other[step].astype(jnp.float32)
        total[step] = value.astype(total.dtype)
        return carry

    lax.fori_loop(0, total.shape[0], one, 0)


def reduce_kernel(count, *refs):
    grads, refs = refs[:count], refs[count:]
    gq, dx, vec = refs[:3]
    outs, refs = refs[3 : 3 + count], refs[3 + count :]
    out_q, out_x, out_vec = refs[:3]
    refs = refs[3:]
    sums, refs = refs[:count], refs[count:]
    first, refs = refs[: count + 1], refs[count + 1 :]
    second, refs = refs[: count + 1], refs[count + 1 :]
    lines, refs = refs[:count], refs[count:]
    sum_q, all_q, sum_x, line_x, vec_mate, vec_line, vec_flat, send, recv = refs
    dp, row, col = place()
    links = Links(send, recv)
    mate = (dp, row, 1 - col)
    peers = [lax.rem(row + k, ROWS) for k in (1, 2, 3)]
    at_row = lambda other: (dp, other, col)
    at_dp = lambda flip: (dp ^ flip, row, col)
    owner = row // 2
    meet(
        [at_row(peer) for peer in peers]
        + [at_dp(1), at_dp(2), mate]
        + [(dp, peer, 1 - col) for peer in peers]
    )
    widths = [grad.shape[3] // 2 for grad in grads]
    feat = dx.shape[2] // 2
    turns = [(1, 2) if i % 2 == 0 else (2, 1) for i in range(count + 1)]

    slot_x, slot_q, slot_v = links.slots(1), links.slots(1), links.slots(1)
    slot_g = [links.slots(1) for _ in grads]
    links.push(vec, vec_mate, slot_v, mate)
    links.push(dx.at[:, :, columns(1 - col, feat)], sum_x, slot_x, mate)
    links.push(gq.at[:, 1 - col], sum_q, slot_q, mate)
    for i in range(count):
        links.push(grads[i].at[:, :, :, columns(1 - col, widths[i])], sums[i], slot_g[i], mate)

    links.arrive(vec_mate, slot_v, mate)
    out_vec[...] = vec[...] + vec_mate[...]
    slot_vl = links.slots(3)
    for n, peer in enumerate(peers):
        links.push(out_vec, vec_line.at[2 - n], slot_vl + 2 - n, at_row(peer))

    links.arrive(sum_x, slot_x, mate)
    tile = dx.shape[1] // 4

    def add_x(step, carry):
        rows = pl.ds(pl.multiple_of((step % 4) * tile, 128), tile)
        sum_x[step // 4, rows] = (
            sum_x[step // 4, rows].astype(jnp.float32)
            + dx[step // 4, rows, columns(col, feat)].astype(jnp.float32)
        ).astype(sum_x.dtype)
        return carry

    lax.fori_loop(0, 16, add_x, 0)
    slot_xl = links.slots(3)
    for n, peer in enumerate(peers):
        links.push(sum_x.at[peer], line_x.at[2 - n], slot_xl + 2 - n, at_row(peer))

    links.arrive(sum_q, slot_q, mate)

    def add_q(step, carry):
        sum_q[step] = (
            sum_q[step].astype(jnp.float32) + gq[step, col].astype(jnp.float32)
        ).astype(sum_q.dtype)
        return carry

    lax.fori_loop(0, 4, add_q, 0)
    slot_ql = links.slots(4)
    side = lax.rem(row, 2)
    own_part = all_q.at[side, pl.ds(2 * col, 2)]
    at_home = owner == col

    def keep_own():
        own_part[...] = sum_q[row]

    pl.when(at_home)(keep_own)
    links.push(sum_q.at[row], own_part, slot_ql + 2 * side + col, mate, jnp.logical_not(at_home))
    for peer in peers:
        links.push(sum_q.at[peer], own_part, slot_ql + 2 * side + col, (dp, peer, owner))

    def send_first(i, total):
        one, two = turns[i]
        base = links.slots(2)
        links.push(total.at[:, dp ^ one], first[i].at[0], base, at_dp(one))
        links.push(total.at[:, dp ^ 3], first[i].at[1], base + 1, at_dp(one))
        return base

    def send_second(i, total, base):
        one, two = turns[i]
        links.arrive(first[i].at[1], base + 1, mate)
        add_into(total.at[:, dp ^ two], first[i].at[1])
        slot = links.slots(1)
        links.push(total.at[:, dp ^ two], second[i], slot, at_dp(two))
        links.arrive(first[i].at[0], base, mate)
        add_into(total.at[:, dp], first[i].at[0])
        return slot

    def share(i, out):
        one, two = turns[i]
        base = links.slots(3)
        links.push(out.at[dp], out.at[dp], base, at_dp(two))
        links.push(out.at[dp], out.at[dp], base + 1, at_dp(one))
        links.arrive(out.at[dp ^ two], base, mate)
        links.push(out.at[dp ^ two], out.at[dp ^ two], base + 2, at_dp(one))
        return base

    def shared(i, out, base):
        one, two = turns[i]
        links.arrive(out.at[dp ^ one], base + 1, mate)
        links.arrive(out.at[dp ^ 3], base + 2, mate)

    started = []
    for i in range(count):
        links.arrive(sums[i], slot_g[i], mate)
        width = widths[i]

        def add_g(step, carry, i=i, width=width):
            k, q = step // 4, step % 4
            sums[i][k, q] = (
                sums[i][k, q].astype(jnp.float32)
                + grads[i][k, q, :, columns(col, width)].astype(jnp.float32)
            ).astype(sums[i].dtype)
            return carry

        lax.fori_loop(0, 16, add_g, 0)
        started.append(send_first(i, sums[i]))
    for j in range(2):
        for e in range(2):
            here = (row == 2 * col + j) & (col == e)
            links.arrive(
                all_q.at[j, pl.ds(2 * e, 2)], slot_ql + 2 * j + e, mate, jnp.logical_not(here)
            )
    started.append(send_first(count, all_q))

    for n in range(3):
        links.arrive(vec_line.at[n], slot_vl + n, mate)
    vec_sum = out_vec[...] + vec_line[0] + vec_line[1] + vec_line[2]
    vec_mate[...] = vec_sum
    slot_v1 = links.slots(2)
    links.push(vec_mate, vec_flat.at[0], slot_v1, at_dp(1))

    totals = list(sums) + [all_q]
    started = [send_second(i, totals[i], started[i]) for i in range(count + 1)]
    slot_z = []
    for i in range(count + 1):
        links.arrive(second[i], started[i], mate)
        add_into(totals[i].at[:, dp], second[i])
        if i < count:
            base = links.slots(3)
            for n, peer in enumerate(peers):
                links.push(
                    sums[i].at[peer, dp], lines[i].at[2 - n], base + 2 - n, at_row(peer)
                )
            slot_z.append(base)
        else:
            for j in range(2):
                out_q[dp, j] = all_q[j, dp]
            slot_share_q = share(count, out_q)

    links.arrive(vec_flat.at[0], slot_v1, mate)
    vec_line[0] = vec_mate[...] + vec_flat[0]
    links.push(vec_line.at[0], vec_flat.at[1], slot_v1 + 1, at_dp(2))

    for n in range(3):
        links.arrive(line_x.at[n], slot_xl + n, mate)

    def finish_x(step, carry):
        rows = pl.ds(pl.multiple_of(step * tile, 128), tile)
        value = sum_x[row, rows].astype(jnp.float32)
        for n in range(3):
            value = value + line_x[n, rows].astype(jnp.float32)
        out_x[rows] = value.astype(out_x.dtype)
        return carry

    lax.fori_loop(0, 4, finish_x, 0)
    shares = []
    for i in range(count):
        for n in range(3):
            links.arrive(lines[i].at[n], slot_z[i] + n, mate)
        value = sums[i][row, dp].astype(jnp.float32)
        for n in range(3):
            value = value + lines[i][n].astype(jnp.float32)
        outs[i][dp] = value.astype(outs[i].dtype)
        shares.append(share(i, outs[i]))
    links.arrive(vec_flat.at[1], slot_v1 + 1, mate)
    vec_total = vec_line[0] + vec_flat[1]
    for i in range(count):
        shared(i, outs[i], shares[i])
    shared(count, out_q, slot_share_q)
    links.drain()
    out_vec[...] = vec_total


def reduce_all(grads, gq, dx, vec):
    count = len(grads)
    low = dx.dtype
    depth = grads[0].shape[0]
    part = depth // ROWS // 4
    widths = [grad.shape[1] // 2 for grad in grads]
    wide = gq.shape[1]
    rows, feat = dx.shape[0] // ROWS, dx.shape[1] // 2
    blocks = lambda lead, width: (lead, 4, part, width)
    outs = [jax.ShapeDtypeStruct((4, part, width), low) for width in widths] + [
        jax.ShapeDtypeStruct((4, 2, part, wide), low),
        jax.ShapeDtypeStruct((rows, feat), low),
        jax.ShapeDtypeStruct(vec.shape, vec.dtype),
    ]
    every = [(ROWS, width) for width in widths] + [(2, wide)]
    return pl.pallas_call(
        functools.partial(reduce_kernel, count),
        out_shape=outs,
        in_specs=[IN_VMEM] * (count + 3),
        out_specs=[IN_VMEM] * len(outs),
        scratch_shapes=[pltpu.VMEM(blocks(ROWS, width), low) for width in widths]
        + [pltpu.VMEM((2, lead, part, width), low) for lead, width in every]
        + [pltpu.VMEM((lead, part, width), low) for lead, width in every]
        + [pltpu.VMEM((3, part, width), low) for width in widths]
        + [
            pltpu.VMEM((ROWS, 2, part, wide), low),
            pltpu.VMEM((2, 4, part, wide), low),
            pltpu.VMEM((ROWS, rows, feat), low),
            pltpu.VMEM((3, rows, feat), low),
            pltpu.VMEM(vec.shape, vec.dtype),
            pltpu.VMEM((3,) + vec.shape, vec.dtype),
            pltpu.VMEM((2,) + vec.shape, vec.dtype),
            pltpu.SemaphoreType.DMA((96,)),
            pltpu.SemaphoreType.DMA((96,)),
        ],
        compiler_params=comm_params(4),
        name="reduce_all",
    )(
        *[grad.reshape(ROWS, 4, part, 2 * width) for grad, width in zip(grads, widths)],
        gq.reshape(ROWS, 2, 2, part, wide),
        dx.reshape(ROWS, rows, 2 * feat),
        vec,
    )


TILE = 256
NEAR = 3


def nt(left, right):
    return lax.dot_general(
        left, right, (((1,), (1,)), ((), ())), preferred_element_type=jnp.float32
    )


def nn(left, right):
    return jnp.dot(left, right, preferred_element_type=jnp.float32)


def attend_kernel(
    heads, x, weights, bias_q, bias_v, ids_col, ids_row,
    q_out, k_out, kt_out, v_out, vt_out, mixed_out, low_out, lse_out,
):
    width = heads * HEAD
    row_tiles = x.shape[0] // TILE
    col = lax.axis_index("col")
    low = x.dtype

    def project_keys(step, carry):
        rows = pl.ds(pl.multiple_of(step * TILE, TILE), TILE)
        both = nn(x[rows], weights[:, width:])
        keys = both[:, :width]
        values = both[:, width:] + bias_v[...]
        keys_t = keys.T
        values_t = values.T
        for h in range(heads):
            part = slice(h * HEAD, (h + 1) * HEAD)
            k_out[h, rows] = keys[:, part].astype(low)
            v_out[h, rows] = values[:, part].astype(low)
            kt_out[h, :, rows] = keys_t[part].astype(low)
            vt_out[h, :, rows] = values_t[part].astype(low)
        return carry

    lax.fori_loop(0, row_tiles, project_keys, 0)
    for j in range(row_tiles // 2):
        block = 2 * j + lax.rem(j + col, 2)
        rows = pl.ds(pl.multiple_of(block * TILE, TILE), TILE)
        query = nn(x[rows], weights[:, :width]) + bias_q[...]
        query = query.astype(low) * jnp.asarray(HEAD**-0.5, low)
        for h in range(heads):
            q_out[h, j] = query[:, h * HEAD : (h + 1) * HEAD]
    for j in range(row_tiles // 2):
        block = 2 * j + lax.rem(j + col, 2)
        rows = pl.ds(pl.multiple_of(block * TILE, TILE), TILE)
        query_ids = ids_row[:, rows]
        tiles = min(2 * j + NEAR, row_tiles)
        length = tiles * TILE
        clear = 2 * j * TILE

        def one_head(h, carry, j=j, query_ids=query_ids, length=length, clear=clear):
            scores = nt(k_out[h, :length], q_out[h, j])
            near = jnp.where(
                ids_col[clear:length] <= query_ids, scores[clear:], masked_score
            )
            top = jnp.max(near, axis=0, keepdims=True)
            if clear:
                top = jnp.maximum(top, jnp.max(scores[:clear], axis=0, keepdims=True))
                weights_far = jnp.exp(scores[:clear] - top)
            weights_near = jnp.exp(near - top)
            mass = jnp.sum(weights_near, axis=0, keepdims=True)
            value = nn(vt_out[h, :, clear:length], weights_near.astype(low))
            if clear:
                mass = mass + jnp.sum(weights_far, axis=0, keepdims=True)
                value = value + nn(vt_out[h, :, :clear], weights_far.astype(low))
            mixed_out[j, h] = value / mass
            lse_out[j, h] = top + jnp.log(mass)
            return carry

        lax.fori_loop(0, heads, one_head, 0)
        low_out[j] = (
            jnp.concatenate([mixed_out[j, h] for h in range(heads)], axis=0).T.astype(low)
        )


def attend(x, weights, bias_q, bias_v, ids, heads):
    length = x.shape[0]
    blocks = length // TILE // 2
    low, f32 = x.dtype, jnp.float32
    shape = jax.ShapeDtypeStruct
    return pl.pallas_call(
        functools.partial(attend_kernel, heads),
        out_shape=[
            shape((heads, blocks, TILE, HEAD), low),
            shape((heads, length, HEAD), low),
            shape((heads, HEAD, length), low),
            shape((heads, length, HEAD), low),
            shape((heads, HEAD, length), low),
            shape((blocks, heads, HEAD, TILE), f32),
            shape((blocks, TILE, heads * HEAD), low),
            shape((blocks, heads, 1, TILE), f32),
        ],
        in_specs=[IN_VMEM] * 6,
        out_specs=[IN_VMEM] * 8,
        compiler_params=pltpu.CompilerParams(vmem_limit_bytes=VMEM_BYTES),
        name="attend",
    )(x, weights, bias_q, bias_v, ids.reshape(-1, 1), ids.reshape(1, -1))


def attend_back_kernel(
    heads, grad_ctx, q, k, kt, v, mixed, lse, ids_col, ids_row, grads, dk, dv
):
    length = k.shape[1]
    row_tiles = length // TILE
    width = heads * HEAD
    low = q.dtype
    col = lax.axis_index("col")
    dk[...] = jnp.zeros_like(dk)
    dv[...] = jnp.zeros_like(dv)
    for j in range(row_tiles // 2):
        block = 2 * j + lax.rem(j + col, 2)
        rows = pl.ds(pl.multiple_of(block * TILE, TILE), TILE)
        other = pl.ds(pl.multiple_of((4 * j + 1 - block) * TILE, TILE), TILE)
        query_ids = ids_row[:, rows]
        tiles = min(2 * j + NEAR, row_tiles)
        length_j = tiles * TILE
        clear = 2 * j * TILE
        grad_t = grad_ctx[j].astype(jnp.float32).T
        parts = []
        for h in range(heads):
            part = slice(h * HEAD, (h + 1) * HEAD)
            grad_h = grad_ctx[j, :, part]
            delta = jnp.sum(grad_t[part] * mixed[j, h], axis=0, keepdims=True)
            query = q[h, j]
            dq = jnp.zeros((HEAD, TILE), jnp.float32)
            spans = ([(0, clear)] if clear else []) + [(clear, length_j)]
            for low_end, high_end in spans:
                probs = jnp.exp(nt(k[h, low_end:high_end], query) - lse[j, h])
                if low_end == clear:
                    probs = jnp.where(ids_col[low_end:high_end] <= query_ids, probs, 0.0)
                slope = nt(v[h, low_end:high_end], grad_h) - delta
                grad_scores = (probs * slope).astype(low)
                dv[h, low_end:high_end] += nn(probs.astype(low), grad_h)
                dk[h, low_end:high_end] += nn(grad_scores, query)
                dq = dq + nn(kt[h, :, low_end:high_end], grad_scores)
            parts.append(dq * HEAD**-0.5)
        grads[rows, :width] = jnp.concatenate(parts, axis=0).T.astype(low)
        grads[other, :width] = jnp.zeros((TILE, width), low)

    def write(step, carry):
        rows = pl.ds(pl.multiple_of(step * TILE, TILE), TILE)
        grads[rows, width:] = jnp.concatenate(
            [dk[h, rows] for h in range(heads)] + [dv[h, rows] for h in range(heads)], axis=1
        ).astype(low)
        return carry

    lax.fori_loop(0, row_tiles, write, 0)


def attend_back(grad_ctx, q, k, kt, v, mixed, lse, ids, heads):
    length = k.shape[1]
    low, f32 = q.dtype, jnp.float32
    return pl.pallas_call(
        functools.partial(attend_back_kernel, heads),
        out_shape=jax.ShapeDtypeStruct((length, 3 * heads * HEAD), low),
        in_specs=[IN_VMEM] * 9,
        out_specs=IN_VMEM,
        scratch_shapes=[pltpu.VMEM((heads, length, HEAD), f32)] * 2,
        compiler_params=pltpu.CompilerParams(vmem_limit_bytes=VMEM_BYTES),
        name="attend_back",
    )(grad_ctx, q, k, kt, v, mixed, lse, ids.reshape(-1, 1), ids.reshape(1, -1))


def norm_rows(hidden, gain, shift):
    row_mean = jnp.mean(hidden, axis=1, keepdims=True)
    row_var = jnp.mean(hidden * hidden, axis=1, keepdims=True) - row_mean * row_mean
    inv_scale = lax.rsqrt(row_var + epsilon)
    normed = (hidden - row_mean) * inv_scale
    return normed * gain + shift, normed, inv_scale


def norm_rows_back(grad, normed, inv_scale, gain):
    scaled = grad * gain
    first = jnp.mean(scaled, axis=1, keepdims=True)
    second = jnp.mean(scaled * normed, axis=1, keepdims=True)
    return inv_scale * (scaled - first - normed * second)


def fast_body(
    layer_input, cotangent, labels, block_ids, w_query, b_query, w_key, w_value, b_value,
    w_output, b_output, ln1_gain, ln1_bias, w_inner, b_inner, w_outer, b_outer,
    ln2_gain, ln2_bias, w_pooler, b_pooler, w_classes, b_classes,
):
    f32, bf16 = jnp.float32, jnp.bfloat16
    dp, row, col = place()
    rows, feat = layer_input.shape
    features = 2 * feat
    hidden = b_inner.shape[0]
    own = rows // 2
    heads = features // HEAD // ROWS
    wide = heads * HEAD
    vectors = jnp.concatenate(
        [b_query, b_value, b_output, ln1_gain, ln1_bias, b_outer, ln2_gain, ln2_bias, b_inner]
    )
    count = vectors.shape[0] // feat
    vectors = jnp.pad(vectors.reshape(count, feat), ((0, -count % 16), (0, 0)))
    shards = [
        jnp.concatenate([w_query, w_key, w_value], axis=1),
        w_output.T,
        w_inner,
        w_outer.T,
    ]
    x_all, cot, vec_all, w_qkv, w_o, w_1, w_2 = gather_all(
        layer_input, cotangent, vectors, shards
    )
    x_all = x_all.reshape(ROWS * rows, features)
    w_qkv = w_qkv.reshape(features, 2, 3, 2, wide)
    home, side = row // 2, lax.rem(row, 2)
    w_heads = lax.dynamic_slice(
        w_qkv, (0, home, 0, side, 0), (features, 1, 3, 1, wide)
    ).reshape(features, 3 * wide)
    w_o = w_o.reshape(features, features)
    w_1 = w_1.reshape(features, 2 * hidden)
    w_2 = w_2.reshape(features, 2 * hidden)
    vec_all = vec_all.astype(f32)
    take = lambda start, number=1: vec_all[:, start : start + number].reshape(1, -1)
    bias_q = lax.dynamic_slice(take(0), (0, row * wide), (1, wide))
    bias_v = lax.dynamic_slice(take(1), (0, row * wide), (1, wide))
    bias_o, gain_one, shift_one, bias_2, gain_two, shift_two = [take(i) for i in range(2, 8)]
    bias_1 = take(8, count - 8)

    q, k, kt, v, vt, mixed, context_own, lse = attend(
        x_all, w_heads, bias_q, bias_v, block_ids, heads
    )
    (context,) = swap_blocks(context_own, 2)
    context = context.transpose(1, 0, 2).reshape(own, features)
    start = row * rows + lax.rem(row + col, 2) * own
    x_own = lax.dynamic_slice_in_dim(x_all, start, own, 0).astype(f32)

    hidden_one = x_own + contract_last(context, w_o) + bias_o
    stream, normed_one, inv_one = norm_rows(hidden_one, gain_one, shift_one)
    stream_low = stream.astype(bf16)
    pre_act = project(stream_low, w_1) + bias_1
    activ = gelu_exact(pre_act).astype(bf16)
    hidden_two = stream + contract_last(activ, w_2) + bias_2
    result, normed_two, inv_two = norm_rows(hidden_two, gain_two, shift_two)
    output = result.astype(bf16)

    holder = ((row == 0) & (col == 0)).astype(f32)
    first = output[0:1]
    pooled = jnp.tanh(project(first, w_pooler) + b_pooler.astype(f32))
    classes = w_classes.astype(f32)
    logits_own = jnp.dot(pooled, classes, precision=highest) + b_classes.astype(f32)
    onehot = (jnp.arange(w_classes.shape[1]) == labels[0]).astype(f32)
    grad_logits = jax.nn.softmax(logits_own, axis=-1) - onehot[None, :]
    grad_pre_pool = jnp.dot(grad_logits, classes.T, precision=highest) * (1.0 - pooled * pooled)
    grad_first = jnp.dot(grad_pre_pool, w_pooler.astype(f32).T, precision=highest)
    grad_result = cot.astype(f32).at[0].add(grad_first[0] * holder)

    total = lambda values: jnp.sum(values, axis=0)
    g_ln2_gain, g_ln2_bias = total(grad_result * normed_two), total(grad_result)
    grad_hidden_two = norm_rows_back(grad_result, normed_two, inv_two, gain_two)
    g_b_outer = total(grad_hidden_two)
    branch_two = grad_hidden_two.astype(bf16)
    g_w2 = contract_first(branch_two, activ)
    grad_pre = (project(branch_two, w_2) * gelu_slope(pre_act)).astype(bf16)
    g_b_inner = total(grad_pre.astype(f32))
    g_w1 = contract_first(stream_low, grad_pre)
    grad_stream = grad_hidden_two + contract_last(grad_pre, w_1)
    g_ln1_gain, g_ln1_bias = total(grad_stream * normed_one), total(grad_stream)
    grad_hidden_one = norm_rows_back(grad_stream, normed_one, inv_one, gain_one)
    g_b_output = total(grad_hidden_one)
    branch_one = grad_hidden_one.astype(bf16)
    g_wo = contract_first(branch_one, context)
    grad_context = project(branch_one, w_o).astype(bf16)
    grad_blocks = grad_context.reshape(own, ROWS, wide).transpose(1, 0, 2)
    grad_ctx, output = swap_blocks(grad_blocks, 3, output)

    grads_low = attend_back(grad_ctx, q, k, kt, v, mixed, lse, block_ids, heads)
    g_qkv = contract_first(x_all, grads_low).astype(bf16)
    grad_x = contract_last(grads_low, w_heads)
    tokens = grad_x.shape[0]
    grad_x = lax.dynamic_update_slice_in_dim(
        grad_x, lax.dynamic_slice_in_dim(grad_x, start, own, 0) + grad_hidden_one, start, 0
    ).astype(bf16)
    bias_sums = total(grads_low.astype(f32))
    spread = lambda part: lax.dynamic_update_slice(
        jnp.zeros((features,), f32), part, (row * wide,)
    )
    classes_count = w_classes.shape[1]
    tail = jnp.pad(
        jnp.concatenate([logits_own[0], grad_logits[0]]) * holder, (0, 128 - 2 * classes_count)
    )
    table = jnp.concatenate(
        [first[0].astype(f32) * holder, grad_pre_pool[0] * holder, pooled[0] * holder, tail]
    )
    sequences = lax.axis_size("dp")
    table = lax.dynamic_update_slice(
        jnp.zeros((sequences, table.shape[0]), f32), table[None], (dp, 0)
    )
    pieces = [
        spread(bias_sums[:wide]), spread(bias_sums[2 * wide :]), g_b_output, g_ln1_gain,
        g_ln1_bias, g_b_outer, g_ln2_gain, g_ln2_bias, g_b_inner, table.reshape(-1),
    ]
    packed = jnp.concatenate(pieces)
    packed = jnp.pad(packed, (0, -packed.shape[0] % 1024)).reshape(-1, 128)
    s_w1, s_w2, s_wo, s_q, grad_input, sums = reduce_all(
        [g.astype(bf16) for g in (g_w1, g_w2, g_wo)], g_qkv, grad_x, packed
    )
    depth = w_query.shape[0]
    s_q = s_q.transpose(0, 2, 1, 3).reshape(depth, 2, 3, wide).transpose(2, 0, 1, 3)
    s_q = s_q.reshape(3, depth, feat).astype(f32)
    sums = sums.reshape(-1)
    found, at = [], 0
    for piece in pieces:
        found.append(sums[at : at + piece.shape[0]])
        at += piece.shape[0]
    own_part = lambda full: lax.dynamic_slice_in_dim(
        full, col * (full.shape[0] // 2), full.shape[0] // 2
    )
    (
        g_b_query, g_b_value, g_b_output, g_ln1_gain, g_ln1_bias, g_b_outer, g_ln2_gain,
        g_ln2_bias, g_b_inner,
    ) = [own_part(full) for full in found[:-1]]
    table = found[-1].reshape(sequences, -1)
    firsts, pre_pools, pools = [
        table[:, i * features : (i + 1) * features] for i in range(3)
    ]
    ends = table[:, 3 * features :]
    all_grads = ends[:, classes_count : 2 * classes_count]
    logits = lax.dynamic_slice_in_dim(ends[:, :classes_count], dp, 1, 0)
    outer = lambda left, right: jnp.sum(left[:, :, None] * right[:, None, :], axis=0)
    return (
        output, logits, grad_input, s_q[0], g_b_query, s_q[1], s_q[2], g_b_value,
        s_wo.reshape(depth, feat).astype(f32).T, g_b_output, g_ln1_gain, g_ln1_bias,
        s_w1.reshape(depth, hidden).astype(f32), g_b_inner,
        s_w2.reshape(depth, hidden).astype(f32).T, g_b_outer, g_ln2_gain, g_ln2_bias,
        outer(firsts, pre_pools), total(pre_pools), outer(pools, all_grads), total(all_grads),
    )


def is_fast(mesh):
    sizes = mesh.shape
    return sizes["dp"] == 4 and sizes["row"] == ROWS and sizes["col"] == 2


def solution(mesh):
    placed = (
        P(("dp", "row"), "col"),
        P(("dp", "row"), "col"),
        P("dp"),
        P("dp"),
        P("row", "col"),
        P("col"),
        P("row", "col"),
        P("row", "col"),
        P("col"),
        P("col", "row"),
        P("col"),
        P("col"),
        P("col"),
        P("row", "col"),
        P("col"),
        P("col", "row"),
        P("col"),
        P("col"),
        P("col"),
        P(),
        P(),
        P(),
        P(),
    )
    return jax.shard_map(
        fast_body if is_fast(mesh) else body,
        mesh=mesh,
        in_specs=placed,
        out_specs=(
            P(("dp", "row"), "col"),
            P("dp", None),
            P(("dp", "row"), "col"),
            P("row", "col"),
            P("col"),
            P("row", "col"),
            P("row", "col"),
            P("col"),
            P("col", "row"),
            P("col"),
            P("col"),
            P("col"),
            P("row", "col"),
            P("col"),
            P("col", "row"),
            P("col"),
            P("col"),
            P("col"),
            P(),
            P(),
            P(),
            P(),
        ),
        check_vma=False,
    )
```

```python
import functools

import jax
import jax.numpy as jnp
from jax import lax
from jax.experimental import pallas as pl
from jax.experimental.pallas import tpu as pltpu
from jax.sharding import PartitionSpec as P

HEAD = 64


highest = lax.Precision.HIGHEST
epsilon = 1e-05
root_half = 0.7071067811865476
inv_root_tau = 0.3989422804014327
masked_score = -1e30


def gelu_exact(values):
    return values * 0.5 * (1.0 + lax.erf(values * root_half))


def gelu_slope(values):
    return 0.5 * (1.0 + lax.erf(values * root_half)) + values * inv_root_tau * jnp.exp(
        -0.5 * values * values
    )


def project(left, right):
    return jnp.dot(left, right, preferred_element_type=jnp.float32)


def contract_first(left, right):
    return lax.dot_general(
        left, right, (((0,), (0,)), ((), ())), preferred_element_type=jnp.float32
    )


def contract_last(left, right):
    return lax.dot_general(
        left, right, (((1,), (1,)), ((), ())), preferred_element_type=jnp.float32
    )


def gather_features(values):
    return lax.all_gather(values, "col", axis=1, tiled=True)


def sum_features(values):
    return lax.psum_scatter(
        values.astype(jnp.bfloat16), "col", scatter_dimension=1, tiled=True
    ).astype(jnp.float32)


def feature_totals(first_part, second_part):
    return lax.psum((jnp.sum(first_part, axis=1), jnp.sum(second_part, axis=1)), "col")


def norm_forward(hidden, gain, shift, features):
    row_total, square_total = feature_totals(hidden, hidden * hidden)
    row_mean = row_total / features
    row_var = square_total / features - row_mean * row_mean
    inv_scale = lax.rsqrt(row_var + epsilon)
    normed = (hidden - row_mean[:, None]) * inv_scale[:, None]
    return (normed * gain + shift, normed, inv_scale)


def norm_backward(grad, normed, inv_scale, gain, features):
    scaled = grad * gain
    first_total, second_total = feature_totals(scaled, scaled * normed)
    return inv_scale[:, None] * (
        scaled - (first_total / features)[:, None] - normed * (second_total / features)[:, None]
    )


def key_split(piece_rows, rows_dev):
    return (piece_rows // rows_dev, rows_dev)


def body(
    layer_input,
    cotangent,
    labels,
    block_ids,
    w_query,
    b_query,
    w_key,
    w_value,
    b_value,
    w_output,
    b_output,
    ln1_gain,
    ln1_bias,
    w_inner,
    b_inner,
    w_outer,
    b_outer,
    ln2_gain,
    ln2_bias,
    w_pooler,
    b_pooler,
    w_classes,
    b_classes,
):
    f32 = jnp.float32
    bf16 = jnp.bfloat16
    rows_dev, feat_col = layer_input.shape
    heads_col = feat_col // HEAD
    features = feat_col * lax.axis_size("col")
    row_index = lax.axis_index("row")
    col_index = lax.axis_index("col")
    seq_index = lax.axis_index("dp")
    seq_count = lax.axis_size("dp")
    score_scale = HEAD ** (-0.5)
    query_ids = lax.dynamic_slice_in_dim(block_ids, row_index * rows_dev, rows_dev)
    last_query = query_ids[rows_dev - 1]
    wq_full, wk_full, wv_full, w1_full = (
        lax.all_gather(w_query, "row", axis=0, tiled=True),
        lax.all_gather(w_key, "row", axis=0, tiled=True),
        lax.all_gather(w_value, "row", axis=0, tiled=True),
        lax.all_gather(w_inner, "row", axis=0, tiled=True),
    )
    wo_full, w2_full = (
        lax.all_gather(w_output, "row", axis=1, tiled=True),
        lax.all_gather(w_outer, "row", axis=1, tiled=True),
    )
    input_whole = gather_features(layer_input)
    queries = (project(input_whole, wq_full) + b_query.astype(f32)).astype(bf16)
    keys_local = project(input_whole, wk_full).astype(bf16)
    values_local = (project(input_whole, wv_full) + b_value.astype(f32)).astype(bf16)
    queries3 = queries.reshape(rows_dev, heads_col, HEAD)
    start_state = (
        jnp.full((heads_col, rows_dev), masked_score, f32),
        jnp.zeros((heads_col, rows_dev), f32),
        jnp.zeros((heads_col, rows_dev, HEAD), f32),
    )
    running = start_state
    keys_piece = lax.all_gather(keys_local, "row", axis=0, tiled=True)
    values_piece = lax.all_gather(values_local, "row", axis=0, tiled=True)
    piece_rows = keys_piece.shape[0]
    number, block_rows = key_split(piece_rows, rows_dev)
    keys4 = keys_piece.reshape(number, block_rows, heads_col, HEAD)
    values4 = values_piece.reshape(number, block_rows, heads_col, HEAD)
    piece_ids = block_ids.reshape(number, block_rows)

    def attend_block_work(state, block_item):
        peak_score, row_mass, accum = state
        keys3, values3, key_ids = block_item
        scores = (
            jnp.einsum("qhd,khd->hqk", queries3, keys3, preferred_element_type=f32) * score_scale
        )
        allowed = (key_ids[None, :] <= query_ids[:, None])[None]
        block_top = jnp.max(jnp.where(allowed, scores, masked_score), axis=2)
        new_peak = jnp.maximum(peak_score, block_top)
        weights = jnp.where(allowed, jnp.exp(scores - new_peak[:, :, None]), 0.0)
        factor = jnp.exp(peak_score - new_peak)
        row_mass = row_mass * factor + jnp.sum(weights, axis=2)
        accum = accum * factor[:, :, None] + jnp.einsum(
            "hqk,khd->hqd", weights.astype(bf16), values3, preferred_element_type=f32
        )
        return (new_peak, row_mass, accum)

    def attend_block_step(state, block_item):
        state = lax.cond(
            block_item[2][0] > last_query, lambda st, item: st, attend_block_work, state, block_item
        )
        return (state, None)

    running, unused = lax.scan(attend_block_step, running, (keys4, values4, piece_ids))
    peak_score, row_mass, accum = running
    mixed = accum / row_mass[:, :, None]
    log_mass = peak_score + jnp.log(row_mass)
    context_low = mixed.transpose(1, 0, 2).reshape(rows_dev, feat_col).astype(bf16)
    attn_branch = sum_features(project(context_low, wo_full))
    hidden_one = layer_input.astype(f32) + attn_branch + b_output.astype(f32)
    gain_one = ln1_gain.astype(f32)
    stream, normed_one, inv_one = norm_forward(hidden_one, gain_one, ln1_bias.astype(f32), features)
    stream_whole = gather_features(stream.astype(bf16))
    pre_act = project(stream_whole, w1_full) + b_inner.astype(f32)
    activ = gelu_exact(pre_act).astype(bf16)
    ffn_branch = sum_features(project(activ, w2_full))
    hidden_two = stream + ffn_branch + b_outer.astype(f32)
    gain_two = ln2_gain.astype(f32)
    result, normed_two, inv_two = norm_forward(hidden_two, gain_two, ln2_bias.astype(f32), features)
    output = result.astype(bf16)
    row_zero = (row_index == 0).astype(f32)
    pool_input = gather_features(output[0:1])
    pooled = jnp.tanh(project(pool_input, w_pooler) + b_pooler.astype(f32))
    classes_f32 = w_classes.astype(f32)
    logits_own = jnp.dot(pooled, classes_f32, precision=highest) + b_classes.astype(f32)
    onehot = (jnp.arange(w_classes.shape[1]) == labels[0]).astype(f32)
    grad_logits = jax.nn.softmax(logits_own, axis=-1) - onehot[None, :]
    g_w_classes = jnp.dot(pooled.T, grad_logits, precision=highest)
    g_b_classes = grad_logits[0]
    grad_pre_pool = jnp.dot(grad_logits, classes_f32.T, precision=highest) * (1.0 - pooled * pooled)
    g_b_pooler = grad_pre_pool[0]
    g_w_pooler = jnp.dot(pool_input.astype(f32).T, grad_pre_pool, precision=highest)
    grad_first = jnp.dot(grad_pre_pool, w_pooler.astype(f32).T, precision=highest)
    first_col = lax.dynamic_slice_in_dim(grad_first[0], col_index * feat_col, feat_col)
    grad_result = cotangent.astype(f32).at[0].add(first_col * row_zero)
    logits_table = lax.dynamic_update_slice_in_dim(
        jnp.zeros((seq_count, w_classes.shape[1]), f32), logits_own * row_zero, seq_index, 0
    )
    g_ln2_gain = jnp.sum(grad_result * normed_two, axis=0)
    g_ln2_bias = jnp.sum(grad_result, axis=0)
    grad_hidden_two = norm_backward(grad_result, normed_two, inv_two, gain_two, features)
    g_b_outer = jnp.sum(grad_hidden_two, axis=0)
    branch_two_whole = gather_features(grad_hidden_two.astype(bf16))
    g_w_outer_full = contract_first(activ, branch_two_whole)
    grad_act = contract_last(branch_two_whole, w2_full)
    grad_pre = (grad_act * gelu_slope(pre_act)).astype(bf16)
    g_b_inner = jnp.sum(grad_pre.astype(f32), axis=0)
    g_w_inner_full = contract_first(stream_whole, grad_pre)
    grad_stream = grad_hidden_two + sum_features(contract_last(grad_pre, w1_full))
    g_ln1_gain = jnp.sum(grad_stream * normed_one, axis=0)
    g_ln1_bias = jnp.sum(grad_stream, axis=0)
    grad_hidden_one = norm_backward(grad_stream, normed_one, inv_one, gain_one, features)
    g_b_output = jnp.sum(grad_hidden_one, axis=0)
    branch_one_whole = gather_features(grad_hidden_one.astype(bf16))
    g_w_output_full = contract_first(context_low, branch_one_whole)
    grad_context = contract_last(branch_one_whole, wo_full).astype(bf16)
    grad_ctx3 = grad_context.reshape(rows_dev, heads_col, HEAD)
    delta = jnp.sum(grad_ctx3.astype(f32).transpose(1, 0, 2) * mixed, axis=2)

    def score_grads(queries_blk, grad_ctx_blk, keys3, values3, allowed, lse_blk, delta_blk):
        scores = (
            jnp.einsum("qhd,khd->hqk", queries_blk, keys3, preferred_element_type=f32) * score_scale
        )
        probs = jnp.where(allowed, jnp.exp(scores - lse_blk[:, :, None]), 0.0)
        grad_probs = jnp.einsum("qhd,khd->hqk", grad_ctx_blk, values3, preferred_element_type=f32)
        grad_scores = (probs * (grad_probs - delta_blk[:, :, None])).astype(bf16)
        return (probs, grad_scores)

    zero_q = jnp.zeros((rows_dev, heads_col, HEAD), f32)
    keys_piece = lax.all_gather(keys_local, "row", axis=0, tiled=True)
    values_piece = lax.all_gather(values_local, "row", axis=0, tiled=True)
    piece_rows = keys_piece.shape[0]
    number, block_rows = key_split(piece_rows, rows_dev)
    keys4 = keys_piece.reshape(number, block_rows, heads_col, HEAD)
    values4 = values_piece.reshape(number, block_rows, heads_col, HEAD)
    piece_ids = block_ids.reshape(number, block_rows)

    def make_block_work(accum_q, block_item):
        keys3, values3, key_ids = block_item
        allowed = (key_ids[None, :] <= query_ids[:, None])[None]
        probs, grad_scores = score_grads(
            queries3, grad_ctx3, keys3, values3, allowed, log_mass, delta
        )
        accum_q = (
            accum_q
            + jnp.einsum("hqk,khd->qhd", grad_scores, keys3, preferred_element_type=f32)
            * score_scale
        )
        part_k = (
            jnp.einsum("hqk,qhd->khd", grad_scores, queries3, preferred_element_type=f32)
            * score_scale
        )
        part_v = jnp.einsum(
            "hqk,qhd->khd", probs.astype(bf16), grad_ctx3, preferred_element_type=f32
        )
        return (accum_q, (part_k, part_v))

    def block_skip(accum_q, block_item):
        empty = jnp.zeros((block_rows, heads_col, HEAD), f32)
        return (accum_q, (empty, empty))

    def make_block_step(accum_q, block_item):
        return lax.cond(
            block_item[2][0] > last_query, block_skip, make_block_work, accum_q, block_item
        )

    grad_q = zero_q
    grad_q, (parts_k, parts_v) = lax.scan(make_block_step, grad_q, (keys4, values4, piece_ids))
    parts_k = parts_k.reshape(piece_rows, feat_col)
    parts_v = parts_v.reshape(piece_rows, feat_col)
    grad_k_all = parts_k
    grad_v_all = parts_v
    back_result = (grad_q, grad_k_all, grad_v_all)
    grad_q3, grad_k_all, grad_v_all = back_result
    grad_keys, grad_values = (
        lax.psum_scatter(
            grad_k_all.astype(jnp.bfloat16), "row", scatter_dimension=0, tiled=True
        ).astype(jnp.float32),
        lax.psum_scatter(
            grad_v_all.astype(jnp.bfloat16), "row", scatter_dimension=0, tiled=True
        ).astype(jnp.float32),
    )
    queries_grad = grad_q3.reshape(rows_dev, feat_col).astype(bf16)
    keys_grad = grad_keys.astype(bf16)
    values_grad = grad_values.astype(bf16)
    g_b_query = jnp.sum(queries_grad.astype(f32), axis=0)
    g_b_value = jnp.sum(values_grad.astype(f32), axis=0)
    g_w_query_full = contract_first(input_whole, queries_grad)
    g_w_key_full = contract_first(input_whole, keys_grad)
    g_w_value_full = contract_first(input_whole, values_grad)
    grad_input_whole = (
        contract_last(queries_grad, wq_full)
        + contract_last(keys_grad, wk_full)
        + contract_last(values_grad, wv_full)
    )
    grad_input = (grad_hidden_one + sum_features(grad_input_whole)).astype(bf16)
    in_rows = w_query.shape[0]
    out_cols = w_output.shape[1]
    (
        sum_wq,
        sum_wk,
        sum_wv,
        sum_w1,
        sum_wo,
        sum_w2,
        g_w_pooler,
        g_b_pooler,
        g_w_classes,
        g_b_classes,
        g_b_query,
        g_b_value,
        g_b_output,
        g_ln1_gain,
        g_ln1_bias,
        g_b_inner,
        g_b_outer,
        g_ln2_gain,
        g_ln2_bias,
        logits_all,
    ) = lax.psum(
        (
            g_w_query_full,
            g_w_key_full,
            g_w_value_full,
            g_w_inner_full,
            g_w_output_full,
            g_w_outer_full,
            g_w_pooler * row_zero,
            g_b_pooler * row_zero,
            g_w_classes * row_zero,
            g_b_classes * row_zero,
            g_b_query,
            g_b_value,
            g_b_output,
            g_ln1_gain,
            g_ln1_bias,
            g_b_inner,
            g_b_outer,
            g_ln2_gain,
            g_ln2_bias,
            logits_table,
        ),
        ("dp", "row"),
    )
    row_start = row_index * in_rows
    col_start = row_index * out_cols
    g_w_query = lax.dynamic_slice_in_dim(sum_wq, row_start, in_rows, 0)
    g_w_key = lax.dynamic_slice_in_dim(sum_wk, row_start, in_rows, 0)
    g_w_value = lax.dynamic_slice_in_dim(sum_wv, row_start, in_rows, 0)
    g_w_inner = lax.dynamic_slice_in_dim(sum_w1, row_start, in_rows, 0)
    g_w_output = lax.dynamic_slice_in_dim(sum_wo, col_start, out_cols, 1)
    g_w_outer = lax.dynamic_slice_in_dim(sum_w2, col_start, out_cols, 1)
    logits = lax.dynamic_slice_in_dim(logits_all, seq_index, 1, 0)
    return (
        output,
        logits,
        grad_input,
        g_w_query,
        g_b_query,
        g_w_key,
        g_w_value,
        g_b_value,
        g_w_output,
        g_b_output,
        g_ln1_gain,
        g_ln1_bias,
        g_w_inner,
        g_b_inner,
        g_w_outer,
        g_b_outer,
        g_ln2_gain,
        g_ln2_bias,
        g_w_pooler,
        g_b_pooler,
        g_w_classes,
        g_b_classes,
    )


MESH_IDS = pl.DeviceIdType.MESH
ROWS = 4
VMEM_BYTES = 64000 * 1024


def place():
    return lax.axis_index("dp"), lax.axis_index("row"), lax.axis_index("col")


class Links:
    def __init__(self, send, recv):
        self.send, self.recv = send, recv
        self.sends, self.recvs, self.open = 0, 0, []

    def slots(self, count):
        base = self.recvs
        self.recvs += count
        return base

    def push(self, source, target, slot, device, when=None):
        copy = pltpu.make_async_remote_copy(
            src_ref=source,
            dst_ref=target,
            send_sem=self.send.at[self.sends],
            recv_sem=self.recv.at[slot],
            device_id=device,
            device_id_type=MESH_IDS,
        )
        self.sends += 1
        if when is None:
            copy.start()
        else:
            pl.when(when)(lambda: copy.start())
        self.open.append((copy, when))

    def arrive(self, target, slot, device, when=None):
        copy = pltpu.make_async_remote_copy(
            src_ref=target,
            dst_ref=target,
            send_sem=self.send.at[0],
            recv_sem=self.recv.at[slot],
            device_id=device,
            device_id_type=MESH_IDS,
        )
        if when is None:
            copy.wait_recv()
        else:
            pl.when(when)(lambda: copy.wait_recv())

    def drain(self):
        for copy, when in self.open:
            if when is None:
                copy.wait_send()
            else:
                pl.when(when)(lambda copy=copy: copy.wait_send())
        self.open = []


def meet(devices):
    barrier = pltpu.get_barrier_semaphore()
    for device in devices:
        pl.semaphore_signal(barrier, inc=1, device_id=device, device_id_type=MESH_IDS)
    pl.semaphore_wait(barrier, len(devices))


def within(value):
    return (value >= 0) & (value < ROWS)


def steps_of_line(row):
    for step in (1, 2, 3):
        for way in (1, -1):
            source = row - way * step
            yield step, way, (3 - step if way == 1 else step - 1), source, within(source)


def columns(col, width):
    return pl.ds(pl.multiple_of(col * width, 128), width)


IN_VMEM = pl.BlockSpec(memory_space=pltpu.VMEM)
IN_PLACE = pl.BlockSpec(memory_space=pl.ANY)


def comm_params(number):
    return pltpu.CompilerParams(
        collective_id=number, has_side_effects=True, vmem_limit_bytes=VMEM_BYTES
    )


TILE = 256
NEAR = 3


def nt(left, right):
    return lax.dot_general(
        left, right, (((1,), (1,)), ((), ())), preferred_element_type=jnp.float32
    )


def nn(left, right):
    return jnp.dot(left, right, preferred_element_type=jnp.float32)


def forward_kernel(widths, heads, x, cot, vec, wq, wk, wv, ids, *refs):
    count = len(widths)
    shards, refs = refs[:count], refs[count:]
    x_all, cot_own, vec_all, w_heads, q_out, k_out, kt_out, v_out, mixed_out, lse_out, context = (
        refs[:11]
    )
    fulls, refs = refs[11 : 11 + count], refs[11 + count :]
    vt_out, ids_col, packs, low_out, send, recv, local = refs
    dp, row, col = place()
    links = Links(send, recv)
    low = x.dtype
    rows_dev, feat = x.shape
    wide = heads * HEAD
    mate = (dp, row, 1 - col)
    at_row = lambda other: (dp, other, col)
    at_dp = lambda flip: (dp ^ flip, row, col)
    home, side = row // 2, lax.rem(row, 2)
    mine = lax.rem(row + col, 2)
    half = rows_dev // 2
    meet([at_row(lax.rem(row + k, ROWS)) for k in (1, 2, 3)] + [at_dp(1), at_dp(2), mate])

    x_at = lambda k: x_all.at[k, :, columns(col, feat)]
    x_mate_at = lambda k: x_all.at[k, :, columns(1 - col, feat)]
    w_at = lambda i, k, q: fulls[i].at[k, q, :, columns(col, widths[i])]
    row_at = lambda i, k: fulls[i].at[k, :, :, columns(col, widths[i])]
    row_mate_at = lambda i, k: fulls[i].at[k, :, :, columns(1 - col, widths[i])]

    line_x, mate_x = links.slots(3), links.slots(4)
    line_q, first_q, second_q, mate_q = (
        links.slots(3), links.slots(3), links.slots(6), links.slots(1),
    )
    mate_cot, mate_vec, swap = links.slots(1), links.slots(1), links.slots(3)
    line_w = [links.slots(3) for _ in widths]
    first_w = [links.slots(3) for _ in widths]
    second_w = [links.slots(6) for _ in widths]
    mate_w = [links.slots(4) for _ in widths]
    steps = list(steps_of_line(row))
    at_step = lambda step: [entry[2:] for entry in steps if entry[0] == step]

    def relay(step, own, full, base):
        for way in (1, -1):
            held, onward = row - way * (step - 1), row + way
            ok = within(held) & within(onward)
            slot = 3 - step if way == 1 else step - 1
            links.push(own if step == 1 else full(held), full(held), base + slot, at_row(onward), ok)

    relay(1, x, x_at, line_x)
    links.push(x, x_at(row), mate_x, mate)
    for j in range(2):
        part = slice(j * wide, (j + 1) * wide)
        packs[j] = jnp.concatenate(
            [wq[:, part], wk[:, part], wv[:, part]], axis=1
        ).reshape(packs.shape[1:])
    for j in range(2):
        k = 2 * col + j
        away = k != row
        slot = lax.rem(row - k + ROWS + 3, ROWS)
        links.push(packs.at[j, dp], w_heads.at[row, dp], line_q + slot, at_row(k), away)

        @pl.when(jnp.logical_not(away))
        def _(j=j):
            w_heads[row] = packs[j]

    links.push(
        cot.at[pl.ds(pl.multiple_of((1 - mine) * half, 128), half)],
        cot_own.at[:, columns(col, feat)],
        mate_cot,
        mate,
    )
    links.push(vec, vec_all.at[col], mate_vec, mate)
    cot_own[:, columns(col, feat)] = cot[pl.ds(pl.multiple_of(mine * half, 128), half)]
    vec_all[col] = vec[...]
    x_all[row, :, columns(col, feat)] = x[...]
    copies = [
        pltpu.make_async_copy(shards[i], row_at(i, row), local.at[i]) for i in range(count)
    ]

    at_home = home == col

    def q_first():
        for slot in range(3):
            k = lax.rem(row + slot + 1, ROWS)
            one = 1 + slot % 2
            links.arrive(w_heads.at[k, dp], line_q + slot, mate, at_home)
            links.push(
                w_heads.at[k, dp], w_heads.at[k, dp], first_q + slot, at_dp(one), at_home
            )

    def q_second():
        for slot in range(3):
            k = lax.rem(row + slot + 1, ROWS)
            one, two = 1 + slot % 2, 2 - slot % 2
            links.arrive(w_heads.at[k, dp ^ one], first_q + slot, mate, at_home)
            for n, q in enumerate((dp, dp ^ one)):
                links.push(
                    w_heads.at[k, q], w_heads.at[k, q], second_q + 2 * slot + n, at_dp(two), at_home
                )

    def q_mate():
        for slot in range(3):
            k = lax.rem(row + slot + 1, ROWS)
            two = 2 - slot % 2
            links.arrive(w_heads.at[k, dp ^ two], second_q + 2 * slot, mate, at_home)
            links.arrive(w_heads.at[k, dp ^ 3], second_q + 2 * slot + 1, mate, at_home)
        links.push(w_heads, w_heads, mate_q, mate, at_home)
        links.arrive(w_heads, mate_q, mate, jnp.logical_not(at_home))

    def x_step(step):
        for slot, k, ok in at_step(step):
            links.arrive(x_at(k), line_x + slot, mate, ok)
        if step < 3:
            relay(step + 1, x, x_at, line_x)
        for slot, k, ok in at_step(step):
            links.push(x_at(k), x_at(k), mate_x + 1 + slot, mate, ok)

    turn = lambda i, slot: (1, 2) if (i + slot) % 2 == 0 else (2, 1)

    def w_relay(step):
        for i in range(count):
            relay(step, shards[i].at[dp], lambda k, i=i: w_at(i, k, dp), line_w[i])

    def w_first(step):
        for i in range(count):
            for slot, k, ok in at_step(step):
                links.arrive(w_at(i, k, dp), line_w[i] + slot, mate, ok)
        if step < 3:
            w_relay(step + 1)
        for i in range(count):
            for slot, k, ok in at_step(step):
                one, two = turn(i, slot)
                links.push(w_at(i, k, dp), w_at(i, k, dp), first_w[i] + slot, at_dp(one), ok)

    def w_second(step):
        for i in range(count):
            for slot, k, ok in at_step(step):
                one, two = turn(i, slot)
                links.arrive(w_at(i, k, dp ^ one), first_w[i] + slot, mate, ok)
                for n, q in enumerate((dp, dp ^ one)):
                    links.push(
                        w_at(i, k, q), w_at(i, k, q), second_w[i] + 2 * slot + n, at_dp(two), ok
                    )

    def w_mate(step):
        for i in range(count):
            for slot, k, ok in at_step(step):
                one, two = turn(i, slot)
                links.arrive(w_at(i, k, dp ^ two), second_w[i] + 2 * slot, mate, ok)
                links.arrive(w_at(i, k, dp ^ 3), second_w[i] + 2 * slot + 1, mate, ok)
                links.push(row_at(i, k), row_at(i, k), mate_w[i] + 1 + slot, mate, ok)

    row_tiles = ROWS * rows_dev // TILE
    per_row = rows_dev // TILE

    def split_ids(step, carry):
        span = pl.ds(pl.multiple_of(step * TILE, TILE), TILE)
        ids_col[span] = jnp.broadcast_to(ids[:, span], (8, TILE)).T[:, :1]
        return carry

    lax.fori_loop(0, row_tiles, split_ids, 0)
    x_step(1)
    q_first()
    x_step(2)
    q_second()
    w_relay(1)
    for copy in copies:
        copy.start()
    for i in range(count):
        links.push(shards[i], row_at(i, row), mate_w[i], mate)
    q_mate()
    links.arrive(vec_all.at[1 - col], mate_vec, mate)
    bias_of = lambda n: jnp.where(
        side == 0, vec_all[home, n : n + 1, :wide], vec_all[home, n : n + 1, wide : 2 * wide]
    )
    bias_q, bias_v = bias_of(0), bias_of(1)
    weights = lambda start, stop: w_heads[:, :, :, start:stop].reshape(2 * feat, stop - start)

    def project_keys(k):
        def one_tile(step, carry):
            here = pl.ds(pl.multiple_of(step * TILE, TILE), TILE)
            rows = pl.ds(pl.multiple_of(k * rows_dev + step * TILE, TILE), TILE)
            both = nn(x_all[k, here], weights(wide, 3 * wide))
            keys = both[:, :wide]
            values = both[:, wide:] + bias_v
            keys_t = keys.T
            values_t = values.T
            for h in range(heads):
                part = slice(h * HEAD, (h + 1) * HEAD)
                k_out[h, rows] = keys[:, part].astype(low)
                v_out[h, rows] = values[:, part].astype(low)
                kt_out[h, :, rows] = keys_t[part].astype(low)
                vt_out[h, :, rows] = values_t[part].astype(low)
            return carry

        lax.fori_loop(0, per_row, one_tile, 0)

    links.arrive(x_mate_at(row), mate_x, mate)
    project_keys(row)
    x_step(3)
    for slot in (0, 2, 1):
        k = lax.rem(row + slot + 1, ROWS)
        links.arrive(x_mate_at(k), mate_x + 1 + slot, mate)
        project_keys(k)

    def project_query(j, carry):
        block = 2 * j + lax.rem(j + col, 2)
        here = pl.ds(pl.multiple_of(lax.rem(block, per_row) * TILE, TILE), TILE)
        query = nn(x_all[block // per_row, here], weights(0, wide)) + bias_q
        query = query.astype(low) * jnp.asarray(HEAD**-0.5, low)
        for h in range(heads):
            q_out[h, j] = query[:, h * HEAD : (h + 1) * HEAD]
        return carry

    blocks = row_tiles // 2
    lax.fori_loop(0, blocks, project_query, 0)
    w_first(1)
    for j in range(blocks):
        block = 2 * j + lax.rem(j + col, 2)
        rows = pl.ds(pl.multiple_of(block * TILE, TILE), TILE)
        query_ids = ids[:, rows]
        length = min(2 * j + NEAR, row_tiles) * TILE
        clear = 2 * j * TILE

        def one_head(h, carry, j=j, query_ids=query_ids, length=length, clear=clear):
            scores = nt(k_out[h, :length], q_out[h, j])
            near = jnp.where(
                ids_col[clear:length] <= query_ids, scores[clear:], masked_score
            )
            top = jnp.max(near, axis=0, keepdims=True)
            if clear:
                top = jnp.maximum(top, jnp.max(scores[:clear], axis=0, keepdims=True))
                weights_far = jnp.exp(scores[:clear] - top)
            weights_near = jnp.exp(near - top)
            mass = jnp.sum(weights_near, axis=0, keepdims=True)
            value = nn(vt_out[h, :, clear:length], weights_near.astype(low))
            if clear:
                mass = mass + jnp.sum(weights_far, axis=0, keepdims=True)
                value = value + nn(vt_out[h, :, :clear], weights_far.astype(low))
            mixed_out[j, h] = value / mass
            lse_out[j, h] = top + jnp.log(mass)
            return carry

        lax.fori_loop(0, heads, one_head, 0)
        low_out[j] = (
            jnp.concatenate([mixed_out[j, h] for h in range(heads)], axis=0).T.astype(low)
        )
        away = row != j
        slot = lax.rem(row - j + ROWS + 3, ROWS)
        links.push(low_out.at[j], context.at[row], swap + slot, at_row(j), away)

        @pl.when(jnp.logical_not(away))
        def _(j=j):
            context[row] = low_out[j]

        if j == 1:
            w_first(2)
            w_second(1)
    w_first(3)
    w_second(2)
    w_mate(1)
    w_second(3)
    w_mate(2)
    w_mate(3)
    links.arrive(cot_own.at[:, columns(1 - col, feat)], mate_cot, mate)
    for slot in range(3):
        links.arrive(context.at[lax.rem(row + slot + 1, ROWS)], swap + slot, mate)
    for i in range(count):
        links.arrive(row_mate_at(i, row), mate_w[i], mate)
        for slot in range(3):
            k = lax.rem(row + slot + 1, ROWS)
            links.arrive(row_mate_at(i, k), mate_w[i] + 1 + slot, mate)
    for copy in copies:
        copy.wait()
    links.drain()


def forward_links(x, cot, vec, wq, wk, wv, ids, shards):
    widths = [shard.shape[1] for shard in shards]
    rows, feat = x.shape
    low, f32 = x.dtype, jnp.float32
    part = shards[0].shape[0] // 4
    heads = 2 * feat // HEAD // ROWS
    wide = heads * HEAD
    length = ROWS * rows
    blocks = length // TILE // 2
    shape = jax.ShapeDtypeStruct
    shapes = [
        shape((ROWS, rows, 2 * feat), low),
        shape((rows // 2, 2 * feat), low),
        shape((2,) + vec.shape, vec.dtype),
        shape((ROWS, 4, part, 3 * wide), low),
        shape((heads, blocks, TILE, HEAD), low),
        shape((heads, length, HEAD), low),
        shape((heads, HEAD, length), low),
        shape((heads, length, HEAD), low),
        shape((blocks, heads, HEAD, TILE), f32),
        shape((blocks, heads, 1, TILE), f32),
        shape((ROWS, rows // 2, wide), low),
    ] + [shape((ROWS, 4, part, 2 * width), low) for width in widths]
    return pl.pallas_call(
        functools.partial(forward_kernel, widths, heads),
        out_shape=shapes,
        in_specs=[IN_VMEM] * (7 + len(shards)),
        out_specs=[IN_VMEM] * 11 + [IN_PLACE] * len(shards),
        scratch_shapes=[
            pltpu.VMEM((heads, HEAD, length), low),
            pltpu.VMEM((length, 1), jnp.int32),
            pltpu.VMEM((2, 4, part, 3 * wide), low),
            pltpu.VMEM((blocks, TILE, wide), low),
            pltpu.SemaphoreType.DMA((160,)),
            pltpu.SemaphoreType.DMA((96,)),
            pltpu.SemaphoreType.DMA((4,)),
        ],
        compiler_params=comm_params(1),
        name="forward_links",
    )(
        x, cot, vec, wq, wk, wv, ids.reshape(1, -1),
        *[shard.reshape(4, part, -1) for shard in shards],
    )


def swap_kernel(split, *refs):
    blocks, out_blocks = refs[0], refs[1 + split]
    send, recv, local = refs[-3:]
    dp, row, col = place()
    links = Links(send, recv)
    mate = (dp, row, 1 - col)
    peers = [lax.rem(row + k, ROWS) for k in (1, 2, 3)]
    meet([(dp, peer, col) for peer in peers] + ([mate] if split else []))
    base = links.slots(4)
    for number, peer in enumerate(peers):
        links.push(blocks.at[peer], out_blocks.at[row], base + 2 - number, (dp, peer, col))
    keep = [pltpu.make_async_copy(blocks.at[row], out_blocks.at[row], local.at[0])]
    if split:
        whole, halves = refs[1], refs[3]
        half, feat = whole.shape[0], whole.shape[1] // 2
        mine = lax.rem(row + col, 2)
        own_rows = pl.ds(pl.multiple_of(mine * half, 128), half)
        keep.append(
            pltpu.make_async_copy(
                whole.at[:, columns(col, feat)], halves.at[own_rows], local.at[1]
            )
        )
        links.push(whole.at[:, columns(1 - col, feat)], halves.at[own_rows], base + 3, mate)
        other_rows = pl.ds(pl.multiple_of((1 - mine) * half, 128), half)
    for copy in keep:
        copy.start()
    for number, peer in enumerate(peers):
        links.arrive(out_blocks.at[peer], base + number, mate)
    if split:
        links.arrive(halves.at[other_rows], base + 3, mate)
    for copy in keep:
        copy.wait()
    links.drain()


def swap_blocks(blocks, number, whole=None):
    split = 0 if whole is None else 1
    shapes = [jax.ShapeDtypeStruct(blocks.shape, blocks.dtype)]
    if split:
        shapes.append(
            jax.ShapeDtypeStruct((2 * whole.shape[0], whole.shape[1] // 2), whole.dtype)
        )
    return pl.pallas_call(
        functools.partial(swap_kernel, split),
        out_shape=shapes,
        in_specs=[IN_VMEM] * (1 + split),
        out_specs=[IN_VMEM] * (1 + split),
        scratch_shapes=[
            pltpu.SemaphoreType.DMA((4,)),
            pltpu.SemaphoreType.DMA((4,)),
            pltpu.SemaphoreType.DMA((2,)),
        ],
        compiler_params=comm_params(number),
        name="swap_blocks",
    )(blocks, *([whole] if split else []))


def add_into(total, *others):
    def one(step, carry):
        value = total[step].astype(jnp.float32)
        for other in others:
            value = value + other[step].astype(jnp.float32)
        total[step] = value.astype(total.dtype)
        return carry

    lax.fori_loop(0, total.shape[0], one, 0)


def reduce_kernel(count, *refs):
    grads, refs = refs[:count], refs[count:]
    gq, dx, vec = refs[:3]
    outs, refs = refs[3 : 3 + count], refs[3 + count :]
    out_q, out_x, out_vec = refs[:3]
    refs = refs[3:]
    sums, refs = refs[:count], refs[count:]
    first, refs = refs[: count + 1], refs[count + 1 :]
    second, refs = refs[: count + 1], refs[count + 1 :]
    lines, refs = refs[:count], refs[count:]
    sum_q, all_q, sum_x, line_x, vec_mate, vec_line, vec_flat, send, recv = refs
    dp, row, col = place()
    links = Links(send, recv)
    mate = (dp, row, 1 - col)
    peers = [lax.rem(row + k, ROWS) for k in (1, 2, 3)]
    at_row = lambda other: (dp, other, col)
    at_dp = lambda flip: (dp ^ flip, row, col)
    owner = row // 2
    meet(
        [at_row(peer) for peer in peers]
        + [at_dp(1), at_dp(2), mate]
        + [(dp, peer, 1 - col) for peer in peers]
    )
    widths = [grad.shape[3] // 2 for grad in grads]
    feat = dx.shape[2] // 2
    turns = [(1, 2) if i % 2 == 0 else (2, 1) for i in range(count + 1)]

    slot_x, slot_q, slot_v = links.slots(1), links.slots(1), links.slots(1)
    slot_g = [links.slots(1) for _ in grads]
    links.push(vec, vec_mate, slot_v, mate)
    links.push(dx.at[:, :, columns(1 - col, feat)], sum_x, slot_x, mate)
    links.push(gq.at[:, 1 - col], sum_q, slot_q, mate)
    for i in range(count):
        links.push(grads[i].at[:, :, :, columns(1 - col, widths[i])], sums[i], slot_g[i], mate)

    links.arrive(vec_mate, slot_v, mate)
    out_vec[...] = vec[...] + vec_mate[...]
    slot_vl = links.slots(3)
    for n, peer in enumerate(peers):
        links.push(out_vec, vec_line.at[2 - n], slot_vl + 2 - n, at_row(peer))

    links.arrive(sum_x, slot_x, mate)
    tile = dx.shape[1] // 4

    def add_x(step, carry):
        rows = pl.ds(pl.multiple_of((step % 4) * tile, 128), tile)
        sum_x[step // 4, rows] = (
            sum_x[step // 4, rows].astype(jnp.float32)
            + dx[step // 4, rows, columns(col, feat)].astype(jnp.float32)
        ).astype(sum_x.dtype)
        return carry

    lax.fori_loop(0, 16, add_x, 0)
    slot_xl = links.slots(3)
    for n, peer in enumerate(peers):
        links.push(sum_x.at[peer], line_x.at[2 - n], slot_xl + 2 - n, at_row(peer))

    links.arrive(sum_q, slot_q, mate)

    def add_q(step, carry):
        sum_q[step] = (
            sum_q[step].astype(jnp.float32) + gq[step, col].astype(jnp.float32)
        ).astype(sum_q.dtype)
        return carry

    lax.fori_loop(0, 4, add_q, 0)
    slot_ql = links.slots(4)
    side = lax.rem(row, 2)
    own_part = all_q.at[side, pl.ds(2 * col, 2)]
    at_home = owner == col

    def keep_own():
        own_part[...] = sum_q[row]

    pl.when(at_home)(keep_own)
    links.push(sum_q.at[row], own_part, slot_ql + 2 * side + col, mate, jnp.logical_not(at_home))
    for peer in peers:
        links.push(sum_q.at[peer], own_part, slot_ql + 2 * side + col, (dp, peer, owner))

    def send_first(i, total):
        one, two = turns[i]
        base = links.slots(2)
        links.push(total.at[:, dp ^ one], first[i].at[0], base, at_dp(one))
        links.push(total.at[:, dp ^ 3], first[i].at[1], base + 1, at_dp(one))
        return base

    def send_second(i, total, base):
        one, two = turns[i]
        links.arrive(first[i].at[1], base + 1, mate)
        add_into(total.at[:, dp ^ two], first[i].at[1])
        slot = links.slots(1)
        links.push(total.at[:, dp ^ two], second[i], slot, at_dp(two))
        links.arrive(first[i].at[0], base, mate)
        add_into(total.at[:, dp], first[i].at[0])
        return slot

    def share(i, out):
        one, two = turns[i]
        base = links.slots(3)
        links.push(out.at[dp], out.at[dp], base, at_dp(two))
        links.push(out.at[dp], out.at[dp], base + 1, at_dp(one))
        links.arrive(out.at[dp ^ two], base, mate)
        links.push(out.at[dp ^ two], out.at[dp ^ two], base + 2, at_dp(one))
        return base

    def shared(i, out, base):
        one, two = turns[i]
        links.arrive(out.at[dp ^ one], base + 1, mate)
        links.arrive(out.at[dp ^ 3], base + 2, mate)

    started = []
    for i in range(count):
        links.arrive(sums[i], slot_g[i], mate)
        width = widths[i]

        def add_g(step, carry, i=i, width=width):
            k, q = step // 4, step % 4
            sums[i][k, q] = (
                sums[i][k, q].astype(jnp.float32)
                + grads[i][k, q, :, columns(col, width)].astype(jnp.float32)
            ).astype(sums[i].dtype)
            return carry

        lax.fori_loop(0, 16, add_g, 0)
        started.append(send_first(i, sums[i]))
    for j in range(2):
        for e in range(2):
            here = (row == 2 * col + j) & (col == e)
            links.arrive(
                all_q.at[j, pl.ds(2 * e, 2)], slot_ql + 2 * j + e, mate, jnp.logical_not(here)
            )
    started.append(send_first(count, all_q))

    for n in range(3):
        links.arrive(vec_line.at[n], slot_vl + n, mate)
    vec_sum = out_vec[...] + vec_line[0] + vec_line[1] + vec_line[2]
    vec_mate[...] = vec_sum
    slot_v1 = links.slots(2)
    links.push(vec_mate, vec_flat.at[0], slot_v1, at_dp(1))

    totals = list(sums) + [all_q]
    started = [send_second(i, totals[i], started[i]) for i in range(count + 1)]
    slot_z = []
    for i in range(count + 1):
        links.arrive(second[i], started[i], mate)
        add_into(totals[i].at[:, dp], second[i])
        if i < count:
            base = links.slots(3)
            for n, peer in enumerate(peers):
                links.push(
                    sums[i].at[peer, dp], lines[i].at[2 - n], base + 2 - n, at_row(peer)
                )
            slot_z.append(base)
        else:
            for j in range(2):
                out_q[dp, j] = all_q[j, dp]
            slot_share_q = share(count, out_q)

    links.arrive(vec_flat.at[0], slot_v1, mate)
    vec_line[0] = vec_mate[...] + vec_flat[0]
    links.push(vec_line.at[0], vec_flat.at[1], slot_v1 + 1, at_dp(2))

    for n in range(3):
        links.arrive(line_x.at[n], slot_xl + n, mate)

    def finish_x(step, carry):
        rows = pl.ds(pl.multiple_of(step * tile, 128), tile)
        value = sum_x[row, rows].astype(jnp.float32)
        for n in range(3):
            value = value + line_x[n, rows].astype(jnp.float32)
        out_x[rows] = value.astype(out_x.dtype)
        return carry

    lax.fori_loop(0, 4, finish_x, 0)
    shares = []
    for i in range(count):
        for n in range(3):
            links.arrive(lines[i].at[n], slot_z[i] + n, mate)
        value = sums[i][row, dp].astype(jnp.float32)
        for n in range(3):
            value = value + lines[i][n].astype(jnp.float32)
        outs[i][dp] = value.astype(outs[i].dtype)
        shares.append(share(i, outs[i]))
    links.arrive(vec_flat.at[1], slot_v1 + 1, mate)
    vec_total = vec_line[0] + vec_flat[1]
    for i in range(count):
        shared(i, outs[i], shares[i])
    shared(count, out_q, slot_share_q)
    links.drain()
    out_vec[...] = vec_total


def reduce_all(grads, gq, dx, vec):
    count = len(grads)
    low = dx.dtype
    depth = grads[0].shape[0]
    part = depth // ROWS // 4
    widths = [grad.shape[1] // 2 for grad in grads]
    wide = gq.shape[1]
    rows, feat = dx.shape[0] // ROWS, dx.shape[1] // 2
    blocks = lambda lead, width: (lead, 4, part, width)
    outs = [jax.ShapeDtypeStruct((4, part, width), low) for width in widths] + [
        jax.ShapeDtypeStruct((4, 2, part, wide), low),
        jax.ShapeDtypeStruct((rows, feat), low),
        jax.ShapeDtypeStruct(vec.shape, vec.dtype),
    ]
    every = [(ROWS, width) for width in widths] + [(2, wide)]
    return pl.pallas_call(
        functools.partial(reduce_kernel, count),
        out_shape=outs,
        in_specs=[IN_VMEM] * (count + 3),
        out_specs=[IN_VMEM] * len(outs),
        scratch_shapes=[pltpu.VMEM(blocks(ROWS, width), low) for width in widths]
        + [pltpu.VMEM((2, lead, part, width), low) for lead, width in every]
        + [pltpu.VMEM((lead, part, width), low) for lead, width in every]
        + [pltpu.VMEM((3, part, width), low) for width in widths]
        + [
            pltpu.VMEM((ROWS, 2, part, wide), low),
            pltpu.VMEM((2, 4, part, wide), low),
            pltpu.VMEM((ROWS, rows, feat), low),
            pltpu.VMEM((3, rows, feat), low),
            pltpu.VMEM(vec.shape, vec.dtype),
            pltpu.VMEM((3,) + vec.shape, vec.dtype),
            pltpu.VMEM((2,) + vec.shape, vec.dtype),
            pltpu.SemaphoreType.DMA((96,)),
            pltpu.SemaphoreType.DMA((96,)),
        ],
        compiler_params=comm_params(4),
        name="reduce_all",
    )(
        *[grad.reshape(ROWS, 4, part, 2 * width) for grad, width in zip(grads, widths)],
        gq.reshape(ROWS, 2, 2, part, wide),
        dx.reshape(ROWS, rows, 2 * feat),
        vec,
    )


def attend_back_kernel(
    heads, grad_ctx, q, k, kt, v, mixed, lse, ids_col, ids_row, grads, dk, dv
):
    length = k.shape[1]
    row_tiles = length // TILE
    width = heads * HEAD
    low = q.dtype
    col = lax.axis_index("col")
    dk[...] = jnp.zeros_like(dk)
    dv[...] = jnp.zeros_like(dv)
    for j in range(row_tiles // 2):
        block = 2 * j + lax.rem(j + col, 2)
        rows = pl.ds(pl.multiple_of(block * TILE, TILE), TILE)
        other = pl.ds(pl.multiple_of((4 * j + 1 - block) * TILE, TILE), TILE)
        query_ids = ids_row[:, rows]
        tiles = min(2 * j + NEAR, row_tiles)
        length_j = tiles * TILE
        clear = 2 * j * TILE
        grad_t = grad_ctx[j].astype(jnp.float32).T
        parts = []
        for h in range(heads):
            part = slice(h * HEAD, (h + 1) * HEAD)
            grad_h = grad_ctx[j, :, part]
            delta = jnp.sum(grad_t[part] * mixed[j, h], axis=0, keepdims=True)
            query = q[h, j]
            dq = jnp.zeros((HEAD, TILE), jnp.float32)
            spans = ([(0, clear)] if clear else []) + [(clear, length_j)]
            for low_end, high_end in spans:
                probs = jnp.exp(nt(k[h, low_end:high_end], query) - lse[j, h])
                if low_end == clear:
                    probs = jnp.where(ids_col[low_end:high_end] <= query_ids, probs, 0.0)
                slope = nt(v[h, low_end:high_end], grad_h) - delta
                grad_scores = (probs * slope).astype(low)
                dv[h, low_end:high_end] += nn(probs.astype(low), grad_h)
                dk[h, low_end:high_end] += nn(grad_scores, query)
                dq = dq + nn(kt[h, :, low_end:high_end], grad_scores)
            parts.append(dq * HEAD**-0.5)
        grads[rows, :width] = jnp.concatenate(parts, axis=0).T.astype(low)
        grads[other, :width] = jnp.zeros((TILE, width), low)

    def write(step, carry):
        rows = pl.ds(pl.multiple_of(step * TILE, TILE), TILE)
        grads[rows, width:] = jnp.concatenate(
            [dk[h, rows] for h in range(heads)] + [dv[h, rows] for h in range(heads)], axis=1
        ).astype(low)
        return carry

    lax.fori_loop(0, row_tiles, write, 0)


def attend_back(grad_ctx, q, k, kt, v, mixed, lse, ids, heads):
    length = k.shape[1]
    low, f32 = q.dtype, jnp.float32
    return pl.pallas_call(
        functools.partial(attend_back_kernel, heads),
        out_shape=jax.ShapeDtypeStruct((length, 3 * heads * HEAD), low),
        in_specs=[IN_VMEM] * 9,
        out_specs=IN_VMEM,
        scratch_shapes=[pltpu.VMEM((heads, length, HEAD), f32)] * 2,
        compiler_params=pltpu.CompilerParams(vmem_limit_bytes=VMEM_BYTES),
        name="attend_back",
    )(grad_ctx, q, k, kt, v, mixed, lse, ids.reshape(-1, 1), ids.reshape(1, -1))


def norm_rows(hidden, gain, shift):
    row_mean = jnp.mean(hidden, axis=1, keepdims=True)
    row_var = jnp.mean(hidden * hidden, axis=1, keepdims=True) - row_mean * row_mean
    inv_scale = lax.rsqrt(row_var + epsilon)
    normed = (hidden - row_mean) * inv_scale
    return normed * gain + shift, normed, inv_scale


def norm_rows_back(grad, normed, inv_scale, gain):
    scaled = grad * gain
    first = jnp.mean(scaled, axis=1, keepdims=True)
    second = jnp.mean(scaled * normed, axis=1, keepdims=True)
    return inv_scale * (scaled - first - normed * second)


def fast_body(
    layer_input, cotangent, labels, block_ids, w_query, b_query, w_key, w_value, b_value,
    w_output, b_output, ln1_gain, ln1_bias, w_inner, b_inner, w_outer, b_outer,
    ln2_gain, ln2_bias, w_pooler, b_pooler, w_classes, b_classes,
):
    f32, bf16 = jnp.float32, jnp.bfloat16
    dp, row, col = place()
    rows, feat = layer_input.shape
    features = 2 * feat
    hidden = b_inner.shape[0]
    own = rows // 2
    heads = features // HEAD // ROWS
    wide = heads * HEAD
    vectors = [
        b_query, b_value, b_output, ln1_gain, ln1_bias, b_outer, ln2_gain, ln2_bias, b_inner
    ]
    count = sum(vector.shape[0] for vector in vectors) // feat
    padded, at = 0.0, 0
    full = (count + -count % 8) * feat
    for vector in vectors:
        size = vector.shape[0]
        padded = padded + jnp.pad(vector.astype(f32), (at, full - at - size))
        at += size
    (
        x_all, cot, vec_all, w_heads, q, k, kt, v, mixed, lse, context, w_o, w_1, w_2,
    ) = forward_links(
        layer_input, cotangent, padded.reshape(-1, feat), w_query, w_key, w_value, block_ids,
        [w_output.T, w_inner, w_outer.T],
    )
    x_all = x_all.reshape(ROWS * rows, features)
    w_heads = w_heads.reshape(features, 3 * wide)
    w_o = w_o.reshape(features, features)
    w_1 = w_1.reshape(features, 2 * hidden)
    w_2 = w_2.reshape(features, 2 * hidden)
    take = lambda start, number=1: vec_all[:, start : start + number].reshape(1, -1)
    bias_o, gain_one, shift_one, bias_2, gain_two, shift_two = [take(i) for i in range(2, 8)]
    bias_1 = take(8, count - 8)
    context = context.transpose(1, 0, 2).reshape(own, features)
    start = row * rows + lax.rem(row + col, 2) * own
    x_own = lax.dynamic_slice_in_dim(x_all, start, own, 0).astype(f32)

    hidden_one = x_own + contract_last(context, w_o) + bias_o
    stream, normed_one, inv_one = norm_rows(hidden_one, gain_one, shift_one)
    stream_low = stream.astype(bf16)
    pre_act = project(stream_low, w_1) + bias_1
    activ = gelu_exact(pre_act).astype(bf16)
    hidden_two = stream + contract_last(activ, w_2) + bias_2
    result, normed_two, inv_two = norm_rows(hidden_two, gain_two, shift_two)
    output = result.astype(bf16)

    holder = ((row == 0) & (col == 0)).astype(f32)
    first = output[0:1]
    pooled = jnp.tanh(project(first, w_pooler) + b_pooler.astype(f32))
    classes = w_classes.astype(f32)
    logits_own = jnp.dot(pooled, classes, precision=highest) + b_classes.astype(f32)
    onehot = (jnp.arange(w_classes.shape[1]) == labels[0]).astype(f32)
    grad_logits = jax.nn.softmax(logits_own, axis=-1) - onehot[None, :]
    grad_pre_pool = jnp.dot(grad_logits, classes.T, precision=highest) * (1.0 - pooled * pooled)
    grad_first = jnp.dot(grad_pre_pool, w_pooler.astype(f32).T, precision=highest)
    grad_result = cot.astype(f32).at[0].add(grad_first[0] * holder)

    total = lambda values: jnp.sum(values, axis=0)
    g_ln2_gain, g_ln2_bias = total(grad_result * normed_two), total(grad_result)
    grad_hidden_two = norm_rows_back(grad_result, normed_two, inv_two, gain_two)
    g_b_outer = total(grad_hidden_two)
    branch_two = grad_hidden_two.astype(bf16)
    g_w2 = contract_first(branch_two, activ)
    grad_pre = (project(branch_two, w_2) * gelu_slope(pre_act)).astype(bf16)
    g_b_inner = total(grad_pre.astype(f32))
    g_w1 = contract_first(stream_low, grad_pre)
    grad_stream = grad_hidden_two + contract_last(grad_pre, w_1)
    g_ln1_gain, g_ln1_bias = total(grad_stream * normed_one), total(grad_stream)
    grad_hidden_one = norm_rows_back(grad_stream, normed_one, inv_one, gain_one)
    g_b_output = total(grad_hidden_one)
    branch_one = grad_hidden_one.astype(bf16)
    g_wo = contract_first(branch_one, context)
    grad_context = project(branch_one, w_o).astype(bf16)
    grad_blocks = grad_context.reshape(own, ROWS, wide).transpose(1, 0, 2)
    grad_ctx, output = swap_blocks(grad_blocks, 3, output)

    grads_low = attend_back(grad_ctx, q, k, kt, v, mixed, lse, block_ids, heads)
    g_qkv = contract_first(x_all, grads_low).astype(bf16)
    grad_x = contract_last(grads_low, w_heads)
    tokens = grad_x.shape[0]
    grad_x = lax.dynamic_update_slice_in_dim(
        grad_x, lax.dynamic_slice_in_dim(grad_x, start, own, 0) + grad_hidden_one, start, 0
    ).astype(bf16)
    bias_sums = total(grads_low.astype(f32))
    spread = lambda part: lax.dynamic_update_slice(
        jnp.zeros((features,), f32), part, (row * wide,)
    )
    classes_count = w_classes.shape[1]
    tail = jnp.pad(
        jnp.concatenate([logits_own[0], grad_logits[0]]) * holder, (0, 128 - 2 * classes_count)
    )
    table = jnp.concatenate(
        [first[0].astype(f32) * holder, grad_pre_pool[0] * holder, pooled[0] * holder, tail]
    )
    sequences = lax.axis_size("dp")
    table = lax.dynamic_update_slice(
        jnp.zeros((sequences, table.shape[0]), f32), table[None], (dp, 0)
    )
    pieces = [
        spread(bias_sums[:wide]), spread(bias_sums[2 * wide :]), g_b_output, g_ln1_gain,
        g_ln1_bias, g_b_outer, g_ln2_gain, g_ln2_bias, g_b_inner, table.reshape(-1),
    ]
    packed = jnp.concatenate(pieces)
    packed = jnp.pad(packed, (0, -packed.shape[0] % 1024)).reshape(-1, 128)
    s_w1, s_w2, s_wo, s_q, grad_input, sums = reduce_all(
        [g.astype(bf16) for g in (g_w1, g_w2, g_wo)], g_qkv, grad_x, packed
    )
    depth = w_query.shape[0]
    s_q = s_q.transpose(0, 2, 1, 3).reshape(depth, 2, 3, wide).transpose(2, 0, 1, 3)
    s_q = s_q.reshape(3, depth, feat).astype(f32)
    sums = sums.reshape(-1)
    found, at = [], 0
    for piece in pieces:
        found.append(sums[at : at + piece.shape[0]])
        at += piece.shape[0]
    own_part = lambda full: lax.dynamic_slice_in_dim(
        full, col * (full.shape[0] // 2), full.shape[0] // 2
    )
    (
        g_b_query, g_b_value, g_b_output, g_ln1_gain, g_ln1_bias, g_b_outer, g_ln2_gain,
        g_ln2_bias, g_b_inner,
    ) = [own_part(full) for full in found[:-1]]
    table = found[-1].reshape(sequences, -1)
    firsts, pre_pools, pools = [
        table[:, i * features : (i + 1) * features] for i in range(3)
    ]
    ends = table[:, 3 * features :]
    all_grads = ends[:, classes_count : 2 * classes_count]
    logits = lax.dynamic_slice_in_dim(ends[:, :classes_count], dp, 1, 0)
    outer = lambda left, right: jnp.sum(left[:, :, None] * right[:, None, :], axis=0)
    return (
        output, logits, grad_input, s_q[0], g_b_query, s_q[1], s_q[2], g_b_value,
        s_wo.reshape(depth, feat).astype(f32).T, g_b_output, g_ln1_gain, g_ln1_bias,
        s_w1.reshape(depth, hidden).astype(f32), g_b_inner,
        s_w2.reshape(depth, hidden).astype(f32).T, g_b_outer, g_ln2_gain, g_ln2_bias,
        outer(firsts, pre_pools), total(pre_pools), outer(pools, all_grads), total(all_grads),
    )


def is_fast(mesh):
    sizes = mesh.shape
    return sizes["dp"] == 4 and sizes["row"] == ROWS and sizes["col"] == 2


def solution(mesh):
    placed = (
        P(("dp", "row"), "col"),
        P(("dp", "row"), "col"),
        P("dp"),
        P("dp"),
        P("row", "col"),
        P("col"),
        P("row", "col"),
        P("row", "col"),
        P("col"),
        P("col", "row"),
        P("col"),
        P("col"),
        P("col"),
        P("row", "col"),
        P("col"),
        P("col", "row"),
        P("col"),
        P("col"),
        P("col"),
        P(),
        P(),
        P(),
        P(),
    )
    return jax.shard_map(
        fast_body if is_fast(mesh) else body,
        mesh=mesh,
        in_specs=placed,
        out_specs=(
            P(("dp", "row"), "col"),
            P("dp", None),
            P(("dp", "row"), "col"),
            P("row", "col"),
            P("col"),
            P("row", "col"),
            P("row", "col"),
            P("col"),
            P("col", "row"),
            P("col"),
            P("col"),
            P("col"),
            P("row", "col"),
            P("col"),
            P("col", "row"),
            P("col"),
            P("col"),
            P("col"),
            P(),
            P(),
            P(),
            P(),
        ),
        check_vma=False,
    )
```

```python
import functools

import jax
import jax.numpy as jnp
from jax import lax
from jax.experimental import pallas as pl
from jax.experimental.pallas import tpu as pltpu
from jax.sharding import PartitionSpec as P

HEAD = 64


highest = lax.Precision.HIGHEST
epsilon = 1e-05
root_half = 0.7071067811865476
inv_root_tau = 0.3989422804014327
masked_score = -1e30


def gelu_exact(values):
    return values * 0.5 * (1.0 + lax.erf(values * root_half))


def gelu_slope(values):
    return 0.5 * (1.0 + lax.erf(values * root_half)) + values * inv_root_tau * jnp.exp(
        -0.5 * values * values
    )


def project(left, right):
    return jnp.dot(left, right, preferred_element_type=jnp.float32)


def contract_first(left, right):
    return lax.dot_general(
        left, right, (((0,), (0,)), ((), ())), preferred_element_type=jnp.float32
    )


def contract_last(left, right):
    return lax.dot_general(
        left, right, (((1,), (1,)), ((), ())), preferred_element_type=jnp.float32
    )


def gather_features(values):
    return lax.all_gather(values, "col", axis=1, tiled=True)


def sum_features(values):
    return lax.psum_scatter(
        values.astype(jnp.bfloat16), "col", scatter_dimension=1, tiled=True
    ).astype(jnp.float32)


def feature_totals(first_part, second_part):
    return lax.psum((jnp.sum(first_part, axis=1), jnp.sum(second_part, axis=1)), "col")


def norm_forward(hidden, gain, shift, features):
    row_total, square_total = feature_totals(hidden, hidden * hidden)
    row_mean = row_total / features
    row_var = square_total / features - row_mean * row_mean
    inv_scale = lax.rsqrt(row_var + epsilon)
    normed = (hidden - row_mean[:, None]) * inv_scale[:, None]
    return (normed * gain + shift, normed, inv_scale)


def norm_backward(grad, normed, inv_scale, gain, features):
    scaled = grad * gain
    first_total, second_total = feature_totals(scaled, scaled * normed)
    return inv_scale[:, None] * (
        scaled - (first_total / features)[:, None] - normed * (second_total / features)[:, None]
    )


def key_split(piece_rows, rows_dev):
    return (piece_rows // rows_dev, rows_dev)


def body(
    layer_input,
    cotangent,
    labels,
    block_ids,
    w_query,
    b_query,
    w_key,
    w_value,
    b_value,
    w_output,
    b_output,
    ln1_gain,
    ln1_bias,
    w_inner,
    b_inner,
    w_outer,
    b_outer,
    ln2_gain,
    ln2_bias,
    w_pooler,
    b_pooler,
    w_classes,
    b_classes,
):
    f32 = jnp.float32
    bf16 = jnp.bfloat16
    rows_dev, feat_col = layer_input.shape
    heads_col = feat_col // HEAD
    features = feat_col * lax.axis_size("col")
    row_index = lax.axis_index("row")
    col_index = lax.axis_index("col")
    seq_index = lax.axis_index("dp")
    seq_count = lax.axis_size("dp")
    score_scale = HEAD ** (-0.5)
    query_ids = lax.dynamic_slice_in_dim(block_ids, row_index * rows_dev, rows_dev)
    last_query = query_ids[rows_dev - 1]
    wq_full, wk_full, wv_full, w1_full = (
        lax.all_gather(w_query, "row", axis=0, tiled=True),
        lax.all_gather(w_key, "row", axis=0, tiled=True),
        lax.all_gather(w_value, "row", axis=0, tiled=True),
        lax.all_gather(w_inner, "row", axis=0, tiled=True),
    )
    wo_full, w2_full = (
        lax.all_gather(w_output, "row", axis=1, tiled=True),
        lax.all_gather(w_outer, "row", axis=1, tiled=True),
    )
    input_whole = gather_features(layer_input)
    queries = (project(input_whole, wq_full) + b_query.astype(f32)).astype(bf16)
    keys_local = project(input_whole, wk_full).astype(bf16)
    values_local = (project(input_whole, wv_full) + b_value.astype(f32)).astype(bf16)
    queries3 = queries.reshape(rows_dev, heads_col, HEAD)
    start_state = (
        jnp.full((heads_col, rows_dev), masked_score, f32),
        jnp.zeros((heads_col, rows_dev), f32),
        jnp.zeros((heads_col, rows_dev, HEAD), f32),
    )
    running = start_state
    keys_piece = lax.all_gather(keys_local, "row", axis=0, tiled=True)
    values_piece = lax.all_gather(values_local, "row", axis=0, tiled=True)
    piece_rows = keys_piece.shape[0]
    number, block_rows = key_split(piece_rows, rows_dev)
    keys4 = keys_piece.reshape(number, block_rows, heads_col, HEAD)
    values4 = values_piece.reshape(number, block_rows, heads_col, HEAD)
    piece_ids = block_ids.reshape(number, block_rows)

    def attend_block_work(state, block_item):
        peak_score, row_mass, accum = state
        keys3, values3, key_ids = block_item
        scores = (
            jnp.einsum("qhd,khd->hqk", queries3, keys3, preferred_element_type=f32) * score_scale
        )
        allowed = (key_ids[None, :] <= query_ids[:, None])[None]
        block_top = jnp.max(jnp.where(allowed, scores, masked_score), axis=2)
        new_peak = jnp.maximum(peak_score, block_top)
        weights = jnp.where(allowed, jnp.exp(scores - new_peak[:, :, None]), 0.0)
        factor = jnp.exp(peak_score - new_peak)
        row_mass = row_mass * factor + jnp.sum(weights, axis=2)
        accum = accum * factor[:, :, None] + jnp.einsum(
            "hqk,khd->hqd", weights.astype(bf16), values3, preferred_element_type=f32
        )
        return (new_peak, row_mass, accum)

    def attend_block_step(state, block_item):
        state = lax.cond(
            block_item[2][0] > last_query, lambda st, item: st, attend_block_work, state, block_item
        )
        return (state, None)

    running, unused = lax.scan(attend_block_step, running, (keys4, values4, piece_ids))
    peak_score, row_mass, accum = running
    mixed = accum / row_mass[:, :, None]
    log_mass = peak_score + jnp.log(row_mass)
    context_low = mixed.transpose(1, 0, 2).reshape(rows_dev, feat_col).astype(bf16)
    attn_branch = sum_features(project(context_low, wo_full))
    hidden_one = layer_input.astype(f32) + attn_branch + b_output.astype(f32)
    gain_one = ln1_gain.astype(f32)
    stream, normed_one, inv_one = norm_forward(hidden_one, gain_one, ln1_bias.astype(f32), features)
    stream_whole = gather_features(stream.astype(bf16))
    pre_act = project(stream_whole, w1_full) + b_inner.astype(f32)
    activ = gelu_exact(pre_act).astype(bf16)
    ffn_branch = sum_features(project(activ, w2_full))
    hidden_two = stream + ffn_branch + b_outer.astype(f32)
    gain_two = ln2_gain.astype(f32)
    result, normed_two, inv_two = norm_forward(hidden_two, gain_two, ln2_bias.astype(f32), features)
    output = result.astype(bf16)
    row_zero = (row_index == 0).astype(f32)
    pool_input = gather_features(output[0:1])
    pooled = jnp.tanh(project(pool_input, w_pooler) + b_pooler.astype(f32))
    classes_f32 = w_classes.astype(f32)
    logits_own = jnp.dot(pooled, classes_f32, precision=highest) + b_classes.astype(f32)
    onehot = (jnp.arange(w_classes.shape[1]) == labels[0]).astype(f32)
    grad_logits = jax.nn.softmax(logits_own, axis=-1) - onehot[None, :]
    g_w_classes = jnp.dot(pooled.T, grad_logits, precision=highest)
    g_b_classes = grad_logits[0]
    grad_pre_pool = jnp.dot(grad_logits, classes_f32.T, precision=highest) * (1.0 - pooled * pooled)
    g_b_pooler = grad_pre_pool[0]
    g_w_pooler = jnp.dot(pool_input.astype(f32).T, grad_pre_pool, precision=highest)
    grad_first = jnp.dot(grad_pre_pool, w_pooler.astype(f32).T, precision=highest)
    first_col = lax.dynamic_slice_in_dim(grad_first[0], col_index * feat_col, feat_col)
    grad_result = cotangent.astype(f32).at[0].add(first_col * row_zero)
    logits_table = lax.dynamic_update_slice_in_dim(
        jnp.zeros((seq_count, w_classes.shape[1]), f32), logits_own * row_zero, seq_index, 0
    )
    g_ln2_gain = jnp.sum(grad_result * normed_two, axis=0)
    g_ln2_bias = jnp.sum(grad_result, axis=0)
    grad_hidden_two = norm_backward(grad_result, normed_two, inv_two, gain_two, features)
    g_b_outer = jnp.sum(grad_hidden_two, axis=0)
    branch_two_whole = gather_features(grad_hidden_two.astype(bf16))
    g_w_outer_full = contract_first(activ, branch_two_whole)
    grad_act = contract_last(branch_two_whole, w2_full)
    grad_pre = (grad_act * gelu_slope(pre_act)).astype(bf16)
    g_b_inner = jnp.sum(grad_pre.astype(f32), axis=0)
    g_w_inner_full = contract_first(stream_whole, grad_pre)
    grad_stream = grad_hidden_two + sum_features(contract_last(grad_pre, w1_full))
    g_ln1_gain = jnp.sum(grad_stream * normed_one, axis=0)
    g_ln1_bias = jnp.sum(grad_stream, axis=0)
    grad_hidden_one = norm_backward(grad_stream, normed_one, inv_one, gain_one, features)
    g_b_output = jnp.sum(grad_hidden_one, axis=0)
    branch_one_whole = gather_features(grad_hidden_one.astype(bf16))
    g_w_output_full = contract_first(context_low, branch_one_whole)
    grad_context = contract_last(branch_one_whole, wo_full).astype(bf16)
    grad_ctx3 = grad_context.reshape(rows_dev, heads_col, HEAD)
    delta = jnp.sum(grad_ctx3.astype(f32).transpose(1, 0, 2) * mixed, axis=2)

    def score_grads(queries_blk, grad_ctx_blk, keys3, values3, allowed, lse_blk, delta_blk):
        scores = (
            jnp.einsum("qhd,khd->hqk", queries_blk, keys3, preferred_element_type=f32) * score_scale
        )
        probs = jnp.where(allowed, jnp.exp(scores - lse_blk[:, :, None]), 0.0)
        grad_probs = jnp.einsum("qhd,khd->hqk", grad_ctx_blk, values3, preferred_element_type=f32)
        grad_scores = (probs * (grad_probs - delta_blk[:, :, None])).astype(bf16)
        return (probs, grad_scores)

    zero_q = jnp.zeros((rows_dev, heads_col, HEAD), f32)
    keys_piece = lax.all_gather(keys_local, "row", axis=0, tiled=True)
    values_piece = lax.all_gather(values_local, "row", axis=0, tiled=True)
    piece_rows = keys_piece.shape[0]
    number, block_rows = key_split(piece_rows, rows_dev)
    keys4 = keys_piece.reshape(number, block_rows, heads_col, HEAD)
    values4 = values_piece.reshape(number, block_rows, heads_col, HEAD)
    piece_ids = block_ids.reshape(number, block_rows)

    def make_block_work(accum_q, block_item):
        keys3, values3, key_ids = block_item
        allowed = (key_ids[None, :] <= query_ids[:, None])[None]
        probs, grad_scores = score_grads(
            queries3, grad_ctx3, keys3, values3, allowed, log_mass, delta
        )
        accum_q = (
            accum_q
            + jnp.einsum("hqk,khd->qhd", grad_scores, keys3, preferred_element_type=f32)
            * score_scale
        )
        part_k = (
            jnp.einsum("hqk,qhd->khd", grad_scores, queries3, preferred_element_type=f32)
            * score_scale
        )
        part_v = jnp.einsum(
            "hqk,qhd->khd", probs.astype(bf16), grad_ctx3, preferred_element_type=f32
        )
        return (accum_q, (part_k, part_v))

    def block_skip(accum_q, block_item):
        empty = jnp.zeros((block_rows, heads_col, HEAD), f32)
        return (accum_q, (empty, empty))

    def make_block_step(accum_q, block_item):
        return lax.cond(
            block_item[2][0] > last_query, block_skip, make_block_work, accum_q, block_item
        )

    grad_q = zero_q
    grad_q, (parts_k, parts_v) = lax.scan(make_block_step, grad_q, (keys4, values4, piece_ids))
    parts_k = parts_k.reshape(piece_rows, feat_col)
    parts_v = parts_v.reshape(piece_rows, feat_col)
    grad_k_all = parts_k
    grad_v_all = parts_v
    back_result = (grad_q, grad_k_all, grad_v_all)
    grad_q3, grad_k_all, grad_v_all = back_result
    grad_keys, grad_values = (
        lax.psum_scatter(
            grad_k_all.astype(jnp.bfloat16), "row", scatter_dimension=0, tiled=True
        ).astype(jnp.float32),
        lax.psum_scatter(
            grad_v_all.astype(jnp.bfloat16), "row", scatter_dimension=0, tiled=True
        ).astype(jnp.float32),
    )
    queries_grad = grad_q3.reshape(rows_dev, feat_col).astype(bf16)
    keys_grad = grad_keys.astype(bf16)
    values_grad = grad_values.astype(bf16)
    g_b_query = jnp.sum(queries_grad.astype(f32), axis=0)
    g_b_value = jnp.sum(values_grad.astype(f32), axis=0)
    g_w_query_full = contract_first(input_whole, queries_grad)
    g_w_key_full = contract_first(input_whole, keys_grad)
    g_w_value_full = contract_first(input_whole, values_grad)
    grad_input_whole = (
        contract_last(queries_grad, wq_full)
        + contract_last(keys_grad, wk_full)
        + contract_last(values_grad, wv_full)
    )
    grad_input = (grad_hidden_one + sum_features(grad_input_whole)).astype(bf16)
    in_rows = w_query.shape[0]
    out_cols = w_output.shape[1]
    (
        sum_wq,
        sum_wk,
        sum_wv,
        sum_w1,
        sum_wo,
        sum_w2,
        g_w_pooler,
        g_b_pooler,
        g_w_classes,
        g_b_classes,
        g_b_query,
        g_b_value,
        g_b_output,
        g_ln1_gain,
        g_ln1_bias,
        g_b_inner,
        g_b_outer,
        g_ln2_gain,
        g_ln2_bias,
        logits_all,
    ) = lax.psum(
        (
            g_w_query_full,
            g_w_key_full,
            g_w_value_full,
            g_w_inner_full,
            g_w_output_full,
            g_w_outer_full,
            g_w_pooler * row_zero,
            g_b_pooler * row_zero,
            g_w_classes * row_zero,
            g_b_classes * row_zero,
            g_b_query,
            g_b_value,
            g_b_output,
            g_ln1_gain,
            g_ln1_bias,
            g_b_inner,
            g_b_outer,
            g_ln2_gain,
            g_ln2_bias,
            logits_table,
        ),
        ("dp", "row"),
    )
    row_start = row_index * in_rows
    col_start = row_index * out_cols
    g_w_query = lax.dynamic_slice_in_dim(sum_wq, row_start, in_rows, 0)
    g_w_key = lax.dynamic_slice_in_dim(sum_wk, row_start, in_rows, 0)
    g_w_value = lax.dynamic_slice_in_dim(sum_wv, row_start, in_rows, 0)
    g_w_inner = lax.dynamic_slice_in_dim(sum_w1, row_start, in_rows, 0)
    g_w_output = lax.dynamic_slice_in_dim(sum_wo, col_start, out_cols, 1)
    g_w_outer = lax.dynamic_slice_in_dim(sum_w2, col_start, out_cols, 1)
    logits = lax.dynamic_slice_in_dim(logits_all, seq_index, 1, 0)
    return (
        output,
        logits,
        grad_input,
        g_w_query,
        g_b_query,
        g_w_key,
        g_w_value,
        g_b_value,
        g_w_output,
        g_b_output,
        g_ln1_gain,
        g_ln1_bias,
        g_w_inner,
        g_b_inner,
        g_w_outer,
        g_b_outer,
        g_ln2_gain,
        g_ln2_bias,
        g_w_pooler,
        g_b_pooler,
        g_w_classes,
        g_b_classes,
    )


MESH_IDS = pl.DeviceIdType.MESH
ROWS = 4
VMEM_BYTES = 64000 * 1024


def place():
    return lax.axis_index("dp"), lax.axis_index("row"), lax.axis_index("col")


class Links:
    def __init__(self, send, recv):
        self.send, self.recv = send, recv
        self.sends, self.recvs, self.open = 0, 0, []

    def slots(self, count):
        base = self.recvs
        self.recvs += count
        return base

    def push(self, source, target, slot, device, when=None):
        copy = pltpu.make_async_remote_copy(
            src_ref=source,
            dst_ref=target,
            send_sem=self.send.at[self.sends],
            recv_sem=self.recv.at[slot],
            device_id=device,
            device_id_type=MESH_IDS,
        )
        self.sends += 1
        if when is None:
            copy.start()
        else:
            pl.when(when)(lambda: copy.start())
        self.open.append((copy, when))

    def arrive(self, target, slot, device, when=None):
        copy = pltpu.make_async_remote_copy(
            src_ref=target,
            dst_ref=target,
            send_sem=self.send.at[0],
            recv_sem=self.recv.at[slot],
            device_id=device,
            device_id_type=MESH_IDS,
        )
        if when is None:
            copy.wait_recv()
        else:
            pl.when(when)(lambda: copy.wait_recv())

    def drain(self):
        for copy, when in self.open:
            if when is None:
                copy.wait_send()
            else:
                pl.when(when)(lambda copy=copy: copy.wait_send())
        self.open = []


def meet(devices):
    barrier = pltpu.get_barrier_semaphore()
    for device in devices:
        pl.semaphore_signal(barrier, inc=1, device_id=device, device_id_type=MESH_IDS)
    pl.semaphore_wait(barrier, len(devices))


def within(value):
    return (value >= 0) & (value < ROWS)


def steps_of_line(row):
    for step in (1, 2, 3):
        for way in (1, -1):
            source = row - way * step
            yield step, way, (3 - step if way == 1 else step - 1), source, within(source)


def columns(col, width):
    return pl.ds(pl.multiple_of(col * width, 128), width)


IN_VMEM = pl.BlockSpec(memory_space=pltpu.VMEM)
IN_PLACE = pl.BlockSpec(memory_space=pl.ANY)


def comm_params(number):
    return pltpu.CompilerParams(
        collective_id=number, has_side_effects=True, vmem_limit_bytes=VMEM_BYTES
    )


TILE = 256
NEAR = 3


def nt(left, right):
    return lax.dot_general(
        left, right, (((1,), (1,)), ((), ())), preferred_element_type=jnp.float32
    )


def nn(left, right):
    return jnp.dot(left, right, preferred_element_type=jnp.float32)


def forward_kernel(widths, heads, x, cot, vec, wq, wk, wv, ids, *refs):
    count = len(widths)
    shards, refs = refs[:count], refs[count:]
    x_all, cot_own, vec_all, w_heads, q_out, kv_out, kt_out, mixed_out, lse_out, context = refs[:10]
    fulls, refs = refs[10 : 10 + count], refs[10 + count :]
    vt_out, ids_col, packs, low_out, send, recv, local = refs
    dp, row, col = place()
    links = Links(send, recv)
    low = x.dtype
    rows_dev, feat = x.shape
    wide = heads * HEAD
    mate = (dp, row, 1 - col)
    at_row = lambda other: (dp, other, col)
    at_dp = lambda flip: (dp ^ flip, row, col)
    home, side = row // 2, lax.rem(row, 2)
    mine = lax.rem(row + col, 2)
    half = rows_dev // 2
    meet([at_row(lax.rem(row + k, ROWS)) for k in (1, 2, 3)] + [at_dp(1), at_dp(2), mate])

    x_at = lambda k: x_all.at[k, :, columns(col, feat)]
    x_mate_at = lambda k: x_all.at[k, :, columns(1 - col, feat)]
    w_at = lambda i, k, q: fulls[i].at[k, q, :, columns(col, widths[i])]
    row_at = lambda i, k: fulls[i].at[k, :, :, columns(col, widths[i])]
    row_mate_at = lambda i, k: fulls[i].at[k, :, :, columns(1 - col, widths[i])]

    line_x, mate_x = links.slots(3), links.slots(4)
    line_q, first_q, second_q, mate_q = (
        links.slots(3), links.slots(3), links.slots(6), links.slots(1),
    )
    mate_cot, mate_vec, swap = links.slots(1), links.slots(1), links.slots(3)
    line_w = [links.slots(3) for _ in widths]
    first_w = [links.slots(3) for _ in widths]
    second_w = [links.slots(6) for _ in widths]
    mate_w = [links.slots(4) for _ in widths]
    steps = list(steps_of_line(row))
    at_step = lambda step: [entry[2:] for entry in steps if entry[0] == step]

    def relay(step, own, full, base):
        for way in (1, -1):
            held, onward = row - way * (step - 1), row + way
            ok = within(held) & within(onward)
            slot = 3 - step if way == 1 else step - 1
            links.push(own if step == 1 else full(held), full(held), base + slot, at_row(onward), ok)

    relay(1, x, x_at, line_x)
    links.push(x, x_at(row), mate_x, mate)
    for j in range(2):
        pieces = []
        for h in range(heads):
            part = slice(j * wide + h * HEAD, j * wide + (h + 1) * HEAD)
            pieces += [wk[:, part], wv[:, part]]
        pieces.append(wq[:, j * wide : (j + 1) * wide])
        packs[j] = jnp.concatenate(pieces, axis=1).reshape(packs.shape[1:])
    for j in range(2):
        k = 2 * col + j
        away = k != row
        slot = lax.rem(row - k + ROWS + 3, ROWS)
        links.push(packs.at[j, dp], w_heads.at[row, dp], line_q + slot, at_row(k), away)

        @pl.when(jnp.logical_not(away))
        def _(j=j):
            w_heads[row] = packs[j]

    links.push(
        cot.at[pl.ds(pl.multiple_of((1 - mine) * half, 128), half)],
        cot_own.at[:, columns(col, feat)],
        mate_cot,
        mate,
    )
    links.push(vec, vec_all.at[col], mate_vec, mate)
    cot_own[:, columns(col, feat)] = cot[pl.ds(pl.multiple_of(mine * half, 128), half)]
    vec_all[col] = vec[...]
    x_all[row, :, columns(col, feat)] = x[...]
    copies = [
        pltpu.make_async_copy(shards[i], row_at(i, row), local.at[i]) for i in range(count)
    ]

    at_home = home == col

    def q_first():
        for slot in range(3):
            k = lax.rem(row + slot + 1, ROWS)
            one = 1 + slot % 2
            links.arrive(w_heads.at[k, dp], line_q + slot, mate, at_home)
            links.push(
                w_heads.at[k, dp], w_heads.at[k, dp], first_q + slot, at_dp(one), at_home
            )

    def q_second():
        for slot in range(3):
            k = lax.rem(row + slot + 1, ROWS)
            one, two = 1 + slot % 2, 2 - slot % 2
            links.arrive(w_heads.at[k, dp ^ one], first_q + slot, mate, at_home)
            for n, q in enumerate((dp, dp ^ one)):
                links.push(
                    w_heads.at[k, q], w_heads.at[k, q], second_q + 2 * slot + n, at_dp(two), at_home
                )

    def q_mate():
        for slot in range(3):
            k = lax.rem(row + slot + 1, ROWS)
            two = 2 - slot % 2
            links.arrive(w_heads.at[k, dp ^ two], second_q + 2 * slot, mate, at_home)
            links.arrive(w_heads.at[k, dp ^ 3], second_q + 2 * slot + 1, mate, at_home)
        links.push(w_heads, w_heads, mate_q, mate, at_home)
        links.arrive(w_heads, mate_q, mate, jnp.logical_not(at_home))

    def x_step(step):
        for slot, k, ok in at_step(step):
            links.arrive(x_at(k), line_x + slot, mate, ok)
        if step < 3:
            relay(step + 1, x, x_at, line_x)
        for slot, k, ok in at_step(step):
            links.push(x_at(k), x_at(k), mate_x + 1 + slot, mate, ok)

    turn = lambda i, slot: (1, 2) if (i + slot) % 2 == 0 else (2, 1)

    def w_relay(step):
        for i in range(count):
            relay(step, shards[i].at[dp], lambda k, i=i: w_at(i, k, dp), line_w[i])

    def w_first(step):
        for i in range(count):
            for slot, k, ok in at_step(step):
                links.arrive(w_at(i, k, dp), line_w[i] + slot, mate, ok)
        if step < 3:
            w_relay(step + 1)
        for i in range(count):
            for slot, k, ok in at_step(step):
                one, two = turn(i, slot)
                links.push(w_at(i, k, dp), w_at(i, k, dp), first_w[i] + slot, at_dp(one), ok)

    def w_second(step):
        for i in range(count):
            for slot, k, ok in at_step(step):
                one, two = turn(i, slot)
                links.arrive(w_at(i, k, dp ^ one), first_w[i] + slot, mate, ok)
                for n, q in enumerate((dp, dp ^ one)):
                    links.push(
                        w_at(i, k, q), w_at(i, k, q), second_w[i] + 2 * slot + n, at_dp(two), ok
                    )

    def w_mate(step):
        for i in range(count):
            for slot, k, ok in at_step(step):
                one, two = turn(i, slot)
                links.arrive(w_at(i, k, dp ^ two), second_w[i] + 2 * slot, mate, ok)
                links.arrive(w_at(i, k, dp ^ 3), second_w[i] + 2 * slot + 1, mate, ok)
                links.push(row_at(i, k), row_at(i, k), mate_w[i] + 1 + slot, mate, ok)

    row_tiles = ROWS * rows_dev // TILE
    per_row = rows_dev // TILE

    def split_ids(step, carry):
        span = pl.ds(pl.multiple_of(step * TILE, TILE), TILE)
        ids_col[span] = jnp.broadcast_to(ids[:, span], (8, TILE)).T[:, :1]
        return carry

    lax.fori_loop(0, row_tiles, split_ids, 0)
    x_step(1)
    q_first()
    x_step(2)
    q_second()
    w_relay(1)
    for copy in copies:
        copy.start()
    for i in range(count):
        links.push(shards[i], row_at(i, row), mate_w[i], mate)
    q_mate()
    links.arrive(vec_all.at[1 - col], mate_vec, mate)
    bias_of = lambda n: jnp.where(
        side == 0, vec_all[home, n : n + 1, :wide], vec_all[home, n : n + 1, wide : 2 * wide]
    )
    bias_q, bias_v = bias_of(0), bias_of(1)
    blank = jnp.zeros((1, HEAD), jnp.float32)
    bias_kv = jnp.concatenate(
        sum([[blank, bias_v[:, h * HEAD : (h + 1) * HEAD]] for h in range(heads)], []), axis=1
    )
    weights = lambda start, stop: w_heads[:, :, :, start:stop].reshape(2 * feat, stop - start)

    def project_keys(k):
        def one_tile(step, carry):
            here = pl.ds(pl.multiple_of(step * TILE, TILE), TILE)
            rows = pl.ds(pl.multiple_of(k * rows_dev + step * TILE, TILE), TILE)
            both = nn(x_all[k, here], weights(0, 2 * wide)) + bias_kv
            both_t = both.T
            for h in range(heads):
                at = 2 * h * HEAD
                kv_out[h, rows] = both[:, at : at + 2 * HEAD].astype(low)
                kt_out[h, :, rows] = both_t[at : at + HEAD].astype(low)
                vt_out[h, :, rows] = both_t[at + HEAD : at + 2 * HEAD].astype(low)
            return carry

        lax.fori_loop(0, per_row, one_tile, 0)

    links.arrive(x_mate_at(row), mate_x, mate)
    project_keys(row)
    x_step(3)
    for slot in (0, 2, 1):
        k = lax.rem(row + slot + 1, ROWS)
        links.arrive(x_mate_at(k), mate_x + 1 + slot, mate)
        project_keys(k)
        if slot == 2:
            w_first(1)

    def project_query(j, carry):
        block = 2 * j + lax.rem(j + col, 2)
        here = pl.ds(pl.multiple_of(lax.rem(block, per_row) * TILE, TILE), TILE)
        query = nn(x_all[block // per_row, here], weights(2 * wide, 3 * wide)) + bias_q
        query = query.astype(low) * jnp.asarray(HEAD**-0.5, low)
        for h in range(heads):
            q_out[h, j] = jnp.concatenate(
                [query[:, h * HEAD : (h + 1) * HEAD], jnp.zeros((TILE, HEAD), low)], axis=1
            )
        return carry

    blocks = row_tiles // 2
    lax.fori_loop(0, blocks, project_query, 0)
    w_first(2)
    for j in range(blocks):
        block = 2 * j + lax.rem(j + col, 2)
        rows = pl.ds(pl.multiple_of(block * TILE, TILE), TILE)
        query_ids = ids[:, rows]
        length = min(2 * j + NEAR, row_tiles) * TILE
        clear = 2 * j * TILE

        def one_head(h, carry, j=j, query_ids=query_ids, length=length, clear=clear):
            scores = nt(kv_out[h, :length], q_out[h, j])
            near = jnp.where(
                ids_col[clear:length] <= query_ids, scores[clear:], masked_score
            )
            top = jnp.max(near, axis=0, keepdims=True)
            if clear:
                top = jnp.maximum(top, jnp.max(scores[:clear], axis=0, keepdims=True))
                weights_far = jnp.exp(scores[:clear] - top)
            weights_near = jnp.exp(near - top)
            mass = jnp.sum(weights_near, axis=0, keepdims=True)
            value = nn(vt_out[h, :, clear:length], weights_near.astype(low))
            if clear:
                mass = mass + jnp.sum(weights_far, axis=0, keepdims=True)
                value = value + nn(vt_out[h, :, :clear], weights_far.astype(low))
            mixed_out[j, h] = value / mass
            lse_out[j, h] = top + jnp.log(mass)
            return carry

        lax.fori_loop(0, heads, one_head, 0)
        low_out[j] = (
            jnp.concatenate([mixed_out[j, h] for h in range(heads)], axis=0).T.astype(low)
        )
        away = row != j
        slot = lax.rem(row - j + ROWS + 3, ROWS)
        links.push(low_out.at[j], context.at[row], swap + slot, at_row(j), away)

        @pl.when(jnp.logical_not(away))
        def _(j=j):
            context[row] = low_out[j]

        if j == 0:
            w_second(1)
        if j == 1:
            w_first(3)
            w_second(2)
            w_mate(1)
        if j == 2:
            w_second(3)
            w_mate(2)
    w_mate(3)
    links.arrive(cot_own.at[:, columns(1 - col, feat)], mate_cot, mate)
    for slot in range(3):
        links.arrive(context.at[lax.rem(row + slot + 1, ROWS)], swap + slot, mate)
    for i in range(count):
        links.arrive(row_mate_at(i, row), mate_w[i], mate)
        for slot in range(3):
            k = lax.rem(row + slot + 1, ROWS)
            links.arrive(row_mate_at(i, k), mate_w[i] + 1 + slot, mate)
    for copy in copies:
        copy.wait()
    links.drain()


def forward_links(x, cot, vec, wq, wk, wv, ids, shards):
    widths = [shard.shape[1] for shard in shards]
    rows, feat = x.shape
    low, f32 = x.dtype, jnp.float32
    part = shards[0].shape[0] // 4
    heads = 2 * feat // HEAD // ROWS
    wide = heads * HEAD
    length = ROWS * rows
    blocks = length // TILE // 2
    shape = jax.ShapeDtypeStruct
    shapes = [
        shape((ROWS, rows, 2 * feat), low),
        shape((rows // 2, 2 * feat), low),
        shape((2,) + vec.shape, vec.dtype),
        shape((ROWS, 4, part, 3 * wide), low),
        shape((heads, blocks, TILE, 2 * HEAD), low),
        shape((heads, length, 2 * HEAD), low),
        shape((heads, HEAD, length), low),
        shape((blocks, heads, HEAD, TILE), f32),
        shape((blocks, heads, 1, TILE), f32),
        shape((ROWS, rows // 2, wide), low),
    ] + [shape((ROWS, 4, part, 2 * width), low) for width in widths]
    return pl.pallas_call(
        functools.partial(forward_kernel, widths, heads),
        out_shape=shapes,
        in_specs=[IN_VMEM] * (7 + len(shards)),
        out_specs=[IN_VMEM] * 10 + [IN_PLACE] * len(shards),
        scratch_shapes=[
            pltpu.VMEM((heads, HEAD, length), low),
            pltpu.VMEM((length, 1), jnp.int32),
            pltpu.VMEM((2, 4, part, 3 * wide), low),
            pltpu.VMEM((blocks, TILE, wide), low),
            pltpu.SemaphoreType.DMA((160,)),
            pltpu.SemaphoreType.DMA((96,)),
            pltpu.SemaphoreType.DMA((4,)),
        ],
        compiler_params=comm_params(1),
        name="forward_links",
    )(
        x, cot, vec, wq, wk, wv, ids.reshape(1, -1),
        *[shard.reshape(4, part, -1) for shard in shards],
    )


def add_into(total, *others):
    def one(step, carry):
        value = total[step].astype(jnp.float32)
        for other in others:
            value = value + other[step].astype(jnp.float32)
        total[step] = value.astype(total.dtype)
        return carry

    lax.fori_loop(0, total.shape[0], one, 0)


def middle_kernel(
    heads, context_in, cot, vec_all, labels, b_pooler, w_classes, b_classes, w_pooler,
    w_o, x_all, w_1_far, w_2_far,
    output, late, stream_out, grad_pre_out, branch_two_out, activ_out, branch_one_out, context,
    grad_blocks, packed, x_own, w_1, w_2, slope, total, sems,
):
    f32, low = jnp.float32, output.dtype
    dp, row, col = place()
    own, features = output.shape
    wide = features // ROWS
    hidden = w_1.shape[1]
    chunk = features
    mine = lax.rem(row + col, 2)
    copies = [
        pltpu.make_async_copy(
            x_all.at[row, pl.ds(pl.multiple_of(mine * own, 128), own)], x_own, sems.at[0]
        ),
        pltpu.make_async_copy(w_1_far, w_1, sems.at[1]),
        pltpu.make_async_copy(w_2_far, w_2, sems.at[2]),
    ]
    for copy in copies:
        copy.start()
    vector = lambda n: jnp.concatenate([vec_all[0, n : n + 1], vec_all[1, n : n + 1]], axis=1)
    context[...] = jnp.concatenate([context_in[r] for r in range(ROWS)], axis=1)
    value = nt(context[...], w_o[...])
    copies[0].wait()
    hidden_one = x_own[...].astype(f32) + value + vector(2)
    gain_one, gain_two = vector(3), vector(6)
    stream, normed_one, inv_one = norm_rows(hidden_one, gain_one, vector(4))
    late[...] = stream
    stream_out[...] = stream.astype(low)
    total[...] = jnp.zeros_like(total)
    bias_1 = [
        jnp.concatenate(
            [vec_all[c, 8 + 2 * n : 9 + 2 * n], vec_all[c, 9 + 2 * n : 10 + 2 * n]], axis=1
        )
        for c in range(2)
        for n in range(hidden // chunk // 2)
    ]
    copies[1].wait()
    copies[2].wait()
    for n in range(hidden // chunk):
        span = slice(n * chunk, (n + 1) * chunk)
        pre_act = nn(stream_out[...], w_1[:, span]) + bias_1[n]
        half = 0.5 * (1.0 + lax.erf(pre_act * root_half))
        slope[:, span] = half + pre_act * inv_root_tau * jnp.exp(-0.5 * pre_act * pre_act)
        activ_out[:, span] = (pre_act * half).astype(low)
        total[...] += nt(activ_out[:, span], w_2[:, span])
    hidden_two = late[...] + total[...] + vector(5)
    result, normed_two, inv_two = norm_rows(hidden_two, gain_two, vector(7))
    output[...] = result.astype(low)

    classes = b_classes.shape[1]
    first = output[:8]
    pooled = jnp.tanh(nn(first, w_pooler[...])[:1] + b_pooler[...].astype(f32))
    lane = lax.broadcasted_iota(jnp.int32, (1, 128), 1)
    logits = jnp.full((1, 128), masked_score, f32)
    rows = [w_classes[n : n + 1].astype(f32) for n in range(classes)]
    for n in range(classes):
        logit = jnp.sum(pooled * rows[n], axis=1, keepdims=True) + b_classes[:, n : n + 1].astype(f32)
        logits = jnp.where(lane == n, logit, logits)
    odds = jnp.exp(logits - jnp.max(logits, axis=1, keepdims=True))
    odds = odds / jnp.sum(odds, axis=1, keepdims=True)
    grad_logits = odds - (lane == labels[0, 0]).astype(f32)
    grad_pool = jnp.zeros((1, features), f32)
    for n in range(classes):
        grad_pool = grad_pool + grad_logits[:, n : n + 1] * rows[n]
    grad_pool = grad_pool * (1.0 - pooled * pooled)
    high = grad_pool.astype(low)
    rest = grad_pool - high.astype(f32)
    mid = rest.astype(low)
    last = (rest - mid.astype(f32)).astype(low)
    split = jnp.concatenate(
        [high.astype(f32), mid.astype(f32), last.astype(f32), jnp.zeros((5, features), f32)]
    ).astype(low)
    grad_first = jnp.sum(nt(split, w_pooler[...]), axis=0, keepdims=True)
    holder = ((row == 0) & (col == 0)).astype(f32)
    top = (lax.broadcasted_iota(jnp.int32, (own, 1), 0) == 0).astype(f32) * holder
    grad_result = cot[...].astype(f32) + top * grad_first

    tokens = lambda values: jnp.sum(values, axis=0, keepdims=True)
    g_gain_two, g_shift_two = tokens(grad_result * normed_two), tokens(grad_result)
    grad_two = norm_rows_back(grad_result, normed_two, inv_two, gain_two)
    g_bias_two = tokens(grad_two)
    late[...] = grad_two
    branch_two_out[...] = grad_two.astype(low)
    total[...] = jnp.zeros_like(total)
    g_bias_one = []
    for n in range(hidden // chunk):
        span = slice(n * chunk, (n + 1) * chunk)
        grad_pre = (nn(branch_two_out[...], w_2[:, span]) * slope[:, span]).astype(low)
        grad_pre_out[:, span] = grad_pre
        g_bias_one.append(tokens(grad_pre.astype(f32)))
        total[...] += nt(grad_pre_out[:, span], w_1[:, span])
    grad_stream = late[...] + total[...]
    g_gain_one, g_shift_one = tokens(grad_stream * normed_one), tokens(grad_stream)
    grad_one = norm_rows_back(grad_stream, normed_one, inv_one, gain_one)
    late[...] = grad_one
    branch_one_out[...] = grad_one.astype(low)
    grad_context = nn(branch_one_out[...], w_o[...]).astype(low)
    for r in range(ROWS):
        grad_blocks[r] = grad_context[:, r * wide : (r + 1) * wide]

    feat = features // 2
    packed[...] = jnp.zeros_like(packed)
    vectors = [tokens(grad_one), g_gain_one, g_shift_one, g_bias_two, g_gain_two, g_shift_two]
    for n, value in enumerate(vectors):
        for c in range(2):
            packed[8 + 8 * c + n // 2, pl.ds((n % 2) * feat, feat)] = value[
                0, c * feat : (c + 1) * feat
            ]
    for n, value in enumerate(g_bias_one):
        packed[8 + 8 * (n // 2) + 3 + n % 2] = value[0]
    spare = jnp.zeros((1, features - 128), f32)
    shifted = pltpu.roll(jnp.where(lane < classes, grad_logits, 0.0), classes, 1)
    tail = jnp.concatenate([jnp.where(lane < classes, logits, shifted), spare], axis=1)
    for n, value in enumerate((first[:1].astype(f32), grad_pool, pooled, tail)):
        here = lax.broadcasted_iota(jnp.int32, (4, features), 0) == dp
        packed[24 + 4 * n : 28 + 4 * n] = jnp.where(here, value * holder, 0.0)


def middle(
    context, cot, vec_all, labels, b_pooler, w_classes, b_classes, w_pooler, w_o, x_all, w_1, w_2
):
    low, f32 = cot.dtype, jnp.float32
    own, features = cot.shape
    hidden = w_1.shape[1]
    heads = features // HEAD // ROWS
    shape = jax.ShapeDtypeStruct
    narrow, broad = shape((own, features), low), shape((own, hidden), low)
    return pl.pallas_call(
        functools.partial(middle_kernel, heads),
        out_shape=[
            narrow, shape((own, features), f32), narrow, broad, narrow, broad, narrow, narrow,
            shape((ROWS, own, features // ROWS), low), shape((40, features), f32),
        ],
        in_specs=[IN_VMEM] * 3 + [pl.BlockSpec(memory_space=pltpu.SMEM)] + [IN_VMEM] * 5
        + [IN_PLACE] * 3,
        out_specs=[IN_VMEM] * 10,
        scratch_shapes=[
            pltpu.VMEM((own, features), low),
            pltpu.VMEM((features, hidden), low),
            pltpu.VMEM((features, hidden), low),
            pltpu.VMEM((own, hidden), f32),
            pltpu.VMEM((own, features), f32),
            pltpu.SemaphoreType.DMA((3,)),
        ],
        compiler_params=pltpu.CompilerParams(vmem_limit_bytes=VMEM_BYTES),
        name="middle",
    )(
        context, cot, vec_all, labels.reshape(1, 1), b_pooler.reshape(1, -1), w_classes.T,
        b_classes.reshape(1, -1), w_pooler, w_o, x_all, w_1, w_2,
    )


CHUNK = 384


def backward_kernel(
    heads, blocks_in, output, late, stream, grad_pre, branch_two, activ, branch_one, context,
    q, kv, kt, mixed, lse, ids, x_all, w_heads, vec_in, *refs,
):
    out_g, refs = refs[:5], refs[5:]
    out_q, out_x, halves, vec, refs = refs[0], refs[1], refs[2], refs[3], refs[4:]
    pairs, refs = refs[:5], refs[5:]
    mates, refs = refs[:5], refs[5:]
    first, refs = refs[:6], refs[6:]
    second, refs = refs[:6], refs[6:]
    lines, refs = refs[:5], refs[5:]
    (
        grad_ctx, both, delta, dq, dkv, grads, grads_t, w_t, turned, ids_col, dx, sum_x,
        line_x, gq, sum_q, all_q, vec_mate, vec_line, vec_flat, send, recv,
    ) = refs
    dp, row, col = place()
    links = Links(send, recv)
    low, f32 = q.dtype, jnp.float32
    mate = (dp, row, 1 - col)
    peers = [lax.rem(row + n, ROWS) for n in (1, 2, 3)]
    at_row = lambda other: (dp, other, col)
    at_dp = lambda flip: (dp ^ flip, row, col)
    home, side = row // 2, lax.rem(row, 2)
    mine = lax.rem(row + col, 2)
    length = kv.shape[1]
    wide = heads * HEAD
    rows_dev, feat = out_x.shape
    half = rows_dev // 2
    row_tiles = length // TILE
    blocks = row_tiles // 2
    meet(
        [at_row(peer) for peer in peers]
        + [at_dp(1), at_dp(2), mate]
        + [(dp, peer, 1 - col) for peer in peers]
    )

    swap, slot_o = links.slots(3), links.slots(1)
    for n, peer in enumerate(peers):
        links.push(blocks_in.at[peer], grad_ctx.at[row], swap + 2 - n, at_row(peer))
    own_rows = pl.ds(pl.multiple_of(mine * half, 128), half)
    other_rows = pl.ds(pl.multiple_of((1 - mine) * half, 128), half)
    links.push(output.at[:, columns(1 - col, feat)], halves.at[own_rows], slot_o, mate)
    halves[own_rows] = output[:, columns(col, feat)]
    grad_ctx[row] = blocks_in[row]

    lefts = (stream, branch_two, branch_one)
    for n in range(3):
        turned[n] = lefts[n][...].astype(f32).T.astype(low)
    feeds = [(0, grad_pre, 0), (1, activ, 0), (0, grad_pre, 1), (1, activ, 1), (2, context, 0)]
    turns = [(1, 2), (2, 1), (1, 2), (2, 1), (1, 2), (2, 1)]
    widths = [out.shape[2] for out in out_g]
    slot_g = [links.slots(1) for _ in widths]

    def local_grad(i):
        left, right, part = feeds[i]
        width = widths[i]
        per = width // CHUNK

        def one(step, carry):
            which, n = step // per, step % per
            core = jnp.where(which == 0, 1 - col, col)
            start = core * (right.shape[1] // 2) + part * width + n * CHUNK
            value = nn(turned[left], right[:, pl.ds(pl.multiple_of(start, 128), CHUNK)])
            pairs[i][which, :, :, :, pl.ds(pl.multiple_of(n * CHUNK, 128), CHUNK)] = (
                value.astype(low).reshape(pairs[i].shape[1:4] + (CHUNK,))
            )
            return carry

        lax.fori_loop(0, 2 * per, one, 0)
        links.push(pairs[i].at[0], mates[i], slot_g[i], mate)

    totals = [pair.at[1] for pair in pairs] + [all_q]

    def send_first(i):
        one, two = turns[i]
        base = links.slots(2)
        links.push(totals[i].at[:, dp ^ 3], first[i].at[1], base + 1, at_dp(one))
        links.push(totals[i].at[:, dp ^ one], first[i].at[0], base, at_dp(one))
        return base

    def join(i):
        links.arrive(mates[i], slot_g[i], mate)

        def one(step, carry):
            at, q_at = step // 4, step % 4
            pairs[i][1, at, q_at] = (
                pairs[i][1, at, q_at].astype(f32) + mates[i][at, q_at].astype(f32)
            ).astype(low)
            return carry

        lax.fori_loop(0, 16, one, 0)
        return send_first(i)

    def send_second(i, base):
        one, two = turns[i]
        links.arrive(first[i].at[1], base + 1, mate)
        add_into(totals[i].at[:, dp ^ two], first[i].at[1])
        slot = links.slots(1)
        links.push(totals[i].at[:, dp ^ two], second[i], slot, at_dp(two))
        links.arrive(first[i].at[0], base, mate)
        add_into(totals[i].at[:, dp], first[i].at[0])
        return slot

    def send_line(i, slot):
        links.arrive(second[i], slot, mate)
        add_into(totals[i].at[:, dp], second[i])
        base = links.slots(3)
        for n, peer in enumerate(peers):
            links.push(totals[i].at[peer, dp], lines[i].at[2 - n], base + 2 - n, at_row(peer))
        return base

    def share(i, out):
        one, two = turns[i]
        base = links.slots(3)
        links.push(out.at[dp], out.at[dp], base, at_dp(two))
        links.push(out.at[dp], out.at[dp], base + 1, at_dp(one))
        return base

    def share_on(i, out, base):
        one, two = turns[i]
        links.arrive(out.at[dp ^ two], base, mate)
        links.push(out.at[dp ^ two], out.at[dp ^ two], base + 2, at_dp(one))

    def shared(i, out, base):
        one, two = turns[i]
        links.arrive(out.at[dp ^ one], base + 1, mate)
        links.arrive(out.at[dp ^ 3], base + 2, mate)

    stage = [None] * 6
    local_grad(0)
    local_grad(1)
    w_t[...] = w_heads[...].reshape(2 * feat, 3 * wide).astype(f32).T.astype(low)

    def split_ids(step, carry):
        span = pl.ds(pl.multiple_of(step * TILE, TILE), TILE)
        ids_col[span] = jnp.broadcast_to(ids[:, span], (8, TILE)).T[:, :1]
        return carry

    lax.fori_loop(0, row_tiles, split_ids, 0)
    dkv[...] = jnp.zeros_like(dkv)
    local_grad(2)
    stage[0] = join(0)
    for n, peer in enumerate(peers):
        links.arrive(grad_ctx.at[peer], swap + n, mate)

    def split_grad(j, carry):
        grad = grad_ctx[j]
        grad_t = grad.astype(f32).T
        for h in range(heads):
            part = slice(h * HEAD, (h + 1) * HEAD)
            both[h, j, :TILE] = q[h, j]
            both[h, j, TILE:] = jnp.concatenate(
                [jnp.zeros((TILE, HEAD), low), grad[:, part]], axis=1
            )
            delta[h, j] = jnp.sum(grad_t[part] * mixed[j, h], axis=0, keepdims=True)
        return carry

    lax.fori_loop(0, blocks, split_grad, 0)
    for j in range(blocks):
        block = 2 * j + lax.rem(j + col, 2)
        rows = pl.ds(pl.multiple_of(block * TILE, TILE), TILE)
        query_ids = ids[:, rows]
        far = 2 * j * TILE
        spans = ([(0, far)] if far else []) + [(far, min(2 * j + NEAR, row_tiles) * TILE)]

        def one_head(h, carry, j=j, query_ids=query_ids, far=far, spans=spans):
            total = jnp.zeros((HEAD, TILE), f32)
            for start, stop in spans:
                raw = nt(kv[h, start:stop], both[h, j])
                probs = jnp.exp(raw[:, :TILE] - lse[j, h])
                if start == far:
                    probs = jnp.where(ids_col[start:stop] <= query_ids, probs, 0.0)
                grad_scores = (probs * (raw[:, TILE:] - delta[h, j])).astype(low)
                dkv[h, start:stop] += nn(
                    jnp.concatenate([grad_scores, probs.astype(low)], axis=1), both[h, j]
                )
                total = total + nn(kt[h, :, start:stop], grad_scores)
            dq[j, h] = total * HEAD**-0.5
            return carry

        lax.fori_loop(0, heads, one_head, 0)
        if j == 0:
            stage[1] = join(1)
        if j == 1:
            stage[2] = join(2)
        if j == 2:
            stage[0], stage[1] = send_second(0, stage[0]), send_second(1, stage[1])
    stage[0], stage[1] = send_line(0, stage[0]), send_line(1, stage[1])

    def gather_q(j, carry):
        block = 2 * j + lax.rem(j + col, 2)
        rows = pl.ds(pl.multiple_of(block * TILE, TILE), TILE)
        other = pl.ds(pl.multiple_of((4 * j + 1 - block) * TILE, TILE), TILE)
        value = jnp.concatenate([dq[j, h] for h in range(heads)], axis=0)
        grads_t[2 * wide :, rows] = value.astype(low)
        grads_t[2 * wide :, other] = jnp.zeros((wide, TILE), low)
        grads[rows, 2 * wide :] = value.T.astype(low)
        grads[other, 2 * wide :] = jnp.zeros((TILE, wide), low)
        return carry + jnp.sum(value.T, axis=0, keepdims=True)

    bias_q = lax.fori_loop(0, blocks, gather_q, jnp.zeros((1, wide), f32))

    def gather_kv(step, carry):
        rows = pl.ds(pl.multiple_of(step * TILE, TILE), TILE)
        value = jnp.concatenate([dkv[h, rows] for h in range(heads)], axis=1)
        grads[rows, : 2 * wide] = value.astype(low)
        grads_t[: 2 * wide, rows] = value.T.astype(low)
        return carry + jnp.sum(value, axis=0, keepdims=True)

    bias_kv = lax.fori_loop(0, row_tiles, gather_kv, jnp.zeros((1, 2 * wide), f32))

    slot_x, slot_xl = links.slots(4), links.slots(3)
    per_row = rows_dev // TILE
    own_block = 2 * row + mine

    def token_grads(at):
        def one(step, carry):
            here = pl.ds(pl.multiple_of(step * TILE, TILE), TILE)
            rows = pl.ds(pl.multiple_of((at * per_row + step) * TILE, TILE), TILE)
            value = nn(grads[rows], w_t[...])
            is_own = (at * per_row + step == own_block).astype(f32)
            dx[at, here] = (value + late[...] * is_own).astype(low)
            return carry

        lax.fori_loop(0, per_row, one, 0)

    for n, peer in enumerate(peers):
        token_grads(peer)
        links.push(
            dx.at[peer, :, columns(1 - col, feat)], sum_x.at[peer], slot_x + n, mate
        )
    token_grads(row)
    links.push(dx.at[row, :, columns(1 - col, feat)], sum_x.at[row], slot_x + 3, mate)

    def join_x(at, slot):
        links.arrive(sum_x.at[at], slot, mate)

        def one(step, carry):
            here = pl.ds(pl.multiple_of(step * 128, 128), 128)
            sum_x[at, here] = (
                sum_x[at, here].astype(f32) + dx[at, here, columns(col, feat)].astype(f32)
            ).astype(low)
            return carry

        lax.fori_loop(0, rows_dev // 128, one, 0)

    for n, peer in enumerate(peers):
        join_x(peer, slot_x + n)
        links.push(sum_x.at[peer], line_x.at[2 - n], slot_xl + 2 - n, at_row(peer))

    for n in range(2):
        span = slice(n * CHUNK, (n + 1) * CHUNK)
        value = nn(grads_t[...], x_all[:, :, span].reshape(length, CHUNK)).T
        gq[2 * n : 2 * n + 2] = value.astype(low).reshape((2,) + gq.shape[1:])
    slot_q, slot_ql = links.slots(1), links.slots(4)
    links.push(gq.at[:, 1 - col], sum_q, slot_q, mate)
    here = lax.broadcasted_iota(jnp.int32, (8, 2 * feat), 0) == row
    value = jnp.concatenate([bias_kv, bias_q, jnp.zeros((1, 2 * feat - 3 * wide), f32)], axis=1)
    vec[8:] = vec_in[8:]
    vec[:8] = jnp.where(here, value, 0.0)
    slot_v = links.slots(1)
    links.push(vec, vec_mate, slot_v, mate)
    local_grad(3)
    local_grad(4)
    links.arrive(sum_q, slot_q, mate)

    def add_q(step, carry):
        sum_q[step] = (sum_q[step].astype(f32) + gq[step, col].astype(f32)).astype(low)
        return carry

    lax.fori_loop(0, ROWS, add_q, 0)
    own_part = all_q.at[side, pl.ds(2 * col, 2)]
    at_home = home == col

    def keep_own():
        own_part[...] = sum_q[row]

    pl.when(at_home)(keep_own)
    links.push(sum_q.at[row], own_part, slot_ql + 2 * side + col, mate, jnp.logical_not(at_home))
    for peer in peers:
        links.push(sum_q.at[peer], own_part, slot_ql + 2 * side + col, (dp, peer, home))
    stage[2] = send_second(2, stage[2])
    links.arrive(vec_mate, slot_v, mate)
    vec_mate[...] = vec[...] + vec_mate[...]
    slot_vl, slot_vd = links.slots(3), links.slots(2)
    for n, peer in enumerate(peers):
        links.push(vec_mate, vec_line.at[2 - n], slot_vl + 2 - n, at_row(peer))
    stage[3] = join(3)
    stage[4] = join(4)
    stage[2] = send_line(2, stage[2])
    join_x(row, slot_x + 3)
    stage[3] = send_second(3, stage[3])
    stage[4] = send_second(4, stage[4])
    stage[3] = send_line(3, stage[3])
    stage[4] = send_line(4, stage[4])

    def finish_line(i):
        for n in range(3):
            links.arrive(lines[i].at[n], stage[i] + n, mate)
        value = pairs[i][1, row, dp].astype(f32)
        for n in range(3):
            value = value + lines[i][n].astype(f32)
        out_g[i][dp] = value.astype(low)
        stage[i] = share(i, out_g[i])

    finish_line(0)
    finish_line(1)
    for n in range(3):
        links.arrive(line_x.at[n], slot_xl + n, mate)

    def finish_x(step, carry):
        rows = pl.ds(pl.multiple_of(step * 128, 128), 128)
        value = sum_x[row, rows].astype(f32)
        for n in range(3):
            value = value + line_x[n, rows].astype(f32)
        out_x[rows] = value.astype(low)
        return carry

    lax.fori_loop(0, rows_dev // 128, finish_x, 0)
    share_on(0, out_g[0], stage[0])
    share_on(1, out_g[1], stage[1])
    finish_line(2)
    finish_line(3)
    for j in range(2):
        for e in range(2):
            here = (row == 2 * col + j) & (col == e)
            links.arrive(
                all_q.at[j, pl.ds(2 * e, 2)], slot_ql + 2 * j + e, mate, jnp.logical_not(here)
            )
    stage[5] = send_first(5)
    for n in range(3):
        links.arrive(vec_line.at[n], slot_vl + n, mate)
    vec_sum = vec_mate[...] + vec_line[0] + vec_line[1] + vec_line[2]
    vec_line[1] = vec_sum
    links.push(vec_line.at[1], vec_flat.at[0], slot_vd, at_dp(1))
    finish_line(4)
    share_on(2, out_g[2], stage[2])
    share_on(3, out_g[3], stage[3])
    stage[5] = send_second(5, stage[5])
    links.arrive(vec_flat.at[0], slot_vd, mate)
    vec_line[0] = vec_line[1] + vec_flat[0]
    links.push(vec_line.at[0], vec_flat.at[1], slot_vd + 1, at_dp(2))
    share_on(4, out_g[4], stage[4])
    links.arrive(second[5], stage[5], mate)
    add_into(all_q.at[:, dp], second[5])
    for j in range(2):
        out_q[dp, j] = all_q[j, dp]
    stage[5] = share(5, out_q)
    share_on(5, out_q, stage[5])
    links.arrive(vec_flat.at[1], slot_vd + 1, mate)
    vec_total = vec_line[0] + vec_flat[1]
    for i in range(5):
        shared(i, out_g[i], stage[i])
    shared(5, out_q, stage[5])
    links.arrive(halves.at[other_rows], slot_o, mate)
    links.drain()
    vec[...] = vec_total


def backward_links(
    grad_blocks, output, late, stream, grad_pre, branch_two, activ, branch_one, context,
    q, kv, kt, mixed, lse, ids, x_all, w_heads, vec,
):
    low, f32 = q.dtype, jnp.float32
    heads, length = kv.shape[0], kv.shape[1]
    wide = heads * HEAD
    own, features = output.shape
    hidden = activ.shape[1]
    part = features // ROWS // 4
    widths = [hidden // 4] * 4 + [features // 2]
    rows, feat = 2 * own, features // 2
    blocks = length // TILE // 2
    shape = jax.ShapeDtypeStruct
    outs = [shape((4, part, width), low) for width in widths] + [
        shape((4, 2, part, 3 * wide), low),
        shape((rows, feat), low),
        shape((rows, feat), low),
        shape(vec.shape, f32),
    ]
    every = [(ROWS, width) for width in widths] + [(2, 3 * wide)]
    return pl.pallas_call(
        functools.partial(backward_kernel, heads),
        out_shape=outs,
        in_specs=[IN_VMEM] * 18,
        out_specs=[IN_VMEM] * len(outs),
        scratch_shapes=[pltpu.VMEM((2, ROWS, 4, part, width), low) for width in widths]
        + [pltpu.VMEM((ROWS, 4, part, width), low) for width in widths]
        + [pltpu.VMEM((2, lead, part, width), low) for lead, width in every]
        + [pltpu.VMEM((lead, part, width), low) for lead, width in every]
        + [pltpu.VMEM((3, part, width), low) for width in widths]
        + [
            pltpu.VMEM((ROWS, own, wide), low),
            pltpu.VMEM((heads, blocks, 2 * TILE, 2 * HEAD), low),
            pltpu.VMEM((heads, blocks, 1, TILE), f32),
            pltpu.VMEM((blocks, heads, HEAD, TILE), f32),
            pltpu.VMEM((heads, length, 2 * HEAD), f32),
            pltpu.VMEM((length, 3 * wide), low),
            pltpu.VMEM((3 * wide, length), low),
            pltpu.VMEM((3 * wide, features), low),
            pltpu.VMEM((3, features, own), low),
            pltpu.VMEM((length, 1), jnp.int32),
            pltpu.VMEM((ROWS, rows, features), low),
            pltpu.VMEM((ROWS, rows, feat), low),
            pltpu.VMEM((3, rows, feat), low),
            pltpu.VMEM((ROWS, 2, 2, part, 3 * wide), low),
            pltpu.VMEM((ROWS, 2, part, 3 * wide), low),
            pltpu.VMEM((2, 4, part, 3 * wide), low),
            pltpu.VMEM(vec.shape, f32),
            pltpu.VMEM((3,) + vec.shape, f32),
            pltpu.VMEM((2,) + vec.shape, f32),
            pltpu.SemaphoreType.DMA((128,)),
            pltpu.SemaphoreType.DMA((128,)),
        ],
        compiler_params=comm_params(2),
        name="backward_links",
    )(
        grad_blocks, output, late, stream, grad_pre, branch_two, activ, branch_one, context,
        q, kv, kt, mixed, lse, ids.reshape(1, -1), x_all, w_heads, vec,
    )


def put_lanes(target, value):
    for n in range(target.shape[0]):
        target[n : n + 1] = value[:, n * 128 : (n + 1) * 128]


def finish_kernel(
    heads, g1a, g1b, g2a, g2b, go, gq, x_in, out_in, vec,
    out, logits, grad_x, o_q, o_bq, o_k, o_v, o_bv, o_o, o_bo, o_g1, o_s1, o_1, o_b1, o_2, o_b2,
    o_g2, o_s2, o_p, o_bp, o_c, o_bc,
):
    dp, _, col = place()
    f32 = jnp.float32
    wide = heads * HEAD
    classes = logits.shape[1]
    depth, feat = o_q.shape
    part = g1a.shape[2]
    out[...] = out_in[...]
    grad_x[...] = x_in[...]
    flat = lambda ref: ref[...].astype(f32).reshape(depth, ref.shape[2])
    for target, first, second in ((o_1, g1a, g1b), (o_2, g2a, g2b)):
        target[:, :part] = flat(first)
        target[:, part:] = flat(second)
    o_o[...] = flat(go)
    bias_q, bias_v = [], []
    for j in range(2):
        value = gq[:, j].astype(f32).reshape(depth, 3 * wide)
        o_q[:, j * wide : (j + 1) * wide] = value[:, 2 * wide :]
        for target, shift in ((o_k, 0), (o_v, HEAD)):
            target[:, j * wide : (j + 1) * wide] = jnp.concatenate(
                [value[:, 2 * h * HEAD + shift :][:, :HEAD] for h in range(heads)], axis=1
            )
        bias = jnp.where(col == 0, vec[j : j + 1], vec[2 + j : 3 + j])
        bias_q.append(bias[:, 2 * wide : 3 * wide])
        bias_v += [bias[:, 2 * h * HEAD + HEAD :][:, :HEAD] for h in range(heads)]
    put_lanes(o_bq, jnp.concatenate(bias_q, axis=1))
    put_lanes(o_bv, jnp.concatenate(bias_v, axis=1))
    own = jnp.where(col == 0, vec[8:16], vec[16:24])
    for n, target in enumerate((o_bo, o_g1, o_s1, o_b2, o_g2, o_s2)):
        put_lanes(target, own[n // 2 : n // 2 + 1, (n % 2) * feat : (n % 2 + 1) * feat])
    put_lanes(o_b1, jnp.concatenate([own[3:4], own[4:5]], axis=1))
    firsts, seconds = vec[24:32], vec[32:40]
    first_t, second_t = firsts.T, seconds.T
    pooler = jnp.zeros(o_p.shape, f32)
    head = jnp.zeros((o_p.shape[0], 128), f32)
    bias = jnp.zeros((1, 2 * feat), f32)
    tails = seconds[4:8, :128]
    for s in range(4):
        pooler = pooler + first_t[:, s : s + 1] * firsts[4 + s : 5 + s]
        bias = bias + firsts[4 + s : 5 + s]
        head = head + second_t[:, s : s + 1] * tails[s : s + 1]
    o_p[...] = pooler
    put_lanes(o_bp, bias)
    o_c[...] = head[:, classes : 2 * classes]
    o_bc[...] = jnp.sum(tails, axis=0, keepdims=True)[:, classes : 2 * classes]
    own_tail = jnp.zeros((1, 128), f32)
    for s in range(4):
        own_tail = jnp.where(dp == s, tails[s : s + 1], own_tail)
    logits[...] = own_tail[:, :classes]


def finish(pieces, classes, heads):
    g1a, g1b, g2a, g2b, go, gq, x_in, out_in, vec = pieces
    f32 = jnp.float32
    depth = go.shape[0] * go.shape[1]
    feat, hidden = go.shape[2], 2 * g1a.shape[2]
    features = vec.shape[1]
    shape = jax.ShapeDtypeStruct
    vector = lambda size: shape((size // 128, 128) if size % 128 == 0 else (1, size), f32)
    square = shape((depth, feat), f32)
    outs = [
        shape(out_in.shape, out_in.dtype), vector(classes), shape(x_in.shape, x_in.dtype),
        square, vector(feat), square, square, vector(feat), square, vector(feat), vector(feat),
        vector(feat), shape((depth, hidden), f32), vector(hidden), shape((depth, hidden), f32),
        vector(feat), vector(feat), vector(feat), shape((features, features), f32),
        vector(features), shape((features, classes), f32), vector(classes),
    ]
    return pl.pallas_call(
        functools.partial(finish_kernel, heads),
        out_shape=outs,
        in_specs=[IN_VMEM] * len(pieces),
        out_specs=[IN_VMEM] * len(outs),
        compiler_params=pltpu.CompilerParams(vmem_limit_bytes=VMEM_BYTES),
        name="finish",
    )(*pieces)


def norm_rows(hidden, gain, shift):
    row_mean = jnp.mean(hidden, axis=1, keepdims=True)
    row_var = jnp.mean(hidden * hidden, axis=1, keepdims=True) - row_mean * row_mean
    inv_scale = lax.rsqrt(row_var + epsilon)
    normed = (hidden - row_mean) * inv_scale
    return normed * gain + shift, normed, inv_scale


def norm_rows_back(grad, normed, inv_scale, gain):
    scaled = grad * gain
    first = jnp.mean(scaled, axis=1, keepdims=True)
    second = jnp.mean(scaled * normed, axis=1, keepdims=True)
    return inv_scale * (scaled - first - normed * second)


def fast_body(
    layer_input, cotangent, labels, block_ids, w_query, b_query, w_key, w_value, b_value,
    w_output, b_output, ln1_gain, ln1_bias, w_inner, b_inner, w_outer, b_outer,
    ln2_gain, ln2_bias, w_pooler, b_pooler, w_classes, b_classes,
):
    f32 = jnp.float32
    feat = layer_input.shape[1]
    features = 2 * feat
    hidden = b_inner.shape[0]
    heads = features // HEAD // ROWS
    vectors = [
        b_query, b_value, b_output, ln1_gain, ln1_bias, b_outer, ln2_gain, ln2_bias, b_inner
    ]
    count = sum(vector.shape[0] for vector in vectors) // feat
    padded, at = 0.0, 0
    full = (count + -count % 8) * feat
    for vector in vectors:
        size = vector.shape[0]
        padded = padded + jnp.pad(vector.astype(f32), (at, full - at - size))
        at += size
    (
        x_all, cot, vec_all, w_heads, q, kv, kt, mixed, lse, context, w_o, w_1, w_2,
    ) = forward_links(
        layer_input, cotangent, padded.reshape(-1, feat), w_query, w_key, w_value, block_ids,
        [w_output.T, w_inner, w_outer.T],
    )
    w_o = w_o.reshape(features, features)
    w_1 = w_1.reshape(features, 2 * hidden)
    w_2 = w_2.reshape(features, 2 * hidden)
    (
        output, late, stream, grad_pre, branch_two, activ, branch_one, context, grad_blocks, packed
    ) = middle(
        context, cot, vec_all, labels, b_pooler, w_classes, b_classes, w_pooler, w_o, x_all, w_1, w_2
    )
    s_1a, s_2a, s_1b, s_2b, s_wo, s_q, grad_input, output, sums = backward_links(
        grad_blocks, output, late, stream, grad_pre, branch_two, activ, branch_one, context,
        q, kv, kt, mixed, lse, block_ids, x_all, w_heads, packed,
    )
    outs = finish((s_1a, s_1b, s_2a, s_2b, s_wo, s_q, grad_input, output, sums), w_classes.shape[1], heads)
    flat = (4, 7, 9, 10, 11, 13, 15, 16, 17, 19, 21)
    turned = (8, 14)
    return tuple(
        out.reshape(-1) if n in flat else out.T if n in turned else out
        for n, out in enumerate(outs)
    )


def is_fast(mesh):
    sizes = mesh.shape
    return sizes["dp"] == 4 and sizes["row"] == ROWS and sizes["col"] == 2


def solution(mesh):
    placed = (
        P(("dp", "row"), "col"),
        P(("dp", "row"), "col"),
        P("dp"),
        P("dp"),
        P("row", "col"),
        P("col"),
        P("row", "col"),
        P("row", "col"),
        P("col"),
        P("col", "row"),
        P("col"),
        P("col"),
        P("col"),
        P("row", "col"),
        P("col"),
        P("col", "row"),
        P("col"),
        P("col"),
        P("col"),
        P(),
        P(),
        P(),
        P(),
    )
    return jax.shard_map(
        fast_body if is_fast(mesh) else body,
        mesh=mesh,
        in_specs=placed,
        out_specs=(
            P(("dp", "row"), "col"),
            P("dp", None),
            P(("dp", "row"), "col"),
            P("row", "col"),
            P("col"),
            P("row", "col"),
            P("row", "col"),
            P("col"),
            P("col", "row"),
            P("col"),
            P("col"),
            P("col"),
            P("row", "col"),
            P("col"),
            P("col", "row"),
            P("col"),
            P("col"),
            P("col"),
            P(),
            P(),
            P(),
            P(),
        ),
        check_vma=False,
    )
```

```python
import functools

import jax
import jax.numpy as jnp
from jax import lax
from jax.experimental import pallas as pl
from jax.experimental.pallas import tpu as pltpu
from jax.sharding import PartitionSpec as P

HEAD = 64


highest = lax.Precision.HIGHEST
epsilon = 1e-05
root_half = 0.7071067811865476
inv_root_tau = 0.3989422804014327
masked_score = -1e30


def gelu_exact(values):
    return values * 0.5 * (1.0 + lax.erf(values * root_half))


def gelu_slope(values):
    return 0.5 * (1.0 + lax.erf(values * root_half)) + values * inv_root_tau * jnp.exp(
        -0.5 * values * values
    )


def project(left, right):
    return jnp.dot(left, right, preferred_element_type=jnp.float32)


def contract_first(left, right):
    return lax.dot_general(
        left, right, (((0,), (0,)), ((), ())), preferred_element_type=jnp.float32
    )


def contract_last(left, right):
    return lax.dot_general(
        left, right, (((1,), (1,)), ((), ())), preferred_element_type=jnp.float32
    )


def gather_features(values):
    return lax.all_gather(values, "col", axis=1, tiled=True)


def sum_features(values):
    return lax.psum_scatter(
        values.astype(jnp.bfloat16), "col", scatter_dimension=1, tiled=True
    ).astype(jnp.float32)


def feature_totals(first_part, second_part):
    return lax.psum((jnp.sum(first_part, axis=1), jnp.sum(second_part, axis=1)), "col")


def norm_forward(hidden, gain, shift, features):
    row_total, square_total = feature_totals(hidden, hidden * hidden)
    row_mean = row_total / features
    row_var = square_total / features - row_mean * row_mean
    inv_scale = lax.rsqrt(row_var + epsilon)
    normed = (hidden - row_mean[:, None]) * inv_scale[:, None]
    return (normed * gain + shift, normed, inv_scale)


def norm_backward(grad, normed, inv_scale, gain, features):
    scaled = grad * gain
    first_total, second_total = feature_totals(scaled, scaled * normed)
    return inv_scale[:, None] * (
        scaled - (first_total / features)[:, None] - normed * (second_total / features)[:, None]
    )


def key_split(piece_rows, rows_dev):
    return (piece_rows // rows_dev, rows_dev)


def body(
    layer_input,
    cotangent,
    labels,
    block_ids,
    w_query,
    b_query,
    w_key,
    w_value,
    b_value,
    w_output,
    b_output,
    ln1_gain,
    ln1_bias,
    w_inner,
    b_inner,
    w_outer,
    b_outer,
    ln2_gain,
    ln2_bias,
    w_pooler,
    b_pooler,
    w_classes,
    b_classes,
):
    f32 = jnp.float32
    bf16 = jnp.bfloat16
    rows_dev, feat_col = layer_input.shape
    heads_col = feat_col // HEAD
    features = feat_col * lax.axis_size("col")
    row_index = lax.axis_index("row")
    col_index = lax.axis_index("col")
    seq_index = lax.axis_index("dp")
    seq_count = lax.axis_size("dp")
    score_scale = HEAD ** (-0.5)
    query_ids = lax.dynamic_slice_in_dim(block_ids, row_index * rows_dev, rows_dev)
    last_query = query_ids[rows_dev - 1]
    wq_full, wk_full, wv_full, w1_full = (
        lax.all_gather(w_query, "row", axis=0, tiled=True),
        lax.all_gather(w_key, "row", axis=0, tiled=True),
        lax.all_gather(w_value, "row", axis=0, tiled=True),
        lax.all_gather(w_inner, "row", axis=0, tiled=True),
    )
    wo_full, w2_full = (
        lax.all_gather(w_output, "row", axis=1, tiled=True),
        lax.all_gather(w_outer, "row", axis=1, tiled=True),
    )
    input_whole = gather_features(layer_input)
    queries = (project(input_whole, wq_full) + b_query.astype(f32)).astype(bf16)
    keys_local = project(input_whole, wk_full).astype(bf16)
    values_local = (project(input_whole, wv_full) + b_value.astype(f32)).astype(bf16)
    queries3 = queries.reshape(rows_dev, heads_col, HEAD)
    start_state = (
        jnp.full((heads_col, rows_dev), masked_score, f32),
        jnp.zeros((heads_col, rows_dev), f32),
        jnp.zeros((heads_col, rows_dev, HEAD), f32),
    )
    running = start_state
    keys_piece = lax.all_gather(keys_local, "row", axis=0, tiled=True)
    values_piece = lax.all_gather(values_local, "row", axis=0, tiled=True)
    piece_rows = keys_piece.shape[0]
    number, block_rows = key_split(piece_rows, rows_dev)
    keys4 = keys_piece.reshape(number, block_rows, heads_col, HEAD)
    values4 = values_piece.reshape(number, block_rows, heads_col, HEAD)
    piece_ids = block_ids.reshape(number, block_rows)

    def attend_block_work(state, block_item):
        peak_score, row_mass, accum = state
        keys3, values3, key_ids = block_item
        scores = (
            jnp.einsum("qhd,khd->hqk", queries3, keys3, preferred_element_type=f32) * score_scale
        )
        allowed = (key_ids[None, :] <= query_ids[:, None])[None]
        block_top = jnp.max(jnp.where(allowed, scores, masked_score), axis=2)
        new_peak = jnp.maximum(peak_score, block_top)
        weights = jnp.where(allowed, jnp.exp(scores - new_peak[:, :, None]), 0.0)
        factor = jnp.exp(peak_score - new_peak)
        row_mass = row_mass * factor + jnp.sum(weights, axis=2)
        accum = accum * factor[:, :, None] + jnp.einsum(
            "hqk,khd->hqd", weights.astype(bf16), values3, preferred_element_type=f32
        )
        return (new_peak, row_mass, accum)

    def attend_block_step(state, block_item):
        state = lax.cond(
            block_item[2][0] > last_query, lambda st, item: st, attend_block_work, state, block_item
        )
        return (state, None)

    running, unused = lax.scan(attend_block_step, running, (keys4, values4, piece_ids))
    peak_score, row_mass, accum = running
    mixed = accum / row_mass[:, :, None]
    log_mass = peak_score + jnp.log(row_mass)
    context_low = mixed.transpose(1, 0, 2).reshape(rows_dev, feat_col).astype(bf16)
    attn_branch = sum_features(project(context_low, wo_full))
    hidden_one = layer_input.astype(f32) + attn_branch + b_output.astype(f32)
    gain_one = ln1_gain.astype(f32)
    stream, normed_one, inv_one = norm_forward(hidden_one, gain_one, ln1_bias.astype(f32), features)
    stream_whole = gather_features(stream.astype(bf16))
    pre_act = project(stream_whole, w1_full) + b_inner.astype(f32)
    activ = gelu_exact(pre_act).astype(bf16)
    ffn_branch = sum_features(project(activ, w2_full))
    hidden_two = stream + ffn_branch + b_outer.astype(f32)
    gain_two = ln2_gain.astype(f32)
    result, normed_two, inv_two = norm_forward(hidden_two, gain_two, ln2_bias.astype(f32), features)
    output = result.astype(bf16)
    row_zero = (row_index == 0).astype(f32)
    pool_input = gather_features(output[0:1])
    pooled = jnp.tanh(project(pool_input, w_pooler) + b_pooler.astype(f32))
    classes_f32 = w_classes.astype(f32)
    logits_own = jnp.dot(pooled, classes_f32, precision=highest) + b_classes.astype(f32)
    onehot = (jnp.arange(w_classes.shape[1]) == labels[0]).astype(f32)
    grad_logits = jax.nn.softmax(logits_own, axis=-1) - onehot[None, :]
    g_w_classes = jnp.dot(pooled.T, grad_logits, precision=highest)
    g_b_classes = grad_logits[0]
    grad_pre_pool = jnp.dot(grad_logits, classes_f32.T, precision=highest) * (1.0 - pooled * pooled)
    g_b_pooler = grad_pre_pool[0]
    g_w_pooler = jnp.dot(pool_input.astype(f32).T, grad_pre_pool, precision=highest)
    grad_first = jnp.dot(grad_pre_pool, w_pooler.astype(f32).T, precision=highest)
    first_col = lax.dynamic_slice_in_dim(grad_first[0], col_index * feat_col, feat_col)
    grad_result = cotangent.astype(f32).at[0].add(first_col * row_zero)
    logits_table = lax.dynamic_update_slice_in_dim(
        jnp.zeros((seq_count, w_classes.shape[1]), f32), logits_own * row_zero, seq_index, 0
    )
    g_ln2_gain = jnp.sum(grad_result * normed_two, axis=0)
    g_ln2_bias = jnp.sum(grad_result, axis=0)
    grad_hidden_two = norm_backward(grad_result, normed_two, inv_two, gain_two, features)
    g_b_outer = jnp.sum(grad_hidden_two, axis=0)
    branch_two_whole = gather_features(grad_hidden_two.astype(bf16))
    g_w_outer_full = contract_first(activ, branch_two_whole)
    grad_act = contract_last(branch_two_whole, w2_full)
    grad_pre = (grad_act * gelu_slope(pre_act)).astype(bf16)
    g_b_inner = jnp.sum(grad_pre.astype(f32), axis=0)
    g_w_inner_full = contract_first(stream_whole, grad_pre)
    grad_stream = grad_hidden_two + sum_features(contract_last(grad_pre, w1_full))
    g_ln1_gain = jnp.sum(grad_stream * normed_one, axis=0)
    g_ln1_bias = jnp.sum(grad_stream, axis=0)
    grad_hidden_one = norm_backward(grad_stream, normed_one, inv_one, gain_one, features)
    g_b_output = jnp.sum(grad_hidden_one, axis=0)
    branch_one_whole = gather_features(grad_hidden_one.astype(bf16))
    g_w_output_full = contract_first(context_low, branch_one_whole)
    grad_context = contract_last(branch_one_whole, wo_full).astype(bf16)
    grad_ctx3 = grad_context.reshape(rows_dev, heads_col, HEAD)
    delta = jnp.sum(grad_ctx3.astype(f32).transpose(1, 0, 2) * mixed, axis=2)

    def score_grads(queries_blk, grad_ctx_blk, keys3, values3, allowed, lse_blk, delta_blk):
        scores = (
            jnp.einsum("qhd,khd->hqk", queries_blk, keys3, preferred_element_type=f32) * score_scale
        )
        probs = jnp.where(allowed, jnp.exp(scores - lse_blk[:, :, None]), 0.0)
        grad_probs = jnp.einsum("qhd,khd->hqk", grad_ctx_blk, values3, preferred_element_type=f32)
        grad_scores = (probs * (grad_probs - delta_blk[:, :, None])).astype(bf16)
        return (probs, grad_scores)

    zero_q = jnp.zeros((rows_dev, heads_col, HEAD), f32)
    keys_piece = lax.all_gather(keys_local, "row", axis=0, tiled=True)
    values_piece = lax.all_gather(values_local, "row", axis=0, tiled=True)
    piece_rows = keys_piece.shape[0]
    number, block_rows = key_split(piece_rows, rows_dev)
    keys4 = keys_piece.reshape(number, block_rows, heads_col, HEAD)
    values4 = values_piece.reshape(number, block_rows, heads_col, HEAD)
    piece_ids = block_ids.reshape(number, block_rows)

    def make_block_work(accum_q, block_item):
        keys3, values3, key_ids = block_item
        allowed = (key_ids[None, :] <= query_ids[:, None])[None]
        probs, grad_scores = score_grads(
            queries3, grad_ctx3, keys3, values3, allowed, log_mass, delta
        )
        accum_q = (
            accum_q
            + jnp.einsum("hqk,khd->qhd", grad_scores, keys3, preferred_element_type=f32)
            * score_scale
        )
        part_k = (
            jnp.einsum("hqk,qhd->khd", grad_scores, queries3, preferred_element_type=f32)
            * score_scale
        )
        part_v = jnp.einsum(
            "hqk,qhd->khd", probs.astype(bf16), grad_ctx3, preferred_element_type=f32
        )
        return (accum_q, (part_k, part_v))

    def block_skip(accum_q, block_item):
        empty = jnp.zeros((block_rows, heads_col, HEAD), f32)
        return (accum_q, (empty, empty))

    def make_block_step(accum_q, block_item):
        return lax.cond(
            block_item[2][0] > last_query, block_skip, make_block_work, accum_q, block_item
        )

    grad_q = zero_q
    grad_q, (parts_k, parts_v) = lax.scan(make_block_step, grad_q, (keys4, values4, piece_ids))
    parts_k = parts_k.reshape(piece_rows, feat_col)
    parts_v = parts_v.reshape(piece_rows, feat_col)
    grad_k_all = parts_k
    grad_v_all = parts_v
    back_result = (grad_q, grad_k_all, grad_v_all)
    grad_q3, grad_k_all, grad_v_all = back_result
    grad_keys, grad_values = (
        lax.psum_scatter(
            grad_k_all.astype(jnp.bfloat16), "row", scatter_dimension=0, tiled=True
        ).astype(jnp.float32),
        lax.psum_scatter(
            grad_v_all.astype(jnp.bfloat16), "row", scatter_dimension=0, tiled=True
        ).astype(jnp.float32),
    )
    queries_grad = grad_q3.reshape(rows_dev, feat_col).astype(bf16)
    keys_grad = grad_keys.astype(bf16)
    values_grad = grad_values.astype(bf16)
    g_b_query = jnp.sum(queries_grad.astype(f32), axis=0)
    g_b_value = jnp.sum(values_grad.astype(f32), axis=0)
    g_w_query_full = contract_first(input_whole, queries_grad)
    g_w_key_full = contract_first(input_whole, keys_grad)
    g_w_value_full = contract_first(input_whole, values_grad)
    grad_input_whole = (
        contract_last(queries_grad, wq_full)
        + contract_last(keys_grad, wk_full)
        + contract_last(values_grad, wv_full)
    )
    grad_input = (grad_hidden_one + sum_features(grad_input_whole)).astype(bf16)
    in_rows = w_query.shape[0]
    out_cols = w_output.shape[1]
    (
        sum_wq,
        sum_wk,
        sum_wv,
        sum_w1,
        sum_wo,
        sum_w2,
        g_w_pooler,
        g_b_pooler,
        g_w_classes,
        g_b_classes,
        g_b_query,
        g_b_value,
        g_b_output,
        g_ln1_gain,
        g_ln1_bias,
        g_b_inner,
        g_b_outer,
        g_ln2_gain,
        g_ln2_bias,
        logits_all,
    ) = lax.psum(
        (
            g_w_query_full,
            g_w_key_full,
            g_w_value_full,
            g_w_inner_full,
            g_w_output_full,
            g_w_outer_full,
            g_w_pooler * row_zero,
            g_b_pooler * row_zero,
            g_w_classes * row_zero,
            g_b_classes * row_zero,
            g_b_query,
            g_b_value,
            g_b_output,
            g_ln1_gain,
            g_ln1_bias,
            g_b_inner,
            g_b_outer,
            g_ln2_gain,
            g_ln2_bias,
            logits_table,
        ),
        ("dp", "row"),
    )
    row_start = row_index * in_rows
    col_start = row_index * out_cols
    g_w_query = lax.dynamic_slice_in_dim(sum_wq, row_start, in_rows, 0)
    g_w_key = lax.dynamic_slice_in_dim(sum_wk, row_start, in_rows, 0)
    g_w_value = lax.dynamic_slice_in_dim(sum_wv, row_start, in_rows, 0)
    g_w_inner = lax.dynamic_slice_in_dim(sum_w1, row_start, in_rows, 0)
    g_w_output = lax.dynamic_slice_in_dim(sum_wo, col_start, out_cols, 1)
    g_w_outer = lax.dynamic_slice_in_dim(sum_w2, col_start, out_cols, 1)
    logits = lax.dynamic_slice_in_dim(logits_all, seq_index, 1, 0)
    return (
        output,
        logits,
        grad_input,
        g_w_query,
        g_b_query,
        g_w_key,
        g_w_value,
        g_b_value,
        g_w_output,
        g_b_output,
        g_ln1_gain,
        g_ln1_bias,
        g_w_inner,
        g_b_inner,
        g_w_outer,
        g_b_outer,
        g_ln2_gain,
        g_ln2_bias,
        g_w_pooler,
        g_b_pooler,
        g_w_classes,
        g_b_classes,
    )


MESH_IDS = pl.DeviceIdType.MESH
ROWS = 4
VMEM_BYTES = 64000 * 1024


def place():
    return lax.axis_index("dp"), lax.axis_index("row"), lax.axis_index("col")


class Links:
    def __init__(self, send, recv):
        self.send, self.recv = send, recv
        self.sends, self.recvs, self.open = 0, 0, []

    def slots(self, count):
        base = self.recvs
        self.recvs += count
        return base

    def push(self, source, target, slot, device, when=None):
        copy = pltpu.make_async_remote_copy(
            src_ref=source,
            dst_ref=target,
            send_sem=self.send.at[self.sends],
            recv_sem=self.recv.at[slot],
            device_id=device,
            device_id_type=MESH_IDS,
        )
        self.sends += 1
        if when is None:
            copy.start()
        else:
            pl.when(when)(lambda: copy.start())
        self.open.append((copy, when))

    def arrive(self, target, slot, device, when=None):
        copy = pltpu.make_async_remote_copy(
            src_ref=target,
            dst_ref=target,
            send_sem=self.send.at[0],
            recv_sem=self.recv.at[slot],
            device_id=device,
            device_id_type=MESH_IDS,
        )
        if when is None:
            copy.wait_recv()
        else:
            pl.when(when)(lambda: copy.wait_recv())

    def drain(self):
        for copy, when in self.open:
            if when is None:
                copy.wait_send()
            else:
                pl.when(when)(lambda copy=copy: copy.wait_send())
        self.open = []


def meet(devices):
    barrier = pltpu.get_barrier_semaphore()
    for device in devices:
        pl.semaphore_signal(barrier, inc=1, device_id=device, device_id_type=MESH_IDS)
    pl.semaphore_wait(barrier, len(devices))


def within(value):
    return (value >= 0) & (value < ROWS)


def steps_of_line(row):
    for step in (1, 2, 3):
        for way in (1, -1):
            source = row - way * step
            yield step, way, (3 - step if way == 1 else step - 1), source, within(source)


def columns(col, width):
    return pl.ds(pl.multiple_of(col * width, 128), width)


IN_VMEM = pl.BlockSpec(memory_space=pltpu.VMEM)
IN_PLACE = pl.BlockSpec(memory_space=pl.ANY)


def comm_params(number):
    return pltpu.CompilerParams(
        collective_id=number, has_side_effects=True, vmem_limit_bytes=VMEM_BYTES
    )


TILE = 256
NEAR = 3


def nt(left, right):
    return lax.dot_general(
        left, right, (((1,), (1,)), ((), ())), preferred_element_type=jnp.float32
    )


def nn(left, right):
    return jnp.dot(left, right, preferred_element_type=jnp.float32)


def forward_kernel(
    widths, heads, x, cot, vec, wq, wk, wv, ids, labels, w_classes, b_classes, w_pooler, *refs
):
    count = len(widths)
    shards, refs = refs[:count], refs[count:]
    x_all, w_heads, q_out, kv_out, kt_out, mixed_out, lse_out = refs[:7]
    (
        output, late, stream_out, grad_pre_out, branch_two_out, activ_out, branch_one_out,
        context, grad_blocks, packed,
    ) = refs[7:17]
    fulls, refs = refs[17 : 17 + count], refs[17 + count :]
    (
        cot_own, vec_all, context_in, vt_out, ids_col, packs, low_out, slope, total, send, recv,
        local,
    ) = refs
    dp, row, col = place()
    links = Links(send, recv)
    low = x.dtype
    rows_dev, feat = x.shape
    wide = heads * HEAD
    mate = (dp, row, 1 - col)
    at_row = lambda other: (dp, other, col)
    at_dp = lambda flip: (dp ^ flip, row, col)
    home, side = row // 2, lax.rem(row, 2)
    mine = lax.rem(row + col, 2)
    half = rows_dev // 2
    meet([at_row(lax.rem(row + k, ROWS)) for k in (1, 2, 3)] + [at_dp(1), at_dp(2), mate])

    x_at = lambda k: x_all.at[k, :, columns(col, feat)]
    x_mate_at = lambda k: x_all.at[k, :, columns(1 - col, feat)]
    w_at = lambda i, k, q: fulls[i].at[k, q, :, columns(col, widths[i])]
    row_at = lambda i, k: fulls[i].at[k, :, :, columns(col, widths[i])]
    row_mate_at = lambda i, k: fulls[i].at[k, :, :, columns(1 - col, widths[i])]

    line_x, mate_x = links.slots(3), links.slots(4)
    line_q, first_q, second_q, mate_q = (
        links.slots(3), links.slots(3), links.slots(6), links.slots(1),
    )
    mate_cot, mate_vec, swap = links.slots(1), links.slots(1), links.slots(3)
    line_w = [links.slots(3) for _ in widths]
    first_w = [links.slots(3) for _ in widths]
    second_w = [links.slots(6) for _ in widths]
    mate_w = [links.slots(4) for _ in widths]
    steps = list(steps_of_line(row))
    at_step = lambda step: [entry[2:] for entry in steps if entry[0] == step]

    def relay(step, own, full, base):
        for way in (1, -1):
            held, onward = row - way * (step - 1), row + way
            ok = within(held) & within(onward)
            slot = 3 - step if way == 1 else step - 1
            links.push(own if step == 1 else full(held), full(held), base + slot, at_row(onward), ok)

    relay(1, x, x_at, line_x)
    links.push(x, x_at(row), mate_x, mate)
    for j in range(2):
        pieces = []
        for h in range(heads):
            part = slice(j * wide + h * HEAD, j * wide + (h + 1) * HEAD)
            pieces += [wk[:, part], wv[:, part]]
        pieces.append(wq[:, j * wide : (j + 1) * wide])
        packs[j] = jnp.concatenate(pieces, axis=1).reshape(packs.shape[1:])
    for j in range(2):
        k = 2 * col + j
        away = k != row
        slot = lax.rem(row - k + ROWS + 3, ROWS)
        links.push(packs.at[j, dp], w_heads.at[row, dp], line_q + slot, at_row(k), away)

        @pl.when(jnp.logical_not(away))
        def _(j=j):
            w_heads[row] = packs[j]

    links.push(
        cot.at[pl.ds(pl.multiple_of((1 - mine) * half, 128), half)],
        cot_own.at[:, columns(col, feat)],
        mate_cot,
        mate,
    )
    links.push(vec, vec_all.at[col], mate_vec, mate)
    cot_own[:, columns(col, feat)] = cot[pl.ds(pl.multiple_of(mine * half, 128), half)]
    vec_all[col] = vec[...]
    x_all[row, :, columns(col, feat)] = x[...]
    copies = [
        pltpu.make_async_copy(shards[i], row_at(i, row), local.at[i]) for i in range(count)
    ]

    at_home = home == col

    def q_first():
        for slot in range(3):
            k = lax.rem(row + slot + 1, ROWS)
            one = 1 + slot % 2
            links.arrive(w_heads.at[k, dp], line_q + slot, mate, at_home)
            links.push(
                w_heads.at[k, dp], w_heads.at[k, dp], first_q + slot, at_dp(one), at_home
            )

    def q_second():
        for slot in range(3):
            k = lax.rem(row + slot + 1, ROWS)
            one, two = 1 + slot % 2, 2 - slot % 2
            links.arrive(w_heads.at[k, dp ^ one], first_q + slot, mate, at_home)
            for n, q in enumerate((dp, dp ^ one)):
                links.push(
                    w_heads.at[k, q], w_heads.at[k, q], second_q + 2 * slot + n, at_dp(two), at_home
                )

    def q_mate():
        for slot in range(3):
            k = lax.rem(row + slot + 1, ROWS)
            two = 2 - slot % 2
            links.arrive(w_heads.at[k, dp ^ two], second_q + 2 * slot, mate, at_home)
            links.arrive(w_heads.at[k, dp ^ 3], second_q + 2 * slot + 1, mate, at_home)
        links.push(w_heads, w_heads, mate_q, mate, at_home)
        links.arrive(w_heads, mate_q, mate, jnp.logical_not(at_home))

    def x_step(step):
        for slot, k, ok in at_step(step):
            links.arrive(x_at(k), line_x + slot, mate, ok)
        if step < 3:
            relay(step + 1, x, x_at, line_x)
        for slot, k, ok in at_step(step):
            links.push(x_at(k), x_at(k), mate_x + 1 + slot, mate, ok)

    turn = lambda i, slot: (1, 2) if (i + slot) % 2 == 0 else (2, 1)

    def w_start(at_left, at_right):
        for way, ok in ((1, row == at_right), (-1, row == at_left)):
            slot = 2 if way == 1 else 0
            for i in range(count):
                links.push(
                    shards[i].at[dp], w_at(i, row, dp), line_w[i] + slot, at_row(row + way), ok
                )

    def w_first(step):
        for i in range(count):
            for slot, k, ok in at_step(step):
                links.arrive(w_at(i, k, dp), line_w[i] + slot, mate, ok)
            if step < 3:
                relay(step + 1, None, lambda k, i=i: w_at(i, k, dp), line_w[i])
            for slot, k, ok in at_step(step):
                one, two = turn(i, slot)
                links.push(w_at(i, k, dp), w_at(i, k, dp), first_w[i] + slot, at_dp(one), ok)

    def w_second(step):
        for i in range(count):
            for slot, k, ok in at_step(step):
                one, two = turn(i, slot)
                links.arrive(w_at(i, k, dp ^ one), first_w[i] + slot, mate, ok)
                for n, q in enumerate((dp, dp ^ one)):
                    links.push(
                        w_at(i, k, q), w_at(i, k, q), second_w[i] + 2 * slot + n, at_dp(two), ok
                    )

    def w_mate(step, items):
        for i in items:
            for slot, k, ok in at_step(step):
                one, two = turn(i, slot)
                links.arrive(w_at(i, k, dp ^ two), second_w[i] + 2 * slot, mate, ok)
                links.arrive(w_at(i, k, dp ^ 3), second_w[i] + 2 * slot + 1, mate, ok)
                links.push(row_at(i, k), row_at(i, k), mate_w[i] + 1 + slot, mate, ok)

    def w_ready(i):
        w_mate(3, (i,))
        copies[i].wait()
        links.arrive(row_mate_at(i, row), mate_w[i], mate)
        for slot in range(3):
            k = lax.rem(row + slot + 1, ROWS)
            links.arrive(row_mate_at(i, k), mate_w[i] + 1 + slot, mate)

    row_tiles = ROWS * rows_dev // TILE
    per_row = rows_dev // TILE

    def split_ids(step, carry):
        span = pl.ds(pl.multiple_of(step * TILE, TILE), TILE)
        ids_col[span] = jnp.broadcast_to(ids[:, span], (8, TILE)).T[:, :1]
        return carry

    lax.fori_loop(0, row_tiles, split_ids, 0)
    w_start(3, 0)
    x_step(1)
    w_start(2, 1)
    q_first()
    x_step(2)
    w_start(1, 2)
    q_second()
    for copy in copies:
        copy.start()
    for i in range(count):
        links.push(shards[i], row_at(i, row), mate_w[i], mate)
    q_mate()
    links.arrive(vec_all.at[1 - col], mate_vec, mate)
    bias_of = lambda n: jnp.where(
        side == 0, vec_all[home, n : n + 1, :wide], vec_all[home, n : n + 1, wide : 2 * wide]
    )
    bias_q, bias_v = bias_of(0), bias_of(1)
    blank = jnp.zeros((1, HEAD), jnp.float32)
    bias_kv = jnp.concatenate(
        sum([[blank, bias_v[:, h * HEAD : (h + 1) * HEAD]] for h in range(heads)], []), axis=1
    )
    weights = lambda start, stop: w_heads[:, :, :, start:stop].reshape(2 * feat, stop - start)

    def project_keys(k):
        def one_tile(step, carry):
            here = pl.ds(pl.multiple_of(step * TILE, TILE), TILE)
            rows = pl.ds(pl.multiple_of(k * rows_dev + step * TILE, TILE), TILE)
            both = nn(x_all[k, here], weights(0, 2 * wide)) + bias_kv
            both_t = both.T
            for h in range(heads):
                at = 2 * h * HEAD
                kv_out[h, rows] = both[:, at : at + 2 * HEAD].astype(low)
                kt_out[h, :, rows] = both_t[at : at + HEAD].astype(low)
                vt_out[h, :, rows] = both_t[at + HEAD : at + 2 * HEAD].astype(low)
            return carry

        lax.fori_loop(0, per_row, one_tile, 0)

    links.arrive(x_mate_at(row), mate_x, mate)
    project_keys(row)
    x_step(3)
    for slot in (0, 2, 1):
        k = lax.rem(row + slot + 1, ROWS)
        links.arrive(x_mate_at(k), mate_x + 1 + slot, mate)
        project_keys(k)
        if slot == 2:
            w_first(1)

    def project_query(j, carry):
        block = 2 * j + lax.rem(j + col, 2)
        here = pl.ds(pl.multiple_of(lax.rem(block, per_row) * TILE, TILE), TILE)
        query = nn(x_all[block // per_row, here], weights(2 * wide, 3 * wide)) + bias_q
        query = query.astype(low) * jnp.asarray(HEAD**-0.5, low)
        for h in range(heads):
            q_out[h, j] = jnp.concatenate(
                [query[:, h * HEAD : (h + 1) * HEAD], jnp.zeros((TILE, HEAD), low)], axis=1
            )
        return carry

    blocks = row_tiles // 2
    lax.fori_loop(0, blocks, project_query, 0)
    w_first(2)
    for j in range(blocks):
        block = 2 * j + lax.rem(j + col, 2)
        rows = pl.ds(pl.multiple_of(block * TILE, TILE), TILE)
        query_ids = ids[:, rows]
        length = min(2 * j + NEAR, row_tiles) * TILE
        clear = 2 * j * TILE

        def one_head(h, carry, j=j, query_ids=query_ids, length=length, clear=clear):
            scores = nt(kv_out[h, :length], q_out[h, j])
            near = jnp.where(
                ids_col[clear:length] <= query_ids, scores[clear:], masked_score
            )
            top = jnp.max(near, axis=0, keepdims=True)
            if clear:
                top = jnp.maximum(top, jnp.max(scores[:clear], axis=0, keepdims=True))
                weights_far = jnp.exp(scores[:clear] - top)
            weights_near = jnp.exp(near - top)
            mass = jnp.sum(weights_near, axis=0, keepdims=True)
            value = nn(vt_out[h, :, clear:length], weights_near.astype(low))
            if clear:
                mass = mass + jnp.sum(weights_far, axis=0, keepdims=True)
                value = value + nn(vt_out[h, :, :clear], weights_far.astype(low))
            mixed_out[j, h] = value / mass
            lse_out[j, h] = top + jnp.log(mass)
            return carry

        lax.fori_loop(0, heads, one_head, 0)
        low_out[j] = (
            jnp.concatenate([mixed_out[j, h] for h in range(heads)], axis=0).T.astype(low)
        )
        away = row != j
        slot = lax.rem(row - j + ROWS + 3, ROWS)
        links.push(low_out.at[j], context_in.at[row], swap + slot, at_row(j), away)

        @pl.when(jnp.logical_not(away))
        def _(j=j):
            context_in[row] = low_out[j]

        if j == 0:
            w_second(1)
        if j == 1:
            w_first(3)
            w_second(2)
            w_mate(1, range(count))
        if j == 2:
            w_second(3)
            w_mate(2, range(count))

    f32 = jnp.float32
    own, features = output.shape
    hidden = 2 * widths[1]
    chunk = features
    w_o, w_1, w_2 = fulls
    part_of = lambda full, span: full[:, :, :, span].reshape(features, span.stop - span.start)
    vector = lambda n: jnp.concatenate([vec_all[0, n : n + 1], vec_all[1, n : n + 1]], axis=1)
    links.arrive(cot_own.at[:, columns(1 - col, feat)], mate_cot, mate)
    for slot in range(3):
        links.arrive(context_in.at[lax.rem(row + slot + 1, ROWS)], swap + slot, mate)
    context[...] = jnp.concatenate([context_in[r] for r in range(ROWS)], axis=1)
    w_ready(0)
    value = nt(context[...], w_o[...].reshape(features, features))
    own_rows = pl.ds(pl.multiple_of(mine * own, 128), own)
    hidden_one = x_all[row, own_rows].astype(f32) + value + vector(2)
    gain_one, gain_two = vector(3), vector(6)
    stream, normed_one, inv_one = norm_rows(hidden_one, gain_one, vector(4))
    late[...] = stream
    stream_out[...] = stream.astype(low)
    total[...] = jnp.zeros_like(total)
    bias_1 = [
        jnp.concatenate(
            [vec_all[c, 8 + 2 * n : 9 + 2 * n], vec_all[c, 9 + 2 * n : 10 + 2 * n]], axis=1
        )
        for c in range(2)
        for n in range(hidden // chunk // 2)
    ]
    w_ready(1)
    for n in range(hidden // chunk):
        span = slice(n * chunk, (n + 1) * chunk)
        pre_act = nn(stream_out[...], part_of(w_1, span)) + bias_1[n]
        half = 0.5 * (1.0 + lax.erf(pre_act * root_half))
        slope[:, span] = half + pre_act * inv_root_tau * jnp.exp(-0.5 * pre_act * pre_act)
        activ_out[:, span] = (pre_act * half).astype(low)
    w_ready(2)
    for n in range(hidden // chunk):
        span = slice(n * chunk, (n + 1) * chunk)
        total[...] += nt(activ_out[:, span], part_of(w_2, span))
    hidden_two = late[...] + total[...] + vector(5)
    result, normed_two, inv_two = norm_rows(hidden_two, gain_two, vector(7))
    output[...] = result.astype(low)

    classes = b_classes.shape[1]
    first = output[:8]
    pooled = jnp.tanh(nn(first, w_pooler[...])[:1] + jnp.concatenate([vec_all[0, 12:13], vec_all[0, 13:14]], axis=1))
    lane = lax.broadcasted_iota(jnp.int32, (1, 128), 1)
    logits = jnp.full((1, 128), masked_score, f32)
    rows = [w_classes[n : n + 1].astype(f32) for n in range(classes)]
    for n in range(classes):
        logit = jnp.sum(pooled * rows[n], axis=1, keepdims=True) + b_classes[:, n : n + 1].astype(f32)
        logits = jnp.where(lane == n, logit, logits)
    odds = jnp.exp(logits - jnp.max(logits, axis=1, keepdims=True))
    odds = odds / jnp.sum(odds, axis=1, keepdims=True)
    grad_logits = odds - (lane == labels[0, 0]).astype(f32)
    grad_pool = jnp.zeros((1, features), f32)
    for n in range(classes):
        grad_pool = grad_pool + grad_logits[:, n : n + 1] * rows[n]
    grad_pool = grad_pool * (1.0 - pooled * pooled)
    high = grad_pool.astype(low)
    rest = grad_pool - high.astype(f32)
    mid = rest.astype(low)
    last = (rest - mid.astype(f32)).astype(low)
    split = jnp.concatenate(
        [high.astype(f32), mid.astype(f32), last.astype(f32), jnp.zeros((5, features), f32)]
    ).astype(low)
    grad_first = jnp.sum(nt(split, w_pooler[...]), axis=0, keepdims=True)
    holder = ((row == 0) & (col == 0)).astype(f32)
    top = (lax.broadcasted_iota(jnp.int32, (own, 1), 0) == 0).astype(f32) * holder
    grad_result = cot_own[...].astype(f32) + top * grad_first

    tokens = lambda values: jnp.sum(values, axis=0, keepdims=True)
    g_gain_two, g_shift_two = tokens(grad_result * normed_two), tokens(grad_result)
    grad_two = norm_rows_back(grad_result, normed_two, inv_two, gain_two)
    g_bias_two = tokens(grad_two)
    late[...] = grad_two
    branch_two_out[...] = grad_two.astype(low)
    total[...] = jnp.zeros_like(total)
    g_bias_one = []
    for n in range(hidden // chunk):
        span = slice(n * chunk, (n + 1) * chunk)
        grad_pre = (nn(branch_two_out[...], part_of(w_2, span)) * slope[:, span]).astype(low)
        grad_pre_out[:, span] = grad_pre
        g_bias_one.append(tokens(grad_pre.astype(f32)))
        total[...] += nt(grad_pre_out[:, span], part_of(w_1, span))
    grad_stream = late[...] + total[...]
    g_gain_one, g_shift_one = tokens(grad_stream * normed_one), tokens(grad_stream)
    grad_one = norm_rows_back(grad_stream, normed_one, inv_one, gain_one)
    late[...] = grad_one
    branch_one_out[...] = grad_one.astype(low)
    grad_context = nn(branch_one_out[...], w_o[...].reshape(features, features)).astype(low)
    for r in range(ROWS):
        grad_blocks[r] = grad_context[:, r * wide : (r + 1) * wide]

    packed[...] = jnp.zeros_like(packed)
    vectors = [tokens(grad_one), g_gain_one, g_shift_one, g_bias_two, g_gain_two, g_shift_two]
    for n, value in enumerate(vectors):
        for c in range(2):
            packed[8 + 8 * c + n // 2, pl.ds((n % 2) * feat, feat)] = value[
                0, c * feat : (c + 1) * feat
            ]
    for n, value in enumerate(g_bias_one):
        packed[8 + 8 * (n // 2) + 3 + n % 2] = value[0]
    spare = jnp.zeros((1, features - 128), f32)
    shifted = pltpu.roll(jnp.where(lane < classes, grad_logits, 0.0), classes, 1)
    tail = jnp.concatenate([jnp.where(lane < classes, logits, shifted), spare], axis=1)
    for n, value in enumerate((first[:1].astype(f32), grad_pool, pooled, tail)):
        packed[24 + n : 25 + n] = value * holder
    links.drain()


def forward_links(x, cot, vec, wq, wk, wv, ids, labels, w_classes, b_classes, w_pooler, shards):
    widths = [shard.shape[1] for shard in shards]
    rows, feat = x.shape
    low, f32 = x.dtype, jnp.float32
    part = shards[0].shape[0] // 4
    features, hidden = 2 * feat, 2 * widths[1]
    heads = features // HEAD // ROWS
    wide = heads * HEAD
    length, own = ROWS * rows, rows // 2
    blocks = length // TILE // 2
    shape = jax.ShapeDtypeStruct
    narrow, broad = shape((own, features), low), shape((own, hidden), low)
    shapes = [
        shape((ROWS, rows, features), low),
        shape((ROWS, 4, part, 3 * wide), low),
        shape((heads, blocks, TILE, 2 * HEAD), low),
        shape((heads, length, 2 * HEAD), low),
        shape((heads, HEAD, length), low),
        shape((blocks, heads, HEAD, TILE), f32),
        shape((blocks, heads, 1, TILE), f32),
        narrow, shape((own, features), f32), narrow, broad, narrow, broad, narrow, narrow,
        shape((ROWS, own, wide), low), shape((32, features), f32),
    ]
    return pl.pallas_call(
        functools.partial(forward_kernel, widths, heads),
        out_shape=shapes,
        in_specs=[IN_VMEM] * 7 + [pl.BlockSpec(memory_space=pltpu.SMEM)]
        + [IN_VMEM] * (3 + len(shards)),
        out_specs=[IN_VMEM] * len(shapes),
        scratch_shapes=[pltpu.VMEM((ROWS, 4, part, 2 * width), low) for width in widths]
        + [
            pltpu.VMEM((own, features), low),
            pltpu.VMEM((2,) + vec.shape, f32),
            pltpu.VMEM((ROWS, own, wide), low),
            pltpu.VMEM((heads, HEAD, length), low),
            pltpu.VMEM((length, 1), jnp.int32),
            pltpu.VMEM((2, 4, part, 3 * wide), low),
            pltpu.VMEM((blocks, TILE, wide), low),
            pltpu.VMEM((own, hidden), f32),
            pltpu.VMEM((own, features), f32),
            pltpu.SemaphoreType.DMA((160,)),
            pltpu.SemaphoreType.DMA((96,)),
            pltpu.SemaphoreType.DMA((4,)),
        ],
        compiler_params=comm_params(1),
        name="forward_links",
    )(
        x, cot, vec, wq, wk, wv, ids.reshape(1, -1), labels.reshape(1, 1), w_classes.T,
        b_classes.reshape(1, -1), w_pooler, *[shard.reshape(4, part, -1) for shard in shards],
    )


def add_into(total, *others):
    def one(step, carry):
        value = total[step].astype(jnp.float32)
        for other in others:
            value = value + other[step].astype(jnp.float32)
        total[step] = value.astype(total.dtype)
        return carry

    lax.fori_loop(0, total.shape[0], one, 0)


CHUNK = 384
PLAN = (
    "g0",
    "g1",
    "r0",
    "c0",
    "g2",
    "g3",
    "c1",
    "g4",
    "d0",
    "a0",
    "s0",
    "s1",
    "c2",
    "a1",
    "c3",
    "a2",
    "l1",
    "l0",
    "c4",
    "a3",
    "h1",
    "h0",
    "w0",
    "t0",
    "s2",
    "t1",
    "t2",
    "x0",
    "s3",
    "q0",
    "x1",
    "s4",
    "t3",
    "v0",
    "x2",
    "l2",
    "l3",
    "l4",
    "v1",
    "f0",
    "f1",
    "h2",
    "q1",
    "h3",
    "h4",
    "k0",
    "v2",
    "n0",
    "n1",
    "s5",
    "v3",
    "f2",
    "f3",
    "f4",
    "x3",
    "q2",
    "n2",
    "n3",
    "n4",
    "n5",
    "k1",
    "v4",
)


def backward_kernel(
    heads, blocks_in, output, late, stream, grad_pre, branch_two, activ, branch_one, context,
    q, kv, kt, mixed, lse, ids, x_all, w_heads, vec_in, *refs,
):
    out_g, refs = refs[:5], refs[5:]
    out_q, out_x, halves, vec, refs = refs[0], refs[1], refs[2], refs[3], refs[4:]
    pairs, refs = refs[:5], refs[5:]
    mates, refs = refs[:5], refs[5:]
    first, refs = refs[:6], refs[6:]
    second, refs = refs[:6], refs[6:]
    lines, refs = refs[:5], refs[5:]
    (
        grad_ctx, both, delta, dq, dkv, grads, grads_t, w_t, turned, ids_col, dx, sum_x,
        line_x, gq, sum_q, all_q, vec_own, vec_mate, vec_line, vec_flat, vec_table, send, recv,
    ) = refs
    dp, row, col = place()
    links = Links(send, recv)
    low, f32 = q.dtype, jnp.float32
    mate = (dp, row, 1 - col)
    peers = [lax.rem(row + n, ROWS) for n in (1, 2, 3)]
    at_row = lambda other: (dp, other, col)
    at_dp = lambda flip: (dp ^ flip, row, col)
    home, side = row // 2, lax.rem(row, 2)
    mine = lax.rem(row + col, 2)
    length = kv.shape[1]
    wide = heads * HEAD
    rows_dev, feat = out_x.shape
    half = rows_dev // 2
    row_tiles = length // TILE
    blocks = row_tiles // 2
    meet(
        [at_row(peer) for peer in peers]
        + [at_dp(1), at_dp(2), mate]
        + [(dp, peer, 1 - col) for peer in peers]
    )

    swap, slot_o = links.slots(3), links.slots(1)
    for n, peer in enumerate(peers):
        links.push(blocks_in.at[peer], grad_ctx.at[row], swap + 2 - n, at_row(peer))
    own_rows = pl.ds(pl.multiple_of(mine * half, 128), half)
    other_rows = pl.ds(pl.multiple_of((1 - mine) * half, 128), half)
    links.push(output.at[:, columns(1 - col, feat)], halves.at[own_rows], slot_o, mate)
    halves[own_rows] = output[:, columns(col, feat)]
    grad_ctx[row] = blocks_in[row]

    lefts = (stream, branch_two, branch_one)
    for n in range(3):
        turned[n] = lefts[n][...].astype(f32).T.astype(low)
    feeds = [(0, grad_pre, 0), (1, activ, 0), (0, grad_pre, 1), (1, activ, 1), (2, context, 0)]
    turns = [(1, 2), (2, 1), (1, 2), (2, 1), (1, 2), (2, 1)]
    widths = [out.shape[2] for out in out_g]
    slot_g = [links.slots(1) for _ in widths]

    def local_grad(i):
        left, right, part = feeds[i]
        width = widths[i]
        per = width // CHUNK

        def one(step, carry):
            which, n = step // per, step % per
            core = jnp.where(which == 0, 1 - col, col)
            start = core * (right.shape[1] // 2) + part * width + n * CHUNK
            value = nn(turned[left], right[:, pl.ds(pl.multiple_of(start, 128), CHUNK)])
            pairs[i][which, :, :, :, pl.ds(pl.multiple_of(n * CHUNK, 128), CHUNK)] = (
                value.astype(low).reshape(pairs[i].shape[1:4] + (CHUNK,))
            )
            return carry

        lax.fori_loop(0, 2 * per, one, 0)
        links.push(pairs[i].at[0], mates[i], slot_g[i], mate)

    totals = [pair.at[1] for pair in pairs] + [all_q]

    def send_first(i):
        one, two = turns[i]
        base = links.slots(2)
        links.push(totals[i].at[:, dp ^ 3], first[i].at[1], base + 1, at_dp(one))
        links.push(totals[i].at[:, dp ^ one], first[i].at[0], base, at_dp(one))
        return base

    def join(i):
        links.arrive(mates[i], slot_g[i], mate)

        def one(step, carry):
            at, q_at = step // 4, step % 4
            pairs[i][1, at, q_at] = (
                pairs[i][1, at, q_at].astype(f32) + mates[i][at, q_at].astype(f32)
            ).astype(low)
            return carry

        lax.fori_loop(0, 16, one, 0)
        stage[i] = send_first(i)

    def send_second(i):
        one, two = turns[i]
        base = stage[i]
        links.arrive(first[i].at[1], base + 1, mate)
        add_into(totals[i].at[:, dp ^ two], first[i].at[1])
        slot = links.slots(1)
        links.push(totals[i].at[:, dp ^ two], second[i], slot, at_dp(two))
        stage[i] = (base, slot)

    def send_line(i):
        links.arrive(first[i].at[0], stage[i][0], mate)
        links.arrive(second[i], stage[i][1], mate)
        add_into(totals[i].at[:, dp], first[i].at[0], second[i])
        base = links.slots(3)
        links.push(totals[i].at[row ^ 3, dp], lines[i].at[1], base + 1, at_row(row ^ 1))
        links.push(totals[i].at[row ^ 1, dp], lines[i].at[0], base, at_row(row ^ 1))
        stage[i] = base

    def halve_line(i):
        links.arrive(lines[i].at[1], stage[i] + 1, mate)
        pairs[i][1, row ^ 2, dp] = (
            pairs[i][1, row ^ 2, dp].astype(f32) + lines[i][1].astype(f32)
        ).astype(low)
        links.push(totals[i].at[row ^ 2, dp], lines[i].at[2], stage[i] + 2, at_row(row ^ 2))

    def share(i, out):
        one, two = turns[i]
        base = links.slots(3)
        links.push(out.at[dp], out.at[dp], base, at_dp(two))
        links.push(out.at[dp], out.at[dp], base + 1, at_dp(one))
        return base

    def share_on(i, out, base):
        one, two = turns[i]
        links.arrive(out.at[dp ^ two], base, mate)
        links.push(out.at[dp ^ two], out.at[dp ^ two], base + 2, at_dp(one))

    def shared(i, out, base):
        one, two = turns[i]
        links.arrive(out.at[dp ^ one], base + 1, mate)
        links.arrive(out.at[dp ^ 3], base + 2, mate)

    stage = [None] * 6
    slot_x, slot_xl = links.slots(4), links.slots(3)
    slot_q, slot_ql = links.slots(1), links.slots(4)
    slot_v, slot_vl, slot_vd = links.slots(1), links.slots(3), links.slots(5)
    order = (row ^ 3, row ^ 1, row ^ 2, row)
    per_row = rows_dev // TILE
    own_block = 2 * row + mine
    own_part = all_q.at[side, pl.ds(2 * col, 2)]
    at_home = home == col
    sums = {}

    def split_ids(step, carry):
        span = pl.ds(pl.multiple_of(step * TILE, TILE), TILE)
        ids_col[span] = jnp.broadcast_to(ids[:, span], (8, TILE)).T[:, :1]
        return carry

    def split_grad(j, carry):
        grad = grad_ctx[j]
        grad_t = grad.astype(f32).T
        for h in range(heads):
            part = slice(h * HEAD, (h + 1) * HEAD)
            both[h, j, :TILE] = q[h, j]
            both[h, j, TILE:] = jnp.concatenate(
                [jnp.zeros((TILE, HEAD), low), grad[:, part]], axis=1
            )
            delta[h, j] = jnp.sum(grad_t[part] * mixed[j, h], axis=0, keepdims=True)
        return carry

    def ready():
        w_t[...] = w_heads[...].reshape(2 * feat, 3 * wide).astype(f32).T.astype(low)
        lax.fori_loop(0, row_tiles, split_ids, 0)
        dkv[...] = jnp.zeros_like(dkv)

    def take_context():
        for n, peer in enumerate(peers):
            links.arrive(grad_ctx.at[peer], swap + n, mate)
        lax.fori_loop(0, blocks, split_grad, 0)

    def attend_back(j):
        block = 2 * j + lax.rem(j + col, 2)
        rows = pl.ds(pl.multiple_of(block * TILE, TILE), TILE)
        query_ids = ids[:, rows]
        far = 2 * j * TILE
        spans = ([(0, far)] if far else []) + [(far, min(2 * j + NEAR, row_tiles) * TILE)]

        def one_head(h, carry, j=j, query_ids=query_ids, far=far, spans=spans):
            total = jnp.zeros((HEAD, TILE), f32)
            for start, stop in spans:
                raw = nt(kv[h, start:stop], both[h, j])
                probs = jnp.exp(raw[:, :TILE] - lse[j, h])
                if start == far:
                    probs = jnp.where(ids_col[start:stop] <= query_ids, probs, 0.0)
                grad_scores = (probs * (raw[:, TILE:] - delta[h, j])).astype(low)
                dkv[h, start:stop] += nn(
                    jnp.concatenate([grad_scores, probs.astype(low)], axis=1), both[h, j]
                )
                total = total + nn(kt[h, :, start:stop], grad_scores)
            dq[j, h] = total * HEAD**-0.5
            return carry

        lax.fori_loop(0, heads, one_head, 0)

    def gather_q(j, carry):
        block = 2 * j + lax.rem(j + col, 2)
        rows = pl.ds(pl.multiple_of(block * TILE, TILE), TILE)
        other = pl.ds(pl.multiple_of((4 * j + 1 - block) * TILE, TILE), TILE)
        value = jnp.concatenate([dq[j, h] for h in range(heads)], axis=0)
        grads_t[2 * wide :, rows] = value.astype(low)
        grads_t[2 * wide :, other] = jnp.zeros((wide, TILE), low)
        grads[rows, 2 * wide :] = value.T.astype(low)
        grads[other, 2 * wide :] = jnp.zeros((TILE, wide), low)
        return carry + jnp.sum(value.T, axis=0, keepdims=True)

    def gather_kv(step, carry):
        rows = pl.ds(pl.multiple_of(step * TILE, TILE), TILE)
        value = jnp.concatenate([dkv[h, rows] for h in range(heads)], axis=1)
        grads[rows, : 2 * wide] = value.astype(low)
        grads_t[: 2 * wide, rows] = value.T.astype(low)
        return carry + jnp.sum(value, axis=0, keepdims=True)

    def weight_grads():
        sums["q"] = lax.fori_loop(0, blocks, gather_q, jnp.zeros((1, wide), f32))
        sums["kv"] = lax.fori_loop(0, row_tiles, gather_kv, jnp.zeros((1, 2 * wide), f32))
        for n in range(2):
            span = slice(n * CHUNK, (n + 1) * CHUNK)
            value = nn(grads_t[...], x_all[:, :, span].reshape(length, CHUNK)).T
            gq[2 * n : 2 * n + 2] = value.astype(low).reshape((2,) + gq.shape[1:])
        links.push(gq.at[:, 1 - col], sum_q, slot_q, mate)

    def token_grads(at):
        def one(step, carry):
            here = pl.ds(pl.multiple_of(step * TILE, TILE), TILE)
            rows = pl.ds(pl.multiple_of((at * per_row + step) * TILE, TILE), TILE)
            value = nn(grads[rows], w_t[...])
            is_own = (at * per_row + step == own_block).astype(f32)
            dx[at, here] = (value + late[...] * is_own).astype(low)
            return carry

        lax.fori_loop(0, per_row, one, 0)

    def send_tokens(n):
        token_grads(order[n])
        links.push(
            dx.at[order[n], :, columns(1 - col, feat)], sum_x.at[order[n]], slot_x + n, mate
        )

    def join_x(at, slot):
        links.arrive(sum_x.at[at], slot, mate)

        def one(step, carry):
            here = pl.ds(pl.multiple_of(step * 128, 128), 128)
            sum_x[at, here] = (
                sum_x[at, here].astype(f32) + dx[at, here, columns(col, feat)].astype(f32)
            ).astype(low)
            return carry

        lax.fori_loop(0, rows_dev // 128, one, 0)

    def line_tokens(n):
        join_x(order[n], slot_x + n)
        if n < 2:
            links.push(sum_x.at[order[n]], line_x.at[1 - n], slot_xl + 1 - n, at_row(row ^ 1))

    def halve_x(step, carry):
        rows = pl.ds(pl.multiple_of(step * 128, 128), 128)
        sum_x[row ^ 2, rows] = (
            sum_x[row ^ 2, rows].astype(f32) + line_x[1, rows].astype(f32)
        ).astype(low)
        return carry

    def halve_tokens():
        links.arrive(line_x.at[1], slot_xl + 1, mate)
        lax.fori_loop(0, rows_dev // 128, halve_x, 0)
        links.push(sum_x.at[row ^ 2], line_x.at[2], slot_xl + 2, at_row(row ^ 2))

    def finish_x(step, carry):
        rows = pl.ds(pl.multiple_of(step * 128, 128), 128)
        value = sum_x[row, rows].astype(f32)
        for n in (0, 2):
            value = value + line_x[n, rows].astype(f32)
        out_x[rows] = value.astype(low)
        return carry

    def finish_tokens():
        for n in (0, 2):
            links.arrive(line_x.at[n], slot_xl + n, mate)
        lax.fori_loop(0, rows_dev // 128, finish_x, 0)

    def add_q(step, carry):
        sum_q[step] = (sum_q[step].astype(f32) + gq[step, col].astype(f32)).astype(low)
        return carry

    def keep_own():
        own_part[...] = sum_q[row]

    def line_q():
        links.arrive(sum_q, slot_q, mate)
        lax.fori_loop(0, ROWS, add_q, 0)
        pl.when(at_home)(keep_own)
        slot = slot_ql + 2 * side + col
        links.push(sum_q.at[row], own_part, slot, mate, jnp.logical_not(at_home))
        for peer in peers:
            links.push(sum_q.at[peer], own_part, slot, (dp, peer, home))

    def first_q():
        for j in range(2):
            for e in range(2):
                here = (row == 2 * col + j) & (col == e)
                links.arrive(
                    all_q.at[j, pl.ds(2 * e, 2)], slot_ql + 2 * j + e, mate, jnp.logical_not(here)
                )
        stage[5] = send_first(5)

    def finish_q():
        links.arrive(first[5].at[0], stage[5][0], mate)
        links.arrive(second[5], stage[5][1], mate)
        add_into(all_q.at[:, dp], first[5].at[0], second[5])
        for j in range(2):
            out_q[dp, j] = all_q[j, dp]
        stage[5] = share(5, out_q)

    def finish_line(i):
        for n in (0, 2):
            links.arrive(lines[i].at[n], stage[i] + n, mate)
        value = pairs[i][1, row, dp].astype(f32)
        for n in (0, 2):
            value = value + lines[i][n].astype(f32)
        out_g[i][dp] = value.astype(low)
        stage[i] = share(i, out_g[i])

    def sums_mate():
        value = jnp.concatenate(
            [sums["kv"], sums["q"], jnp.zeros((1, 2 * feat - 3 * wide), f32)], axis=1
        )
        here = lax.broadcasted_iota(jnp.int32, (8, 2 * feat), 0) == 5 + side
        for c in range(2):
            part = vec_in[8 + 8 * c : 16 + 8 * c] + jnp.where(here & (home == c), value, 0.0)
            vec_own[jnp.where(col == c, 0, 1), :8] = part
        vec_own[0, 8:] = vec_in[24:]
        vec_own[1, 8:] = vec_in[24:]
        links.push(vec_own.at[1], vec_mate, slot_v, mate)

    def sums_line():
        links.arrive(vec_mate, slot_v, mate)
        vec_mate[...] = vec_own[0] + vec_mate[...]
        for n, peer in enumerate(peers):
            links.push(vec_mate, vec_line.at[2 - n], slot_vl + 2 - n, at_row(peer))

    def sums_first():
        for n in range(3):
            links.arrive(vec_line.at[n], slot_vl + n, mate)
        vec_sum = vec_mate[...] + vec_line[0] + vec_line[1] + vec_line[2]
        vec_flat[2] = vec_sum[:8]
        vec_table[dp] = vec_sum[8:]
        links.push(vec_flat.at[2], vec_flat.at[0], slot_vd, at_dp(1))
        links.push(vec_table.at[dp], vec_table.at[dp], slot_vd + 1, at_dp(1))
        links.push(vec_table.at[dp], vec_table.at[dp], slot_vd + 2, at_dp(2))

    def sums_second():
        links.arrive(vec_flat.at[0], slot_vd, mate)
        vec_flat[3] = vec_flat[2] + vec_flat[0]
        links.push(vec_flat.at[3], vec_flat.at[1], slot_vd + 3, at_dp(2))
        links.arrive(vec_table.at[dp ^ 1], slot_vd + 1, mate)
        links.push(vec_table.at[dp ^ 1], vec_table.at[dp ^ 1], slot_vd + 4, at_dp(2))

    def sums_last():
        links.arrive(vec_flat.at[1], slot_vd + 3, mate)
        links.arrive(vec_table.at[dp ^ 2], slot_vd + 2, mate)
        links.arrive(vec_table.at[dp ^ 3], slot_vd + 4, mate)
        vec[:8] = vec_flat[3] + vec_flat[1]
        for n in range(4):
            vec[8 + 8 * n : 16 + 8 * n] = vec_table[n]

    def out_of(i):
        return out_q if i == 5 else out_g[i]

    work = {
        "g": local_grad, "c": join, "s": send_second, "l": send_line, "h": halve_line,
        "f": finish_line, "n": lambda i: share_on(i, out_of(i), stage[i]),
        "r": lambda _: ready(), "d": lambda _: take_context(), "a": attend_back,
        "w": lambda _: weight_grads(), "t": send_tokens, "x": line_tokens,
        "k": lambda n: (halve_tokens, finish_tokens)[n](),
        "q": lambda n: (line_q, first_q, finish_q)[n](),
        "v": lambda n: (sums_mate, sums_line, sums_first, sums_second, sums_last)[n](),
    }
    for entry in PLAN:
        work[entry[0]](int(entry[1]))
    for i in range(6):
        shared(i, out_of(i), stage[i])
    links.arrive(halves.at[other_rows], slot_o, mate)
    links.drain()


def backward_links(
    grad_blocks, output, late, stream, grad_pre, branch_two, activ, branch_one, context,
    q, kv, kt, mixed, lse, ids, x_all, w_heads, vec,
):
    low, f32 = q.dtype, jnp.float32
    heads, length = kv.shape[0], kv.shape[1]
    wide = heads * HEAD
    own, features = output.shape
    hidden = activ.shape[1]
    part = features // ROWS // 4
    widths = [hidden // 4] * 4 + [features // 2]
    rows, feat = 2 * own, features // 2
    blocks = length // TILE // 2
    shape = jax.ShapeDtypeStruct
    outs = [shape((4, part, width), low) for width in widths] + [
        shape((4, 2, part, 3 * wide), low),
        shape((rows, feat), low),
        shape((rows, feat), low),
        shape((40, features), f32),
    ]
    every = [(ROWS, width) for width in widths] + [(2, 3 * wide)]
    return pl.pallas_call(
        functools.partial(backward_kernel, heads),
        out_shape=outs,
        in_specs=[IN_VMEM] * 18,
        out_specs=[IN_VMEM] * len(outs),
        scratch_shapes=[pltpu.VMEM((2, ROWS, 4, part, width), low) for width in widths]
        + [pltpu.VMEM((ROWS, 4, part, width), low) for width in widths]
        + [pltpu.VMEM((2, lead, part, width), low) for lead, width in every]
        + [pltpu.VMEM((lead, part, width), low) for lead, width in every]
        + [pltpu.VMEM((3, part, width), low) for width in widths]
        + [
            pltpu.VMEM((ROWS, own, wide), low),
            pltpu.VMEM((heads, blocks, 2 * TILE, 2 * HEAD), low),
            pltpu.VMEM((heads, blocks, 1, TILE), f32),
            pltpu.VMEM((blocks, heads, HEAD, TILE), f32),
            pltpu.VMEM((heads, length, 2 * HEAD), f32),
            pltpu.VMEM((length, 3 * wide), low),
            pltpu.VMEM((3 * wide, length), low),
            pltpu.VMEM((3 * wide, features), low),
            pltpu.VMEM((3, features, own), low),
            pltpu.VMEM((length, 1), jnp.int32),
            pltpu.VMEM((ROWS, rows, features), low),
            pltpu.VMEM((ROWS, rows, feat), low),
            pltpu.VMEM((3, rows, feat), low),
            pltpu.VMEM((ROWS, 2, 2, part, 3 * wide), low),
            pltpu.VMEM((ROWS, 2, part, 3 * wide), low),
            pltpu.VMEM((2, 4, part, 3 * wide), low),
            pltpu.VMEM((2, 16, features), f32),
            pltpu.VMEM((16, features), f32),
            pltpu.VMEM((3, 16, features), f32),
            pltpu.VMEM((4, 8, features), f32),
            pltpu.VMEM((4, 8, features), f32),
            pltpu.SemaphoreType.DMA((128,)),
            pltpu.SemaphoreType.DMA((128,)),
        ],
        compiler_params=comm_params(2),
        name="backward_links",
    )(
        grad_blocks, output, late, stream, grad_pre, branch_two, activ, branch_one, context,
        q, kv, kt, mixed, lse, ids.reshape(1, -1), x_all, w_heads, vec,
    )


def put_lanes(target, value):
    for n in range(target.shape[0]):
        target[n : n + 1] = value[:, n * 128 : (n + 1) * 128]


def finish_kernel(
    heads, g1a, g1b, g2a, g2b, go, gq, x_in, out_in, vec,
    out, logits, grad_x, o_q, o_bq, o_k, o_v, o_bv, o_o, o_bo, o_g1, o_s1, o_1, o_b1, o_2, o_b2,
    o_g2, o_s2, o_p, o_bp, o_c, o_bc,
):
    dp = lax.axis_index("dp")
    f32 = jnp.float32
    wide = heads * HEAD
    classes = logits.shape[1]
    depth, feat = o_q.shape
    part = g1a.shape[2]
    out[...] = out_in[...]
    grad_x[...] = x_in[...]
    flat = lambda ref: ref[...].astype(f32).reshape(depth, ref.shape[2])
    for target, first, second in ((o_1, g1a, g1b), (o_2, g2a, g2b)):
        target[:, :part] = flat(first)
        target[:, part:] = flat(second)
    o_o[...] = flat(go)
    bias_q, bias_v = [], []
    for j in range(2):
        value = gq[:, j].astype(f32).reshape(depth, 3 * wide)
        o_q[:, j * wide : (j + 1) * wide] = value[:, 2 * wide :]
        for target, shift in ((o_k, 0), (o_v, HEAD)):
            target[:, j * wide : (j + 1) * wide] = jnp.concatenate(
                [value[:, 2 * h * HEAD + shift :][:, :HEAD] for h in range(heads)], axis=1
            )
        bias = vec[5 + j : 6 + j]
        bias_q.append(bias[:, 2 * wide : 3 * wide])
        bias_v += [bias[:, 2 * h * HEAD + HEAD :][:, :HEAD] for h in range(heads)]
    put_lanes(o_bq, jnp.concatenate(bias_q, axis=1))
    put_lanes(o_bv, jnp.concatenate(bias_v, axis=1))
    own = vec[:8]
    for n, target in enumerate((o_bo, o_g1, o_s1, o_b2, o_g2, o_s2)):
        put_lanes(target, own[n // 2 : n // 2 + 1, (n % 2) * feat : (n % 2 + 1) * feat])
    put_lanes(o_b1, jnp.concatenate([own[3:4], own[4:5]], axis=1))
    table = vec[8:40]
    table_t = table.T
    pooler = jnp.zeros(o_p.shape, f32)
    head = [jnp.zeros((1, 2 * feat), f32) for _ in range(classes)]
    bias = jnp.zeros((1, 2 * feat), f32)
    ends = jnp.zeros((1, 128), f32)
    own_tail = jnp.zeros((1, 128), f32)
    for s in range(4):
        at = 8 * s
        slope, tail = table[at + 1 : at + 2], table[at + 3 : at + 4, :128]
        pooler = pooler + table_t[:, at : at + 1] * slope
        bias = bias + slope
        for n in range(classes):
            head[n] = head[n] + table[at + 2 : at + 3] * tail[:, classes + n : classes + n + 1]
        ends = ends + tail
        own_tail = jnp.where(dp == s, tail, own_tail)
    o_p[...] = pooler
    put_lanes(o_bp, bias)
    o_c[...] = jnp.concatenate(head, axis=0)
    o_bc[...] = ends[:, classes : 2 * classes]
    logits[...] = own_tail[:, :classes]


def finish(pieces, classes, heads):
    g1a, g1b, g2a, g2b, go, gq, x_in, out_in, vec = pieces
    f32 = jnp.float32
    depth = go.shape[0] * go.shape[1]
    feat, hidden = go.shape[2], 2 * g1a.shape[2]
    features = vec.shape[1]
    shape = jax.ShapeDtypeStruct
    vector = lambda size: shape((size // 128, 128) if size % 128 == 0 else (1, size), f32)
    square = shape((depth, feat), f32)
    outs = [
        shape(out_in.shape, out_in.dtype), vector(classes), shape(x_in.shape, x_in.dtype),
        square, vector(feat), square, square, vector(feat), square, vector(feat), vector(feat),
        vector(feat), shape((depth, hidden), f32), vector(hidden), shape((depth, hidden), f32),
        vector(feat), vector(feat), vector(feat), shape((features, features), f32),
        vector(features), shape((classes, features), f32), vector(classes),
    ]
    return pl.pallas_call(
        functools.partial(finish_kernel, heads),
        out_shape=outs,
        in_specs=[IN_VMEM] * len(pieces),
        out_specs=[IN_VMEM] * len(outs),
        compiler_params=pltpu.CompilerParams(vmem_limit_bytes=VMEM_BYTES),
        name="finish",
    )(*pieces)


def norm_rows(hidden, gain, shift):
    row_mean = jnp.mean(hidden, axis=1, keepdims=True)
    row_var = jnp.mean(hidden * hidden, axis=1, keepdims=True) - row_mean * row_mean
    inv_scale = lax.rsqrt(row_var + epsilon)
    normed = (hidden - row_mean) * inv_scale
    return normed * gain + shift, normed, inv_scale


def norm_rows_back(grad, normed, inv_scale, gain):
    scaled = grad * gain
    first = jnp.mean(scaled, axis=1, keepdims=True)
    second = jnp.mean(scaled * normed, axis=1, keepdims=True)
    return inv_scale * (scaled - first - normed * second)


def fast_body(
    layer_input, cotangent, labels, block_ids, w_query, b_query, w_key, w_value, b_value,
    w_output, b_output, ln1_gain, ln1_bias, w_inner, b_inner, w_outer, b_outer,
    ln2_gain, ln2_bias, w_pooler, b_pooler, w_classes, b_classes,
):
    f32 = jnp.float32
    feat = layer_input.shape[1]
    heads = 2 * feat // HEAD // ROWS
    vectors = [
        b_query, b_value, b_output, ln1_gain, ln1_bias, b_outer, ln2_gain, ln2_bias, b_inner,
        b_pooler,
    ]
    count = sum(vector.shape[0] for vector in vectors) // feat
    padded, at = 0.0, 0
    full = (count + -count % 8) * feat
    for vector in vectors:
        size = vector.shape[0]
        padded = padded + jnp.pad(vector.astype(f32), (at, full - at - size))
        at += size
    (
        x_all, w_heads, q, kv, kt, mixed, lse, output, late, stream, grad_pre, branch_two, activ,
        branch_one, context, grad_blocks, packed,
    ) = forward_links(
        layer_input, cotangent, padded.reshape(-1, feat), w_query, w_key, w_value, block_ids, labels, w_classes,
        b_classes, w_pooler, [w_output.T, w_inner, w_outer.T],
    )
    s_1a, s_2a, s_1b, s_2b, s_wo, s_q, grad_input, output, sums = backward_links(
        grad_blocks, output, late, stream, grad_pre, branch_two, activ, branch_one, context,
        q, kv, kt, mixed, lse, block_ids, x_all, w_heads, packed,
    )
    outs = finish((s_1a, s_1b, s_2a, s_2b, s_wo, s_q, grad_input, output, sums), w_classes.shape[1], heads)
    flat = (4, 7, 9, 10, 11, 13, 15, 16, 17, 19, 21)
    turned = (8, 14, 20)
    return tuple(
        out.reshape(-1) if n in flat else out.T if n in turned else out
        for n, out in enumerate(outs)
    )


def is_fast(mesh):
    sizes = mesh.shape
    return sizes["dp"] == 4 and sizes["row"] == ROWS and sizes["col"] == 2


def solution(mesh):
    placed = (
        P(("dp", "row"), "col"),
        P(("dp", "row"), "col"),
        P("dp"),
        P("dp"),
        P("row", "col"),
        P("col"),
        P("row", "col"),
        P("row", "col"),
        P("col"),
        P("col", "row"),
        P("col"),
        P("col"),
        P("col"),
        P("row", "col"),
        P("col"),
        P("col", "row"),
        P("col"),
        P("col"),
        P("col"),
        P(),
        P(),
        P(),
        P(),
    )
    return jax.shard_map(
        fast_body if is_fast(mesh) else body,
        mesh=mesh,
        in_specs=placed,
        out_specs=(
            P(("dp", "row"), "col"),
            P("dp", None),
            P(("dp", "row"), "col"),
            P("row", "col"),
            P("col"),
            P("row", "col"),
            P("row", "col"),
            P("col"),
            P("col", "row"),
            P("col"),
            P("col"),
            P("col"),
            P("row", "col"),
            P("col"),
            P("col", "row"),
            P("col"),
            P("col"),
            P("col"),
            P(),
            P(),
            P(),
            P(),
        ),
        check_vma=False,
    )
```

```python
import functools

import jax
import jax.numpy as jnp
from jax import lax
from jax.experimental import pallas as pl
from jax.experimental.pallas import tpu as pltpu
from jax.sharding import PartitionSpec as P

HEAD = 64


highest = lax.Precision.HIGHEST
epsilon = 1e-05
root_half = 0.7071067811865476
inv_root_tau = 0.3989422804014327
masked_score = -1e30


def gelu_exact(values):
    return values * 0.5 * (1.0 + lax.erf(values * root_half))


def gelu_slope(values):
    return 0.5 * (1.0 + lax.erf(values * root_half)) + values * inv_root_tau * jnp.exp(
        -0.5 * values * values
    )


def project(left, right):
    return jnp.dot(left, right, preferred_element_type=jnp.float32)


def contract_first(left, right):
    return lax.dot_general(
        left, right, (((0,), (0,)), ((), ())), preferred_element_type=jnp.float32
    )


def contract_last(left, right):
    return lax.dot_general(
        left, right, (((1,), (1,)), ((), ())), preferred_element_type=jnp.float32
    )


def gather_features(values):
    return lax.all_gather(values, "col", axis=1, tiled=True)


def sum_features(values):
    return lax.psum_scatter(
        values.astype(jnp.bfloat16), "col", scatter_dimension=1, tiled=True
    ).astype(jnp.float32)


def feature_totals(first_part, second_part):
    return lax.psum((jnp.sum(first_part, axis=1), jnp.sum(second_part, axis=1)), "col")


def norm_forward(hidden, gain, shift, features):
    row_total, square_total = feature_totals(hidden, hidden * hidden)
    row_mean = row_total / features
    row_var = square_total / features - row_mean * row_mean
    inv_scale = lax.rsqrt(row_var + epsilon)
    normed = (hidden - row_mean[:, None]) * inv_scale[:, None]
    return (normed * gain + shift, normed, inv_scale)


def norm_backward(grad, normed, inv_scale, gain, features):
    scaled = grad * gain
    first_total, second_total = feature_totals(scaled, scaled * normed)
    return inv_scale[:, None] * (
        scaled - (first_total / features)[:, None] - normed * (second_total / features)[:, None]
    )


def key_split(piece_rows, rows_dev):
    return (piece_rows // rows_dev, rows_dev)


def body(
    layer_input,
    cotangent,
    labels,
    block_ids,
    w_query,
    b_query,
    w_key,
    w_value,
    b_value,
    w_output,
    b_output,
    ln1_gain,
    ln1_bias,
    w_inner,
    b_inner,
    w_outer,
    b_outer,
    ln2_gain,
    ln2_bias,
    w_pooler,
    b_pooler,
    w_classes,
    b_classes,
):
    f32 = jnp.float32
    bf16 = jnp.bfloat16
    rows_dev, feat_col = layer_input.shape
    heads_col = feat_col // HEAD
    features = feat_col * lax.axis_size("col")
    row_index = lax.axis_index("row")
    col_index = lax.axis_index("col")
    seq_index = lax.axis_index("dp")
    seq_count = lax.axis_size("dp")
    score_scale = HEAD ** (-0.5)
    query_ids = lax.dynamic_slice_in_dim(block_ids, row_index * rows_dev, rows_dev)
    last_query = query_ids[rows_dev - 1]
    wq_full, wk_full, wv_full, w1_full = (
        lax.all_gather(w_query, "row", axis=0, tiled=True),
        lax.all_gather(w_key, "row", axis=0, tiled=True),
        lax.all_gather(w_value, "row", axis=0, tiled=True),
        lax.all_gather(w_inner, "row", axis=0, tiled=True),
    )
    wo_full, w2_full = (
        lax.all_gather(w_output, "row", axis=1, tiled=True),
        lax.all_gather(w_outer, "row", axis=1, tiled=True),
    )
    input_whole = gather_features(layer_input)
    queries = (project(input_whole, wq_full) + b_query.astype(f32)).astype(bf16)
    keys_local = project(input_whole, wk_full).astype(bf16)
    values_local = (project(input_whole, wv_full) + b_value.astype(f32)).astype(bf16)
    queries3 = queries.reshape(rows_dev, heads_col, HEAD)
    start_state = (
        jnp.full((heads_col, rows_dev), masked_score, f32),
        jnp.zeros((heads_col, rows_dev), f32),
        jnp.zeros((heads_col, rows_dev, HEAD), f32),
    )
    running = start_state
    keys_piece = lax.all_gather(keys_local, "row", axis=0, tiled=True)
    values_piece = lax.all_gather(values_local, "row", axis=0, tiled=True)
    piece_rows = keys_piece.shape[0]
    number, block_rows = key_split(piece_rows, rows_dev)
    keys4 = keys_piece.reshape(number, block_rows, heads_col, HEAD)
    values4 = values_piece.reshape(number, block_rows, heads_col, HEAD)
    piece_ids = block_ids.reshape(number, block_rows)

    def attend_block_work(state, block_item):
        peak_score, row_mass, accum = state
        keys3, values3, key_ids = block_item
        scores = (
            jnp.einsum("qhd,khd->hqk", queries3, keys3, preferred_element_type=f32) * score_scale
        )
        allowed = (key_ids[None, :] <= query_ids[:, None])[None]
        block_top = jnp.max(jnp.where(allowed, scores, masked_score), axis=2)
        new_peak = jnp.maximum(peak_score, block_top)
        weights = jnp.where(allowed, jnp.exp(scores - new_peak[:, :, None]), 0.0)
        factor = jnp.exp(peak_score - new_peak)
        row_mass = row_mass * factor + jnp.sum(weights, axis=2)
        accum = accum * factor[:, :, None] + jnp.einsum(
            "hqk,khd->hqd", weights.astype(bf16), values3, preferred_element_type=f32
        )
        return (new_peak, row_mass, accum)

    def attend_block_step(state, block_item):
        state = lax.cond(
            block_item[2][0] > last_query, lambda st, item: st, attend_block_work, state, block_item
        )
        return (state, None)

    running, unused = lax.scan(attend_block_step, running, (keys4, values4, piece_ids))
    peak_score, row_mass, accum = running
    mixed = accum / row_mass[:, :, None]
    log_mass = peak_score + jnp.log(row_mass)
    context_low = mixed.transpose(1, 0, 2).reshape(rows_dev, feat_col).astype(bf16)
    attn_branch = sum_features(project(context_low, wo_full))
    hidden_one = layer_input.astype(f32) + attn_branch + b_output.astype(f32)
    gain_one = ln1_gain.astype(f32)
    stream, normed_one, inv_one = norm_forward(hidden_one, gain_one, ln1_bias.astype(f32), features)
    stream_whole = gather_features(stream.astype(bf16))
    pre_act = project(stream_whole, w1_full) + b_inner.astype(f32)
    activ = gelu_exact(pre_act).astype(bf16)
    ffn_branch = sum_features(project(activ, w2_full))
    hidden_two = stream + ffn_branch + b_outer.astype(f32)
    gain_two = ln2_gain.astype(f32)
    result, normed_two, inv_two = norm_forward(hidden_two, gain_two, ln2_bias.astype(f32), features)
    output = result.astype(bf16)
    row_zero = (row_index == 0).astype(f32)
    pool_input = gather_features(output[0:1])
    pooled = jnp.tanh(project(pool_input, w_pooler) + b_pooler.astype(f32))
    classes_f32 = w_classes.astype(f32)
    logits_own = jnp.dot(pooled, classes_f32, precision=highest) + b_classes.astype(f32)
    onehot = (jnp.arange(w_classes.shape[1]) == labels[0]).astype(f32)
    grad_logits = jax.nn.softmax(logits_own, axis=-1) - onehot[None, :]
    g_w_classes = jnp.dot(pooled.T, grad_logits, precision=highest)
    g_b_classes = grad_logits[0]
    grad_pre_pool = jnp.dot(grad_logits, classes_f32.T, precision=highest) * (1.0 - pooled * pooled)
    g_b_pooler = grad_pre_pool[0]
    g_w_pooler = jnp.dot(pool_input.astype(f32).T, grad_pre_pool, precision=highest)
    grad_first = jnp.dot(grad_pre_pool, w_pooler.astype(f32).T, precision=highest)
    first_col = lax.dynamic_slice_in_dim(grad_first[0], col_index * feat_col, feat_col)
    grad_result = cotangent.astype(f32).at[0].add(first_col * row_zero)
    logits_table = lax.dynamic_update_slice_in_dim(
        jnp.zeros((seq_count, w_classes.shape[1]), f32), logits_own * row_zero, seq_index, 0
    )
    g_ln2_gain = jnp.sum(grad_result * normed_two, axis=0)
    g_ln2_bias = jnp.sum(grad_result, axis=0)
    grad_hidden_two = norm_backward(grad_result, normed_two, inv_two, gain_two, features)
    g_b_outer = jnp.sum(grad_hidden_two, axis=0)
    branch_two_whole = gather_features(grad_hidden_two.astype(bf16))
    g_w_outer_full = contract_first(activ, branch_two_whole)
    grad_act = contract_last(branch_two_whole, w2_full)
    grad_pre = (grad_act * gelu_slope(pre_act)).astype(bf16)
    g_b_inner = jnp.sum(grad_pre.astype(f32), axis=0)
    g_w_inner_full = contract_first(stream_whole, grad_pre)
    grad_stream = grad_hidden_two + sum_features(contract_last(grad_pre, w1_full))
    g_ln1_gain = jnp.sum(grad_stream * normed_one, axis=0)
    g_ln1_bias = jnp.sum(grad_stream, axis=0)
    grad_hidden_one = norm_backward(grad_stream, normed_one, inv_one, gain_one, features)
    g_b_output = jnp.sum(grad_hidden_one, axis=0)
    branch_one_whole = gather_features(grad_hidden_one.astype(bf16))
    g_w_output_full = contract_first(context_low, branch_one_whole)
    grad_context = contract_last(branch_one_whole, wo_full).astype(bf16)
    grad_ctx3 = grad_context.reshape(rows_dev, heads_col, HEAD)
    delta = jnp.sum(grad_ctx3.astype(f32).transpose(1, 0, 2) * mixed, axis=2)

    def score_grads(queries_blk, grad_ctx_blk, keys3, values3, allowed, lse_blk, delta_blk):
        scores = (
            jnp.einsum("qhd,khd->hqk", queries_blk, keys3, preferred_element_type=f32) * score_scale
        )
        probs = jnp.where(allowed, jnp.exp(scores - lse_blk[:, :, None]), 0.0)
        grad_probs = jnp.einsum("qhd,khd->hqk", grad_ctx_blk, values3, preferred_element_type=f32)
        grad_scores = (probs * (grad_probs - delta_blk[:, :, None])).astype(bf16)
        return (probs, grad_scores)

    zero_q = jnp.zeros((rows_dev, heads_col, HEAD), f32)
    keys_piece = lax.all_gather(keys_local, "row", axis=0, tiled=True)
    values_piece = lax.all_gather(values_local, "row", axis=0, tiled=True)
    piece_rows = keys_piece.shape[0]
    number, block_rows = key_split(piece_rows, rows_dev)
    keys4 = keys_piece.reshape(number, block_rows, heads_col, HEAD)
    values4 = values_piece.reshape(number, block_rows, heads_col, HEAD)
    piece_ids = block_ids.reshape(number, block_rows)

    def make_block_work(accum_q, block_item):
        keys3, values3, key_ids = block_item
        allowed = (key_ids[None, :] <= query_ids[:, None])[None]
        probs, grad_scores = score_grads(
            queries3, grad_ctx3, keys3, values3, allowed, log_mass, delta
        )
        accum_q = (
            accum_q
            + jnp.einsum("hqk,khd->qhd", grad_scores, keys3, preferred_element_type=f32)
            * score_scale
        )
        part_k = (
            jnp.einsum("hqk,qhd->khd", grad_scores, queries3, preferred_element_type=f32)
            * score_scale
        )
        part_v = jnp.einsum(
            "hqk,qhd->khd", probs.astype(bf16), grad_ctx3, preferred_element_type=f32
        )
        return (accum_q, (part_k, part_v))

    def block_skip(accum_q, block_item):
        empty = jnp.zeros((block_rows, heads_col, HEAD), f32)
        return (accum_q, (empty, empty))

    def make_block_step(accum_q, block_item):
        return lax.cond(
            block_item[2][0] > last_query, block_skip, make_block_work, accum_q, block_item
        )

    grad_q = zero_q
    grad_q, (parts_k, parts_v) = lax.scan(make_block_step, grad_q, (keys4, values4, piece_ids))
    parts_k = parts_k.reshape(piece_rows, feat_col)
    parts_v = parts_v.reshape(piece_rows, feat_col)
    grad_k_all = parts_k
    grad_v_all = parts_v
    back_result = (grad_q, grad_k_all, grad_v_all)
    grad_q3, grad_k_all, grad_v_all = back_result
    grad_keys, grad_values = (
        lax.psum_scatter(
            grad_k_all.astype(jnp.bfloat16), "row", scatter_dimension=0, tiled=True
        ).astype(jnp.float32),
        lax.psum_scatter(
            grad_v_all.astype(jnp.bfloat16), "row", scatter_dimension=0, tiled=True
        ).astype(jnp.float32),
    )
    queries_grad = grad_q3.reshape(rows_dev, feat_col).astype(bf16)
    keys_grad = grad_keys.astype(bf16)
    values_grad = grad_values.astype(bf16)
    g_b_query = jnp.sum(queries_grad.astype(f32), axis=0)
    g_b_value = jnp.sum(values_grad.astype(f32), axis=0)
    g_w_query_full = contract_first(input_whole, queries_grad)
    g_w_key_full = contract_first(input_whole, keys_grad)
    g_w_value_full = contract_first(input_whole, values_grad)
    grad_input_whole = (
        contract_last(queries_grad, wq_full)
        + contract_last(keys_grad, wk_full)
        + contract_last(values_grad, wv_full)
    )
    grad_input = (grad_hidden_one + sum_features(grad_input_whole)).astype(bf16)
    in_rows = w_query.shape[0]
    out_cols = w_output.shape[1]
    (
        sum_wq,
        sum_wk,
        sum_wv,
        sum_w1,
        sum_wo,
        sum_w2,
        g_w_pooler,
        g_b_pooler,
        g_w_classes,
        g_b_classes,
        g_b_query,
        g_b_value,
        g_b_output,
        g_ln1_gain,
        g_ln1_bias,
        g_b_inner,
        g_b_outer,
        g_ln2_gain,
        g_ln2_bias,
        logits_all,
    ) = lax.psum(
        (
            g_w_query_full,
            g_w_key_full,
            g_w_value_full,
            g_w_inner_full,
            g_w_output_full,
            g_w_outer_full,
            g_w_pooler * row_zero,
            g_b_pooler * row_zero,
            g_w_classes * row_zero,
            g_b_classes * row_zero,
            g_b_query,
            g_b_value,
            g_b_output,
            g_ln1_gain,
            g_ln1_bias,
            g_b_inner,
            g_b_outer,
            g_ln2_gain,
            g_ln2_bias,
            logits_table,
        ),
        ("dp", "row"),
    )
    row_start = row_index * in_rows
    col_start = row_index * out_cols
    g_w_query = lax.dynamic_slice_in_dim(sum_wq, row_start, in_rows, 0)
    g_w_key = lax.dynamic_slice_in_dim(sum_wk, row_start, in_rows, 0)
    g_w_value = lax.dynamic_slice_in_dim(sum_wv, row_start, in_rows, 0)
    g_w_inner = lax.dynamic_slice_in_dim(sum_w1, row_start, in_rows, 0)
    g_w_output = lax.dynamic_slice_in_dim(sum_wo, col_start, out_cols, 1)
    g_w_outer = lax.dynamic_slice_in_dim(sum_w2, col_start, out_cols, 1)
    logits = lax.dynamic_slice_in_dim(logits_all, seq_index, 1, 0)
    return (
        output,
        logits,
        grad_input,
        g_w_query,
        g_b_query,
        g_w_key,
        g_w_value,
        g_b_value,
        g_w_output,
        g_b_output,
        g_ln1_gain,
        g_ln1_bias,
        g_w_inner,
        g_b_inner,
        g_w_outer,
        g_b_outer,
        g_ln2_gain,
        g_ln2_bias,
        g_w_pooler,
        g_b_pooler,
        g_w_classes,
        g_b_classes,
    )


MESH_IDS = pl.DeviceIdType.MESH
ROWS = 4
VMEM_BYTES = 64000 * 1024


def place():
    return lax.axis_index("dp"), lax.axis_index("row"), lax.axis_index("col")


class Links:
    def __init__(self, send, recv):
        self.send, self.recv = send, recv
        self.sends, self.recvs, self.open = 0, 0, []

    def slots(self, count):
        base = self.recvs
        self.recvs += count
        return base

    def push(self, source, target, slot, device, when=None):
        copy = pltpu.make_async_remote_copy(
            src_ref=source,
            dst_ref=target,
            send_sem=self.send.at[self.sends],
            recv_sem=self.recv.at[slot],
            device_id=device,
            device_id_type=MESH_IDS,
        )
        self.sends += 1
        if when is None:
            copy.start()
        else:
            pl.when(when)(lambda: copy.start())
        self.open.append((copy, when))

    def arrive(self, target, slot, device, when=None):
        copy = pltpu.make_async_remote_copy(
            src_ref=target,
            dst_ref=target,
            send_sem=self.send.at[0],
            recv_sem=self.recv.at[slot],
            device_id=device,
            device_id_type=MESH_IDS,
        )
        if when is None:
            copy.wait_recv()
        else:
            pl.when(when)(lambda: copy.wait_recv())

    def drain(self):
        for copy, when in self.open:
            if when is None:
                copy.wait_send()
            else:
                pl.when(when)(lambda copy=copy: copy.wait_send())
        self.open = []


def meet(devices):
    barrier = pltpu.get_barrier_semaphore()
    for device in devices:
        pl.semaphore_signal(barrier, inc=1, device_id=device, device_id_type=MESH_IDS)
    pl.semaphore_wait(barrier, len(devices))


def within(value):
    return (value >= 0) & (value < ROWS)


def steps_of_line(row):
    for step in (1, 2, 3):
        for way in (1, -1):
            source = row - way * step
            yield step, way, (3 - step if way == 1 else step - 1), source, within(source)


def columns(col, width):
    return pl.ds(pl.multiple_of(col * width, 128), width)


IN_VMEM = pl.BlockSpec(memory_space=pltpu.VMEM)
IN_PLACE = pl.BlockSpec(memory_space=pl.ANY)


def comm_params(number):
    return pltpu.CompilerParams(
        collective_id=number, has_side_effects=True, vmem_limit_bytes=VMEM_BYTES
    )


TILE = 256
NEAR = 3


def nt(left, right):
    return lax.dot_general(
        left, right, (((1,), (1,)), ((), ())), preferred_element_type=jnp.float32
    )


def nn(left, right):
    return jnp.dot(left, right, preferred_element_type=jnp.float32)


def forward_kernel(
    widths, heads, x, cot, vec, wq, wk, wv, ids, labels, w_classes, b_classes, pooler_far, *refs
):
    count = len(widths)
    shards, refs = refs[:count], refs[count:]
    far_outs = refs[:7] + refs[12:13] + refs[10:11]
    (
        output, late, stream_out, _, branch_two_out, _, branch_one_out, context,
        grad_blocks, packed,
    ) = refs[7:17]
    fulls, refs = refs[17 : 17 + count], refs[17 + count :]
    (
        x_all, w_heads, q_out, kv_out, kt_out, mixed_out, lse_out, activ_out, grad_pre_out,
        cot_own, vec_all, context_in, vt_out, ids_col, packs, low_out, slope, total, w_pooler, send, recv, local,
    ) = refs
    near_outs = (x_all, w_heads, q_out, kv_out, kt_out, mixed_out, lse_out, activ_out, grad_pre_out)
    write_out = [
        pltpu.make_async_copy(near, far, local.at[count + 11 + n])
        for n, (near, far) in enumerate(zip(near_outs, far_outs))
    ]
    dp, row, col = place()
    links = Links(send, recv)
    low = x.dtype
    rows_dev, feat = x.shape
    wide = heads * HEAD
    mate = (dp, row, 1 - col)
    at_row = lambda other: (dp, other, col)
    at_dp = lambda flip: (dp ^ flip, row, col)
    home, side = row // 2, lax.rem(row, 2)
    mine = lax.rem(row + col, 2)
    half = rows_dev // 2
    meet([at_row(lax.rem(row + k, ROWS)) for k in (1, 2, 3)] + [at_dp(1), at_dp(2), mate])

    x_at = lambda k: x_all.at[k, :, columns(col, feat)]
    x_mate_at = lambda k: x_all.at[k, :, columns(1 - col, feat)]
    w_at = lambda i, k, q: fulls[i].at[k, q, :, columns(col, widths[i])]
    row_at = lambda i, k: fulls[i].at[k, :, :, columns(col, widths[i])]
    row_mate_at = lambda i, k: fulls[i].at[k, :, :, columns(1 - col, widths[i])]

    line_x, mate_x = links.slots(3), links.slots(4)
    line_q, first_q, second_q, mate_q = (
        links.slots(3), links.slots(3), links.slots(6), links.slots(1),
    )
    mate_cot, mate_vec, swap = links.slots(1), links.slots(1), links.slots(3)
    line_w = [links.slots(3) for _ in widths]
    first_w = [links.slots(3) for _ in widths]
    second_w = [links.slots(6) for _ in widths]
    mate_w = [links.slots(4) for _ in widths]
    steps = list(steps_of_line(row))
    at_step = lambda step: [entry[2:] for entry in steps if entry[0] == step]

    def relay(step, own, full, base):
        for way in (1, -1):
            held, onward = row - way * (step - 1), row + way
            ok = within(held) & within(onward)
            slot = 3 - step if way == 1 else step - 1
            links.push(own if step == 1 else full(held), full(held), base + slot, at_row(onward), ok)

    relay(1, x, x_at, line_x)
    links.push(x, x_at(row), mate_x, mate)
    for j in range(2):
        pieces = []
        for h in range(heads):
            part = slice(j * wide + h * HEAD, j * wide + (h + 1) * HEAD)
            pieces += [wk[:, part], wv[:, part]]
        pieces.append(wq[:, j * wide : (j + 1) * wide])
        packs[j] = jnp.concatenate(pieces, axis=1).reshape(packs.shape[1:])
    for j in range(2):
        k = 2 * col + j
        away = k != row
        slot = lax.rem(row - k + ROWS + 3, ROWS)
        links.push(packs.at[j, dp], w_heads.at[row, dp], line_q + slot, at_row(k), away)

        @pl.when(jnp.logical_not(away))
        def _(j=j):
            w_heads[row] = packs[j]

    links.push(
        cot.at[pl.ds(pl.multiple_of((1 - mine) * half, 128), half)],
        cot_own.at[:, columns(col, feat)],
        mate_cot,
        mate,
    )
    links.push(vec, vec_all.at[col], mate_vec, mate)
    vec_all[col] = vec[...]
    read_in = [
        pltpu.make_async_copy(x, x_at(row), local.at[count + 8]),
        pltpu.make_async_copy(
            cot.at[pl.ds(pl.multiple_of(mine * half, 128), half)],
            cot_own.at[:, columns(col, feat)],
            local.at[count + 9],
        ),
        pltpu.make_async_copy(pooler_far, w_pooler, local.at[count + 10]),
    ]
    for copy in read_in:
        copy.start()
    copies = [
        pltpu.make_async_copy(shards[i], row_at(i, row), local.at[i]) for i in range(count)
    ]

    at_home = home == col

    def q_first():
        for slot in range(3):
            k = lax.rem(row + slot + 1, ROWS)
            one = 1 + slot % 2
            links.arrive(w_heads.at[k, dp], line_q + slot, mate, at_home)
            links.push(
                w_heads.at[k, dp], w_heads.at[k, dp], first_q + slot, at_dp(one), at_home
            )

    def q_second():
        for slot in range(3):
            k = lax.rem(row + slot + 1, ROWS)
            one, two = 1 + slot % 2, 2 - slot % 2
            links.arrive(w_heads.at[k, dp ^ one], first_q + slot, mate, at_home)
            for n, q in enumerate((dp, dp ^ one)):
                links.push(
                    w_heads.at[k, q], w_heads.at[k, q], second_q + 2 * slot + n, at_dp(two), at_home
                )

    def q_mate():
        for slot in range(3):
            k = lax.rem(row + slot + 1, ROWS)
            two = 2 - slot % 2
            links.arrive(w_heads.at[k, dp ^ two], second_q + 2 * slot, mate, at_home)
            links.arrive(w_heads.at[k, dp ^ 3], second_q + 2 * slot + 1, mate, at_home)
        links.push(w_heads, w_heads, mate_q, mate, at_home)
        links.arrive(w_heads, mate_q, mate, jnp.logical_not(at_home))

    def x_step(step):
        for slot, k, ok in at_step(step):
            links.arrive(x_at(k), line_x + slot, mate, ok)
        if step < 3:
            relay(step + 1, x, x_at, line_x)
        for slot, k, ok in at_step(step):
            links.push(x_at(k), x_at(k), mate_x + 1 + slot, mate, ok)

    turn = lambda i, slot: (1, 2) if (i + slot) % 2 == 0 else (2, 1)

    def w_start(at_left, at_right):
        for way, ok in ((1, row == at_right), (-1, row == at_left)):
            slot = 2 if way == 1 else 0
            for i in range(count):
                links.push(
                    shards[i].at[dp], w_at(i, row, dp), line_w[i] + slot, at_row(row + way), ok
                )

    def w_first(step):
        for i in range(count):
            for slot, k, ok in at_step(step):
                links.arrive(w_at(i, k, dp), line_w[i] + slot, mate, ok)
            if step < 3:
                relay(step + 1, None, lambda k, i=i: w_at(i, k, dp), line_w[i])
            for slot, k, ok in at_step(step):
                one, two = turn(i, slot)
                links.push(w_at(i, k, dp), w_at(i, k, dp), first_w[i] + slot, at_dp(one), ok)

    def w_second(step):
        for i in range(count):
            for slot, k, ok in at_step(step):
                one, two = turn(i, slot)
                links.arrive(w_at(i, k, dp ^ one), first_w[i] + slot, mate, ok)
                for n, q in enumerate((dp, dp ^ one)):
                    links.push(
                        w_at(i, k, q), w_at(i, k, q), second_w[i] + 2 * slot + n, at_dp(two), ok
                    )

    def w_mate(step, items):
        for i in items:
            for slot, k, ok in at_step(step):
                one, two = turn(i, slot)
                links.arrive(w_at(i, k, dp ^ two), second_w[i] + 2 * slot, mate, ok)
                links.arrive(w_at(i, k, dp ^ 3), second_w[i] + 2 * slot + 1, mate, ok)
                links.push(row_at(i, k), row_at(i, k), mate_w[i] + 1 + slot, mate, ok)

    def w_ready(i):
        w_mate(3, (i,))
        copies[i].wait()
        links.arrive(row_mate_at(i, row), mate_w[i], mate)
        for slot in range(3):
            k = lax.rem(row + slot + 1, ROWS)
            links.arrive(row_mate_at(i, k), mate_w[i] + 1 + slot, mate)

    row_tiles = ROWS * rows_dev // TILE
    per_row = rows_dev // TILE

    def split_ids(step, carry):
        span = pl.ds(pl.multiple_of(step * TILE, TILE), TILE)
        ids_col[span] = jnp.broadcast_to(ids[:, span], (8, TILE)).T[:, :1]
        return carry

    lax.fori_loop(0, row_tiles, split_ids, 0)
    w_start(3, 0)
    x_step(1)
    w_start(2, 1)
    q_first()
    x_step(2)
    w_start(1, 2)
    q_second()
    for copy in copies:
        copy.start()
    for i in range(count):
        links.push(shards[i], row_at(i, row), mate_w[i], mate)
    q_mate()
    links.arrive(vec_all.at[1 - col], mate_vec, mate)
    bias_of = lambda n: jnp.where(
        side == 0, vec_all[home, n : n + 1, :wide], vec_all[home, n : n + 1, wide : 2 * wide]
    )
    bias_q, bias_v = bias_of(0), bias_of(1)
    blank = jnp.zeros((1, HEAD), jnp.float32)
    bias_kv = jnp.concatenate(
        sum([[blank, bias_v[:, h * HEAD : (h + 1) * HEAD]] for h in range(heads)], []), axis=1
    )
    weights = lambda start, stop: w_heads[:, :, :, start:stop].reshape(2 * feat, stop - start)

    def project_keys(k):
        def one_tile(step, carry):
            here = pl.ds(pl.multiple_of(step * TILE, TILE), TILE)
            rows = pl.ds(pl.multiple_of(k * rows_dev + step * TILE, TILE), TILE)
            both = nn(x_all[k, here], weights(0, 2 * wide)) + bias_kv
            both_t = both.T
            for h in range(heads):
                at = 2 * h * HEAD
                kv_out[h, rows] = both[:, at : at + 2 * HEAD].astype(low)
                kt_out[h, :, rows] = both_t[at : at + HEAD].astype(low)
                vt_out[h, :, rows] = both_t[at + HEAD : at + 2 * HEAD].astype(low)
            return carry

        lax.fori_loop(0, per_row, one_tile, 0)

    links.arrive(x_mate_at(row), mate_x, mate)
    read_in[0].wait()
    project_keys(row)
    w_first(1)
    x_step(3)
    for slot in (0, 2, 1):
        k = lax.rem(row + slot + 1, ROWS)
        links.arrive(x_mate_at(k), mate_x + 1 + slot, mate)
        project_keys(k)

    def project_query(j, carry):
        block = 2 * j + lax.rem(j + col, 2)
        here = pl.ds(pl.multiple_of(lax.rem(block, per_row) * TILE, TILE), TILE)
        query = nn(x_all[block // per_row, here], weights(2 * wide, 3 * wide)) + bias_q
        query = query.astype(low) * jnp.asarray(HEAD**-0.5, low)
        for h in range(heads):
            q_out[h, j] = jnp.concatenate(
                [query[:, h * HEAD : (h + 1) * HEAD], jnp.zeros((TILE, HEAD), low)], axis=1
            )
        return carry

    blocks = row_tiles // 2
    lax.fori_loop(0, blocks, project_query, 0)
    for copy in write_out[:5]:
        copy.start()
    w_first(2)
    for j in range(blocks):
        block = 2 * j + lax.rem(j + col, 2)
        rows = pl.ds(pl.multiple_of(block * TILE, TILE), TILE)
        query_ids = ids[:, rows]
        length = min(2 * j + NEAR, row_tiles) * TILE
        clear = 2 * j * TILE

        def one_head(h, carry, j=j, query_ids=query_ids, length=length, clear=clear):
            scores = nt(kv_out[h, :length], q_out[h, j])
            near = jnp.where(
                ids_col[clear:length] <= query_ids, scores[clear:], masked_score
            )
            top = jnp.max(near, axis=0, keepdims=True)
            if clear:
                top = jnp.maximum(top, jnp.max(scores[:clear], axis=0, keepdims=True))
                weights_far = jnp.exp(scores[:clear] - top)
            weights_near = jnp.exp(near - top)
            mass = jnp.sum(weights_near, axis=0, keepdims=True)
            value = nn(vt_out[h, :, clear:length], weights_near.astype(low))
            if clear:
                mass = mass + jnp.sum(weights_far, axis=0, keepdims=True)
                value = value + nn(vt_out[h, :, :clear], weights_far.astype(low))
            mixed_out[j, h] = value / mass
            lse_out[j, h] = top + jnp.log(mass)
            return carry

        lax.fori_loop(0, heads, one_head, 0)
        low_out[j] = (
            jnp.concatenate([mixed_out[j, h] for h in range(heads)], axis=0).T.astype(low)
        )
        away = row != j
        slot = lax.rem(row - j + ROWS + 3, ROWS)
        links.push(low_out.at[j], context_in.at[row], swap + slot, at_row(j), away)

        @pl.when(jnp.logical_not(away))
        def _(j=j):
            context_in[row] = low_out[j]

        if j == 0:
            w_second(1)
        if j == 1:
            w_first(3)
            w_second(2)
            w_mate(1, range(count))
        if j == 2:
            w_second(3)
            w_mate(2, range(count))

    for copy in write_out[5:7]:
        copy.start()
    f32 = jnp.float32
    own, features = output.shape
    hidden = 2 * widths[1]
    chunk = features
    w_o, w_1, w_2 = fulls
    part_of = lambda full, span: full[:, :, :, span].reshape(features, span.stop - span.start)
    vector = lambda n: jnp.concatenate([vec_all[0, n : n + 1], vec_all[1, n : n + 1]], axis=1)
    links.arrive(cot_own.at[:, columns(1 - col, feat)], mate_cot, mate)
    read_in[1].wait()
    read_in[2].wait()
    for slot in range(3):
        links.arrive(context_in.at[lax.rem(row + slot + 1, ROWS)], swap + slot, mate)
    context[...] = jnp.concatenate([context_in[r] for r in range(ROWS)], axis=1)
    w_ready(0)
    value = nt(context[...], w_o[...].reshape(features, features))
    own_rows = pl.ds(pl.multiple_of(mine * own, 128), own)
    hidden_one = x_all[row, own_rows].astype(f32) + value + vector(2)
    gain_one, gain_two = vector(3), vector(6)
    stream, normed_one, inv_one = norm_rows(hidden_one, gain_one, vector(4))
    late[...] = stream
    stream_out[...] = stream.astype(low)
    total[...] = jnp.zeros_like(total)
    bias_1 = [
        jnp.concatenate(
            [vec_all[c, 8 + 2 * n : 9 + 2 * n], vec_all[c, 9 + 2 * n : 10 + 2 * n]], axis=1
        )
        for c in range(2)
        for n in range(hidden // chunk // 2)
    ]
    w_ready(1)
    for n in range(hidden // chunk):
        span = slice(n * chunk, (n + 1) * chunk)
        pre_act = nn(stream_out[...], part_of(w_1, span)) + bias_1[n]
        half = 0.5 * (1.0 + lax.erf(pre_act * root_half))
        slope[:, span] = half + pre_act * inv_root_tau * jnp.exp(-0.5 * pre_act * pre_act)
        activ_out[:, span] = (pre_act * half).astype(low)
    write_out[7].start()
    w_ready(2)
    for n in range(hidden // chunk):
        span = slice(n * chunk, (n + 1) * chunk)
        total[...] += nt(activ_out[:, span], part_of(w_2, span))
    hidden_two = late[...] + total[...] + vector(5)
    result, normed_two, inv_two = norm_rows(hidden_two, gain_two, vector(7))
    output[...] = result.astype(low)

    classes = b_classes.shape[1]
    first = output[:8]
    pooled = jnp.tanh(nn(first, w_pooler[...])[:1] + jnp.concatenate([vec_all[0, 12:13], vec_all[0, 13:14]], axis=1))
    lane = lax.broadcasted_iota(jnp.int32, (1, 128), 1)
    logits = jnp.full((1, 128), masked_score, f32)
    rows = [w_classes[n : n + 1].astype(f32) for n in range(classes)]
    for n in range(classes):
        logit = jnp.sum(pooled * rows[n], axis=1, keepdims=True) + b_classes[:, n : n + 1].astype(f32)
        logits = jnp.where(lane == n, logit, logits)
    odds = jnp.exp(logits - jnp.max(logits, axis=1, keepdims=True))
    odds = odds / jnp.sum(odds, axis=1, keepdims=True)
    grad_logits = odds - (lane == labels[0, 0]).astype(f32)
    grad_pool = jnp.zeros((1, features), f32)
    for n in range(classes):
        grad_pool = grad_pool + grad_logits[:, n : n + 1] * rows[n]
    grad_pool = grad_pool * (1.0 - pooled * pooled)
    high = grad_pool.astype(low)
    rest = grad_pool - high.astype(f32)
    mid = rest.astype(low)
    last = (rest - mid.astype(f32)).astype(low)
    split = jnp.concatenate(
        [high.astype(f32), mid.astype(f32), last.astype(f32), jnp.zeros((5, features), f32)]
    ).astype(low)
    grad_first = jnp.sum(nt(split, w_pooler[...]), axis=0, keepdims=True)
    holder = ((row == 0) & (col == 0)).astype(f32)
    top = (lax.broadcasted_iota(jnp.int32, (own, 1), 0) == 0).astype(f32) * holder
    grad_result = cot_own[...].astype(f32) + top * grad_first

    tokens = lambda values: jnp.sum(values, axis=0, keepdims=True)
    g_gain_two, g_shift_two = tokens(grad_result * normed_two), tokens(grad_result)
    grad_two = norm_rows_back(grad_result, normed_two, inv_two, gain_two)
    g_bias_two = tokens(grad_two)
    late[...] = grad_two
    branch_two_out[...] = grad_two.astype(low)
    total[...] = jnp.zeros_like(total)
    g_bias_one = []
    for n in range(hidden // chunk):
        span = slice(n * chunk, (n + 1) * chunk)
        grad_pre = (nn(branch_two_out[...], part_of(w_2, span)) * slope[:, span]).astype(low)
        grad_pre_out[:, span] = grad_pre
        g_bias_one.append(tokens(grad_pre.astype(f32)))
        total[...] += nt(grad_pre_out[:, span], part_of(w_1, span))
    write_out[8].start()
    grad_stream = late[...] + total[...]
    g_gain_one, g_shift_one = tokens(grad_stream * normed_one), tokens(grad_stream)
    grad_one = norm_rows_back(grad_stream, normed_one, inv_one, gain_one)
    late[...] = grad_one
    branch_one_out[...] = grad_one.astype(low)
    grad_context = nn(branch_one_out[...], w_o[...].reshape(features, features)).astype(low)
    for r in range(ROWS):
        grad_blocks[r] = grad_context[:, r * wide : (r + 1) * wide]

    packed[...] = jnp.zeros_like(packed)
    vectors = [tokens(grad_one), g_gain_one, g_shift_one, g_bias_two, g_gain_two, g_shift_two]
    for n, value in enumerate(vectors):
        for c in range(2):
            packed[8 + 8 * c + n // 2, pl.ds((n % 2) * feat, feat)] = value[
                0, c * feat : (c + 1) * feat
            ]
    for n, value in enumerate(g_bias_one):
        packed[8 + 8 * (n // 2) + 3 + n % 2] = value[0]
    spare = jnp.zeros((1, features - 128), f32)
    shifted = pltpu.roll(jnp.where(lane < classes, grad_logits, 0.0), classes, 1)
    tail = jnp.concatenate([jnp.where(lane < classes, logits, shifted), spare], axis=1)
    for n, value in enumerate((first[:1].astype(f32), grad_pool, pooled, tail)):
        packed[24 + n : 25 + n] = value * holder
    for copy in write_out:
        copy.wait()
    links.drain()


def forward_links(x, cot, vec, wq, wk, wv, ids, labels, w_classes, b_classes, w_pooler, shards):
    widths = [shard.shape[1] for shard in shards]
    rows, feat = x.shape
    low, f32 = x.dtype, jnp.float32
    part = shards[0].shape[0] // 4
    features, hidden = 2 * feat, 2 * widths[1]
    heads = features // HEAD // ROWS
    wide = heads * HEAD
    length, own = ROWS * rows, rows // 2
    blocks = length // TILE // 2
    shape = jax.ShapeDtypeStruct
    narrow, broad = shape((own, features), low), shape((own, hidden), low)
    shapes = [
        shape((ROWS, rows, features), low),
        shape((ROWS, 4, part, 3 * wide), low),
        shape((heads, blocks, TILE, 2 * HEAD), low),
        shape((heads, length, 2 * HEAD), low),
        shape((heads, HEAD, length), low),
        shape((blocks, heads, HEAD, TILE), f32),
        shape((blocks, heads, 1, TILE), f32),
        narrow, shape((own, features), f32), narrow, broad, narrow, broad, narrow, narrow,
        shape((ROWS, own, wide), low), shape((32, features), f32),
    ]
    return pl.pallas_call(
        functools.partial(forward_kernel, widths, heads),
        out_shape=shapes,
        in_specs=[IN_PLACE] * 2 + [IN_VMEM] * 5 + [pl.BlockSpec(memory_space=pltpu.SMEM)]
        + [IN_VMEM] * 2 + [IN_PLACE] * (1 + len(shards)),
        out_specs=[IN_PLACE] * 7 + [IN_VMEM] * 3 + [IN_PLACE, IN_VMEM, IN_PLACE] + [IN_VMEM] * 4,
        scratch_shapes=[pltpu.VMEM((ROWS, 4, part, 2 * width), low) for width in widths]
        + [pltpu.VMEM(out.shape, out.dtype) for out in shapes[:7] + [broad, broad]]
        + [
            pltpu.VMEM((own, features), low),
            pltpu.VMEM((2,) + vec.shape, f32),
            pltpu.VMEM((ROWS, own, wide), low),
            pltpu.VMEM((heads, HEAD, length), low),
            pltpu.VMEM((length, 1), jnp.int32),
            pltpu.VMEM((2, 4, part, 3 * wide), low),
            pltpu.VMEM((blocks, TILE, wide), low),
            pltpu.VMEM((own, hidden), f32),
            pltpu.VMEM((own, features), f32),
            pltpu.VMEM(w_pooler.shape, low),
            pltpu.SemaphoreType.DMA((160,)),
            pltpu.SemaphoreType.DMA((96,)),
            pltpu.SemaphoreType.DMA((24,)),
        ],
        compiler_params=comm_params(1),
        name="forward_links",
    )(
        x, cot, vec, wq, wk, wv, ids.reshape(1, -1), labels.reshape(1, 1), w_classes.T,
        b_classes.reshape(1, -1), w_pooler, *[shard.reshape(4, part, -1) for shard in shards],
    )


def add_into(total, *others):
    def one(step, carry):
        value = total[step].astype(jnp.float32)
        for other in others:
            value = value + other[step].astype(jnp.float32)
        total[step] = value.astype(total.dtype)
        return carry

    lax.fori_loop(0, total.shape[0], one, 0)


CHUNK = 384
PLAN = (
    "g0",
    "g1",
    "r0",
    "c0",
    "g2",
    "g3",
    "c1",
    "g4",
    "d0",
    "a0",
    "s0",
    "s1",
    "c2",
    "a1",
    "c3",
    "a2",
    "l1",
    "l0",
    "c4",
    "a3",
    "h1",
    "h0",
    "w0",
    "s2",
    "s3",
    "q0",
    "t0",
    "t1",
    "x0",
    "s4",
    "t2",
    "l2",
    "x1",
    "l3",
    "t3",
    "f0",
    "f1",
    "v0",
    "l4",
    "x2",
    "n0",
    "n1",
    "v1",
    "h2",
    "q1",
    "h3",
    "h4",
    "k0",
    "v2",
    "s5",
    "v3",
    "f2",
    "f3",
    "f4",
    "x3",
    "q2",
    "n2",
    "n3",
    "n4",
    "n5",
    "k1",
    "v4",
)


def backward_kernel(
    heads, blocks_in, output, late_far, stream, pre_far, branch_two, activ_far, branch_one, context,
    q_far, kv_far, kt_far, mixed_far, lse_far, ids, x_far, w_far, vec_in, *refs,
):
    out_g, refs = refs[:5], refs[5:]
    out_q, out_x, halves, vec, refs = refs[0], refs[1], refs[2], refs[3], refs[4:]
    pairs, refs = refs[:5], refs[5:]
    mates, refs = refs[:5], refs[5:]
    first, refs = refs[:6], refs[6:]
    second, refs = refs[:6], refs[6:]
    lines, refs = refs[:5], refs[5:]
    (
        grad_ctx, both, delta, dq, dkv, grads, grads_t, w_t, turned, ids_col, dx, sum_x,
        line_x, gq, sum_q, all_q, vec_own, vec_mate, vec_line, vec_flat, vec_table,
        w_heads, q, kv, kt, mixed, lse, x_all, grad_pre, activ, late, send, recv, local,
    ) = refs
    nears = (w_heads, q, kv, kt, mixed, lse, x_all, grad_pre, activ, late)
    fars = (w_far, q_far, kv_far, kt_far, mixed_far, lse_far, x_far, pre_far, activ_far, late_far)
    reads = [
        pltpu.make_async_copy(far, near, local.at[n]) for n, (far, near) in enumerate(zip(fars, nears))
    ]
    for n in (7, 8, 0, 1, 2, 3, 4, 5, 6, 9):
        reads[n].start()
    dp, row, col = place()
    links = Links(send, recv)
    low, f32 = q.dtype, jnp.float32
    mate = (dp, row, 1 - col)
    peers = [lax.rem(row + n, ROWS) for n in (1, 2, 3)]
    at_row = lambda other: (dp, other, col)
    at_dp = lambda flip: (dp ^ flip, row, col)
    home, side = row // 2, lax.rem(row, 2)
    mine = lax.rem(row + col, 2)
    length = kv.shape[1]
    wide = heads * HEAD
    rows_dev, feat = out_x.shape
    half = rows_dev // 2
    row_tiles = length // TILE
    blocks = row_tiles // 2
    meet(
        [at_row(peer) for peer in peers]
        + [at_dp(1), at_dp(2), mate]
        + [(dp, peer, 1 - col) for peer in peers]
    )

    swap, slot_o = links.slots(3), links.slots(1)
    for n, peer in enumerate(peers):
        links.push(blocks_in.at[peer], grad_ctx.at[row], swap + 2 - n, at_row(peer))
    own_rows = pl.ds(pl.multiple_of(mine * half, 128), half)
    other_rows = pl.ds(pl.multiple_of((1 - mine) * half, 128), half)
    links.push(output.at[:, columns(1 - col, feat)], halves.at[own_rows], slot_o, mate)
    reads += [
        pltpu.make_async_copy(output.at[:, columns(col, feat)], halves.at[own_rows], local.at[10]),
        pltpu.make_async_copy(blocks_in.at[row], grad_ctx.at[row], local.at[11]),
    ]
    reads[10].start()
    reads[11].start()

    lefts = (stream, branch_two, branch_one)
    for n in range(3):
        turned[n] = lefts[n][...].astype(f32).T.astype(low)
    feeds = [(0, grad_pre, 0), (1, activ, 0), (0, grad_pre, 1), (1, activ, 1), (2, context, 0)]
    turns = [(1, 2), (2, 1), (1, 2), (2, 1), (1, 2), (2, 1)]
    widths = [out.shape[2] for out in out_g]
    slot_g = [links.slots(1) for _ in widths]

    def local_grad(i):
        if i < 2:
            reads[7 + i].wait()
        left, right, part = feeds[i]
        width = widths[i]
        per = width // CHUNK

        def one(step, carry):
            which, n = step // per, step % per
            core = jnp.where(which == 0, 1 - col, col)
            start = core * (right.shape[1] // 2) + part * width + n * CHUNK
            value = nn(turned[left], right[:, pl.ds(pl.multiple_of(start, 128), CHUNK)])
            pairs[i][which, :, :, :, pl.ds(pl.multiple_of(n * CHUNK, 128), CHUNK)] = (
                value.astype(low).reshape(pairs[i].shape[1:4] + (CHUNK,))
            )
            return carry

        lax.fori_loop(0, 2 * per, one, 0)
        links.push(pairs[i].at[0], mates[i], slot_g[i], mate)

    totals = [pair.at[1] for pair in pairs] + [all_q]

    def send_first(i):
        one, two = turns[i]
        base = links.slots(2)
        links.push(totals[i].at[:, dp ^ 3], first[i].at[1], base + 1, at_dp(one))
        links.push(totals[i].at[:, dp ^ one], first[i].at[0], base, at_dp(one))
        return base

    def join(i):
        links.arrive(mates[i], slot_g[i], mate)

        def one(step, carry):
            at, q_at = step // 4, step % 4
            pairs[i][1, at, q_at] = (
                pairs[i][1, at, q_at].astype(f32) + mates[i][at, q_at].astype(f32)
            ).astype(low)
            return carry

        lax.fori_loop(0, 16, one, 0)
        stage[i] = send_first(i)

    def send_second(i):
        one, two = turns[i]
        base = stage[i]
        links.arrive(first[i].at[1], base + 1, mate)
        add_into(totals[i].at[:, dp ^ two], first[i].at[1])
        slot = links.slots(1)
        links.push(totals[i].at[:, dp ^ two], second[i], slot, at_dp(two))
        stage[i] = (base, slot)

    def send_line(i):
        links.arrive(first[i].at[0], stage[i][0], mate)
        links.arrive(second[i], stage[i][1], mate)
        add_into(totals[i].at[:, dp], first[i].at[0], second[i])
        base = links.slots(3)
        links.push(totals[i].at[row ^ 3, dp], lines[i].at[1], base + 1, at_row(row ^ 1))
        links.push(totals[i].at[row ^ 1, dp], lines[i].at[0], base, at_row(row ^ 1))
        stage[i] = base

    def halve_line(i):
        links.arrive(lines[i].at[1], stage[i] + 1, mate)
        pairs[i][1, row ^ 2, dp] = (
            pairs[i][1, row ^ 2, dp].astype(f32) + lines[i][1].astype(f32)
        ).astype(low)
        links.push(totals[i].at[row ^ 2, dp], lines[i].at[2], stage[i] + 2, at_row(row ^ 2))

    def share(i, out):
        one, two = turns[i]
        base = links.slots(3)
        links.push(out.at[dp], out.at[dp], base, at_dp(two))
        links.push(out.at[dp], out.at[dp], base + 1, at_dp(one))
        return base

    def share_on(i, out, base):
        one, two = turns[i]
        links.arrive(out.at[dp ^ two], base, mate)
        links.push(out.at[dp ^ two], out.at[dp ^ two], base + 2, at_dp(one))

    def shared(i, out, base):
        one, two = turns[i]
        links.arrive(out.at[dp ^ one], base + 1, mate)
        links.arrive(out.at[dp ^ 3], base + 2, mate)

    stage = [None] * 6
    slot_x, slot_xl = links.slots(4), links.slots(3)
    slot_q, slot_ql = links.slots(1), links.slots(4)
    slot_v, slot_vl, slot_vd = links.slots(1), links.slots(3), links.slots(5)
    order = (row ^ 3, row ^ 1, row ^ 2, row)
    per_row = rows_dev // TILE
    own_block = 2 * row + mine
    own_part = all_q.at[side, pl.ds(2 * col, 2)]
    at_home = home == col
    sums = {}

    def split_ids(step, carry):
        span = pl.ds(pl.multiple_of(step * TILE, TILE), TILE)
        ids_col[span] = jnp.broadcast_to(ids[:, span], (8, TILE)).T[:, :1]
        return carry

    def split_grad(j, carry):
        grad = grad_ctx[j]
        grad_t = grad.astype(f32).T
        for h in range(heads):
            part = slice(h * HEAD, (h + 1) * HEAD)
            both[h, j, :TILE] = q[h, j]
            both[h, j, TILE:] = jnp.concatenate(
                [jnp.zeros((TILE, HEAD), low), grad[:, part]], axis=1
            )
            delta[h, j] = jnp.sum(grad_t[part] * mixed[j, h], axis=0, keepdims=True)
        return carry

    def ready():
        reads[0].wait()
        w_t[...] = w_heads[...].reshape(2 * feat, 3 * wide).astype(f32).T.astype(low)
        lax.fori_loop(0, row_tiles, split_ids, 0)
        dkv[...] = jnp.zeros_like(dkv)

    def take_context():
        for n, peer in enumerate(peers):
            links.arrive(grad_ctx.at[peer], swap + n, mate)
        for copy in reads[1:6] + reads[11:]:
            copy.wait()
        lax.fori_loop(0, blocks, split_grad, 0)

    def attend_back(j):
        block = 2 * j + lax.rem(j + col, 2)
        rows = pl.ds(pl.multiple_of(block * TILE, TILE), TILE)
        query_ids = ids[:, rows]
        far = 2 * j * TILE
        spans = ([(0, far)] if far else []) + [(far, min(2 * j + NEAR, row_tiles) * TILE)]

        def one_head(h, carry, j=j, query_ids=query_ids, far=far, spans=spans):
            total = jnp.zeros((HEAD, TILE), f32)
            for start, stop in spans:
                raw = nt(kv[h, start:stop], both[h, j])
                probs = jnp.exp(raw[:, :TILE] - lse[j, h])
                if start == far:
                    probs = jnp.where(ids_col[start:stop] <= query_ids, probs, 0.0)
                grad_scores = (probs * (raw[:, TILE:] - delta[h, j])).astype(low)
                dkv[h, start:stop] += nn(
                    jnp.concatenate([grad_scores, probs.astype(low)], axis=1), both[h, j]
                )
                total = total + nn(kt[h, :, start:stop], grad_scores)
            dq[j, h] = total * HEAD**-0.5
            return carry

        lax.fori_loop(0, heads, one_head, 0)

    def gather_q(j, carry):
        block = 2 * j + lax.rem(j + col, 2)
        rows = pl.ds(pl.multiple_of(block * TILE, TILE), TILE)
        other = pl.ds(pl.multiple_of((4 * j + 1 - block) * TILE, TILE), TILE)
        value = jnp.concatenate([dq[j, h] for h in range(heads)], axis=0)
        grads_t[2 * wide :, rows] = value.astype(low)
        grads_t[2 * wide :, other] = jnp.zeros((wide, TILE), low)
        grads[rows, 2 * wide :] = value.T.astype(low)
        grads[other, 2 * wide :] = jnp.zeros((TILE, wide), low)
        return carry + jnp.sum(value.T, axis=0, keepdims=True)

    def gather_kv(step, carry):
        rows = pl.ds(pl.multiple_of(step * TILE, TILE), TILE)
        value = jnp.concatenate([dkv[h, rows] for h in range(heads)], axis=1)
        grads[rows, : 2 * wide] = value.astype(low)
        grads_t[: 2 * wide, rows] = value.T.astype(low)
        return carry + jnp.sum(value, axis=0, keepdims=True)

    def weight_grads():
        reads[6].wait()
        reads[9].wait()
        reads[10].wait()
        sums["q"] = lax.fori_loop(0, blocks, gather_q, jnp.zeros((1, wide), f32))
        sums["kv"] = lax.fori_loop(0, row_tiles, gather_kv, jnp.zeros((1, 2 * wide), f32))
        for n in range(2):
            span = slice(n * CHUNK, (n + 1) * CHUNK)
            value = nn(grads_t[...], x_all[:, :, span].reshape(length, CHUNK)).T
            gq[2 * n : 2 * n + 2] = value.astype(low).reshape((2,) + gq.shape[1:])
        links.push(gq.at[:, 1 - col], sum_q, slot_q, mate)

    def token_grads(at):
        def one(step, carry):
            here = pl.ds(pl.multiple_of(step * TILE, TILE), TILE)
            rows = pl.ds(pl.multiple_of((at * per_row + step) * TILE, TILE), TILE)
            value = nn(grads[rows], w_t[...])
            is_own = (at * per_row + step == own_block).astype(f32)
            dx[at, here] = (value + late[...] * is_own).astype(low)
            return carry

        lax.fori_loop(0, per_row, one, 0)

    def send_tokens(n):
        token_grads(order[n])
        links.push(
            dx.at[order[n], :, columns(1 - col, feat)], sum_x.at[order[n]], slot_x + n, mate
        )

    def join_x(at, slot):
        links.arrive(sum_x.at[at], slot, mate)

        def one(step, carry):
            here = pl.ds(pl.multiple_of(step * 128, 128), 128)
            sum_x[at, here] = (
                sum_x[at, here].astype(f32) + dx[at, here, columns(col, feat)].astype(f32)
            ).astype(low)
            return carry

        lax.fori_loop(0, rows_dev // 128, one, 0)

    def line_tokens(n):
        join_x(order[n], slot_x + n)
        if n < 2:
            links.push(sum_x.at[order[n]], line_x.at[1 - n], slot_xl + 1 - n, at_row(row ^ 1))

    def halve_x(step, carry):
        rows = pl.ds(pl.multiple_of(step * 128, 128), 128)
        sum_x[row ^ 2, rows] = (
            sum_x[row ^ 2, rows].astype(f32) + line_x[1, rows].astype(f32)
        ).astype(low)
        return carry

    def halve_tokens():
        links.arrive(line_x.at[1], slot_xl + 1, mate)
        lax.fori_loop(0, rows_dev // 128, halve_x, 0)
        links.push(sum_x.at[row ^ 2], line_x.at[2], slot_xl + 2, at_row(row ^ 2))

    def finish_x(step, carry):
        rows = pl.ds(pl.multiple_of(step * 128, 128), 128)
        value = sum_x[row, rows].astype(f32)
        for n in (0, 2):
            value = value + line_x[n, rows].astype(f32)
        out_x[rows] = value.astype(low)
        return carry

    def finish_tokens():
        for n in (0, 2):
            links.arrive(line_x.at[n], slot_xl + n, mate)
        lax.fori_loop(0, rows_dev // 128, finish_x, 0)

    def add_q(step, carry):
        sum_q[step] = (sum_q[step].astype(f32) + gq[step, col].astype(f32)).astype(low)
        return carry

    def keep_own():
        own_part[...] = sum_q[row]

    def line_q():
        links.arrive(sum_q, slot_q, mate)
        lax.fori_loop(0, ROWS, add_q, 0)
        pl.when(at_home)(keep_own)
        slot = slot_ql + 2 * side + col
        links.push(sum_q.at[row], own_part, slot, mate, jnp.logical_not(at_home))
        for peer in peers:
            links.push(sum_q.at[peer], own_part, slot, (dp, peer, home))

    def first_q():
        for j in range(2):
            for e in range(2):
                here = (row == 2 * col + j) & (col == e)
                links.arrive(
                    all_q.at[j, pl.ds(2 * e, 2)], slot_ql + 2 * j + e, mate, jnp.logical_not(here)
                )
        stage[5] = send_first(5)

    def finish_q():
        links.arrive(first[5].at[0], stage[5][0], mate)
        links.arrive(second[5], stage[5][1], mate)
        add_into(all_q.at[:, dp], first[5].at[0], second[5])
        for j in range(2):
            out_q[dp, j] = all_q[j, dp]
        stage[5] = share(5, out_q)

    def finish_line(i):
        for n in (0, 2):
            links.arrive(lines[i].at[n], stage[i] + n, mate)
        value = pairs[i][1, row, dp].astype(f32)
        for n in (0, 2):
            value = value + lines[i][n].astype(f32)
        out_g[i][dp] = value.astype(low)
        stage[i] = share(i, out_g[i])

    def sums_mate():
        value = jnp.concatenate(
            [sums["kv"], sums["q"], jnp.zeros((1, 2 * feat - 3 * wide), f32)], axis=1
        )
        here = lax.broadcasted_iota(jnp.int32, (8, 2 * feat), 0) == 5 + side
        for c in range(2):
            part = vec_in[8 + 8 * c : 16 + 8 * c] + jnp.where(here & (home == c), value, 0.0)
            vec_own[jnp.where(col == c, 0, 1), :8] = part
        vec_own[0, 8:] = vec_in[24:]
        vec_own[1, 8:] = vec_in[24:]
        links.push(vec_own.at[1], vec_mate, slot_v, mate)

    def sums_line():
        links.arrive(vec_mate, slot_v, mate)
        vec_mate[...] = vec_own[0] + vec_mate[...]
        for n, peer in enumerate(peers):
            links.push(vec_mate, vec_line.at[2 - n], slot_vl + 2 - n, at_row(peer))

    def sums_first():
        for n in range(3):
            links.arrive(vec_line.at[n], slot_vl + n, mate)
        vec_sum = vec_mate[...] + vec_line[0] + vec_line[1] + vec_line[2]
        vec_flat[2] = vec_sum[:8]
        vec_table[dp] = vec_sum[8:]
        links.push(vec_flat.at[2], vec_flat.at[0], slot_vd, at_dp(1))
        links.push(vec_table.at[dp], vec_table.at[dp], slot_vd + 1, at_dp(1))
        links.push(vec_table.at[dp], vec_table.at[dp], slot_vd + 2, at_dp(2))

    def sums_second():
        links.arrive(vec_flat.at[0], slot_vd, mate)
        vec_flat[3] = vec_flat[2] + vec_flat[0]
        links.push(vec_flat.at[3], vec_flat.at[1], slot_vd + 3, at_dp(2))
        links.arrive(vec_table.at[dp ^ 1], slot_vd + 1, mate)
        links.push(vec_table.at[dp ^ 1], vec_table.at[dp ^ 1], slot_vd + 4, at_dp(2))

    def sums_last():
        links.arrive(vec_flat.at[1], slot_vd + 3, mate)
        links.arrive(vec_table.at[dp ^ 2], slot_vd + 2, mate)
        links.arrive(vec_table.at[dp ^ 3], slot_vd + 4, mate)
        vec[:8] = vec_flat[3] + vec_flat[1]
        for n in range(4):
            vec[8 + 8 * n : 16 + 8 * n] = vec_table[n]

    def out_of(i):
        return out_q if i == 5 else out_g[i]

    work = {
        "g": local_grad, "c": join, "s": send_second, "l": send_line, "h": halve_line,
        "f": finish_line, "n": lambda i: share_on(i, out_of(i), stage[i]),
        "r": lambda _: ready(), "d": lambda _: take_context(), "a": attend_back,
        "w": lambda _: weight_grads(), "t": send_tokens, "x": line_tokens,
        "k": lambda n: (halve_tokens, finish_tokens)[n](),
        "q": lambda n: (line_q, first_q, finish_q)[n](),
        "v": lambda n: (sums_mate, sums_line, sums_first, sums_second, sums_last)[n](),
    }
    for entry in PLAN:
        work[entry[0]](int(entry[1]))
    for i in range(6):
        shared(i, out_of(i), stage[i])
    links.arrive(halves.at[other_rows], slot_o, mate)
    links.drain()


def backward_links(
    grad_blocks, output, late, stream, grad_pre, branch_two, activ, branch_one, context,
    q, kv, kt, mixed, lse, ids, x_all, w_heads, vec,
):
    low, f32 = q.dtype, jnp.float32
    heads, length = kv.shape[0], kv.shape[1]
    wide = heads * HEAD
    own, features = output.shape
    hidden = activ.shape[1]
    part = features // ROWS // 4
    widths = [hidden // 4] * 4 + [features // 2]
    rows, feat = 2 * own, features // 2
    blocks = length // TILE // 2
    shape = jax.ShapeDtypeStruct
    outs = [shape((4, part, width), low) for width in widths] + [
        shape((4, 2, part, 3 * wide), low),
        shape((rows, feat), low),
        shape((rows, feat), low),
        shape((40, features), f32),
    ]
    every = [(ROWS, width) for width in widths] + [(2, 3 * wide)]
    return pl.pallas_call(
        functools.partial(backward_kernel, heads),
        out_shape=outs,
        in_specs=[IN_PLACE] * 3 + [IN_VMEM, IN_PLACE] * 2 + [IN_VMEM] * 2 + [IN_PLACE] * 5
        + [IN_VMEM] + [IN_PLACE] * 2 + [IN_VMEM],
        out_specs=[IN_VMEM] * len(outs),
        scratch_shapes=[pltpu.VMEM((2, ROWS, 4, part, width), low) for width in widths]
        + [pltpu.VMEM((ROWS, 4, part, width), low) for width in widths]
        + [pltpu.VMEM((2, lead, part, width), low) for lead, width in every]
        + [pltpu.VMEM((lead, part, width), low) for lead, width in every]
        + [pltpu.VMEM((3, part, width), low) for width in widths]
        + [
            pltpu.VMEM((ROWS, own, wide), low),
            pltpu.VMEM((heads, blocks, 2 * TILE, 2 * HEAD), low),
            pltpu.VMEM((heads, blocks, 1, TILE), f32),
            pltpu.VMEM((blocks, heads, HEAD, TILE), f32),
            pltpu.VMEM((heads, length, 2 * HEAD), f32),
            pltpu.VMEM((length, 3 * wide), low),
            pltpu.VMEM((3 * wide, length), low),
            pltpu.VMEM((3 * wide, features), low),
            pltpu.VMEM((3, features, own), low),
            pltpu.VMEM((length, 1), jnp.int32),
            pltpu.VMEM((ROWS, rows, features), low),
            pltpu.VMEM((ROWS, rows, feat), low),
            pltpu.VMEM((3, rows, feat), low),
            pltpu.VMEM((ROWS, 2, 2, part, 3 * wide), low),
            pltpu.VMEM((ROWS, 2, part, 3 * wide), low),
            pltpu.VMEM((2, 4, part, 3 * wide), low),
            pltpu.VMEM((2, 16, features), f32),
            pltpu.VMEM((16, features), f32),
            pltpu.VMEM((3, 16, features), f32),
            pltpu.VMEM((4, 8, features), f32),
            pltpu.VMEM((4, 8, features), f32),
        ]
        + [pltpu.VMEM(far.shape, far.dtype)
            for far in (w_heads, q, kv, kt, mixed, lse, x_all, grad_pre, activ, late)]
        + [
            pltpu.SemaphoreType.DMA((128,)),
            pltpu.SemaphoreType.DMA((128,)),
            pltpu.SemaphoreType.DMA((12,)),
        ],
        compiler_params=comm_params(2),
        name="backward_links",
    )(
        grad_blocks, output, late, stream, grad_pre, branch_two, activ, branch_one, context,
        q, kv, kt, mixed, lse, ids.reshape(1, -1), x_all, w_heads, vec,
    )


def put_lanes(target, value):
    for n in range(target.shape[0]):
        target[n : n + 1] = value[:, n * 128 : (n + 1) * 128]


def finish_kernel(
    heads, g1a, g1b, g2a, g2b, go, gq, x_in, out_in, vec,
    out, logits, grad_x, o_q, o_bq, o_k, o_v, o_bv, o_o, o_bo, o_g1, o_s1, far_1, o_b1, far_2, o_b2,
    o_g2, o_s2, far_p, o_bp, o_c, o_bc, o_1, o_2, o_p, sems,
):
    dp = lax.axis_index("dp")
    f32 = jnp.float32
    wide = heads * HEAD
    classes = logits.shape[1]
    depth, feat = o_q.shape
    part = g1a.shape[2]
    write_out = [
        pltpu.make_async_copy(near, far, sems.at[n])
        for n, (near, far) in enumerate(((o_p, far_p), (o_1, far_1), (o_2, far_2)))
    ]
    table = vec[8:40]
    table_t = table.T
    pooler = jnp.zeros(o_p.shape, f32)
    head = [jnp.zeros((1, 2 * feat), f32) for _ in range(classes)]
    total = jnp.zeros((1, 2 * feat), f32)
    ends = jnp.zeros((1, 128), f32)
    own_tail = jnp.zeros((1, 128), f32)
    for s in range(4):
        at = 8 * s
        slope, tail = table[at + 1 : at + 2], table[at + 3 : at + 4, :128]
        pooler = pooler + table_t[:, at : at + 1] * slope
        total = total + slope
        for n in range(classes):
            head[n] = head[n] + table[at + 2 : at + 3] * tail[:, classes + n : classes + n + 1]
        ends = ends + tail
        own_tail = jnp.where(dp == s, tail, own_tail)
    o_p[...] = pooler
    write_out[0].start()
    flat = lambda ref: ref[...].astype(f32).reshape(depth, ref.shape[2])
    for target, first, second in ((o_1, g1a, g1b), (o_2, g2a, g2b)):
        target[:, :part] = flat(first)
        target[:, part:] = flat(second)
        write_out[1 if target is o_1 else 2].start()
    out[...] = out_in[...]
    grad_x[...] = x_in[...]
    o_o[...] = flat(go)
    bias_q, bias_v = [], []
    for j in range(2):
        value = gq[:, j].astype(f32).reshape(depth, 3 * wide)
        o_q[:, j * wide : (j + 1) * wide] = value[:, 2 * wide :]
        for target, shift in ((o_k, 0), (o_v, HEAD)):
            target[:, j * wide : (j + 1) * wide] = jnp.concatenate(
                [value[:, 2 * h * HEAD + shift :][:, :HEAD] for h in range(heads)], axis=1
            )
        bias = vec[5 + j : 6 + j]
        bias_q.append(bias[:, 2 * wide : 3 * wide])
        bias_v += [bias[:, 2 * h * HEAD + HEAD :][:, :HEAD] for h in range(heads)]
    put_lanes(o_bq, jnp.concatenate(bias_q, axis=1))
    put_lanes(o_bv, jnp.concatenate(bias_v, axis=1))
    own = vec[:8]
    for n, target in enumerate((o_bo, o_g1, o_s1, o_b2, o_g2, o_s2)):
        put_lanes(target, own[n // 2 : n // 2 + 1, (n % 2) * feat : (n % 2 + 1) * feat])
    put_lanes(o_b1, jnp.concatenate([own[3:4], own[4:5]], axis=1))
    put_lanes(o_bp, total)
    o_c[...] = jnp.concatenate(head, axis=0)
    o_bc[...] = ends[:, classes : 2 * classes]
    logits[...] = own_tail[:, :classes]
    for copy in write_out:
        copy.wait()


def finish(pieces, classes, heads):
    g1a, g1b, g2a, g2b, go, gq, x_in, out_in, vec = pieces
    f32 = jnp.float32
    depth = go.shape[0] * go.shape[1]
    feat, hidden = go.shape[2], 2 * g1a.shape[2]
    features = vec.shape[1]
    shape = jax.ShapeDtypeStruct
    vector = lambda size: shape((size // 128, 128) if size % 128 == 0 else (1, size), f32)
    square = shape((depth, feat), f32)
    outs = [
        shape(out_in.shape, out_in.dtype), vector(classes), shape(x_in.shape, x_in.dtype),
        square, vector(feat), square, square, vector(feat), square, vector(feat), vector(feat),
        vector(feat), shape((depth, hidden), f32), vector(hidden), shape((depth, hidden), f32),
        vector(feat), vector(feat), vector(feat), shape((features, features), f32),
        vector(features), shape((classes, features), f32), vector(classes),
    ]
    return pl.pallas_call(
        functools.partial(finish_kernel, heads),
        out_shape=outs,
        in_specs=[IN_VMEM] * len(pieces),
        out_specs=[IN_PLACE if n in (12, 14, 18) else IN_VMEM for n in range(len(outs))],
        scratch_shapes=[pltpu.VMEM(outs[n].shape, f32) for n in (12, 14, 18)]
        + [pltpu.SemaphoreType.DMA((3,))],
        compiler_params=pltpu.CompilerParams(vmem_limit_bytes=VMEM_BYTES),
        name="finish",
    )(*pieces)


def norm_rows(hidden, gain, shift):
    row_mean = jnp.mean(hidden, axis=1, keepdims=True)
    row_var = jnp.mean(hidden * hidden, axis=1, keepdims=True) - row_mean * row_mean
    inv_scale = lax.rsqrt(row_var + epsilon)
    normed = (hidden - row_mean) * inv_scale
    return normed * gain + shift, normed, inv_scale


def norm_rows_back(grad, normed, inv_scale, gain):
    scaled = grad * gain
    first = jnp.mean(scaled, axis=1, keepdims=True)
    second = jnp.mean(scaled * normed, axis=1, keepdims=True)
    return inv_scale * (scaled - first - normed * second)


def fast_body(
    layer_input, cotangent, labels, block_ids, w_query, b_query, w_key, w_value, b_value,
    w_output, b_output, ln1_gain, ln1_bias, w_inner, b_inner, w_outer, b_outer,
    ln2_gain, ln2_bias, w_pooler, b_pooler, w_classes, b_classes,
):
    f32 = jnp.float32
    feat = layer_input.shape[1]
    heads = 2 * feat // HEAD // ROWS
    vectors = [
        b_query, b_value, b_output, ln1_gain, ln1_bias, b_outer, ln2_gain, ln2_bias, b_inner,
        b_pooler,
    ]
    count = sum(vector.shape[0] for vector in vectors) // feat
    padded, at = 0.0, 0
    full = (count + -count % 8) * feat
    for vector in vectors:
        size = vector.shape[0]
        padded = padded + jnp.pad(vector.astype(f32), (at, full - at - size))
        at += size
    (
        x_all, w_heads, q, kv, kt, mixed, lse, output, late, stream, grad_pre, branch_two, activ,
        branch_one, context, grad_blocks, packed,
    ) = forward_links(
        layer_input, cotangent, padded.reshape(-1, feat), w_query, w_key, w_value, block_ids, labels, w_classes,
        b_classes, w_pooler, [w_output.T, w_inner, w_outer.T],
    )
    s_1a, s_2a, s_1b, s_2b, s_wo, s_q, grad_input, output, sums = backward_links(
        grad_blocks, output, late, stream, grad_pre, branch_two, activ, branch_one, context,
        q, kv, kt, mixed, lse, block_ids, x_all, w_heads, packed,
    )
    outs = finish((s_1a, s_1b, s_2a, s_2b, s_wo, s_q, grad_input, output, sums), w_classes.shape[1], heads)
    flat = (4, 7, 9, 10, 11, 13, 15, 16, 17, 19, 21)
    turned = (8, 14, 20)
    return tuple(
        out.reshape(-1) if n in flat else out.T if n in turned else out
        for n, out in enumerate(outs)
    )


def is_fast(mesh):
    sizes = mesh.shape
    return sizes["dp"] == 4 and sizes["row"] == ROWS and sizes["col"] == 2


def solution(mesh):
    placed = (
        P(("dp", "row"), "col"),
        P(("dp", "row"), "col"),
        P("dp"),
        P("dp"),
        P("row", "col"),
        P("col"),
        P("row", "col"),
        P("row", "col"),
        P("col"),
        P("col", "row"),
        P("col"),
        P("col"),
        P("col"),
        P("row", "col"),
        P("col"),
        P("col", "row"),
        P("col"),
        P("col"),
        P("col"),
        P(),
        P(),
        P(),
        P(),
    )
    return jax.shard_map(
        fast_body if is_fast(mesh) else body,
        mesh=mesh,
        in_specs=placed,
        out_specs=(
            P(("dp", "row"), "col"),
            P("dp", None),
            P(("dp", "row"), "col"),
            P("row", "col"),
            P("col"),
            P("row", "col"),
            P("row", "col"),
            P("col"),
            P("col", "row"),
            P("col"),
            P("col"),
            P("col"),
            P("row", "col"),
            P("col"),
            P("col", "row"),
            P("col"),
            P("col"),
            P("col"),
            P(),
            P(),
            P(),
            P(),
        ),
        check_vma=False,
    )
```

```python
import functools

import jax
import jax.numpy as jnp
from jax import lax
from jax.experimental import pallas as pl
from jax.experimental.pallas import tpu as pltpu
from jax.sharding import PartitionSpec as P

HEAD = 64


highest = lax.Precision.HIGHEST
epsilon = 1e-05
root_half = 0.7071067811865476
inv_root_tau = 0.3989422804014327
masked_score = -1e30


def gelu_exact(values):
    return values * 0.5 * (1.0 + lax.erf(values * root_half))


def gelu_slope(values):
    return 0.5 * (1.0 + lax.erf(values * root_half)) + values * inv_root_tau * jnp.exp(
        -0.5 * values * values
    )


def project(left, right):
    return jnp.dot(left, right, preferred_element_type=jnp.float32)


def contract_first(left, right):
    return lax.dot_general(
        left, right, (((0,), (0,)), ((), ())), preferred_element_type=jnp.float32
    )


def contract_last(left, right):
    return lax.dot_general(
        left, right, (((1,), (1,)), ((), ())), preferred_element_type=jnp.float32
    )


def gather_features(values):
    return lax.all_gather(values, "col", axis=1, tiled=True)


def sum_features(values):
    return lax.psum_scatter(
        values.astype(jnp.bfloat16), "col", scatter_dimension=1, tiled=True
    ).astype(jnp.float32)


def feature_totals(first_part, second_part):
    return lax.psum((jnp.sum(first_part, axis=1), jnp.sum(second_part, axis=1)), "col")


def norm_forward(hidden, gain, shift, features):
    row_total, square_total = feature_totals(hidden, hidden * hidden)
    row_mean = row_total / features
    row_var = square_total / features - row_mean * row_mean
    inv_scale = lax.rsqrt(row_var + epsilon)
    normed = (hidden - row_mean[:, None]) * inv_scale[:, None]
    return (normed * gain + shift, normed, inv_scale)


def norm_backward(grad, normed, inv_scale, gain, features):
    scaled = grad * gain
    first_total, second_total = feature_totals(scaled, scaled * normed)
    return inv_scale[:, None] * (
        scaled - (first_total / features)[:, None] - normed * (second_total / features)[:, None]
    )


def key_split(piece_rows, rows_dev):
    return (piece_rows // rows_dev, rows_dev)


def body(
    layer_input,
    cotangent,
    labels,
    block_ids,
    w_query,
    b_query,
    w_key,
    w_value,
    b_value,
    w_output,
    b_output,
    ln1_gain,
    ln1_bias,
    w_inner,
    b_inner,
    w_outer,
    b_outer,
    ln2_gain,
    ln2_bias,
    w_pooler,
    b_pooler,
    w_classes,
    b_classes,
):
    f32 = jnp.float32
    bf16 = jnp.bfloat16
    rows_dev, feat_col = layer_input.shape
    heads_col = feat_col // HEAD
    features = feat_col * lax.axis_size("col")
    row_index = lax.axis_index("row")
    col_index = lax.axis_index("col")
    seq_index = lax.axis_index("dp")
    seq_count = lax.axis_size("dp")
    score_scale = HEAD ** (-0.5)
    query_ids = lax.dynamic_slice_in_dim(block_ids, row_index * rows_dev, rows_dev)
    last_query = query_ids[rows_dev - 1]
    wq_full, wk_full, wv_full, w1_full = (
        lax.all_gather(w_query, "row", axis=0, tiled=True),
        lax.all_gather(w_key, "row", axis=0, tiled=True),
        lax.all_gather(w_value, "row", axis=0, tiled=True),
        lax.all_gather(w_inner, "row", axis=0, tiled=True),
    )
    wo_full, w2_full = (
        lax.all_gather(w_output, "row", axis=1, tiled=True),
        lax.all_gather(w_outer, "row", axis=1, tiled=True),
    )
    input_whole = gather_features(layer_input)
    queries = (project(input_whole, wq_full) + b_query.astype(f32)).astype(bf16)
    keys_local = project(input_whole, wk_full).astype(bf16)
    values_local = (project(input_whole, wv_full) + b_value.astype(f32)).astype(bf16)
    queries3 = queries.reshape(rows_dev, heads_col, HEAD)
    start_state = (
        jnp.full((heads_col, rows_dev), masked_score, f32),
        jnp.zeros((heads_col, rows_dev), f32),
        jnp.zeros((heads_col, rows_dev, HEAD), f32),
    )
    running = start_state
    keys_piece = lax.all_gather(keys_local, "row", axis=0, tiled=True)
    values_piece = lax.all_gather(values_local, "row", axis=0, tiled=True)
    piece_rows = keys_piece.shape[0]
    number, block_rows = key_split(piece_rows, rows_dev)
    keys4 = keys_piece.reshape(number, block_rows, heads_col, HEAD)
    values4 = values_piece.reshape(number, block_rows, heads_col, HEAD)
    piece_ids = block_ids.reshape(number, block_rows)

    def attend_block_work(state, block_item):
        peak_score, row_mass, accum = state
        keys3, values3, key_ids = block_item
        scores = (
            jnp.einsum("qhd,khd->hqk", queries3, keys3, preferred_element_type=f32) * score_scale
        )
        allowed = (key_ids[None, :] <= query_ids[:, None])[None]
        block_top = jnp.max(jnp.where(allowed, scores, masked_score), axis=2)
        new_peak = jnp.maximum(peak_score, block_top)
        weights = jnp.where(allowed, jnp.exp(scores - new_peak[:, :, None]), 0.0)
        factor = jnp.exp(peak_score - new_peak)
        row_mass = row_mass * factor + jnp.sum(weights, axis=2)
        accum = accum * factor[:, :, None] + jnp.einsum(
            "hqk,khd->hqd", weights.astype(bf16), values3, preferred_element_type=f32
        )
        return (new_peak, row_mass, accum)

    def attend_block_step(state, block_item):
        state = lax.cond(
            block_item[2][0] > last_query, lambda st, item: st, attend_block_work, state, block_item
        )
        return (state, None)

    running, unused = lax.scan(attend_block_step, running, (keys4, values4, piece_ids))
    peak_score, row_mass, accum = running
    mixed = accum / row_mass[:, :, None]
    log_mass = peak_score + jnp.log(row_mass)
    context_low = mixed.transpose(1, 0, 2).reshape(rows_dev, feat_col).astype(bf16)
    attn_branch = sum_features(project(context_low, wo_full))
    hidden_one = layer_input.astype(f32) + attn_branch + b_output.astype(f32)
    gain_one = ln1_gain.astype(f32)
    stream, normed_one, inv_one = norm_forward(hidden_one, gain_one, ln1_bias.astype(f32), features)
    stream_whole = gather_features(stream.astype(bf16))
    pre_act = project(stream_whole, w1_full) + b_inner.astype(f32)
    activ = gelu_exact(pre_act).astype(bf16)
    ffn_branch = sum_features(project(activ, w2_full))
    hidden_two = stream + ffn_branch + b_outer.astype(f32)
    gain_two = ln2_gain.astype(f32)
    result, normed_two, inv_two = norm_forward(hidden_two, gain_two, ln2_bias.astype(f32), features)
    output = result.astype(bf16)
    row_zero = (row_index == 0).astype(f32)
    pool_input = gather_features(output[0:1])
    pooled = jnp.tanh(project(pool_input, w_pooler) + b_pooler.astype(f32))
    classes_f32 = w_classes.astype(f32)
    logits_own = jnp.dot(pooled, classes_f32, precision=highest) + b_classes.astype(f32)
    onehot = (jnp.arange(w_classes.shape[1]) == labels[0]).astype(f32)
    grad_logits = jax.nn.softmax(logits_own, axis=-1) - onehot[None, :]
    g_w_classes = jnp.dot(pooled.T, grad_logits, precision=highest)
    g_b_classes = grad_logits[0]
    grad_pre_pool = jnp.dot(grad_logits, classes_f32.T, precision=highest) * (1.0 - pooled * pooled)
    g_b_pooler = grad_pre_pool[0]
    g_w_pooler = jnp.dot(pool_input.astype(f32).T, grad_pre_pool, precision=highest)
    grad_first = jnp.dot(grad_pre_pool, w_pooler.astype(f32).T, precision=highest)
    first_col = lax.dynamic_slice_in_dim(grad_first[0], col_index * feat_col, feat_col)
    grad_result = cotangent.astype(f32).at[0].add(first_col * row_zero)
    logits_table = lax.dynamic_update_slice_in_dim(
        jnp.zeros((seq_count, w_classes.shape[1]), f32), logits_own * row_zero, seq_index, 0
    )
    g_ln2_gain = jnp.sum(grad_result * normed_two, axis=0)
    g_ln2_bias = jnp.sum(grad_result, axis=0)
    grad_hidden_two = norm_backward(grad_result, normed_two, inv_two, gain_two, features)
    g_b_outer = jnp.sum(grad_hidden_two, axis=0)
    branch_two_whole = gather_features(grad_hidden_two.astype(bf16))
    g_w_outer_full = contract_first(activ, branch_two_whole)
    grad_act = contract_last(branch_two_whole, w2_full)
    grad_pre = (grad_act * gelu_slope(pre_act)).astype(bf16)
    g_b_inner = jnp.sum(grad_pre.astype(f32), axis=0)
    g_w_inner_full = contract_first(stream_whole, grad_pre)
    grad_stream = grad_hidden_two + sum_features(contract_last(grad_pre, w1_full))
    g_ln1_gain = jnp.sum(grad_stream * normed_one, axis=0)
    g_ln1_bias = jnp.sum(grad_stream, axis=0)
    grad_hidden_one = norm_backward(grad_stream, normed_one, inv_one, gain_one, features)
    g_b_output = jnp.sum(grad_hidden_one, axis=0)
    branch_one_whole = gather_features(grad_hidden_one.astype(bf16))
    g_w_output_full = contract_first(context_low, branch_one_whole)
    grad_context = contract_last(branch_one_whole, wo_full).astype(bf16)
    grad_ctx3 = grad_context.reshape(rows_dev, heads_col, HEAD)
    delta = jnp.sum(grad_ctx3.astype(f32).transpose(1, 0, 2) * mixed, axis=2)

    def score_grads(queries_blk, grad_ctx_blk, keys3, values3, allowed, lse_blk, delta_blk):
        scores = (
            jnp.einsum("qhd,khd->hqk", queries_blk, keys3, preferred_element_type=f32) * score_scale
        )
        probs = jnp.where(allowed, jnp.exp(scores - lse_blk[:, :, None]), 0.0)
        grad_probs = jnp.einsum("qhd,khd->hqk", grad_ctx_blk, values3, preferred_element_type=f32)
        grad_scores = (probs * (grad_probs - delta_blk[:, :, None])).astype(bf16)
        return (probs, grad_scores)

    zero_q = jnp.zeros((rows_dev, heads_col, HEAD), f32)
    keys_piece = lax.all_gather(keys_local, "row", axis=0, tiled=True)
    values_piece = lax.all_gather(values_local, "row", axis=0, tiled=True)
    piece_rows = keys_piece.shape[0]
    number, block_rows = key_split(piece_rows, rows_dev)
    keys4 = keys_piece.reshape(number, block_rows, heads_col, HEAD)
    values4 = values_piece.reshape(number, block_rows, heads_col, HEAD)
    piece_ids = block_ids.reshape(number, block_rows)

    def make_block_work(accum_q, block_item):
        keys3, values3, key_ids = block_item
        allowed = (key_ids[None, :] <= query_ids[:, None])[None]
        probs, grad_scores = score_grads(
            queries3, grad_ctx3, keys3, values3, allowed, log_mass, delta
        )
        accum_q = (
            accum_q
            + jnp.einsum("hqk,khd->qhd", grad_scores, keys3, preferred_element_type=f32)
            * score_scale
        )
        part_k = (
            jnp.einsum("hqk,qhd->khd", grad_scores, queries3, preferred_element_type=f32)
            * score_scale
        )
        part_v = jnp.einsum(
            "hqk,qhd->khd", probs.astype(bf16), grad_ctx3, preferred_element_type=f32
        )
        return (accum_q, (part_k, part_v))

    def block_skip(accum_q, block_item):
        empty = jnp.zeros((block_rows, heads_col, HEAD), f32)
        return (accum_q, (empty, empty))

    def make_block_step(accum_q, block_item):
        return lax.cond(
            block_item[2][0] > last_query, block_skip, make_block_work, accum_q, block_item
        )

    grad_q = zero_q
    grad_q, (parts_k, parts_v) = lax.scan(make_block_step, grad_q, (keys4, values4, piece_ids))
    parts_k = parts_k.reshape(piece_rows, feat_col)
    parts_v = parts_v.reshape(piece_rows, feat_col)
    grad_k_all = parts_k
    grad_v_all = parts_v
    back_result = (grad_q, grad_k_all, grad_v_all)
    grad_q3, grad_k_all, grad_v_all = back_result
    grad_keys, grad_values = (
        lax.psum_scatter(
            grad_k_all.astype(jnp.bfloat16), "row", scatter_dimension=0, tiled=True
        ).astype(jnp.float32),
        lax.psum_scatter(
            grad_v_all.astype(jnp.bfloat16), "row", scatter_dimension=0, tiled=True
        ).astype(jnp.float32),
    )
    queries_grad = grad_q3.reshape(rows_dev, feat_col).astype(bf16)
    keys_grad = grad_keys.astype(bf16)
    values_grad = grad_values.astype(bf16)
    g_b_query = jnp.sum(queries_grad.astype(f32), axis=0)
    g_b_value = jnp.sum(values_grad.astype(f32), axis=0)
    g_w_query_full = contract_first(input_whole, queries_grad)
    g_w_key_full = contract_first(input_whole, keys_grad)
    g_w_value_full = contract_first(input_whole, values_grad)
    grad_input_whole = (
        contract_last(queries_grad, wq_full)
        + contract_last(keys_grad, wk_full)
        + contract_last(values_grad, wv_full)
    )
    grad_input = (grad_hidden_one + sum_features(grad_input_whole)).astype(bf16)
    in_rows = w_query.shape[0]
    out_cols = w_output.shape[1]
    (
        sum_wq,
        sum_wk,
        sum_wv,
        sum_w1,
        sum_wo,
        sum_w2,
        g_w_pooler,
        g_b_pooler,
        g_w_classes,
        g_b_classes,
        g_b_query,
        g_b_value,
        g_b_output,
        g_ln1_gain,
        g_ln1_bias,
        g_b_inner,
        g_b_outer,
        g_ln2_gain,
        g_ln2_bias,
        logits_all,
    ) = lax.psum(
        (
            g_w_query_full,
            g_w_key_full,
            g_w_value_full,
            g_w_inner_full,
            g_w_output_full,
            g_w_outer_full,
            g_w_pooler * row_zero,
            g_b_pooler * row_zero,
            g_w_classes * row_zero,
            g_b_classes * row_zero,
            g_b_query,
            g_b_value,
            g_b_output,
            g_ln1_gain,
            g_ln1_bias,
            g_b_inner,
            g_b_outer,
            g_ln2_gain,
            g_ln2_bias,
            logits_table,
        ),
        ("dp", "row"),
    )
    row_start = row_index * in_rows
    col_start = row_index * out_cols
    g_w_query = lax.dynamic_slice_in_dim(sum_wq, row_start, in_rows, 0)
    g_w_key = lax.dynamic_slice_in_dim(sum_wk, row_start, in_rows, 0)
    g_w_value = lax.dynamic_slice_in_dim(sum_wv, row_start, in_rows, 0)
    g_w_inner = lax.dynamic_slice_in_dim(sum_w1, row_start, in_rows, 0)
    g_w_output = lax.dynamic_slice_in_dim(sum_wo, col_start, out_cols, 1)
    g_w_outer = lax.dynamic_slice_in_dim(sum_w2, col_start, out_cols, 1)
    logits = lax.dynamic_slice_in_dim(logits_all, seq_index, 1, 0)
    return (
        output,
        logits,
        grad_input,
        g_w_query,
        g_b_query,
        g_w_key,
        g_w_value,
        g_b_value,
        g_w_output,
        g_b_output,
        g_ln1_gain,
        g_ln1_bias,
        g_w_inner,
        g_b_inner,
        g_w_outer,
        g_b_outer,
        g_ln2_gain,
        g_ln2_bias,
        g_w_pooler,
        g_b_pooler,
        g_w_classes,
        g_b_classes,
    )


MESH_IDS = pl.DeviceIdType.MESH
ROWS = 4
VMEM_BYTES = 64000 * 1024


def place():
    return lax.axis_index("dp"), lax.axis_index("row"), lax.axis_index("col")


class Links:
    def __init__(self, send, recv):
        self.send, self.recv = send, recv
        self.sends, self.recvs, self.open = 0, 0, []

    def slots(self, count):
        base = self.recvs
        self.recvs += count
        return base

    def push(self, source, target, slot, device, when=None):
        copy = pltpu.make_async_remote_copy(
            src_ref=source,
            dst_ref=target,
            send_sem=self.send.at[self.sends],
            recv_sem=self.recv.at[slot],
            device_id=device,
            device_id_type=MESH_IDS,
        )
        self.sends += 1
        if when is None:
            copy.start()
        else:
            pl.when(when)(lambda: copy.start())
        self.open.append((copy, when))

    def arrive(self, target, slot, device, when=None):
        copy = pltpu.make_async_remote_copy(
            src_ref=target,
            dst_ref=target,
            send_sem=self.send.at[0],
            recv_sem=self.recv.at[slot],
            device_id=device,
            device_id_type=MESH_IDS,
        )
        if when is None:
            copy.wait_recv()
        else:
            pl.when(when)(lambda: copy.wait_recv())

    def drain(self):
        for copy, when in self.open:
            if when is None:
                copy.wait_send()
            else:
                pl.when(when)(lambda copy=copy: copy.wait_send())
        self.open = []


def meet(devices):
    barrier = pltpu.get_barrier_semaphore()
    for device in devices:
        pl.semaphore_signal(barrier, inc=1, device_id=device, device_id_type=MESH_IDS)
    pl.semaphore_wait(barrier, len(devices))


def within(value):
    return (value >= 0) & (value < ROWS)


def steps_of_line(row):
    for step in (1, 2, 3):
        for way in (1, -1):
            source = row - way * step
            yield step, way, (3 - step if way == 1 else step - 1), source, within(source)


def columns(col, width):
    return pl.ds(pl.multiple_of(col * width, 128), width)


IN_VMEM = pl.BlockSpec(memory_space=pltpu.VMEM)
IN_PLACE = pl.BlockSpec(memory_space=pl.ANY)


def comm_params(number):
    return pltpu.CompilerParams(
        collective_id=number, has_side_effects=True, vmem_limit_bytes=VMEM_BYTES
    )


TILE = 256
NEAR = 3


def nt(left, right):
    return lax.dot_general(
        left, right, (((1,), (1,)), ((), ())), preferred_element_type=jnp.float32
    )


def nn(left, right):
    return jnp.dot(left, right, preferred_element_type=jnp.float32)


def forward_kernel(
    widths, heads, x, cot, vec, wq, wk, wv, ids, labels, w_classes, b_classes, pooler_far, *refs
):
    count = len(widths)
    shards, refs = refs[:count], refs[count:]
    far_outs = refs[:7] + refs[12:13] + refs[10:11]
    (
        output, late, stream_out, _, branch_two_out, _, branch_one_out, context,
        grad_blocks, packed,
    ) = refs[7:17]
    fulls, refs = refs[17 : 17 + count], refs[17 + count :]
    (
        x_all, w_heads, q_out, kv_out, kt_out, mixed_out, lse_out, activ_out, grad_pre_out,
        cot_own, vec_all, context_in, vt_out, ids_col, packs, low_out, slope, total, w_pooler, send, recv, local,
    ) = refs
    near_outs = (x_all, w_heads, q_out, kv_out, kt_out, mixed_out, lse_out, activ_out, grad_pre_out)
    write_out = [
        pltpu.make_async_copy(near, far, local.at[count + 11 + n])
        for n, (near, far) in enumerate(zip(near_outs, far_outs))
    ]
    dp, row, col = place()
    links = Links(send, recv)
    low = x.dtype
    rows_dev, feat = x.shape
    wide = heads * HEAD
    mate = (dp, row, 1 - col)
    at_row = lambda other: (dp, other, col)
    at_dp = lambda flip: (dp ^ flip, row, col)
    home, side = row // 2, lax.rem(row, 2)
    mine = lax.rem(row + col, 2)
    half = rows_dev // 2
    meet([at_row(lax.rem(row + k, ROWS)) for k in (1, 2, 3)] + [at_dp(1), at_dp(2), mate])

    x_at = lambda k: x_all.at[k, :, columns(col, feat)]
    x_mate_at = lambda k: x_all.at[k, :, columns(1 - col, feat)]
    w_at = lambda i, k, q: fulls[i].at[k, q, :, columns(col, widths[i])]
    row_at = lambda i, k: fulls[i].at[k, :, :, columns(col, widths[i])]
    row_mate_at = lambda i, k: fulls[i].at[k, :, :, columns(1 - col, widths[i])]

    line_x, mate_x = links.slots(3), links.slots(4)
    line_q, first_q, second_q, mate_q = (
        links.slots(3), links.slots(3), links.slots(6), links.slots(1),
    )
    mate_cot, mate_vec, swap = links.slots(1), links.slots(1), links.slots(3)
    line_w = [links.slots(3) for _ in widths]
    first_w = [links.slots(3) for _ in widths]
    second_w = [links.slots(6) for _ in widths]
    mate_w = [links.slots(4) for _ in widths]
    steps = list(steps_of_line(row))
    at_step = lambda step: [entry[2:] for entry in steps if entry[0] == step]

    def relay(step, own, full, base, group=True):
        for way in (1, -1):
            held, onward = row - way * (step - 1), row + way
            ok = within(held) & within(onward) & group
            slot = 3 - step if way == 1 else step - 1
            links.push(own if step == 1 else full(held), full(held), base + slot, at_row(onward), ok)

    relay(1, x, x_at, line_x)
    links.push(x, x_at(row), mate_x, mate)
    for j in range(2):
        pieces = []
        for h in range(heads):
            part = slice(j * wide + h * HEAD, j * wide + (h + 1) * HEAD)
            pieces += [wk[:, part], wv[:, part]]
        pieces.append(wq[:, j * wide : (j + 1) * wide])
        packs[j] = jnp.concatenate(pieces, axis=1).reshape(packs.shape[1:])
    for j in range(2):
        k = 2 * col + j
        away = k != row
        slot = lax.rem(row - k + ROWS + 3, ROWS)
        links.push(packs.at[j, dp], w_heads.at[row, dp], line_q + slot, at_row(k), away)

        @pl.when(jnp.logical_not(away))
        def _(j=j):
            w_heads[row] = packs[j]

    links.push(
        cot.at[pl.ds(pl.multiple_of((1 - mine) * half, 128), half)],
        cot_own.at[:, columns(col, feat)],
        mate_cot,
        mate,
    )
    links.push(vec, vec_all.at[col], mate_vec, mate)
    vec_all[col] = vec[...]
    read_in = [
        pltpu.make_async_copy(x, x_at(row), local.at[count + 8]),
        pltpu.make_async_copy(
            cot.at[pl.ds(pl.multiple_of(mine * half, 128), half)],
            cot_own.at[:, columns(col, feat)],
            local.at[count + 9],
        ),
        pltpu.make_async_copy(pooler_far, w_pooler, local.at[count + 10]),
    ]
    for copy in read_in:
        copy.start()
    copies = [
        pltpu.make_async_copy(shards[i], row_at(i, row), local.at[i]) for i in range(count)
    ]

    at_home = home == col

    def q_first():
        for slot in range(3):
            k = lax.rem(row + slot + 1, ROWS)
            one = 1 + slot % 2
            links.arrive(w_heads.at[k, dp], line_q + slot, mate, at_home)
            links.push(
                w_heads.at[k, dp], w_heads.at[k, dp], first_q + slot, at_dp(one), at_home
            )

    def q_second():
        for slot in range(3):
            k = lax.rem(row + slot + 1, ROWS)
            one, two = 1 + slot % 2, 2 - slot % 2
            links.arrive(w_heads.at[k, dp ^ one], first_q + slot, mate, at_home)
            for n, q in enumerate((dp, dp ^ one)):
                links.push(
                    w_heads.at[k, q], w_heads.at[k, q], second_q + 2 * slot + n, at_dp(two), at_home
                )

    def q_mate():
        for slot in range(3):
            k = lax.rem(row + slot + 1, ROWS)
            two = 2 - slot % 2
            links.arrive(w_heads.at[k, dp ^ two], second_q + 2 * slot, mate, at_home)
            links.arrive(w_heads.at[k, dp ^ 3], second_q + 2 * slot + 1, mate, at_home)
        links.push(w_heads, w_heads, mate_q, mate, at_home)
        links.arrive(w_heads, mate_q, mate, jnp.logical_not(at_home))

    def x_step(step):
        for slot, k, ok in at_step(step):
            links.arrive(x_at(k), line_x + slot, mate, ok)
        if step < 3:
            relay(step + 1, x, x_at, line_x)
        for slot, k, ok in at_step(step):
            links.push(x_at(k), x_at(k), mate_x + 1 + slot, mate, ok)

    turn = lambda i, slot: (1, 2) if (i + slot) % 2 == 0 else (2, 1)

    def w_start(at_left, at_right):
        for way, ok in ((1, row == at_right), (-1, row == at_left)):
            slot = 2 if way == 1 else 0
            for i in range(count):
                links.push(
                    shards[i].at[dp], w_at(i, row, dp), line_w[i] + slot, at_row(row + way), ok
                )

    inner = (row == 1) | (row == 2)
    groups = {"i": inner, "o": jnp.logical_not(inner)}

    def w_first(step, group):
        for i in range(count):
            for slot, k, ok in at_step(step):
                links.arrive(w_at(i, k, dp), line_w[i] + slot, mate, ok & group)
            if step < 3:
                relay(step + 1, None, lambda k, i=i: w_at(i, k, dp), line_w[i], group)
            for slot, k, ok in at_step(step):
                one, two = turn(i, slot)
                links.push(
                    w_at(i, k, dp), w_at(i, k, dp), first_w[i] + slot, at_dp(one), ok & group
                )

    def w_second(step, group):
        for i in range(count):
            for slot, k, ok in at_step(step):
                one, two = turn(i, slot)
                links.arrive(w_at(i, k, dp ^ one), first_w[i] + slot, mate, ok & group)
                for n, q in enumerate((dp, dp ^ one)):
                    links.push(
                        w_at(i, k, q), w_at(i, k, q), second_w[i] + 2 * slot + n, at_dp(two),
                        ok & group,
                    )

    def w_mate(step, group, items):
        for i in items:
            for slot, k, ok in at_step(step):
                one, two = turn(i, slot)
                links.arrive(
                    w_at(i, k, dp ^ two), second_w[i] + 2 * slot, mate, ok & group
                )
                links.arrive(
                    w_at(i, k, dp ^ 3), second_w[i] + 2 * slot + 1, mate, ok & group
                )
                links.push(row_at(i, k), row_at(i, k), mate_w[i] + 1 + slot, mate, ok & group)

    def advance(point):
        for entry in FLOW[point]:
            step, group = int(entry[1]), groups[entry[2]]
            if entry[0] == "f":
                w_first(step, group)
            elif entry[0] == "s":
                w_second(step, group)
            else:
                w_mate(step, group, range(count))

    def w_ready(i):
        for entry in FLOW["end"]:
            w_mate(int(entry[1]), groups[entry[2]], (i,))
        copies[i].wait()
        links.arrive(row_mate_at(i, row), mate_w[i], mate)
        for slot in range(3):
            k = lax.rem(row + slot + 1, ROWS)
            links.arrive(row_mate_at(i, k), mate_w[i] + 1 + slot, mate)

    row_tiles = ROWS * rows_dev // TILE
    per_row = rows_dev // TILE

    def split_ids(step, carry):
        span = pl.ds(pl.multiple_of(step * TILE, TILE), TILE)
        ids_col[span] = jnp.broadcast_to(ids[:, span], (8, TILE)).T[:, :1]
        return carry

    lax.fori_loop(0, row_tiles, split_ids, 0)
    w_start(3, 0)
    x_step(1)
    w_start(2, 1)
    q_first()
    x_step(2)
    w_start(1, 2)
    q_second()
    for copy in copies:
        copy.start()
    for i in range(count):
        links.push(shards[i], row_at(i, row), mate_w[i], mate)
    q_mate()
    links.arrive(vec_all.at[1 - col], mate_vec, mate)
    bias_of = lambda n: jnp.where(
        side == 0, vec_all[home, n : n + 1, :wide], vec_all[home, n : n + 1, wide : 2 * wide]
    )
    bias_q, bias_v = bias_of(0), bias_of(1)
    blank = jnp.zeros((1, HEAD), jnp.float32)
    bias_kv = jnp.concatenate(
        sum([[blank, bias_v[:, h * HEAD : (h + 1) * HEAD]] for h in range(heads)], []), axis=1
    )
    weights = lambda start, stop: w_heads[:, :, :, start:stop].reshape(2 * feat, stop - start)

    def project_keys(k):
        def one_tile(step, carry):
            here = pl.ds(pl.multiple_of(step * TILE, TILE), TILE)
            rows = pl.ds(pl.multiple_of(k * rows_dev + step * TILE, TILE), TILE)
            both = nn(x_all[k, here], weights(0, 2 * wide)) + bias_kv
            both_t = both.T
            for h in range(heads):
                at = 2 * h * HEAD
                kv_out[h, rows] = both[:, at : at + 2 * HEAD].astype(low)
                kt_out[h, :, rows] = both_t[at : at + HEAD].astype(low)
                vt_out[h, :, rows] = both_t[at + HEAD : at + 2 * HEAD].astype(low)
            return carry

        lax.fori_loop(0, per_row, one_tile, 0)

    links.arrive(x_mate_at(row), mate_x, mate)
    read_in[0].wait()
    project_keys(row)
    advance("x2")
    x_step(3)
    for slot in (0, 2, 1):
        k = lax.rem(row + slot + 1, ROWS)
        links.arrive(x_mate_at(k), mate_x + 1 + slot, mate)
        project_keys(k)

    def project_query(j, carry):
        block = 2 * j + lax.rem(j + col, 2)
        here = pl.ds(pl.multiple_of(lax.rem(block, per_row) * TILE, TILE), TILE)
        query = nn(x_all[block // per_row, here], weights(2 * wide, 3 * wide)) + bias_q
        query = query.astype(low) * jnp.asarray(HEAD**-0.5, low)
        for h in range(heads):
            q_out[h, j] = jnp.concatenate(
                [query[:, h * HEAD : (h + 1) * HEAD], jnp.zeros((TILE, HEAD), low)], axis=1
            )
        return carry

    blocks = row_tiles // 2
    lax.fori_loop(0, blocks, project_query, 0)
    for copy in write_out[:5]:
        copy.start()
    advance("pq")
    for j in range(blocks):
        block = 2 * j + lax.rem(j + col, 2)
        rows = pl.ds(pl.multiple_of(block * TILE, TILE), TILE)
        query_ids = ids[:, rows]
        length = min(2 * j + NEAR, row_tiles) * TILE
        clear = 2 * j * TILE

        def one_head(h, carry, j=j, query_ids=query_ids, length=length, clear=clear):
            scores = nt(kv_out[h, :length], q_out[h, j])
            near = jnp.where(
                ids_col[clear:length] <= query_ids, scores[clear:], masked_score
            )
            top = jnp.max(near, axis=0, keepdims=True)
            if clear:
                top = jnp.maximum(top, jnp.max(scores[:clear], axis=0, keepdims=True))
                weights_far = jnp.exp(scores[:clear] - top)
            weights_near = jnp.exp(near - top)
            mass = jnp.sum(weights_near, axis=0, keepdims=True)
            value = nn(vt_out[h, :, clear:length], weights_near.astype(low))
            if clear:
                mass = mass + jnp.sum(weights_far, axis=0, keepdims=True)
                value = value + nn(vt_out[h, :, :clear], weights_far.astype(low))
            mixed_out[j, h] = value / mass
            lse_out[j, h] = top + jnp.log(mass)
            return carry

        lax.fori_loop(0, heads, one_head, 0)
        low_out[j] = (
            jnp.concatenate([mixed_out[j, h] for h in range(heads)], axis=0).T.astype(low)
        )
        away = row != j
        slot = lax.rem(row - j + ROWS + 3, ROWS)
        links.push(low_out.at[j], context_in.at[row], swap + slot, at_row(j), away)

        @pl.when(jnp.logical_not(away))
        def _(j=j):
            context_in[row] = low_out[j]

        advance("a%d" % j)

    for copy in write_out[5:7]:
        copy.start()
    f32 = jnp.float32
    own, features = output.shape
    hidden = 2 * widths[1]
    chunk = features
    w_o, w_1, w_2 = fulls
    part_of = lambda full, span: full[:, :, :, span].reshape(features, span.stop - span.start)
    vector = lambda n: jnp.concatenate([vec_all[0, n : n + 1], vec_all[1, n : n + 1]], axis=1)
    links.arrive(cot_own.at[:, columns(1 - col, feat)], mate_cot, mate)
    read_in[1].wait()
    read_in[2].wait()
    for slot in range(3):
        links.arrive(context_in.at[lax.rem(row + slot + 1, ROWS)], swap + slot, mate)
    context[...] = jnp.concatenate([context_in[r] for r in range(ROWS)], axis=1)
    w_ready(0)
    value = nt(context[...], w_o[...].reshape(features, features))
    own_rows = pl.ds(pl.multiple_of(mine * own, 128), own)
    hidden_one = x_all[row, own_rows].astype(f32) + value + vector(2)
    gain_one, gain_two = vector(3), vector(6)
    stream, normed_one, inv_one = norm_rows(hidden_one, gain_one, vector(4))
    late[...] = stream
    stream_out[...] = stream.astype(low)
    total[...] = jnp.zeros_like(total)
    bias_1 = [
        jnp.concatenate(
            [vec_all[c, 8 + 2 * n : 9 + 2 * n], vec_all[c, 9 + 2 * n : 10 + 2 * n]], axis=1
        )
        for c in range(2)
        for n in range(hidden // chunk // 2)
    ]
    w_ready(1)
    for n in range(hidden // chunk):
        span = slice(n * chunk, (n + 1) * chunk)
        pre_act = nn(stream_out[...], part_of(w_1, span)) + bias_1[n]
        half = 0.5 * (1.0 + lax.erf(pre_act * root_half))
        slope[:, span] = half + pre_act * inv_root_tau * jnp.exp(-0.5 * pre_act * pre_act)
        activ_out[:, span] = (pre_act * half).astype(low)
    write_out[7].start()
    w_ready(2)
    for n in range(hidden // chunk):
        span = slice(n * chunk, (n + 1) * chunk)
        total[...] += nt(activ_out[:, span], part_of(w_2, span))
    hidden_two = late[...] + total[...] + vector(5)
    result, normed_two, inv_two = norm_rows(hidden_two, gain_two, vector(7))
    output[...] = result.astype(low)

    classes = b_classes.shape[1]
    first = output[:8]
    pooled = jnp.tanh(nn(first, w_pooler[...])[:1] + jnp.concatenate([vec_all[0, 12:13], vec_all[0, 13:14]], axis=1))
    lane = lax.broadcasted_iota(jnp.int32, (1, 128), 1)
    logits = jnp.full((1, 128), masked_score, f32)
    rows = [w_classes[n : n + 1].astype(f32) for n in range(classes)]
    for n in range(classes):
        logit = jnp.sum(pooled * rows[n], axis=1, keepdims=True) + b_classes[:, n : n + 1].astype(f32)
        logits = jnp.where(lane == n, logit, logits)
    odds = jnp.exp(logits - jnp.max(logits, axis=1, keepdims=True))
    odds = odds / jnp.sum(odds, axis=1, keepdims=True)
    grad_logits = odds - (lane == labels[0, 0]).astype(f32)
    grad_pool = jnp.zeros((1, features), f32)
    for n in range(classes):
        grad_pool = grad_pool + grad_logits[:, n : n + 1] * rows[n]
    grad_pool = grad_pool * (1.0 - pooled * pooled)
    high = grad_pool.astype(low)
    rest = grad_pool - high.astype(f32)
    mid = rest.astype(low)
    last = (rest - mid.astype(f32)).astype(low)
    split = jnp.concatenate(
        [high.astype(f32), mid.astype(f32), last.astype(f32), jnp.zeros((5, features), f32)]
    ).astype(low)
    grad_first = jnp.sum(nt(split, w_pooler[...]), axis=0, keepdims=True)
    holder = ((row == 0) & (col == 0)).astype(f32)
    top = (lax.broadcasted_iota(jnp.int32, (own, 1), 0) == 0).astype(f32) * holder
    grad_result = cot_own[...].astype(f32) + top * grad_first

    tokens = lambda values: jnp.sum(values, axis=0, keepdims=True)
    g_gain_two, g_shift_two = tokens(grad_result * normed_two), tokens(grad_result)
    grad_two = norm_rows_back(grad_result, normed_two, inv_two, gain_two)
    g_bias_two = tokens(grad_two)
    late[...] = grad_two
    branch_two_out[...] = grad_two.astype(low)
    total[...] = jnp.zeros_like(total)
    g_bias_one = []
    for n in range(hidden // chunk):
        span = slice(n * chunk, (n + 1) * chunk)
        grad_pre = (nn(branch_two_out[...], part_of(w_2, span)) * slope[:, span]).astype(low)
        grad_pre_out[:, span] = grad_pre
        g_bias_one.append(tokens(grad_pre.astype(f32)))
        total[...] += nt(grad_pre_out[:, span], part_of(w_1, span))
    write_out[8].start()
    grad_stream = late[...] + total[...]
    g_gain_one, g_shift_one = tokens(grad_stream * normed_one), tokens(grad_stream)
    grad_one = norm_rows_back(grad_stream, normed_one, inv_one, gain_one)
    late[...] = grad_one
    branch_one_out[...] = grad_one.astype(low)
    grad_context = nn(branch_one_out[...], w_o[...].reshape(features, features)).astype(low)
    for r in range(ROWS):
        grad_blocks[r] = grad_context[:, r * wide : (r + 1) * wide]

    packed[...] = jnp.zeros_like(packed)
    vectors = [tokens(grad_one), g_gain_one, g_shift_one, g_bias_two, g_gain_two, g_shift_two]
    for n, value in enumerate(vectors):
        for c in range(2):
            packed[8 + 8 * c + n // 2, pl.ds((n % 2) * feat, feat)] = value[
                0, c * feat : (c + 1) * feat
            ]
    for n, value in enumerate(g_bias_one):
        packed[8 + 8 * (n // 2) + 3 + n % 2] = value[0]
    spare = jnp.zeros((1, features - 128), f32)
    shifted = pltpu.roll(jnp.where(lane < classes, grad_logits, 0.0), classes, 1)
    tail = jnp.concatenate([jnp.where(lane < classes, logits, shifted), spare], axis=1)
    for n, value in enumerate((first[:1].astype(f32), grad_pool, pooled, tail)):
        packed[24 + n : 25 + n] = value * holder
    for copy in write_out:
        copy.wait()
    links.drain()


def forward_links(x, cot, vec, wq, wk, wv, ids, labels, w_classes, b_classes, w_pooler, shards):
    widths = [shard.shape[1] for shard in shards]
    rows, feat = x.shape
    low, f32 = x.dtype, jnp.float32
    part = shards[0].shape[0] // 4
    features, hidden = 2 * feat, 2 * widths[1]
    heads = features // HEAD // ROWS
    wide = heads * HEAD
    length, own = ROWS * rows, rows // 2
    blocks = length // TILE // 2
    shape = jax.ShapeDtypeStruct
    narrow, broad = shape((own, features), low), shape((own, hidden), low)
    shapes = [
        shape((ROWS, rows, features), low),
        shape((ROWS, 4, part, 3 * wide), low),
        shape((heads, blocks, TILE, 2 * HEAD), low),
        shape((heads, length, 2 * HEAD), low),
        shape((heads, HEAD, length), low),
        shape((blocks, heads, HEAD, TILE), f32),
        shape((blocks, heads, 1, TILE), f32),
        narrow, shape((own, features), f32), narrow, broad, narrow, broad, narrow, narrow,
        shape((ROWS, own, wide), low), shape((32, features), f32),
    ]
    return pl.pallas_call(
        functools.partial(forward_kernel, widths, heads),
        out_shape=shapes,
        in_specs=[IN_PLACE] * 2 + [IN_VMEM] * 5 + [pl.BlockSpec(memory_space=pltpu.SMEM)]
        + [IN_VMEM] * 2 + [IN_PLACE] * (1 + len(shards)),
        out_specs=[IN_PLACE] * 7 + [IN_VMEM] * 3 + [IN_PLACE, IN_VMEM, IN_PLACE] + [IN_VMEM] * 4,
        scratch_shapes=[pltpu.VMEM((ROWS, 4, part, 2 * width), low) for width in widths]
        + [pltpu.VMEM(out.shape, out.dtype) for out in shapes[:7] + [broad, broad]]
        + [
            pltpu.VMEM((own, features), low),
            pltpu.VMEM((2,) + vec.shape, f32),
            pltpu.VMEM((ROWS, own, wide), low),
            pltpu.VMEM((heads, HEAD, length), low),
            pltpu.VMEM((length, 1), jnp.int32),
            pltpu.VMEM((2, 4, part, 3 * wide), low),
            pltpu.VMEM((blocks, TILE, wide), low),
            pltpu.VMEM((own, hidden), f32),
            pltpu.VMEM((own, features), f32),
            pltpu.VMEM(w_pooler.shape, low),
            pltpu.SemaphoreType.DMA((256,)),
            pltpu.SemaphoreType.DMA((96,)),
            pltpu.SemaphoreType.DMA((24,)),
        ],
        compiler_params=comm_params(1),
        name="forward_links",
    )(
        x, cot, vec, wq, wk, wv, ids.reshape(1, -1), labels.reshape(1, 1), w_classes.T,
        b_classes.reshape(1, -1), w_pooler, *[shard.reshape(4, part, -1) for shard in shards],
    )


def add_into(total, *others):
    def one(step, carry):
        value = total[step].astype(jnp.float32)
        for other in others:
            value = value + other[step].astype(jnp.float32)
        total[step] = value.astype(total.dtype)
        return carry

    lax.fori_loop(0, total.shape[0], one, 0)


CHUNK = 384
FLOW = {
    "x2": ("f1i",),
    "pq": ("f2i",),
    "a0": ("s1i",),
    "a1": ("s2i", "m1i", "f1o",),
    "a2": ("m2i", "f2o", "s1o",),
    "a3": ("f3o", "s2o", "m1o", "s3o", "m2o",),
    "end": ("m3o",),
}
PLAN = (
    "g0",
    "g1",
    "r0",
    "c0",
    "g2",
    "g3",
    "c1",
    "g4",
    "d0",
    "a0",
    "s0",
    "s1",
    "c2",
    "a1",
    "c3",
    "a2",
    "l1",
    "l0",
    "c4",
    "a3",
    "h1",
    "h0",
    "w0",
    "s2",
    "s3",
    "q0",
    "t0",
    "t1",
    "x0",
    "s4",
    "t2",
    "l2",
    "x1",
    "l3",
    "t3",
    "f0",
    "f1",
    "v0",
    "l4",
    "x2",
    "n0",
    "n1",
    "v1",
    "h2",
    "q1",
    "h3",
    "h4",
    "k0",
    "v2",
    "s5",
    "v3",
    "f2",
    "f3",
    "f4",
    "x3",
    "q2",
    "n2",
    "n3",
    "n4",
    "n5",
    "k1",
    "v4",
)


def backward_kernel(
    heads, blocks_in, output, late_far, stream, pre_far, branch_two, activ_far, branch_one, context,
    q_far, kv_far, kt_far, mixed_far, lse_far, ids, x_far, w_far, vec_in, *refs,
):
    out_g, refs = refs[:5], refs[5:]
    out_q, out_x, halves, vec, refs = refs[0], refs[1], refs[2], refs[3], refs[4:]
    pairs, refs = refs[:5], refs[5:]
    mates, refs = refs[:5], refs[5:]
    first, refs = refs[:6], refs[6:]
    second, refs = refs[:6], refs[6:]
    lines, refs = refs[:5], refs[5:]
    (
        grad_ctx, both, delta, dq, dkv, grads, grads_t, w_t, turned, ids_col, dx, sum_x,
        line_x, gq, sum_q, all_q, vec_own, vec_mate, vec_line, vec_flat, vec_table,
        w_heads, q, kv, kt, mixed, lse, x_all, grad_pre, activ, late, send, recv, local,
    ) = refs
    nears = (w_heads, q, kv, kt, mixed, lse, x_all, grad_pre, activ, late)
    fars = (w_far, q_far, kv_far, kt_far, mixed_far, lse_far, x_far, pre_far, activ_far, late_far)
    reads = [
        pltpu.make_async_copy(far, near, local.at[n]) for n, (far, near) in enumerate(zip(fars, nears))
    ]
    for n in (7, 8, 0, 1, 2, 3, 4, 5, 6, 9):
        reads[n].start()
    dp, row, col = place()
    links = Links(send, recv)
    low, f32 = q.dtype, jnp.float32
    mate = (dp, row, 1 - col)
    peers = [lax.rem(row + n, ROWS) for n in (1, 2, 3)]
    at_row = lambda other: (dp, other, col)
    at_dp = lambda flip: (dp ^ flip, row, col)
    home, side = row // 2, lax.rem(row, 2)
    mine = lax.rem(row + col, 2)
    length = kv.shape[1]
    wide = heads * HEAD
    rows_dev, feat = out_x.shape
    half = rows_dev // 2
    row_tiles = length // TILE
    blocks = row_tiles // 2
    meet(
        [at_row(peer) for peer in peers]
        + [at_dp(1), at_dp(2), mate]
        + [(dp, peer, 1 - col) for peer in peers]
    )

    swap, slot_o = links.slots(3), links.slots(1)
    for n, peer in enumerate(peers):
        links.push(blocks_in.at[peer], grad_ctx.at[row], swap + 2 - n, at_row(peer))
    own_rows = pl.ds(pl.multiple_of(mine * half, 128), half)
    other_rows = pl.ds(pl.multiple_of((1 - mine) * half, 128), half)
    links.push(output.at[:, columns(1 - col, feat)], halves.at[own_rows], slot_o, mate)
    reads += [
        pltpu.make_async_copy(output.at[:, columns(col, feat)], halves.at[own_rows], local.at[10]),
        pltpu.make_async_copy(blocks_in.at[row], grad_ctx.at[row], local.at[11]),
    ]
    reads[10].start()
    reads[11].start()

    lefts = (stream, branch_two, branch_one)
    for n in range(3):
        turned[n] = lefts[n][...].astype(f32).T.astype(low)
    feeds = [(0, grad_pre, 0), (1, activ, 0), (0, grad_pre, 1), (1, activ, 1), (2, context, 0)]
    turns = [(1, 2), (2, 1), (1, 2), (2, 1), (1, 2), (2, 1)]
    widths = [out.shape[2] for out in out_g]
    slot_g = [links.slots(1) for _ in widths]

    def local_grad(i):
        if i < 2:
            reads[7 + i].wait()
        left, right, part = feeds[i]
        width = widths[i]
        per = width // CHUNK

        def one(step, carry):
            which, n = step // per, step % per
            core = jnp.where(which == 0, 1 - col, col)
            start = core * (right.shape[1] // 2) + part * width + n * CHUNK
            value = nn(turned[left], right[:, pl.ds(pl.multiple_of(start, 128), CHUNK)])
            pairs[i][which, :, :, :, pl.ds(pl.multiple_of(n * CHUNK, 128), CHUNK)] = (
                value.astype(low).reshape(pairs[i].shape[1:4] + (CHUNK,))
            )
            return carry

        lax.fori_loop(0, 2 * per, one, 0)
        links.push(pairs[i].at[0], mates[i], slot_g[i], mate)

    totals = [pair.at[1] for pair in pairs] + [all_q]

    def send_first(i):
        one, two = turns[i]
        base = links.slots(2)
        links.push(totals[i].at[:, dp ^ 3], first[i].at[1], base + 1, at_dp(one))
        links.push(totals[i].at[:, dp ^ one], first[i].at[0], base, at_dp(one))
        return base

    def join(i):
        links.arrive(mates[i], slot_g[i], mate)

        def one(step, carry):
            at, q_at = step // 4, step % 4
            pairs[i][1, at, q_at] = (
                pairs[i][1, at, q_at].astype(f32) + mates[i][at, q_at].astype(f32)
            ).astype(low)
            return carry

        lax.fori_loop(0, 16, one, 0)
        stage[i] = send_first(i)

    def send_second(i):
        one, two = turns[i]
        base = stage[i]
        links.arrive(first[i].at[1], base + 1, mate)
        add_into(totals[i].at[:, dp ^ two], first[i].at[1])
        slot = links.slots(1)
        links.push(totals[i].at[:, dp ^ two], second[i], slot, at_dp(two))
        stage[i] = (base, slot)

    def send_line(i):
        links.arrive(first[i].at[0], stage[i][0], mate)
        links.arrive(second[i], stage[i][1], mate)
        add_into(totals[i].at[:, dp], first[i].at[0], second[i])
        base = links.slots(3)
        links.push(totals[i].at[row ^ 3, dp], lines[i].at[1], base + 1, at_row(row ^ 1))
        links.push(totals[i].at[row ^ 1, dp], lines[i].at[0], base, at_row(row ^ 1))
        stage[i] = base

    def halve_line(i):
        links.arrive(lines[i].at[1], stage[i] + 1, mate)
        pairs[i][1, row ^ 2, dp] = (
            pairs[i][1, row ^ 2, dp].astype(f32) + lines[i][1].astype(f32)
        ).astype(low)
        links.push(totals[i].at[row ^ 2, dp], lines[i].at[2], stage[i] + 2, at_row(row ^ 2))

    def share(i, out):
        one, two = turns[i]
        base = links.slots(3)
        links.push(out.at[dp], out.at[dp], base, at_dp(two))
        links.push(out.at[dp], out.at[dp], base + 1, at_dp(one))
        return base

    def share_on(i, out, base):
        one, two = turns[i]
        links.arrive(out.at[dp ^ two], base, mate)
        links.push(out.at[dp ^ two], out.at[dp ^ two], base + 2, at_dp(one))

    def shared(i, out, base):
        one, two = turns[i]
        links.arrive(out.at[dp ^ one], base + 1, mate)
        links.arrive(out.at[dp ^ 3], base + 2, mate)

    stage = [None] * 6
    slot_x, slot_xl = links.slots(4), links.slots(3)
    slot_q, slot_ql = links.slots(1), links.slots(4)
    slot_v, slot_vl, slot_vd = links.slots(1), links.slots(3), links.slots(5)
    order = (row ^ 3, row ^ 1, row ^ 2, row)
    per_row = rows_dev // TILE
    own_block = 2 * row + mine
    own_part = all_q.at[side, pl.ds(2 * col, 2)]
    at_home = home == col
    sums = {}

    def split_ids(step, carry):
        span = pl.ds(pl.multiple_of(step * TILE, TILE), TILE)
        ids_col[span] = jnp.broadcast_to(ids[:, span], (8, TILE)).T[:, :1]
        return carry

    def split_grad(j, carry):
        grad = grad_ctx[j]
        grad_t = grad.astype(f32).T
        for h in range(heads):
            part = slice(h * HEAD, (h + 1) * HEAD)
            both[h, j, :TILE] = q[h, j]
            both[h, j, TILE:] = jnp.concatenate(
                [jnp.zeros((TILE, HEAD), low), grad[:, part]], axis=1
            )
            delta[h, j] = jnp.sum(grad_t[part] * mixed[j, h], axis=0, keepdims=True)
        return carry

    def ready():
        reads[0].wait()
        w_t[...] = w_heads[...].reshape(2 * feat, 3 * wide).astype(f32).T.astype(low)
        lax.fori_loop(0, row_tiles, split_ids, 0)
        dkv[...] = jnp.zeros_like(dkv)

    def take_context():
        for n, peer in enumerate(peers):
            links.arrive(grad_ctx.at[peer], swap + n, mate)
        for copy in reads[1:6] + reads[11:]:
            copy.wait()
        lax.fori_loop(0, blocks, split_grad, 0)

    def attend_back(j):
        block = 2 * j + lax.rem(j + col, 2)
        rows = pl.ds(pl.multiple_of(block * TILE, TILE), TILE)
        query_ids = ids[:, rows]
        far = 2 * j * TILE
        spans = ([(0, far)] if far else []) + [(far, min(2 * j + NEAR, row_tiles) * TILE)]

        def one_head(h, carry, j=j, query_ids=query_ids, far=far, spans=spans):
            total = jnp.zeros((HEAD, TILE), f32)
            for start, stop in spans:
                raw = nt(kv[h, start:stop], both[h, j])
                probs = jnp.exp(raw[:, :TILE] - lse[j, h])
                if start == far:
                    probs = jnp.where(ids_col[start:stop] <= query_ids, probs, 0.0)
                grad_scores = (probs * (raw[:, TILE:] - delta[h, j])).astype(low)
                dkv[h, start:stop] += nn(
                    jnp.concatenate([grad_scores, probs.astype(low)], axis=1), both[h, j]
                )
                total = total + nn(kt[h, :, start:stop], grad_scores)
            dq[j, h] = total * HEAD**-0.5
            return carry

        lax.fori_loop(0, heads, one_head, 0)

    def gather_q(j, carry):
        block = 2 * j + lax.rem(j + col, 2)
        rows = pl.ds(pl.multiple_of(block * TILE, TILE), TILE)
        other = pl.ds(pl.multiple_of((4 * j + 1 - block) * TILE, TILE), TILE)
        value = jnp.concatenate([dq[j, h] for h in range(heads)], axis=0)
        grads_t[2 * wide :, rows] = value.astype(low)
        grads_t[2 * wide :, other] = jnp.zeros((wide, TILE), low)
        grads[rows, 2 * wide :] = value.T.astype(low)
        grads[other, 2 * wide :] = jnp.zeros((TILE, wide), low)
        return carry + jnp.sum(value.T, axis=0, keepdims=True)

    def gather_kv(step, carry):
        rows = pl.ds(pl.multiple_of(step * TILE, TILE), TILE)
        value = jnp.concatenate([dkv[h, rows] for h in range(heads)], axis=1)
        grads[rows, : 2 * wide] = value.astype(low)
        grads_t[: 2 * wide, rows] = value.T.astype(low)
        return carry + jnp.sum(value, axis=0, keepdims=True)

    def weight_grads():
        reads[6].wait()
        reads[9].wait()
        reads[10].wait()
        sums["q"] = lax.fori_loop(0, blocks, gather_q, jnp.zeros((1, wide), f32))
        sums["kv"] = lax.fori_loop(0, row_tiles, gather_kv, jnp.zeros((1, 2 * wide), f32))
        for n in range(2):
            span = slice(n * CHUNK, (n + 1) * CHUNK)
            value = nn(grads_t[...], x_all[:, :, span].reshape(length, CHUNK)).T
            gq[2 * n : 2 * n + 2] = value.astype(low).reshape((2,) + gq.shape[1:])
        links.push(gq.at[:, 1 - col], sum_q, slot_q, mate)

    def token_grads(at):
        def one(step, carry):
            here = pl.ds(pl.multiple_of(step * TILE, TILE), TILE)
            rows = pl.ds(pl.multiple_of((at * per_row + step) * TILE, TILE), TILE)
            value = nn(grads[rows], w_t[...])
            is_own = (at * per_row + step == own_block).astype(f32)
            dx[at, here] = (value + late[...] * is_own).astype(low)
            return carry

        lax.fori_loop(0, per_row, one, 0)

    def send_tokens(n):
        token_grads(order[n])
        links.push(
            dx.at[order[n], :, columns(1 - col, feat)], sum_x.at[order[n]], slot_x + n, mate
        )

    def join_x(at, slot):
        links.arrive(sum_x.at[at], slot, mate)

        def one(step, carry):
            here = pl.ds(pl.multiple_of(step * 128, 128), 128)
            sum_x[at, here] = (
                sum_x[at, here].astype(f32) + dx[at, here, columns(col, feat)].astype(f32)
            ).astype(low)
            return carry

        lax.fori_loop(0, rows_dev // 128, one, 0)

    def line_tokens(n):
        join_x(order[n], slot_x + n)
        if n < 2:
            links.push(sum_x.at[order[n]], line_x.at[1 - n], slot_xl + 1 - n, at_row(row ^ 1))

    def halve_x(step, carry):
        rows = pl.ds(pl.multiple_of(step * 128, 128), 128)
        sum_x[row ^ 2, rows] = (
            sum_x[row ^ 2, rows].astype(f32) + line_x[1, rows].astype(f32)
        ).astype(low)
        return carry

    def halve_tokens():
        links.arrive(line_x.at[1], slot_xl + 1, mate)
        lax.fori_loop(0, rows_dev // 128, halve_x, 0)
        links.push(sum_x.at[row ^ 2], line_x.at[2], slot_xl + 2, at_row(row ^ 2))

    def finish_x(step, carry):
        rows = pl.ds(pl.multiple_of(step * 128, 128), 128)
        value = sum_x[row, rows].astype(f32)
        for n in (0, 2):
            value = value + line_x[n, rows].astype(f32)
        out_x[rows] = value.astype(low)
        return carry

    def finish_tokens():
        for n in (0, 2):
            links.arrive(line_x.at[n], slot_xl + n, mate)
        lax.fori_loop(0, rows_dev // 128, finish_x, 0)

    def add_q(step, carry):
        sum_q[step] = (sum_q[step].astype(f32) + gq[step, col].astype(f32)).astype(low)
        return carry

    def keep_own():
        own_part[...] = sum_q[row]

    def line_q():
        links.arrive(sum_q, slot_q, mate)
        lax.fori_loop(0, ROWS, add_q, 0)
        pl.when(at_home)(keep_own)
        slot = slot_ql + 2 * side + col
        links.push(sum_q.at[row], own_part, slot, mate, jnp.logical_not(at_home))
        for peer in peers:
            links.push(sum_q.at[peer], own_part, slot, (dp, peer, home))

    def first_q():
        for j in range(2):
            for e in range(2):
                here = (row == 2 * col + j) & (col == e)
                links.arrive(
                    all_q.at[j, pl.ds(2 * e, 2)], slot_ql + 2 * j + e, mate, jnp.logical_not(here)
                )
        stage[5] = send_first(5)

    def finish_q():
        links.arrive(first[5].at[0], stage[5][0], mate)
        links.arrive(second[5], stage[5][1], mate)
        add_into(all_q.at[:, dp], first[5].at[0], second[5])
        for j in range(2):
            out_q[dp, j] = all_q[j, dp]
        stage[5] = share(5, out_q)

    def finish_line(i):
        for n in (0, 2):
            links.arrive(lines[i].at[n], stage[i] + n, mate)
        value = pairs[i][1, row, dp].astype(f32)
        for n in (0, 2):
            value = value + lines[i][n].astype(f32)
        out_g[i][dp] = value.astype(low)
        stage[i] = share(i, out_g[i])

    def sums_mate():
        value = jnp.concatenate(
            [sums["kv"], sums["q"], jnp.zeros((1, 2 * feat - 3 * wide), f32)], axis=1
        )
        here = lax.broadcasted_iota(jnp.int32, (8, 2 * feat), 0) == 5 + side
        for c in range(2):
            part = vec_in[8 + 8 * c : 16 + 8 * c] + jnp.where(here & (home == c), value, 0.0)
            vec_own[jnp.where(col == c, 0, 1), :8] = part
        vec_own[0, 8:] = vec_in[24:]
        vec_own[1, 8:] = vec_in[24:]
        links.push(vec_own.at[1], vec_mate, slot_v, mate)

    def sums_line():
        links.arrive(vec_mate, slot_v, mate)
        vec_mate[...] = vec_own[0] + vec_mate[...]
        for n, peer in enumerate(peers):
            links.push(vec_mate, vec_line.at[2 - n], slot_vl + 2 - n, at_row(peer))

    def sums_first():
        for n in range(3):
            links.arrive(vec_line.at[n], slot_vl + n, mate)
        vec_sum = vec_mate[...] + vec_line[0] + vec_line[1] + vec_line[2]
        vec_flat[2] = vec_sum[:8]
        vec_table[dp] = vec_sum[8:]
        links.push(vec_flat.at[2], vec_flat.at[0], slot_vd, at_dp(1))
        links.push(vec_table.at[dp], vec_table.at[dp], slot_vd + 1, at_dp(1))
        links.push(vec_table.at[dp], vec_table.at[dp], slot_vd + 2, at_dp(2))

    def sums_second():
        links.arrive(vec_flat.at[0], slot_vd, mate)
        vec_flat[3] = vec_flat[2] + vec_flat[0]
        links.push(vec_flat.at[3], vec_flat.at[1], slot_vd + 3, at_dp(2))
        links.arrive(vec_table.at[dp ^ 1], slot_vd + 1, mate)
        links.push(vec_table.at[dp ^ 1], vec_table.at[dp ^ 1], slot_vd + 4, at_dp(2))

    def sums_last():
        links.arrive(vec_flat.at[1], slot_vd + 3, mate)
        links.arrive(vec_table.at[dp ^ 2], slot_vd + 2, mate)
        links.arrive(vec_table.at[dp ^ 3], slot_vd + 4, mate)
        vec[:8] = vec_flat[3] + vec_flat[1]
        for n in range(4):
            vec[8 + 8 * n : 16 + 8 * n] = vec_table[n]

    def out_of(i):
        return out_q if i == 5 else out_g[i]

    work = {
        "g": local_grad, "c": join, "s": send_second, "l": send_line, "h": halve_line,
        "f": finish_line, "n": lambda i: share_on(i, out_of(i), stage[i]),
        "r": lambda _: ready(), "d": lambda _: take_context(), "a": attend_back,
        "w": lambda _: weight_grads(), "t": send_tokens, "x": line_tokens,
        "k": lambda n: (halve_tokens, finish_tokens)[n](),
        "q": lambda n: (line_q, first_q, finish_q)[n](),
        "v": lambda n: (sums_mate, sums_line, sums_first, sums_second, sums_last)[n](),
    }
    for entry in PLAN:
        work[entry[0]](int(entry[1]))
    for i in range(6):
        shared(i, out_of(i), stage[i])
    links.arrive(halves.at[other_rows], slot_o, mate)
    links.drain()


def backward_links(
    grad_blocks, output, late, stream, grad_pre, branch_two, activ, branch_one, context,
    q, kv, kt, mixed, lse, ids, x_all, w_heads, vec,
):
    low, f32 = q.dtype, jnp.float32
    heads, length = kv.shape[0], kv.shape[1]
    wide = heads * HEAD
    own, features = output.shape
    hidden = activ.shape[1]
    part = features // ROWS // 4
    widths = [hidden // 4] * 4 + [features // 2]
    rows, feat = 2 * own, features // 2
    blocks = length // TILE // 2
    shape = jax.ShapeDtypeStruct
    outs = [shape((4, part, width), low) for width in widths] + [
        shape((4, 2, part, 3 * wide), low),
        shape((rows, feat), low),
        shape((rows, feat), low),
        shape((40, features), f32),
    ]
    every = [(ROWS, width) for width in widths] + [(2, 3 * wide)]
    return pl.pallas_call(
        functools.partial(backward_kernel, heads),
        out_shape=outs,
        in_specs=[IN_PLACE] * 3 + [IN_VMEM, IN_PLACE] * 2 + [IN_VMEM] * 2 + [IN_PLACE] * 5
        + [IN_VMEM] + [IN_PLACE] * 2 + [IN_VMEM],
        out_specs=[IN_VMEM] * len(outs),
        scratch_shapes=[pltpu.VMEM((2, ROWS, 4, part, width), low) for width in widths]
        + [pltpu.VMEM((ROWS, 4, part, width), low) for width in widths]
        + [pltpu.VMEM((2, lead, part, width), low) for lead, width in every]
        + [pltpu.VMEM((lead, part, width), low) for lead, width in every]
        + [pltpu.VMEM((3, part, width), low) for width in widths]
        + [
            pltpu.VMEM((ROWS, own, wide), low),
            pltpu.VMEM((heads, blocks, 2 * TILE, 2 * HEAD), low),
            pltpu.VMEM((heads, blocks, 1, TILE), f32),
            pltpu.VMEM((blocks, heads, HEAD, TILE), f32),
            pltpu.VMEM((heads, length, 2 * HEAD), f32),
            pltpu.VMEM((length, 3 * wide), low),
            pltpu.VMEM((3 * wide, length), low),
            pltpu.VMEM((3 * wide, features), low),
            pltpu.VMEM((3, features, own), low),
            pltpu.VMEM((length, 1), jnp.int32),
            pltpu.VMEM((ROWS, rows, features), low),
            pltpu.VMEM((ROWS, rows, feat), low),
            pltpu.VMEM((3, rows, feat), low),
            pltpu.VMEM((ROWS, 2, 2, part, 3 * wide), low),
            pltpu.VMEM((ROWS, 2, part, 3 * wide), low),
            pltpu.VMEM((2, 4, part, 3 * wide), low),
            pltpu.VMEM((2, 16, features), f32),
            pltpu.VMEM((16, features), f32),
            pltpu.VMEM((3, 16, features), f32),
            pltpu.VMEM((4, 8, features), f32),
            pltpu.VMEM((4, 8, features), f32),
        ]
        + [pltpu.VMEM(far.shape, far.dtype)
            for far in (w_heads, q, kv, kt, mixed, lse, x_all, grad_pre, activ, late)]
        + [
            pltpu.SemaphoreType.DMA((128,)),
            pltpu.SemaphoreType.DMA((128,)),
            pltpu.SemaphoreType.DMA((12,)),
        ],
        compiler_params=comm_params(2),
        name="backward_links",
    )(
        grad_blocks, output, late, stream, grad_pre, branch_two, activ, branch_one, context,
        q, kv, kt, mixed, lse, ids.reshape(1, -1), x_all, w_heads, vec,
    )


def put_lanes(target, value):
    for n in range(target.shape[0]):
        target[n : n + 1] = value[:, n * 128 : (n + 1) * 128]


def finish_kernel(
    heads, g1a, g1b, g2a, g2b, go, gq, x_in, out_in, vec,
    out, logits, grad_x, o_q, o_bq, o_k, o_v, o_bv, o_o, o_bo, o_g1, o_s1, far_1, o_b1, far_2, o_b2,
    o_g2, o_s2, far_p, o_bp, o_c, o_bc, o_1, o_2, o_p, sems,
):
    dp = lax.axis_index("dp")
    f32 = jnp.float32
    wide = heads * HEAD
    classes = logits.shape[1]
    depth, feat = o_q.shape
    part = g1a.shape[2]
    write_out = [
        pltpu.make_async_copy(near, far, sems.at[n])
        for n, (near, far) in enumerate(((o_p, far_p), (o_1, far_1), (o_2, far_2)))
    ]
    table = vec[8:40]
    table_t = table.T
    pooler = jnp.zeros(o_p.shape, f32)
    head = [jnp.zeros((1, 2 * feat), f32) for _ in range(classes)]
    total = jnp.zeros((1, 2 * feat), f32)
    ends = jnp.zeros((1, 128), f32)
    own_tail = jnp.zeros((1, 128), f32)
    for s in range(4):
        at = 8 * s
        slope, tail = table[at + 1 : at + 2], table[at + 3 : at + 4, :128]
        pooler = pooler + table_t[:, at : at + 1] * slope
        total = total + slope
        for n in range(classes):
            head[n] = head[n] + table[at + 2 : at + 3] * tail[:, classes + n : classes + n + 1]
        ends = ends + tail
        own_tail = jnp.where(dp == s, tail, own_tail)
    o_p[...] = pooler
    write_out[0].start()
    flat = lambda ref: ref[...].astype(f32).reshape(depth, ref.shape[2])
    for target, first, second in ((o_1, g1a, g1b), (o_2, g2a, g2b)):
        target[:, :part] = flat(first)
        target[:, part:] = flat(second)
        write_out[1 if target is o_1 else 2].start()
    out[...] = out_in[...]
    grad_x[...] = x_in[...]
    o_o[...] = flat(go)
    bias_q, bias_v = [], []
    for j in range(2):
        value = gq[:, j].astype(f32).reshape(depth, 3 * wide)
        o_q[:, j * wide : (j + 1) * wide] = value[:, 2 * wide :]
        for target, shift in ((o_k, 0), (o_v, HEAD)):
            target[:, j * wide : (j + 1) * wide] = jnp.concatenate(
                [value[:, 2 * h * HEAD + shift :][:, :HEAD] for h in range(heads)], axis=1
            )
        bias = vec[5 + j : 6 + j]
        bias_q.append(bias[:, 2 * wide : 3 * wide])
        bias_v += [bias[:, 2 * h * HEAD + HEAD :][:, :HEAD] for h in range(heads)]
    put_lanes(o_bq, jnp.concatenate(bias_q, axis=1))
    put_lanes(o_bv, jnp.concatenate(bias_v, axis=1))
    own = vec[:8]
    for n, target in enumerate((o_bo, o_g1, o_s1, o_b2, o_g2, o_s2)):
        put_lanes(target, own[n // 2 : n // 2 + 1, (n % 2) * feat : (n % 2 + 1) * feat])
    put_lanes(o_b1, jnp.concatenate([own[3:4], own[4:5]], axis=1))
    put_lanes(o_bp, total)
    o_c[...] = jnp.concatenate(head, axis=0)
    o_bc[...] = ends[:, classes : 2 * classes]
    logits[...] = own_tail[:, :classes]
    for copy in write_out:
        copy.wait()


def finish(pieces, classes, heads):
    g1a, g1b, g2a, g2b, go, gq, x_in, out_in, vec = pieces
    f32 = jnp.float32
    depth = go.shape[0] * go.shape[1]
    feat, hidden = go.shape[2], 2 * g1a.shape[2]
    features = vec.shape[1]
    shape = jax.ShapeDtypeStruct
    vector = lambda size: shape((size // 128, 128) if size % 128 == 0 else (1, size), f32)
    square = shape((depth, feat), f32)
    outs = [
        shape(out_in.shape, out_in.dtype), vector(classes), shape(x_in.shape, x_in.dtype),
        square, vector(feat), square, square, vector(feat), square, vector(feat), vector(feat),
        vector(feat), shape((depth, hidden), f32), vector(hidden), shape((depth, hidden), f32),
        vector(feat), vector(feat), vector(feat), shape((features, features), f32),
        vector(features), shape((classes, features), f32), vector(classes),
    ]
    return pl.pallas_call(
        functools.partial(finish_kernel, heads),
        out_shape=outs,
        in_specs=[IN_VMEM] * len(pieces),
        out_specs=[IN_PLACE if n in (12, 14, 18) else IN_VMEM for n in range(len(outs))],
        scratch_shapes=[pltpu.VMEM(outs[n].shape, f32) for n in (12, 14, 18)]
        + [pltpu.SemaphoreType.DMA((3,))],
        compiler_params=pltpu.CompilerParams(vmem_limit_bytes=VMEM_BYTES),
        name="finish",
    )(*pieces)


def norm_rows(hidden, gain, shift):
    row_mean = jnp.mean(hidden, axis=1, keepdims=True)
    row_var = jnp.mean(hidden * hidden, axis=1, keepdims=True) - row_mean * row_mean
    inv_scale = lax.rsqrt(row_var + epsilon)
    normed = (hidden - row_mean) * inv_scale
    return normed * gain + shift, normed, inv_scale


def norm_rows_back(grad, normed, inv_scale, gain):
    scaled = grad * gain
    first = jnp.mean(scaled, axis=1, keepdims=True)
    second = jnp.mean(scaled * normed, axis=1, keepdims=True)
    return inv_scale * (scaled - first - normed * second)


def fast_body(
    layer_input, cotangent, labels, block_ids, w_query, b_query, w_key, w_value, b_value,
    w_output, b_output, ln1_gain, ln1_bias, w_inner, b_inner, w_outer, b_outer,
    ln2_gain, ln2_bias, w_pooler, b_pooler, w_classes, b_classes,
):
    f32 = jnp.float32
    feat = layer_input.shape[1]
    heads = 2 * feat // HEAD // ROWS
    vectors = [
        b_query, b_value, b_output, ln1_gain, ln1_bias, b_outer, ln2_gain, ln2_bias, b_inner,
        b_pooler,
    ]
    count = sum(vector.shape[0] for vector in vectors) // feat
    padded, at = 0.0, 0
    full = (count + -count % 8) * feat
    for vector in vectors:
        size = vector.shape[0]
        padded = padded + jnp.pad(vector.astype(f32), (at, full - at - size))
        at += size
    (
        x_all, w_heads, q, kv, kt, mixed, lse, output, late, stream, grad_pre, branch_two, activ,
        branch_one, context, grad_blocks, packed,
    ) = forward_links(
        layer_input, cotangent, padded.reshape(-1, feat), w_query, w_key, w_value, block_ids, labels, w_classes,
        b_classes, w_pooler, [w_output.T, w_inner, w_outer.T],
    )
    s_1a, s_2a, s_1b, s_2b, s_wo, s_q, grad_input, output, sums = backward_links(
        grad_blocks, output, late, stream, grad_pre, branch_two, activ, branch_one, context,
        q, kv, kt, mixed, lse, block_ids, x_all, w_heads, packed,
    )
    outs = finish((s_1a, s_1b, s_2a, s_2b, s_wo, s_q, grad_input, output, sums), w_classes.shape[1], heads)
    flat = (4, 7, 9, 10, 11, 13, 15, 16, 17, 19, 21)
    turned = (8, 14, 20)
    return tuple(
        out.reshape(-1) if n in flat else out.T if n in turned else out
        for n, out in enumerate(outs)
    )


def is_fast(mesh):
    sizes = mesh.shape
    return sizes["dp"] == 4 and sizes["row"] == ROWS and sizes["col"] == 2


def solution(mesh):
    placed = (
        P(("dp", "row"), "col"),
        P(("dp", "row"), "col"),
        P("dp"),
        P("dp"),
        P("row", "col"),
        P("col"),
        P("row", "col"),
        P("row", "col"),
        P("col"),
        P("col", "row"),
        P("col"),
        P("col"),
        P("col"),
        P("row", "col"),
        P("col"),
        P("col", "row"),
        P("col"),
        P("col"),
        P("col"),
        P(),
        P(),
        P(),
        P(),
    )
    return jax.shard_map(
        fast_body if is_fast(mesh) else body,
        mesh=mesh,
        in_specs=placed,
        out_specs=(
            P(("dp", "row"), "col"),
            P("dp", None),
            P(("dp", "row"), "col"),
            P("row", "col"),
            P("col"),
            P("row", "col"),
            P("row", "col"),
            P("col"),
            P("col", "row"),
            P("col"),
            P("col"),
            P("col"),
            P("row", "col"),
            P("col"),
            P("col", "row"),
            P("col"),
            P("col"),
            P("col"),
            P(),
            P(),
            P(),
            P(),
        ),
        check_vma=False,
    )
```

```python
import functools

import jax
import jax.numpy as jnp
from jax import lax
from jax.experimental import pallas as pl
from jax.experimental.pallas import tpu as pltpu
from jax.sharding import PartitionSpec as P

HEAD = 64


highest = lax.Precision.HIGHEST
epsilon = 1e-05
root_half = 0.7071067811865476
inv_root_tau = 0.3989422804014327
masked_score = -1e30


def gelu_exact(values):
    return values * 0.5 * (1.0 + lax.erf(values * root_half))


def gelu_slope(values):
    return 0.5 * (1.0 + lax.erf(values * root_half)) + values * inv_root_tau * jnp.exp(
        -0.5 * values * values
    )


def project(left, right):
    return jnp.dot(left, right, preferred_element_type=jnp.float32)


def contract_first(left, right):
    return lax.dot_general(
        left, right, (((0,), (0,)), ((), ())), preferred_element_type=jnp.float32
    )


def contract_last(left, right):
    return lax.dot_general(
        left, right, (((1,), (1,)), ((), ())), preferred_element_type=jnp.float32
    )


def gather_features(values):
    return lax.all_gather(values, "col", axis=1, tiled=True)


def sum_features(values):
    return lax.psum_scatter(
        values.astype(jnp.bfloat16), "col", scatter_dimension=1, tiled=True
    ).astype(jnp.float32)


def feature_totals(first_part, second_part):
    return lax.psum((jnp.sum(first_part, axis=1), jnp.sum(second_part, axis=1)), "col")


def norm_forward(hidden, gain, shift, features):
    row_total, square_total = feature_totals(hidden, hidden * hidden)
    row_mean = row_total / features
    row_var = square_total / features - row_mean * row_mean
    inv_scale = lax.rsqrt(row_var + epsilon)
    normed = (hidden - row_mean[:, None]) * inv_scale[:, None]
    return (normed * gain + shift, normed, inv_scale)


def norm_backward(grad, normed, inv_scale, gain, features):
    scaled = grad * gain
    first_total, second_total = feature_totals(scaled, scaled * normed)
    return inv_scale[:, None] * (
        scaled - (first_total / features)[:, None] - normed * (second_total / features)[:, None]
    )


def key_split(piece_rows, rows_dev):
    return (piece_rows // rows_dev, rows_dev)


def body(
    layer_input,
    cotangent,
    labels,
    block_ids,
    w_query,
    b_query,
    w_key,
    w_value,
    b_value,
    w_output,
    b_output,
    ln1_gain,
    ln1_bias,
    w_inner,
    b_inner,
    w_outer,
    b_outer,
    ln2_gain,
    ln2_bias,
    w_pooler,
    b_pooler,
    w_classes,
    b_classes,
):
    f32 = jnp.float32
    bf16 = jnp.bfloat16
    rows_dev, feat_col = layer_input.shape
    heads_col = feat_col // HEAD
    features = feat_col * lax.axis_size("col")
    row_index = lax.axis_index("row")
    col_index = lax.axis_index("col")
    seq_index = lax.axis_index("dp")
    seq_count = lax.axis_size("dp")
    score_scale = HEAD ** (-0.5)
    query_ids = lax.dynamic_slice_in_dim(block_ids, row_index * rows_dev, rows_dev)
    last_query = query_ids[rows_dev - 1]
    wq_full, wk_full, wv_full, w1_full = (
        lax.all_gather(w_query, "row", axis=0, tiled=True),
        lax.all_gather(w_key, "row", axis=0, tiled=True),
        lax.all_gather(w_value, "row", axis=0, tiled=True),
        lax.all_gather(w_inner, "row", axis=0, tiled=True),
    )
    wo_full, w2_full = (
        lax.all_gather(w_output, "row", axis=1, tiled=True),
        lax.all_gather(w_outer, "row", axis=1, tiled=True),
    )
    input_whole = gather_features(layer_input)
    queries = (project(input_whole, wq_full) + b_query.astype(f32)).astype(bf16)
    keys_local = project(input_whole, wk_full).astype(bf16)
    values_local = (project(input_whole, wv_full) + b_value.astype(f32)).astype(bf16)
    queries3 = queries.reshape(rows_dev, heads_col, HEAD)
    start_state = (
        jnp.full((heads_col, rows_dev), masked_score, f32),
        jnp.zeros((heads_col, rows_dev), f32),
        jnp.zeros((heads_col, rows_dev, HEAD), f32),
    )
    running = start_state
    keys_piece = lax.all_gather(keys_local, "row", axis=0, tiled=True)
    values_piece = lax.all_gather(values_local, "row", axis=0, tiled=True)
    piece_rows = keys_piece.shape[0]
    number, block_rows = key_split(piece_rows, rows_dev)
    keys4 = keys_piece.reshape(number, block_rows, heads_col, HEAD)
    values4 = values_piece.reshape(number, block_rows, heads_col, HEAD)
    piece_ids = block_ids.reshape(number, block_rows)

    def attend_block_work(state, block_item):
        peak_score, row_mass, accum = state
        keys3, values3, key_ids = block_item
        scores = (
            jnp.einsum("qhd,khd->hqk", queries3, keys3, preferred_element_type=f32) * score_scale
        )
        allowed = (key_ids[None, :] <= query_ids[:, None])[None]
        block_top = jnp.max(jnp.where(allowed, scores, masked_score), axis=2)
        new_peak = jnp.maximum(peak_score, block_top)
        weights = jnp.where(allowed, jnp.exp(scores - new_peak[:, :, None]), 0.0)
        factor = jnp.exp(peak_score - new_peak)
        row_mass = row_mass * factor + jnp.sum(weights, axis=2)
        accum = accum * factor[:, :, None] + jnp.einsum(
            "hqk,khd->hqd", weights.astype(bf16), values3, preferred_element_type=f32
        )
        return (new_peak, row_mass, accum)

    def attend_block_step(state, block_item):
        state = lax.cond(
            block_item[2][0] > last_query, lambda st, item: st, attend_block_work, state, block_item
        )
        return (state, None)

    running, unused = lax.scan(attend_block_step, running, (keys4, values4, piece_ids))
    peak_score, row_mass, accum = running
    mixed = accum / row_mass[:, :, None]
    log_mass = peak_score + jnp.log(row_mass)
    context_low = mixed.transpose(1, 0, 2).reshape(rows_dev, feat_col).astype(bf16)
    attn_branch = sum_features(project(context_low, wo_full))
    hidden_one = layer_input.astype(f32) + attn_branch + b_output.astype(f32)
    gain_one = ln1_gain.astype(f32)
    stream, normed_one, inv_one = norm_forward(hidden_one, gain_one, ln1_bias.astype(f32), features)
    stream_whole = gather_features(stream.astype(bf16))
    pre_act = project(stream_whole, w1_full) + b_inner.astype(f32)
    activ = gelu_exact(pre_act).astype(bf16)
    ffn_branch = sum_features(project(activ, w2_full))
    hidden_two = stream + ffn_branch + b_outer.astype(f32)
    gain_two = ln2_gain.astype(f32)
    result, normed_two, inv_two = norm_forward(hidden_two, gain_two, ln2_bias.astype(f32), features)
    output = result.astype(bf16)
    row_zero = (row_index == 0).astype(f32)
    pool_input = gather_features(output[0:1])
    pooled = jnp.tanh(project(pool_input, w_pooler) + b_pooler.astype(f32))
    classes_f32 = w_classes.astype(f32)
    logits_own = jnp.dot(pooled, classes_f32, precision=highest) + b_classes.astype(f32)
    onehot = (jnp.arange(w_classes.shape[1]) == labels[0]).astype(f32)
    grad_logits = jax.nn.softmax(logits_own, axis=-1) - onehot[None, :]
    g_w_classes = jnp.dot(pooled.T, grad_logits, precision=highest)
    g_b_classes = grad_logits[0]
    grad_pre_pool = jnp.dot(grad_logits, classes_f32.T, precision=highest) * (1.0 - pooled * pooled)
    g_b_pooler = grad_pre_pool[0]
    g_w_pooler = jnp.dot(pool_input.astype(f32).T, grad_pre_pool, precision=highest)
    grad_first = jnp.dot(grad_pre_pool, w_pooler.astype(f32).T, precision=highest)
    first_col = lax.dynamic_slice_in_dim(grad_first[0], col_index * feat_col, feat_col)
    grad_result = cotangent.astype(f32).at[0].add(first_col * row_zero)
    logits_table = lax.dynamic_update_slice_in_dim(
        jnp.zeros((seq_count, w_classes.shape[1]), f32), logits_own * row_zero, seq_index, 0
    )
    g_ln2_gain = jnp.sum(grad_result * normed_two, axis=0)
    g_ln2_bias = jnp.sum(grad_result, axis=0)
    grad_hidden_two = norm_backward(grad_result, normed_two, inv_two, gain_two, features)
    g_b_outer = jnp.sum(grad_hidden_two, axis=0)
    branch_two_whole = gather_features(grad_hidden_two.astype(bf16))
    g_w_outer_full = contract_first(activ, branch_two_whole)
    grad_act = contract_last(branch_two_whole, w2_full)
    grad_pre = (grad_act * gelu_slope(pre_act)).astype(bf16)
    g_b_inner = jnp.sum(grad_pre.astype(f32), axis=0)
    g_w_inner_full = contract_first(stream_whole, grad_pre)
    grad_stream = grad_hidden_two + sum_features(contract_last(grad_pre, w1_full))
    g_ln1_gain = jnp.sum(grad_stream * normed_one, axis=0)
    g_ln1_bias = jnp.sum(grad_stream, axis=0)
    grad_hidden_one = norm_backward(grad_stream, normed_one, inv_one, gain_one, features)
    g_b_output = jnp.sum(grad_hidden_one, axis=0)
    branch_one_whole = gather_features(grad_hidden_one.astype(bf16))
    g_w_output_full = contract_first(context_low, branch_one_whole)
    grad_context = contract_last(branch_one_whole, wo_full).astype(bf16)
    grad_ctx3 = grad_context.reshape(rows_dev, heads_col, HEAD)
    delta = jnp.sum(grad_ctx3.astype(f32).transpose(1, 0, 2) * mixed, axis=2)

    def score_grads(queries_blk, grad_ctx_blk, keys3, values3, allowed, lse_blk, delta_blk):
        scores = (
            jnp.einsum("qhd,khd->hqk", queries_blk, keys3, preferred_element_type=f32) * score_scale
        )
        probs = jnp.where(allowed, jnp.exp(scores - lse_blk[:, :, None]), 0.0)
        grad_probs = jnp.einsum("qhd,khd->hqk", grad_ctx_blk, values3, preferred_element_type=f32)
        grad_scores = (probs * (grad_probs - delta_blk[:, :, None])).astype(bf16)
        return (probs, grad_scores)

    zero_q = jnp.zeros((rows_dev, heads_col, HEAD), f32)
    keys_piece = lax.all_gather(keys_local, "row", axis=0, tiled=True)
    values_piece = lax.all_gather(values_local, "row", axis=0, tiled=True)
    piece_rows = keys_piece.shape[0]
    number, block_rows = key_split(piece_rows, rows_dev)
    keys4 = keys_piece.reshape(number, block_rows, heads_col, HEAD)
    values4 = values_piece.reshape(number, block_rows, heads_col, HEAD)
    piece_ids = block_ids.reshape(number, block_rows)

    def make_block_work(accum_q, block_item):
        keys3, values3, key_ids = block_item
        allowed = (key_ids[None, :] <= query_ids[:, None])[None]
        probs, grad_scores = score_grads(
            queries3, grad_ctx3, keys3, values3, allowed, log_mass, delta
        )
        accum_q = (
            accum_q
            + jnp.einsum("hqk,khd->qhd", grad_scores, keys3, preferred_element_type=f32)
            * score_scale
        )
        part_k = (
            jnp.einsum("hqk,qhd->khd", grad_scores, queries3, preferred_element_type=f32)
            * score_scale
        )
        part_v = jnp.einsum(
            "hqk,qhd->khd", probs.astype(bf16), grad_ctx3, preferred_element_type=f32
        )
        return (accum_q, (part_k, part_v))

    def block_skip(accum_q, block_item):
        empty = jnp.zeros((block_rows, heads_col, HEAD), f32)
        return (accum_q, (empty, empty))

    def make_block_step(accum_q, block_item):
        return lax.cond(
            block_item[2][0] > last_query, block_skip, make_block_work, accum_q, block_item
        )

    grad_q = zero_q
    grad_q, (parts_k, parts_v) = lax.scan(make_block_step, grad_q, (keys4, values4, piece_ids))
    parts_k = parts_k.reshape(piece_rows, feat_col)
    parts_v = parts_v.reshape(piece_rows, feat_col)
    grad_k_all = parts_k
    grad_v_all = parts_v
    back_result = (grad_q, grad_k_all, grad_v_all)
    grad_q3, grad_k_all, grad_v_all = back_result
    grad_keys, grad_values = (
        lax.psum_scatter(
            grad_k_all.astype(jnp.bfloat16), "row", scatter_dimension=0, tiled=True
        ).astype(jnp.float32),
        lax.psum_scatter(
            grad_v_all.astype(jnp.bfloat16), "row", scatter_dimension=0, tiled=True
        ).astype(jnp.float32),
    )
    queries_grad = grad_q3.reshape(rows_dev, feat_col).astype(bf16)
    keys_grad = grad_keys.astype(bf16)
    values_grad = grad_values.astype(bf16)
    g_b_query = jnp.sum(queries_grad.astype(f32), axis=0)
    g_b_value = jnp.sum(values_grad.astype(f32), axis=0)
    g_w_query_full = contract_first(input_whole, queries_grad)
    g_w_key_full = contract_first(input_whole, keys_grad)
    g_w_value_full = contract_first(input_whole, values_grad)
    grad_input_whole = (
        contract_last(queries_grad, wq_full)
        + contract_last(keys_grad, wk_full)
        + contract_last(values_grad, wv_full)
    )
    grad_input = (grad_hidden_one + sum_features(grad_input_whole)).astype(bf16)
    in_rows = w_query.shape[0]
    out_cols = w_output.shape[1]
    (
        sum_wq,
        sum_wk,
        sum_wv,
        sum_w1,
        sum_wo,
        sum_w2,
        g_w_pooler,
        g_b_pooler,
        g_w_classes,
        g_b_classes,
        g_b_query,
        g_b_value,
        g_b_output,
        g_ln1_gain,
        g_ln1_bias,
        g_b_inner,
        g_b_outer,
        g_ln2_gain,
        g_ln2_bias,
        logits_all,
    ) = lax.psum(
        (
            g_w_query_full,
            g_w_key_full,
            g_w_value_full,
            g_w_inner_full,
            g_w_output_full,
            g_w_outer_full,
            g_w_pooler * row_zero,
            g_b_pooler * row_zero,
            g_w_classes * row_zero,
            g_b_classes * row_zero,
            g_b_query,
            g_b_value,
            g_b_output,
            g_ln1_gain,
            g_ln1_bias,
            g_b_inner,
            g_b_outer,
            g_ln2_gain,
            g_ln2_bias,
            logits_table,
        ),
        ("dp", "row"),
    )
    row_start = row_index * in_rows
    col_start = row_index * out_cols
    g_w_query = lax.dynamic_slice_in_dim(sum_wq, row_start, in_rows, 0)
    g_w_key = lax.dynamic_slice_in_dim(sum_wk, row_start, in_rows, 0)
    g_w_value = lax.dynamic_slice_in_dim(sum_wv, row_start, in_rows, 0)
    g_w_inner = lax.dynamic_slice_in_dim(sum_w1, row_start, in_rows, 0)
    g_w_output = lax.dynamic_slice_in_dim(sum_wo, col_start, out_cols, 1)
    g_w_outer = lax.dynamic_slice_in_dim(sum_w2, col_start, out_cols, 1)
    logits = lax.dynamic_slice_in_dim(logits_all, seq_index, 1, 0)
    return (
        output,
        logits,
        grad_input,
        g_w_query,
        g_b_query,
        g_w_key,
        g_w_value,
        g_b_value,
        g_w_output,
        g_b_output,
        g_ln1_gain,
        g_ln1_bias,
        g_w_inner,
        g_b_inner,
        g_w_outer,
        g_b_outer,
        g_ln2_gain,
        g_ln2_bias,
        g_w_pooler,
        g_b_pooler,
        g_w_classes,
        g_b_classes,
    )


MESH_IDS = pl.DeviceIdType.MESH
ROWS = 4
VMEM_BYTES = 64000 * 1024


def place():
    return lax.axis_index("dp"), lax.axis_index("row"), lax.axis_index("col")


class Links:
    def __init__(self, send, recv):
        self.send, self.recv = send, recv
        self.sends, self.recvs, self.open = 0, 0, []

    def slots(self, count):
        base = self.recvs
        self.recvs += count
        return base

    def push(self, source, target, slot, device, when=None):
        copy = pltpu.make_async_remote_copy(
            src_ref=source,
            dst_ref=target,
            send_sem=self.send.at[self.sends],
            recv_sem=self.recv.at[slot],
            device_id=device,
            device_id_type=MESH_IDS,
        )
        self.sends += 1
        if when is None:
            copy.start()
        else:
            pl.when(when)(lambda: copy.start())
        self.open.append((copy, when))

    def arrive(self, target, slot, device, when=None):
        copy = pltpu.make_async_remote_copy(
            src_ref=target,
            dst_ref=target,
            send_sem=self.send.at[0],
            recv_sem=self.recv.at[slot],
            device_id=device,
            device_id_type=MESH_IDS,
        )
        if when is None:
            copy.wait_recv()
        else:
            pl.when(when)(lambda: copy.wait_recv())

    def drain(self):
        for copy, when in self.open:
            if when is None:
                copy.wait_send()
            else:
                pl.when(when)(lambda copy=copy: copy.wait_send())
        self.open = []


def meet(devices):
    barrier = pltpu.get_barrier_semaphore()
    for device in devices:
        pl.semaphore_signal(barrier, inc=1, device_id=device, device_id_type=MESH_IDS)
    pl.semaphore_wait(barrier, len(devices))


def within(value):
    return (value >= 0) & (value < ROWS)


def steps_of_line(row):
    for step in (1, 2, 3):
        for way in (1, -1):
            source = row - way * step
            yield step, way, (3 - step if way == 1 else step - 1), source, within(source)


def columns(col, width):
    return pl.ds(pl.multiple_of(col * width, 128), width)


IN_VMEM = pl.BlockSpec(memory_space=pltpu.VMEM)
IN_PLACE = pl.BlockSpec(memory_space=pl.ANY)


def comm_params(number):
    return pltpu.CompilerParams(
        collective_id=number, has_side_effects=True, vmem_limit_bytes=VMEM_BYTES
    )


TILE = 256
NEAR = 3


def nt(left, right):
    return lax.dot_general(
        left, right, (((1,), (1,)), ((), ())), preferred_element_type=jnp.float32
    )


def nn(left, right):
    return jnp.dot(left, right, preferred_element_type=jnp.float32)


def forward_kernel(
    widths, heads, x, cot, vec, wq, wk, wv, ids, labels, w_classes, b_classes, pooler_far, *refs
):
    count = len(widths)
    shards, refs = refs[:count], refs[count:]
    far_outs = refs[:7] + refs[12:13] + refs[10:11]
    (
        output, late, stream_out, _, branch_two_out, _, branch_one_out, context,
        grad_blocks, packed,
    ) = refs[7:17]
    fulls, refs = refs[17 : 17 + count], refs[17 + count :]
    (
        x_all, w_heads, q_out, kv_out, kt_out, mixed_out, lse_out, activ_out, grad_pre_out,
        cot_own, vec_all, context_in, vt_out, ids_col, packs, low_out, slope, total, w_pooler, send, recv, local,
    ) = refs
    near_outs = (x_all, w_heads, q_out, kv_out, kt_out, mixed_out, lse_out, activ_out, grad_pre_out)
    write_out = [
        pltpu.make_async_copy(near, far, local.at[count + 11 + n])
        for n, (near, far) in enumerate(zip(near_outs, far_outs))
    ]
    dp, row, col = place()
    links = Links(send, recv)
    low = x.dtype
    rows_dev, feat = x.shape
    wide = heads * HEAD
    mate = (dp, row, 1 - col)
    at_row = lambda other: (dp, other, col)
    at_dp = lambda flip: (dp ^ flip, row, col)
    home, side = row // 2, lax.rem(row, 2)
    mine = lax.rem(row + col, 2)
    half = rows_dev // 2
    meet([at_row(lax.rem(row + k, ROWS)) for k in (1, 2, 3)] + [at_dp(1), at_dp(2), mate])

    x_at = lambda k: x_all.at[k, :, columns(col, feat)]
    x_mate_at = lambda k: x_all.at[k, :, columns(1 - col, feat)]
    w_at = lambda i, k, q: fulls[i].at[k, q, :, columns(col, widths[i])]
    row_at = lambda i, k: fulls[i].at[k, :, :, columns(col, widths[i])]
    row_mate_at = lambda i, k: fulls[i].at[k, :, :, columns(1 - col, widths[i])]

    line_x, mate_x = links.slots(3), links.slots(4)
    line_q, first_q, second_q, mate_q = (
        links.slots(3), links.slots(3), links.slots(6), links.slots(1),
    )
    mate_cot, mate_vec, swap = links.slots(1), links.slots(1), links.slots(3)
    line_w = [links.slots(3) for _ in widths]
    first_w = [links.slots(3) for _ in widths]
    second_w = [links.slots(6) for _ in widths]
    mate_w = [links.slots(4) for _ in widths]
    steps = list(steps_of_line(row))
    at_step = lambda step: [entry[2:] for entry in steps if entry[0] == step]

    def relay(step, own, full, base, group=True):
        for way in (1, -1):
            held, onward = row - way * (step - 1), row + way
            ok = within(held) & within(onward) & group
            slot = 3 - step if way == 1 else step - 1
            links.push(own if step == 1 else full(held), full(held), base + slot, at_row(onward), ok)

    relay(1, x, x_at, line_x)
    links.push(x, x_at(row), mate_x, mate)
    for j in range(2):
        pieces = []
        for h in range(heads):
            part = slice(j * wide + h * HEAD, j * wide + (h + 1) * HEAD)
            pieces += [wk[:, part], wv[:, part]]
        pieces.append(wq[:, j * wide : (j + 1) * wide])
        packs[j] = jnp.concatenate(pieces, axis=1).reshape(packs.shape[1:])
    for j in range(2):
        k = 2 * col + j
        away = k != row
        slot = lax.rem(row - k + ROWS + 3, ROWS)
        links.push(packs.at[j, dp], w_heads.at[row, dp], line_q + slot, at_row(k), away)

        @pl.when(jnp.logical_not(away))
        def _(j=j):
            w_heads[row] = packs[j]

    links.push(
        cot.at[pl.ds(pl.multiple_of((1 - mine) * half, 128), half)],
        cot_own.at[:, columns(col, feat)],
        mate_cot,
        mate,
    )
    links.push(vec, vec_all.at[col], mate_vec, mate)
    vec_all[col] = vec[...]
    read_in = [
        pltpu.make_async_copy(x, x_at(row), local.at[count + 8]),
        pltpu.make_async_copy(
            cot.at[pl.ds(pl.multiple_of(mine * half, 128), half)],
            cot_own.at[:, columns(col, feat)],
            local.at[count + 9],
        ),
        pltpu.make_async_copy(pooler_far, w_pooler, local.at[count + 10]),
    ]
    for copy in read_in:
        copy.start()
    copies = [
        pltpu.make_async_copy(shards[i], row_at(i, row), local.at[i]) for i in range(count)
    ]

    at_home = home == col

    def q_first():
        for slot in range(3):
            k = lax.rem(row + slot + 1, ROWS)
            one = 1 + slot % 2
            links.arrive(w_heads.at[k, dp], line_q + slot, mate, at_home)
            links.push(
                w_heads.at[k, dp], w_heads.at[k, dp], first_q + slot, at_dp(one), at_home
            )

    def q_second():
        for slot in range(3):
            k = lax.rem(row + slot + 1, ROWS)
            one, two = 1 + slot % 2, 2 - slot % 2
            links.arrive(w_heads.at[k, dp ^ one], first_q + slot, mate, at_home)
            for n, q in enumerate((dp, dp ^ one)):
                links.push(
                    w_heads.at[k, q], w_heads.at[k, q], second_q + 2 * slot + n, at_dp(two), at_home
                )

    def q_mate():
        for slot in range(3):
            k = lax.rem(row + slot + 1, ROWS)
            two = 2 - slot % 2
            links.arrive(w_heads.at[k, dp ^ two], second_q + 2 * slot, mate, at_home)
            links.arrive(w_heads.at[k, dp ^ 3], second_q + 2 * slot + 1, mate, at_home)
        links.push(w_heads, w_heads, mate_q, mate, at_home)
        links.arrive(w_heads, mate_q, mate, jnp.logical_not(at_home))

    def x_step(step):
        for slot, k, ok in at_step(step):
            links.arrive(x_at(k), line_x + slot, mate, ok)
        if step < 3:
            relay(step + 1, x, x_at, line_x)
        for slot, k, ok in at_step(step):
            links.push(x_at(k), x_at(k), mate_x + 1 + slot, mate, ok)

    turn = lambda i, slot: (1, 2) if (i + slot) % 2 == 0 else (2, 1)

    def w_start(at_left, at_right):
        for way, ok in ((1, row == at_right), (-1, row == at_left)):
            slot = 2 if way == 1 else 0
            for i in range(count):
                links.push(
                    shards[i].at[dp], w_at(i, row, dp), line_w[i] + slot, at_row(row + way), ok
                )

    inner = (row == 1) | (row == 2)
    groups = {"i": inner, "o": jnp.logical_not(inner)}

    def w_first(step, group):
        for i in range(count):
            for slot, k, ok in at_step(step):
                links.arrive(w_at(i, k, dp), line_w[i] + slot, mate, ok & group)
            if step < 3:
                relay(step + 1, None, lambda k, i=i: w_at(i, k, dp), line_w[i], group)
            for slot, k, ok in at_step(step):
                one, two = turn(i, slot)
                links.push(
                    w_at(i, k, dp), w_at(i, k, dp), first_w[i] + slot, at_dp(one), ok & group
                )

    def w_second(step, group):
        for i in range(count):
            for slot, k, ok in at_step(step):
                one, two = turn(i, slot)
                links.arrive(w_at(i, k, dp ^ one), first_w[i] + slot, mate, ok & group)
                for n, q in enumerate((dp, dp ^ one)):
                    links.push(
                        w_at(i, k, q), w_at(i, k, q), second_w[i] + 2 * slot + n, at_dp(two),
                        ok & group,
                    )

    def w_mate(step, group, items):
        for i in items:
            for slot, k, ok in at_step(step):
                one, two = turn(i, slot)
                links.arrive(
                    w_at(i, k, dp ^ two), second_w[i] + 2 * slot, mate, ok & group
                )
                links.arrive(
                    w_at(i, k, dp ^ 3), second_w[i] + 2 * slot + 1, mate, ok & group
                )
                links.push(row_at(i, k), row_at(i, k), mate_w[i] + 1 + slot, mate, ok & group)

    def advance(point):
        for entry in FLOW[point]:
            step, group = int(entry[1]), groups[entry[2]]
            if entry[0] == "f":
                w_first(step, group)
            elif entry[0] == "s":
                w_second(step, group)
            else:
                w_mate(step, group, range(count))

    def w_ready(i):
        for entry in FLOW["end"]:
            w_mate(int(entry[1]), groups[entry[2]], (i,))
        copies[i].wait()
        links.arrive(row_mate_at(i, row), mate_w[i], mate)
        for slot in range(3):
            k = lax.rem(row + slot + 1, ROWS)
            links.arrive(row_mate_at(i, k), mate_w[i] + 1 + slot, mate)

    row_tiles = ROWS * rows_dev // TILE
    per_row = rows_dev // TILE

    def split_ids(step, carry):
        span = pl.ds(pl.multiple_of(step * TILE, TILE), TILE)
        ids_col[span] = jnp.broadcast_to(ids[:, span], (8, TILE)).T[:, :1]
        return carry

    lax.fori_loop(0, row_tiles, split_ids, 0)
    w_start(3, 0)
    x_step(1)
    w_start(2, 1)
    q_first()
    x_step(2)
    w_start(1, 2)
    q_second()
    for copy in copies:
        copy.start()
    for i in range(count):
        links.push(shards[i], row_at(i, row), mate_w[i], mate)
    q_mate()
    links.arrive(vec_all.at[1 - col], mate_vec, mate)
    bias_of = lambda n: jnp.where(
        side == 0, vec_all[home, n : n + 1, :wide], vec_all[home, n : n + 1, wide : 2 * wide]
    )
    bias_q, bias_v = bias_of(0), bias_of(1)
    blank = jnp.zeros((1, HEAD), jnp.float32)
    bias_kv = jnp.concatenate(
        sum([[blank, bias_v[:, h * HEAD : (h + 1) * HEAD]] for h in range(heads)], []), axis=1
    )
    weights = lambda start, stop: w_heads[:, :, :, start:stop].reshape(2 * feat, stop - start)

    def project_keys(k):
        def one_tile(step, carry):
            here = pl.ds(pl.multiple_of(step * TILE, TILE), TILE)
            rows = pl.ds(pl.multiple_of(k * rows_dev + step * TILE, TILE), TILE)
            both = nn(x_all[k, here], weights(0, 2 * wide)) + bias_kv
            both_t = both.T
            for h in range(heads):
                at = 2 * h * HEAD
                kv_out[h, rows] = both[:, at : at + 2 * HEAD].astype(low)
                kt_out[h, :, rows] = both_t[at : at + HEAD].astype(low)
                vt_out[h, :, rows] = both_t[at + HEAD : at + 2 * HEAD].astype(low)
            return carry

        lax.fori_loop(0, per_row, one_tile, 0)

    links.arrive(x_mate_at(row), mate_x, mate)
    read_in[0].wait()
    project_keys(row)
    advance("x2")
    x_step(3)
    for slot in (0, 2, 1):
        k = lax.rem(row + slot + 1, ROWS)
        links.arrive(x_mate_at(k), mate_x + 1 + slot, mate)
        project_keys(k)

    def project_query(j, carry):
        block = 2 * j + lax.rem(j + col, 2)
        here = pl.ds(pl.multiple_of(lax.rem(block, per_row) * TILE, TILE), TILE)
        query = nn(x_all[block // per_row, here], weights(2 * wide, 3 * wide)) + bias_q
        query = query.astype(low) * jnp.asarray(HEAD**-0.5, low)
        for h in range(heads):
            q_out[h, j] = jnp.concatenate(
                [query[:, h * HEAD : (h + 1) * HEAD], jnp.zeros((TILE, HEAD), low)], axis=1
            )
        return carry

    blocks = row_tiles // 2
    lax.fori_loop(0, blocks, project_query, 0)
    for copy in write_out[:5]:
        copy.start()
    advance("pq")
    for j in range(blocks):
        block = 2 * j + lax.rem(j + col, 2)
        rows = pl.ds(pl.multiple_of(block * TILE, TILE), TILE)
        query_ids = ids[:, rows]
        length = min(2 * j + NEAR, row_tiles) * TILE
        clear = 2 * j * TILE

        def one_head(h, carry, j=j, query_ids=query_ids, length=length, clear=clear):
            scores = nt(kv_out[h, :length], q_out[h, j])
            near = jnp.where(
                ids_col[clear:length] <= query_ids, scores[clear:], masked_score
            )
            top = jnp.max(near, axis=0, keepdims=True)
            if clear:
                top = jnp.maximum(top, jnp.max(scores[:clear], axis=0, keepdims=True))
                weights_far = jnp.exp(scores[:clear] - top)
            weights_near = jnp.exp(near - top)
            mass = jnp.sum(weights_near, axis=0, keepdims=True)
            value = nn(vt_out[h, :, clear:length], weights_near.astype(low))
            if clear:
                mass = mass + jnp.sum(weights_far, axis=0, keepdims=True)
                value = value + nn(vt_out[h, :, :clear], weights_far.astype(low))
            mixed_out[j, h] = value / mass
            lse_out[j, h] = top + jnp.log(mass)
            return carry

        lax.fori_loop(0, heads, one_head, 0)
        low_out[j] = (
            jnp.concatenate([mixed_out[j, h] for h in range(heads)], axis=0).T.astype(low)
        )
        away = row != j
        slot = lax.rem(row - j + ROWS + 3, ROWS)
        links.push(low_out.at[j], context_in.at[row], swap + slot, at_row(j), away)

        @pl.when(jnp.logical_not(away))
        def _(j=j):
            context_in[row] = low_out[j]

        advance("a%d" % j)

    for copy in write_out[5:7]:
        copy.start()
    f32 = jnp.float32
    own, features = output.shape
    hidden = 2 * widths[1]
    chunk = features
    w_o, w_1, w_2 = fulls
    part_of = lambda full, span: full[:, :, :, span].reshape(features, span.stop - span.start)
    vector = lambda n: jnp.concatenate([vec_all[0, n : n + 1], vec_all[1, n : n + 1]], axis=1)
    links.arrive(cot_own.at[:, columns(1 - col, feat)], mate_cot, mate)
    read_in[1].wait()
    read_in[2].wait()
    for slot in range(3):
        links.arrive(context_in.at[lax.rem(row + slot + 1, ROWS)], swap + slot, mate)
    context[...] = jnp.concatenate([context_in[r] for r in range(ROWS)], axis=1)
    w_ready(0)
    value = nt(context[...], w_o[...].reshape(features, features))
    own_rows = pl.ds(pl.multiple_of(mine * own, 128), own)
    hidden_one = x_all[row, own_rows].astype(f32) + value + vector(2)
    gain_one, gain_two = vector(3), vector(6)
    stream, normed_one, inv_one = norm_rows(hidden_one, gain_one, vector(4))
    late[...] = stream
    stream_out[...] = stream.astype(low)
    total[...] = jnp.zeros_like(total)
    bias_1 = [
        jnp.concatenate(
            [vec_all[c, 8 + 2 * n : 9 + 2 * n], vec_all[c, 9 + 2 * n : 10 + 2 * n]], axis=1
        )
        for c in range(2)
        for n in range(hidden // chunk // 2)
    ]
    w_ready(1)
    for n in range(hidden // chunk):
        span = slice(n * chunk, (n + 1) * chunk)
        pre_act = nn(stream_out[...], part_of(w_1, span)) + bias_1[n]
        half = 0.5 * (1.0 + lax.erf(pre_act * root_half))
        slope[:, span] = half + pre_act * inv_root_tau * jnp.exp(-0.5 * pre_act * pre_act)
        activ_out[:, span] = (pre_act * half).astype(low)
    write_out[7].start()
    w_ready(2)
    for n in range(hidden // chunk):
        span = slice(n * chunk, (n + 1) * chunk)
        total[...] += nt(activ_out[:, span], part_of(w_2, span))
    hidden_two = late[...] + total[...] + vector(5)
    result, normed_two, inv_two = norm_rows(hidden_two, gain_two, vector(7))
    output[...] = result.astype(low)

    classes = b_classes.shape[1]
    first = output[:8]
    pooled = jnp.tanh(nn(first, w_pooler[...])[:1] + jnp.concatenate([vec_all[0, 12:13], vec_all[0, 13:14]], axis=1))
    lane = lax.broadcasted_iota(jnp.int32, (1, 128), 1)
    logits = jnp.full((1, 128), masked_score, f32)
    rows = [w_classes[n : n + 1].astype(f32) for n in range(classes)]
    for n in range(classes):
        logit = jnp.sum(pooled * rows[n], axis=1, keepdims=True) + b_classes[:, n : n + 1].astype(f32)
        logits = jnp.where(lane == n, logit, logits)
    odds = jnp.exp(logits - jnp.max(logits, axis=1, keepdims=True))
    odds = odds / jnp.sum(odds, axis=1, keepdims=True)
    grad_logits = odds - (lane == labels[0, 0]).astype(f32)
    grad_pool = jnp.zeros((1, features), f32)
    for n in range(classes):
        grad_pool = grad_pool + grad_logits[:, n : n + 1] * rows[n]
    grad_pool = grad_pool * (1.0 - pooled * pooled)
    high = grad_pool.astype(low)
    rest = grad_pool - high.astype(f32)
    mid = rest.astype(low)
    last = (rest - mid.astype(f32)).astype(low)
    split = jnp.concatenate(
        [high.astype(f32), mid.astype(f32), last.astype(f32), jnp.zeros((5, features), f32)]
    ).astype(low)
    grad_first = jnp.sum(nt(split, w_pooler[...]), axis=0, keepdims=True)
    holder = ((row == 0) & (col == 0)).astype(f32)
    top = (lax.broadcasted_iota(jnp.int32, (own, 1), 0) == 0).astype(f32) * holder
    grad_result = cot_own[...].astype(f32) + top * grad_first

    tokens = lambda values: jnp.sum(values, axis=0, keepdims=True)
    g_gain_two, g_shift_two = tokens(grad_result * normed_two), tokens(grad_result)
    grad_two = norm_rows_back(grad_result, normed_two, inv_two, gain_two)
    g_bias_two = tokens(grad_two)
    late[...] = grad_two
    branch_two_out[...] = grad_two.astype(low)
    total[...] = jnp.zeros_like(total)
    g_bias_one = []
    for n in range(hidden // chunk):
        span = slice(n * chunk, (n + 1) * chunk)
        grad_pre = (nn(branch_two_out[...], part_of(w_2, span)) * slope[:, span]).astype(low)
        grad_pre_out[:, span] = grad_pre
        g_bias_one.append(tokens(grad_pre.astype(f32)))
        total[...] += nt(grad_pre_out[:, span], part_of(w_1, span))
    write_out[8].start()
    grad_stream = late[...] + total[...]
    g_gain_one, g_shift_one = tokens(grad_stream * normed_one), tokens(grad_stream)
    grad_one = norm_rows_back(grad_stream, normed_one, inv_one, gain_one)
    late[...] = grad_one
    branch_one_out[...] = grad_one.astype(low)
    grad_context = nn(branch_one_out[...], w_o[...].reshape(features, features)).astype(low)
    for r in range(ROWS):
        grad_blocks[r] = grad_context[:, r * wide : (r + 1) * wide]

    packed[...] = jnp.zeros_like(packed)
    vectors = [tokens(grad_one), g_gain_one, g_shift_one, g_bias_two, g_gain_two, g_shift_two]
    for n, value in enumerate(vectors):
        for c in range(2):
            packed[8 + 8 * c + n // 2, pl.ds((n % 2) * feat, feat)] = value[
                0, c * feat : (c + 1) * feat
            ]
    for n, value in enumerate(g_bias_one):
        packed[8 + 8 * (n // 2) + 3 + n % 2] = value[0]
    spare = jnp.zeros((1, features - 128), f32)
    shifted = pltpu.roll(jnp.where(lane < classes, grad_logits, 0.0), classes, 1)
    tail = jnp.concatenate([jnp.where(lane < classes, logits, shifted), spare], axis=1)
    for n, value in enumerate((first[:1].astype(f32), grad_pool, pooled, tail)):
        packed[24 + n : 25 + n] = value * holder
    for copy in write_out:
        copy.wait()
    links.drain()


def forward_links(x, cot, vec, wq, wk, wv, ids, labels, w_classes, b_classes, w_pooler, shards):
    widths = [shard.shape[1] for shard in shards]
    rows, feat = x.shape
    low, f32 = x.dtype, jnp.float32
    part = shards[0].shape[0] // 4
    features, hidden = 2 * feat, 2 * widths[1]
    heads = features // HEAD // ROWS
    wide = heads * HEAD
    length, own = ROWS * rows, rows // 2
    blocks = length // TILE // 2
    shape = jax.ShapeDtypeStruct
    narrow, broad = shape((own, features), low), shape((own, hidden), low)
    shapes = [
        shape((ROWS, rows, features), low),
        shape((ROWS, 4, part, 3 * wide), low),
        shape((heads, blocks, TILE, 2 * HEAD), low),
        shape((heads, length, 2 * HEAD), low),
        shape((heads, HEAD, length), low),
        shape((blocks, heads, HEAD, TILE), f32),
        shape((blocks, heads, 1, TILE), f32),
        narrow, shape((own, features), f32), narrow, broad, narrow, broad, narrow, narrow,
        shape((ROWS, own, wide), low), shape((32, features), f32),
    ]
    return pl.pallas_call(
        functools.partial(forward_kernel, widths, heads),
        out_shape=shapes,
        in_specs=[IN_PLACE] * 2 + [IN_VMEM] * 5 + [pl.BlockSpec(memory_space=pltpu.SMEM)]
        + [IN_VMEM] * 2 + [IN_PLACE] * (1 + len(shards)),
        out_specs=[IN_PLACE] * 7 + [IN_VMEM] * 3 + [IN_PLACE, IN_VMEM, IN_PLACE] + [IN_VMEM] * 4,
        scratch_shapes=[pltpu.VMEM((ROWS, 4, part, 2 * width), low) for width in widths]
        + [pltpu.VMEM(out.shape, out.dtype) for out in shapes[:7] + [broad, broad]]
        + [
            pltpu.VMEM((own, features), low),
            pltpu.VMEM((2,) + vec.shape, f32),
            pltpu.VMEM((ROWS, own, wide), low),
            pltpu.VMEM((heads, HEAD, length), low),
            pltpu.VMEM((length, 1), jnp.int32),
            pltpu.VMEM((2, 4, part, 3 * wide), low),
            pltpu.VMEM((blocks, TILE, wide), low),
            pltpu.VMEM((own, hidden), f32),
            pltpu.VMEM((own, features), f32),
            pltpu.VMEM(w_pooler.shape, low),
            pltpu.SemaphoreType.DMA((256,)),
            pltpu.SemaphoreType.DMA((96,)),
            pltpu.SemaphoreType.DMA((24,)),
        ],
        compiler_params=comm_params(1),
        name="forward_links",
    )(
        x, cot, vec, wq, wk, wv, ids.reshape(1, -1), labels.reshape(1, 1), w_classes.T,
        b_classes.reshape(1, -1), w_pooler, *[shard.reshape(4, part, -1) for shard in shards],
    )


def add_into(total, *others):
    def one(step, carry):
        value = total[step].astype(jnp.float32)
        for other in others:
            value = value + other[step].astype(jnp.float32)
        total[step] = value.astype(total.dtype)
        return carry

    lax.fori_loop(0, total.shape[0], one, 0)


CHUNK = 384
FLOW = {
    "x2": ("f1i",),
    "pq": ("f2i", "s1i",),
    "a0": ("s2i",),
    "a1": ("m1i", "f1o",),
    "a2": ("m2i", "f2o", "s1o",),
    "a3": ("f3o", "s2o", "m1o", "s3o", "m2o",),
    "end": ("m3o",),
}
PLAN = (
    "g0",
    "g1",
    "r0",
    "c0",
    "g2",
    "g3",
    "c1",
    "g4",
    "d0",
    "a0",
    "s0",
    "s1",
    "c2",
    "a1",
    "c3",
    "a2",
    "c4",
    "a3",
    "l1",
    "l0",
    "w0",
    "h1",
    "h0",
    "s2",
    "s3",
    "q0",
    "t0",
    "t1",
    "x0",
    "s4",
    "t2",
    "l2",
    "x1",
    "l3",
    "t3",
    "f0",
    "f1",
    "v0",
    "l4",
    "x2",
    "n0",
    "n1",
    "v1",
    "h2",
    "q1",
    "h3",
    "h4",
    "k0",
    "v2",
    "s5",
    "v3",
    "f2",
    "f3",
    "f4",
    "x3",
    "q2",
    "n2",
    "n3",
    "n4",
    "n5",
    "k1",
    "v4",
)


def backward_kernel(
    heads, blocks_in, output, late_far, stream, pre_far, branch_two, activ_far, branch_one, context,
    q_far, kv_far, kt_far, mixed_far, lse_far, ids, x_far, w_far, vec_in, *refs,
):
    out_g, refs = refs[:5], refs[5:]
    out_q, out_x, halves, vec, refs = refs[0], refs[1], refs[2], refs[3], refs[4:]
    pairs, refs = refs[:5], refs[5:]
    mates, refs = refs[:5], refs[5:]
    first, refs = refs[:6], refs[6:]
    second, refs = refs[:6], refs[6:]
    lines, refs = refs[:5], refs[5:]
    (
        grad_ctx, both, delta, dq, dkv, grads, grads_t, w_t, turned, ids_col, dx, sum_x,
        line_x, gq, sum_q, all_q, vec_own, vec_mate, vec_line, vec_flat, vec_table,
        w_heads, q, kv, kt, mixed, lse, x_all, grad_pre, activ, late, send, recv, local,
    ) = refs
    nears = (w_heads, q, kv, kt, mixed, lse, x_all, grad_pre, activ, late)
    fars = (w_far, q_far, kv_far, kt_far, mixed_far, lse_far, x_far, pre_far, activ_far, late_far)
    reads = [
        pltpu.make_async_copy(far, near, local.at[n]) for n, (far, near) in enumerate(zip(fars, nears))
    ]
    for n in (7, 8, 0, 1, 2, 3, 4, 5, 6, 9):
        reads[n].start()
    dp, row, col = place()
    links = Links(send, recv)
    low, f32 = q.dtype, jnp.float32
    mate = (dp, row, 1 - col)
    peers = [lax.rem(row + n, ROWS) for n in (1, 2, 3)]
    at_row = lambda other: (dp, other, col)
    at_dp = lambda flip: (dp ^ flip, row, col)
    home, side = row // 2, lax.rem(row, 2)
    mine = lax.rem(row + col, 2)
    length = kv.shape[1]
    wide = heads * HEAD
    rows_dev, feat = out_x.shape
    half = rows_dev // 2
    row_tiles = length // TILE
    blocks = row_tiles // 2
    meet(
        [at_row(peer) for peer in peers]
        + [at_dp(1), at_dp(2), mate]
        + [(dp, peer, 1 - col) for peer in peers]
    )

    swap, slot_o = links.slots(3), links.slots(1)
    for n, peer in enumerate(peers):
        links.push(blocks_in.at[peer], grad_ctx.at[row], swap + 2 - n, at_row(peer))
    own_rows = pl.ds(pl.multiple_of(mine * half, 128), half)
    other_rows = pl.ds(pl.multiple_of((1 - mine) * half, 128), half)
    links.push(output.at[:, columns(1 - col, feat)], halves.at[own_rows], slot_o, mate)
    reads += [
        pltpu.make_async_copy(output.at[:, columns(col, feat)], halves.at[own_rows], local.at[10]),
        pltpu.make_async_copy(blocks_in.at[row], grad_ctx.at[row], local.at[11]),
    ]
    reads[10].start()
    reads[11].start()

    lefts = (stream, branch_two, branch_one)
    for n in range(3):
        turned[n] = lefts[n][...].astype(f32).T.astype(low)
    feeds = [(0, grad_pre, 0), (1, activ, 0), (0, grad_pre, 1), (1, activ, 1), (2, context, 0)]
    turns = [(1, 2), (2, 1), (1, 2), (2, 1), (1, 2), (2, 1)]
    widths = [out.shape[2] for out in out_g]
    slot_g = [links.slots(1) for _ in widths]

    def local_grad(i):
        if i < 2:
            reads[7 + i].wait()
        left, right, part = feeds[i]
        width = widths[i]
        per = width // CHUNK

        def one(step, carry):
            which, n = step // per, step % per
            core = jnp.where(which == 0, 1 - col, col)
            start = core * (right.shape[1] // 2) + part * width + n * CHUNK
            value = nn(turned[left], right[:, pl.ds(pl.multiple_of(start, 128), CHUNK)])
            pairs[i][which, :, :, :, pl.ds(pl.multiple_of(n * CHUNK, 128), CHUNK)] = (
                value.astype(low).reshape(pairs[i].shape[1:4] + (CHUNK,))
            )
            return carry

        lax.fori_loop(0, 2 * per, one, 0)
        links.push(pairs[i].at[0], mates[i], slot_g[i], mate)

    totals = [pair.at[1] for pair in pairs] + [all_q]

    def send_first(i):
        one, two = turns[i]
        base = links.slots(2)
        links.push(totals[i].at[:, dp ^ 3], first[i].at[1], base + 1, at_dp(one))
        links.push(totals[i].at[:, dp ^ one], first[i].at[0], base, at_dp(one))
        return base

    def join(i):
        links.arrive(mates[i], slot_g[i], mate)

        def one(step, carry):
            at, q_at = step // 4, step % 4
            pairs[i][1, at, q_at] = (
                pairs[i][1, at, q_at].astype(f32) + mates[i][at, q_at].astype(f32)
            ).astype(low)
            return carry

        lax.fori_loop(0, 16, one, 0)
        stage[i] = send_first(i)

    def send_second(i):
        one, two = turns[i]
        base = stage[i]
        links.arrive(first[i].at[1], base + 1, mate)
        add_into(totals[i].at[:, dp ^ two], first[i].at[1])
        slot = links.slots(1)
        links.push(totals[i].at[:, dp ^ two], second[i], slot, at_dp(two))
        stage[i] = (base, slot)

    def send_line(i):
        links.arrive(first[i].at[0], stage[i][0], mate)
        links.arrive(second[i], stage[i][1], mate)
        add_into(totals[i].at[:, dp], first[i].at[0], second[i])
        base = links.slots(3)
        links.push(totals[i].at[row ^ 3, dp], lines[i].at[1], base + 1, at_row(row ^ 1))
        links.push(totals[i].at[row ^ 1, dp], lines[i].at[0], base, at_row(row ^ 1))
        stage[i] = base

    def halve_line(i):
        links.arrive(lines[i].at[1], stage[i] + 1, mate)
        pairs[i][1, row ^ 2, dp] = (
            pairs[i][1, row ^ 2, dp].astype(f32) + lines[i][1].astype(f32)
        ).astype(low)
        links.push(totals[i].at[row ^ 2, dp], lines[i].at[2], stage[i] + 2, at_row(row ^ 2))

    def share(i, out):
        one, two = turns[i]
        base = links.slots(3)
        links.push(out.at[dp], out.at[dp], base, at_dp(two))
        links.push(out.at[dp], out.at[dp], base + 1, at_dp(one))
        return base

    def share_on(i, out, base):
        one, two = turns[i]
        links.arrive(out.at[dp ^ two], base, mate)
        links.push(out.at[dp ^ two], out.at[dp ^ two], base + 2, at_dp(one))

    def shared(i, out, base):
        one, two = turns[i]
        links.arrive(out.at[dp ^ one], base + 1, mate)
        links.arrive(out.at[dp ^ 3], base + 2, mate)

    stage = [None] * 6
    slot_x, slot_xl = links.slots(4), links.slots(3)
    slot_q, slot_ql = links.slots(1), links.slots(4)
    slot_v, slot_vl, slot_vd = links.slots(1), links.slots(3), links.slots(5)
    order = (row ^ 3, row ^ 1, row ^ 2, row)
    per_row = rows_dev // TILE
    own_block = 2 * row + mine
    own_part = all_q.at[side, pl.ds(2 * col, 2)]
    at_home = home == col
    sums = {}

    def split_ids(step, carry):
        span = pl.ds(pl.multiple_of(step * TILE, TILE), TILE)
        ids_col[span] = jnp.broadcast_to(ids[:, span], (8, TILE)).T[:, :1]
        return carry

    def split_grad(j, carry):
        grad = grad_ctx[j]
        grad_t = grad.astype(f32).T
        for h in range(heads):
            part = slice(h * HEAD, (h + 1) * HEAD)
            both[h, j, :TILE] = q[h, j]
            both[h, j, TILE:] = jnp.concatenate(
                [jnp.zeros((TILE, HEAD), low), grad[:, part]], axis=1
            )
            delta[h, j] = jnp.sum(grad_t[part] * mixed[j, h], axis=0, keepdims=True)
        return carry

    def ready():
        reads[0].wait()
        w_t[...] = w_heads[...].reshape(2 * feat, 3 * wide).astype(f32).T.astype(low)
        lax.fori_loop(0, row_tiles, split_ids, 0)
        dkv[...] = jnp.zeros_like(dkv)

    def take_context():
        for n, peer in enumerate(peers):
            links.arrive(grad_ctx.at[peer], swap + n, mate)
        for copy in reads[1:6] + reads[11:]:
            copy.wait()
        lax.fori_loop(0, blocks, split_grad, 0)

    def attend_back(j):
        block = 2 * j + lax.rem(j + col, 2)
        rows = pl.ds(pl.multiple_of(block * TILE, TILE), TILE)
        query_ids = ids[:, rows]
        far = 2 * j * TILE
        spans = ([(0, far)] if far else []) + [(far, min(2 * j + NEAR, row_tiles) * TILE)]

        def one_head(h, carry, j=j, query_ids=query_ids, far=far, spans=spans):
            total = jnp.zeros((HEAD, TILE), f32)
            for start, stop in spans:
                raw = nt(kv[h, start:stop], both[h, j])
                probs = jnp.exp(raw[:, :TILE] - lse[j, h])
                if start == far:
                    probs = jnp.where(ids_col[start:stop] <= query_ids, probs, 0.0)
                grad_scores = (probs * (raw[:, TILE:] - delta[h, j])).astype(low)
                dkv[h, start:stop] += nn(
                    jnp.concatenate([grad_scores, probs.astype(low)], axis=1), both[h, j]
                )
                total = total + nn(kt[h, :, start:stop], grad_scores)
            dq[j, h] = total * HEAD**-0.5
            return carry

        lax.fori_loop(0, heads, one_head, 0)

    def gather_q(j, carry):
        block = 2 * j + lax.rem(j + col, 2)
        rows = pl.ds(pl.multiple_of(block * TILE, TILE), TILE)
        other = pl.ds(pl.multiple_of((4 * j + 1 - block) * TILE, TILE), TILE)
        value = jnp.concatenate([dq[j, h] for h in range(heads)], axis=0)
        grads_t[2 * wide :, rows] = value.astype(low)
        grads_t[2 * wide :, other] = jnp.zeros((wide, TILE), low)
        grads[rows, 2 * wide :] = value.T.astype(low)
        grads[other, 2 * wide :] = jnp.zeros((TILE, wide), low)
        return carry + jnp.sum(value.T, axis=0, keepdims=True)

    def gather_kv(step, carry):
        rows = pl.ds(pl.multiple_of(step * TILE, TILE), TILE)
        value = jnp.concatenate([dkv[h, rows] for h in range(heads)], axis=1)
        grads[rows, : 2 * wide] = value.astype(low)
        grads_t[: 2 * wide, rows] = value.T.astype(low)
        return carry + jnp.sum(value, axis=0, keepdims=True)

    def weight_grads():
        reads[6].wait()
        reads[9].wait()
        reads[10].wait()
        sums["q"] = lax.fori_loop(0, blocks, gather_q, jnp.zeros((1, wide), f32))
        sums["kv"] = lax.fori_loop(0, row_tiles, gather_kv, jnp.zeros((1, 2 * wide), f32))
        for n in range(2):
            span = slice(n * CHUNK, (n + 1) * CHUNK)
            value = nn(grads_t[...], x_all[:, :, span].reshape(length, CHUNK)).T
            gq[2 * n : 2 * n + 2] = value.astype(low).reshape((2,) + gq.shape[1:])
        links.push(gq.at[:, 1 - col], sum_q, slot_q, mate)

    def token_grads(at):
        def one(step, carry):
            here = pl.ds(pl.multiple_of(step * TILE, TILE), TILE)
            rows = pl.ds(pl.multiple_of((at * per_row + step) * TILE, TILE), TILE)
            value = nn(grads[rows], w_t[...])
            is_own = (at * per_row + step == own_block).astype(f32)
            dx[at, here] = (value + late[...] * is_own).astype(low)
            return carry

        lax.fori_loop(0, per_row, one, 0)

    def send_tokens(n):
        token_grads(order[n])
        links.push(
            dx.at[order[n], :, columns(1 - col, feat)], sum_x.at[order[n]], slot_x + n, mate
        )

    def join_x(at, slot):
        links.arrive(sum_x.at[at], slot, mate)

        def one(step, carry):
            here = pl.ds(pl.multiple_of(step * 128, 128), 128)
            sum_x[at, here] = (
                sum_x[at, here].astype(f32) + dx[at, here, columns(col, feat)].astype(f32)
            ).astype(low)
            return carry

        lax.fori_loop(0, rows_dev // 128, one, 0)

    def line_tokens(n):
        join_x(order[n], slot_x + n)
        if n < 2:
            links.push(sum_x.at[order[n]], line_x.at[1 - n], slot_xl + 1 - n, at_row(row ^ 1))

    def halve_x(step, carry):
        rows = pl.ds(pl.multiple_of(step * 128, 128), 128)
        sum_x[row ^ 2, rows] = (
            sum_x[row ^ 2, rows].astype(f32) + line_x[1, rows].astype(f32)
        ).astype(low)
        return carry

    def halve_tokens():
        links.arrive(line_x.at[1], slot_xl + 1, mate)
        lax.fori_loop(0, rows_dev // 128, halve_x, 0)
        links.push(sum_x.at[row ^ 2], line_x.at[2], slot_xl + 2, at_row(row ^ 2))

    def finish_x(step, carry):
        rows = pl.ds(pl.multiple_of(step * 128, 128), 128)
        value = sum_x[row, rows].astype(f32)
        for n in (0, 2):
            value = value + line_x[n, rows].astype(f32)
        out_x[rows] = value.astype(low)
        return carry

    def finish_tokens():
        for n in (0, 2):
            links.arrive(line_x.at[n], slot_xl + n, mate)
        lax.fori_loop(0, rows_dev // 128, finish_x, 0)

    def add_q(step, carry):
        sum_q[step] = (sum_q[step].astype(f32) + gq[step, col].astype(f32)).astype(low)
        return carry

    def keep_own():
        own_part[...] = sum_q[row]

    def line_q():
        links.arrive(sum_q, slot_q, mate)
        lax.fori_loop(0, ROWS, add_q, 0)
        pl.when(at_home)(keep_own)
        slot = slot_ql + 2 * side + col
        links.push(sum_q.at[row], own_part, slot, mate, jnp.logical_not(at_home))
        for peer in peers:
            links.push(sum_q.at[peer], own_part, slot, (dp, peer, home))

    def first_q():
        for j in range(2):
            for e in range(2):
                here = (row == 2 * col + j) & (col == e)
                links.arrive(
                    all_q.at[j, pl.ds(2 * e, 2)], slot_ql + 2 * j + e, mate, jnp.logical_not(here)
                )
        stage[5] = send_first(5)

    def finish_q():
        links.arrive(first[5].at[0], stage[5][0], mate)
        links.arrive(second[5], stage[5][1], mate)
        add_into(all_q.at[:, dp], first[5].at[0], second[5])
        for j in range(2):
            out_q[dp, j] = all_q[j, dp]
        stage[5] = share(5, out_q)

    def finish_line(i):
        for n in (0, 2):
            links.arrive(lines[i].at[n], stage[i] + n, mate)
        value = pairs[i][1, row, dp].astype(f32)
        for n in (0, 2):
            value = value + lines[i][n].astype(f32)
        out_g[i][dp] = value.astype(low)
        stage[i] = share(i, out_g[i])

    def sums_mate():
        value = jnp.concatenate(
            [sums["kv"], sums["q"], jnp.zeros((1, 2 * feat - 3 * wide), f32)], axis=1
        )
        here = lax.broadcasted_iota(jnp.int32, (8, 2 * feat), 0) == 5 + side
        for c in range(2):
            part = vec_in[8 + 8 * c : 16 + 8 * c] + jnp.where(here & (home == c), value, 0.0)
            vec_own[jnp.where(col == c, 0, 1), :8] = part
        vec_own[0, 8:] = vec_in[24:]
        vec_own[1, 8:] = vec_in[24:]
        links.push(vec_own.at[1], vec_mate, slot_v, mate)

    def sums_line():
        links.arrive(vec_mate, slot_v, mate)
        vec_mate[...] = vec_own[0] + vec_mate[...]
        for n, peer in enumerate(peers):
            links.push(vec_mate, vec_line.at[2 - n], slot_vl + 2 - n, at_row(peer))

    def sums_first():
        for n in range(3):
            links.arrive(vec_line.at[n], slot_vl + n, mate)
        vec_sum = vec_mate[...] + vec_line[0] + vec_line[1] + vec_line[2]
        vec_flat[2] = vec_sum[:8]
        vec_table[dp] = vec_sum[8:]
        links.push(vec_flat.at[2], vec_flat.at[0], slot_vd, at_dp(1))
        links.push(vec_table.at[dp], vec_table.at[dp], slot_vd + 1, at_dp(1))
        links.push(vec_table.at[dp], vec_table.at[dp], slot_vd + 2, at_dp(2))

    def sums_second():
        links.arrive(vec_flat.at[0], slot_vd, mate)
        vec_flat[3] = vec_flat[2] + vec_flat[0]
        links.push(vec_flat.at[3], vec_flat.at[1], slot_vd + 3, at_dp(2))
        links.arrive(vec_table.at[dp ^ 1], slot_vd + 1, mate)
        links.push(vec_table.at[dp ^ 1], vec_table.at[dp ^ 1], slot_vd + 4, at_dp(2))

    def sums_last():
        links.arrive(vec_flat.at[1], slot_vd + 3, mate)
        links.arrive(vec_table.at[dp ^ 2], slot_vd + 2, mate)
        links.arrive(vec_table.at[dp ^ 3], slot_vd + 4, mate)
        vec[:8] = vec_flat[3] + vec_flat[1]
        for n in range(4):
            vec[8 + 8 * n : 16 + 8 * n] = vec_table[n]

    def out_of(i):
        return out_q if i == 5 else out_g[i]

    work = {
        "g": local_grad, "c": join, "s": send_second, "l": send_line, "h": halve_line,
        "f": finish_line, "n": lambda i: share_on(i, out_of(i), stage[i]),
        "r": lambda _: ready(), "d": lambda _: take_context(), "a": attend_back,
        "w": lambda _: weight_grads(), "t": send_tokens, "x": line_tokens,
        "k": lambda n: (halve_tokens, finish_tokens)[n](),
        "q": lambda n: (line_q, first_q, finish_q)[n](),
        "v": lambda n: (sums_mate, sums_line, sums_first, sums_second, sums_last)[n](),
    }
    for entry in PLAN:
        work[entry[0]](int(entry[1]))
    for i in range(6):
        shared(i, out_of(i), stage[i])
    links.arrive(halves.at[other_rows], slot_o, mate)
    links.drain()


def backward_links(
    grad_blocks, output, late, stream, grad_pre, branch_two, activ, branch_one, context,
    q, kv, kt, mixed, lse, ids, x_all, w_heads, vec,
):
    low, f32 = q.dtype, jnp.float32
    heads, length = kv.shape[0], kv.shape[1]
    wide = heads * HEAD
    own, features = output.shape
    hidden = activ.shape[1]
    part = features // ROWS // 4
    widths = [hidden // 4] * 4 + [features // 2]
    rows, feat = 2 * own, features // 2
    blocks = length // TILE // 2
    shape = jax.ShapeDtypeStruct
    outs = [shape((4, part, width), low) for width in widths] + [
        shape((4, 2, part, 3 * wide), low),
        shape((rows, feat), low),
        shape((rows, feat), low),
        shape((40, features), f32),
    ]
    every = [(ROWS, width) for width in widths] + [(2, 3 * wide)]
    return pl.pallas_call(
        functools.partial(backward_kernel, heads),
        out_shape=outs,
        in_specs=[IN_PLACE] * 3 + [IN_VMEM, IN_PLACE] * 2 + [IN_VMEM] * 2 + [IN_PLACE] * 5
        + [IN_VMEM] + [IN_PLACE] * 2 + [IN_VMEM],
        out_specs=[IN_VMEM] * len(outs),
        scratch_shapes=[pltpu.VMEM((2, ROWS, 4, part, width), low) for width in widths]
        + [pltpu.VMEM((ROWS, 4, part, width), low) for width in widths]
        + [pltpu.VMEM((2, lead, part, width), low) for lead, width in every]
        + [pltpu.VMEM((lead, part, width), low) for lead, width in every]
        + [pltpu.VMEM((3, part, width), low) for width in widths]
        + [
            pltpu.VMEM((ROWS, own, wide), low),
            pltpu.VMEM((heads, blocks, 2 * TILE, 2 * HEAD), low),
            pltpu.VMEM((heads, blocks, 1, TILE), f32),
            pltpu.VMEM((blocks, heads, HEAD, TILE), f32),
            pltpu.VMEM((heads, length, 2 * HEAD), f32),
            pltpu.VMEM((length, 3 * wide), low),
            pltpu.VMEM((3 * wide, length), low),
            pltpu.VMEM((3 * wide, features), low),
            pltpu.VMEM((3, features, own), low),
            pltpu.VMEM((length, 1), jnp.int32),
            pltpu.VMEM((ROWS, rows, features), low),
            pltpu.VMEM((ROWS, rows, feat), low),
            pltpu.VMEM((3, rows, feat), low),
            pltpu.VMEM((ROWS, 2, 2, part, 3 * wide), low),
            pltpu.VMEM((ROWS, 2, part, 3 * wide), low),
            pltpu.VMEM((2, 4, part, 3 * wide), low),
            pltpu.VMEM((2, 16, features), f32),
            pltpu.VMEM((16, features), f32),
            pltpu.VMEM((3, 16, features), f32),
            pltpu.VMEM((4, 8, features), f32),
            pltpu.VMEM((4, 8, features), f32),
        ]
        + [pltpu.VMEM(far.shape, far.dtype)
            for far in (w_heads, q, kv, kt, mixed, lse, x_all, grad_pre, activ, late)]
        + [
            pltpu.SemaphoreType.DMA((128,)),
            pltpu.SemaphoreType.DMA((128,)),
            pltpu.SemaphoreType.DMA((12,)),
        ],
        compiler_params=comm_params(2),
        name="backward_links",
    )(
        grad_blocks, output, late, stream, grad_pre, branch_two, activ, branch_one, context,
        q, kv, kt, mixed, lse, ids.reshape(1, -1), x_all, w_heads, vec,
    )


def put_lanes(target, value):
    for n in range(target.shape[0]):
        target[n : n + 1] = value[:, n * 128 : (n + 1) * 128]


def finish_kernel(
    heads, g1a, g1b, g2a, g2b, go, gq, x_in, out_in, vec,
    out, logits, grad_x, o_q, o_bq, o_k, o_v, o_bv, o_o, o_bo, o_g1, o_s1, far_1, o_b1, far_2, o_b2,
    o_g2, o_s2, far_p, o_bp, o_c, o_bc, o_1, o_2, o_p, sems,
):
    dp = lax.axis_index("dp")
    f32 = jnp.float32
    wide = heads * HEAD
    classes = logits.shape[1]
    depth, feat = o_q.shape
    part = g1a.shape[2]
    write_out = [
        pltpu.make_async_copy(near, far, sems.at[n])
        for n, (near, far) in enumerate(((o_p, far_p), (o_1, far_1), (o_2, far_2)))
    ]
    table = vec[8:40]
    table_t = table.T
    pooler = jnp.zeros(o_p.shape, f32)
    head = [jnp.zeros((1, 2 * feat), f32) for _ in range(classes)]
    total = jnp.zeros((1, 2 * feat), f32)
    ends = jnp.zeros((1, 128), f32)
    own_tail = jnp.zeros((1, 128), f32)
    for s in range(4):
        at = 8 * s
        slope, tail = table[at + 1 : at + 2], table[at + 3 : at + 4, :128]
        pooler = pooler + table_t[:, at : at + 1] * slope
        total = total + slope
        for n in range(classes):
            head[n] = head[n] + table[at + 2 : at + 3] * tail[:, classes + n : classes + n + 1]
        ends = ends + tail
        own_tail = jnp.where(dp == s, tail, own_tail)
    o_p[...] = pooler
    write_out[0].start()
    flat = lambda ref: ref[...].astype(f32).reshape(depth, ref.shape[2])
    for target, first, second in ((o_1, g1a, g1b), (o_2, g2a, g2b)):
        target[:, :part] = flat(first)
        target[:, part:] = flat(second)
        write_out[1 if target is o_1 else 2].start()
    out[...] = out_in[...]
    grad_x[...] = x_in[...]
    o_o[...] = flat(go)
    bias_q, bias_v = [], []
    for j in range(2):
        value = gq[:, j].astype(f32).reshape(depth, 3 * wide)
        o_q[:, j * wide : (j + 1) * wide] = value[:, 2 * wide :]
        for target, shift in ((o_k, 0), (o_v, HEAD)):
            target[:, j * wide : (j + 1) * wide] = jnp.concatenate(
                [value[:, 2 * h * HEAD + shift :][:, :HEAD] for h in range(heads)], axis=1
            )
        bias = vec[5 + j : 6 + j]
        bias_q.append(bias[:, 2 * wide : 3 * wide])
        bias_v += [bias[:, 2 * h * HEAD + HEAD :][:, :HEAD] for h in range(heads)]
    put_lanes(o_bq, jnp.concatenate(bias_q, axis=1))
    put_lanes(o_bv, jnp.concatenate(bias_v, axis=1))
    own = vec[:8]
    for n, target in enumerate((o_bo, o_g1, o_s1, o_b2, o_g2, o_s2)):
        put_lanes(target, own[n // 2 : n // 2 + 1, (n % 2) * feat : (n % 2 + 1) * feat])
    put_lanes(o_b1, jnp.concatenate([own[3:4], own[4:5]], axis=1))
    put_lanes(o_bp, total)
    o_c[...] = jnp.concatenate(head, axis=0)
    o_bc[...] = ends[:, classes : 2 * classes]
    logits[...] = own_tail[:, :classes]
    for copy in write_out:
        copy.wait()


def finish(pieces, classes, heads):
    g1a, g1b, g2a, g2b, go, gq, x_in, out_in, vec = pieces
    f32 = jnp.float32
    depth = go.shape[0] * go.shape[1]
    feat, hidden = go.shape[2], 2 * g1a.shape[2]
    features = vec.shape[1]
    shape = jax.ShapeDtypeStruct
    vector = lambda size: shape((size // 128, 128) if size % 128 == 0 else (1, size), f32)
    square = shape((depth, feat), f32)
    outs = [
        shape(out_in.shape, out_in.dtype), vector(classes), shape(x_in.shape, x_in.dtype),
        square, vector(feat), square, square, vector(feat), square, vector(feat), vector(feat),
        vector(feat), shape((depth, hidden), f32), vector(hidden), shape((depth, hidden), f32),
        vector(feat), vector(feat), vector(feat), shape((features, features), f32),
        vector(features), shape((classes, features), f32), vector(classes),
    ]
    return pl.pallas_call(
        functools.partial(finish_kernel, heads),
        out_shape=outs,
        in_specs=[IN_VMEM] * len(pieces),
        out_specs=[IN_PLACE if n in (12, 14, 18) else IN_VMEM for n in range(len(outs))],
        scratch_shapes=[pltpu.VMEM(outs[n].shape, f32) for n in (12, 14, 18)]
        + [pltpu.SemaphoreType.DMA((3,))],
        compiler_params=pltpu.CompilerParams(vmem_limit_bytes=VMEM_BYTES),
        name="finish",
    )(*pieces)


def norm_rows(hidden, gain, shift):
    row_mean = jnp.mean(hidden, axis=1, keepdims=True)
    row_var = jnp.mean(hidden * hidden, axis=1, keepdims=True) - row_mean * row_mean
    inv_scale = lax.rsqrt(row_var + epsilon)
    normed = (hidden - row_mean) * inv_scale
    return normed * gain + shift, normed, inv_scale


def norm_rows_back(grad, normed, inv_scale, gain):
    scaled = grad * gain
    first = jnp.mean(scaled, axis=1, keepdims=True)
    second = jnp.mean(scaled * normed, axis=1, keepdims=True)
    return inv_scale * (scaled - first - normed * second)


def fast_body(
    layer_input, cotangent, labels, block_ids, w_query, b_query, w_key, w_value, b_value,
    w_output, b_output, ln1_gain, ln1_bias, w_inner, b_inner, w_outer, b_outer,
    ln2_gain, ln2_bias, w_pooler, b_pooler, w_classes, b_classes,
):
    f32 = jnp.float32
    feat = layer_input.shape[1]
    heads = 2 * feat // HEAD // ROWS
    vectors = [
        b_query, b_value, b_output, ln1_gain, ln1_bias, b_outer, ln2_gain, ln2_bias, b_inner,
        b_pooler,
    ]
    count = sum(vector.shape[0] for vector in vectors) // feat
    padded, at = 0.0, 0
    full = (count + -count % 8) * feat
    for vector in vectors:
        size = vector.shape[0]
        padded = padded + jnp.pad(vector.astype(f32), (at, full - at - size))
        at += size
    (
        x_all, w_heads, q, kv, kt, mixed, lse, output, late, stream, grad_pre, branch_two, activ,
        branch_one, context, grad_blocks, packed,
    ) = forward_links(
        layer_input, cotangent, padded.reshape(-1, feat), w_query, w_key, w_value, block_ids, labels, w_classes,
        b_classes, w_pooler, [w_output.T, w_inner, w_outer.T],
    )
    s_1a, s_2a, s_1b, s_2b, s_wo, s_q, grad_input, output, sums = backward_links(
        grad_blocks, output, late, stream, grad_pre, branch_two, activ, branch_one, context,
        q, kv, kt, mixed, lse, block_ids, x_all, w_heads, packed,
    )
    outs = finish((s_1a, s_1b, s_2a, s_2b, s_wo, s_q, grad_input, output, sums), w_classes.shape[1], heads)
    flat = (4, 7, 9, 10, 11, 13, 15, 16, 17, 19, 21)
    turned = (8, 14, 20)
    return tuple(
        out.reshape(-1) if n in flat else out.T if n in turned else out
        for n, out in enumerate(outs)
    )


def is_fast(mesh):
    sizes = mesh.shape
    return sizes["dp"] == 4 and sizes["row"] == ROWS and sizes["col"] == 2


def solution(mesh):
    placed = (
        P(("dp", "row"), "col"),
        P(("dp", "row"), "col"),
        P("dp"),
        P("dp"),
        P("row", "col"),
        P("col"),
        P("row", "col"),
        P("row", "col"),
        P("col"),
        P("col", "row"),
        P("col"),
        P("col"),
        P("col"),
        P("row", "col"),
        P("col"),
        P("col", "row"),
        P("col"),
        P("col"),
        P("col"),
        P(),
        P(),
        P(),
        P(),
    )
    return jax.shard_map(
        fast_body if is_fast(mesh) else body,
        mesh=mesh,
        in_specs=placed,
        out_specs=(
            P(("dp", "row"), "col"),
            P("dp", None),
            P(("dp", "row"), "col"),
            P("row", "col"),
            P("col"),
            P("row", "col"),
            P("row", "col"),
            P("col"),
            P("col", "row"),
            P("col"),
            P("col"),
            P("col"),
            P("row", "col"),
            P("col"),
            P("col", "row"),
            P("col"),
            P("col"),
            P("col"),
            P(),
            P(),
            P(),
            P(),
        ),
        check_vma=False,
    )
```
